32 devices in a mesh: dp: 8 (over z, core), seq: 4 (over y, x).
Axes of the slice: x: 2, y: 2, z: 4, core: 2. Of those that a mesh axis runs over, the one named last changes fastest.
Arguments:
- char_ids: int32 [4, 8, 1024], P(None, 'dp', 'seq'), may hold values from 0 to 255
- targets: int32 [4, 8, 1024], P(None, 'dp', 'seq'), may hold values from 0 to 255
- seg_ids: int32 [4, 8, 1024], P(None, 'dp', 'seq'), may hold values from 0 to 255, as said below
- lengths: int32 [4, 8], P(None, 'dp'), may hold values from 512 to 1024
- owner_slot: int32 [26], replicated, may hold values from 0 to 39, as said below
- step_count: int32 [1], replicated, may hold values from 2 to 20
- master: float32 [40, 512, 512], P('seq', 'dp'), may hold values from -0.25 to 0.25
- tile_first: float32 [40, 512, 512], P('seq', 'dp'), may hold values from -3.0517578e-05 to 3.0517578e-05
- tile_second: float32 [40, 512, 512], P('seq', 'dp'), may hold values from 9.683462e-12 to 1.5405509e-10
- gain_rows: float32 [6, 512], replicated, may hold values from 0.5 to 1.5
- gain_first: float32 [6, 512], replicated, may hold values from -0.00030517578 to 0.00030517578
- gain_second: float32 [6, 512], replicated, may hold values from 9.683462e-10 to 1.5405508e-08
Outputs:
- loss_value: float32 [1], replicated
- grad_norm: float32 [1], replicated
- master_new: float32 [40, 512, 512], P('seq', 'dp')
- first_new: float32 [40, 512, 512], P('seq', 'dp')
- second_new: float32 [40, 512, 512], P('seq', 'dp')
- weights_low: bfloat16 [40, 512, 512], P('seq', 'dp')
- gains_new: float32 [6, 512], replicated
- gain_first_new: float32 [6, 512], replicated
- gain_second_new: float32 [6, 512], replicated
The draws below stay inside these ranges and needn't reach their ends.
Inputs may be any that keep to these rules, and one draw needn't show every extreme that they name: `seg_ids`: each segment number of a sequence appears, the numbers never fall along the sequence, and a segment has at most 16 characters. `owner_slot`: the 26 matrices have distinct slots; slot s belongs to seq index s // 10; one seq index holds 10 matrices, others fewer.
All inputs are finite; a program needn't handle non-finite values.
Results may differ from the reference program's by a relative error of at most 0.0008.
The reference program's roundings to bfloat16 on the way count: a program that leaves them out, or rounds other values in their place, can miss the bound.
Values may be sent and summed in bfloat16 or wider, within the bound.
A program may use at most 448 MiB of HBM per device.

```python
import math
import jax
import jax.numpy as jnp
import numpy as np
from jax import lax

D = 512
HEADS = 8
HD = 64
VOCAB = 256
NT = 26
NG = 6
MB = 4
L = 1024
SEG = 256
SEQS = 8
TCAP = 10
SLOTS = 40
N_SEQ = 4


def draw_owner_slot(key, part):
    folded = jax.random.fold_in(key, 11)
    first_key, second_key, third_key = jax.random.split(folded, 3)
    full_owner = jax.random.randint(first_key, (), 0, N_SEQ)
    own_block = full_owner * TCAP + jnp.arange(TCAP)
    others = jax.random.permutation(second_key, SLOTS - TCAP)
    others = others + TCAP * (others >= full_owner * TCAP).astype(jnp.int32)
    chosen = jnp.concatenate([own_block, others])[:NT]
    return chosen[jax.random.permutation(third_key, NT)].astype(jnp.int32)


def segment_row_draw(row_key):
    short_key, long_key, group_key, order_key = jax.random.split(row_key, 4)
    quarter = SEG // 4
    short_first = jax.random.randint(short_key, (quarter,), 1, 3).astype(jnp.int32)
    short_lengths = jnp.stack([short_first, 3 - short_first], axis=1).reshape(-1)
    long_first = jax.random.randint(long_key, (quarter,), 3, 11).astype(jnp.int32)
    long_lengths = jnp.stack([long_first, 13 - long_first], axis=1).reshape(-1)
    shift_value = jax.random.randint(group_key, (), 0, 4).astype(jnp.int32)
    group_lengths = jnp.array([16, 3, 3, 4], jnp.int32) + jnp.array([0, 0, 1, -1], jnp.int32) * shift_value
    long_lengths = jnp.concatenate([group_lengths, long_lengths[4:]])
    order_bit = jax.random.randint(order_key, (), 0, 2).astype(jnp.int32)
    dense_first = jnp.concatenate([short_lengths, long_lengths])
    sparse_first = jnp.concatenate([long_lengths, short_lengths])
    seg_lengths = jnp.where(order_bit == 1, dense_first, sparse_first)
    seg_ends = jnp.cumsum(seg_lengths).astype(jnp.int32)
    positions = jnp.arange(L, dtype=jnp.int32)
    return jnp.searchsorted(seg_ends, positions, side='right').astype(jnp.int32)


def draw_seg_ids(key, part):
    folded = jax.random.fold_in(key, 23)
    row_keys = jax.random.split(folded, MB * SEQS)
    rows = jax.vmap(segment_row_draw)(row_keys)
    return rows.reshape(MB, SEQS, L).astype(jnp.int32)


def plant(values, rng, least, top_value):
    longest = values.shape.index(max(values.shape))
    spots = []
    for shift in (0, 1):
        where = [jax.random.randint(jax.random.fold_in(rng, axis), (), 0, length) for axis, length in enumerate(values.shape)]
        where[longest] = (where[longest] + shift) % values.shape[longest]
        spots.append(tuple(where))
    return values.at[spots[0]].set(least).at[spots[1]].set(top_value)


def level_of(stream_key, shape, pieces, least, high):
    def one(axis_at, blocks):
        steps = jax.random.uniform(jax.random.fold_in(jax.random.fold_in(stream_key, 6), axis_at), (blocks,), jnp.float32, least / len(pieces), high / len(pieces))
        return jnp.repeat(jnp.exp(steps), shape[axis_at] // blocks).reshape((-1,) + (1,) * (len(shape) - axis_at - 1))

    factor_of = one(*pieces[0])
    for cut in pieces[1:]:
        factor_of = factor_of * one(*cut)
    return factor_of


def cumulative_ranks(amount, skew):
    weights = [(1 << 20) // math.isqrt(grade ** skew) + 1 for grade in range(1, amount + 1)]
    scale = 1 + sum(weights) // (1 << 30)
    return np.cumsum(np.array([max(1, weight // scale) for weight in weights]))


def ranked_ids(rng, shape, amount, lean):
    table = cumulative_ranks(amount, lean)
    ticket = jax.random.randint(jax.random.fold_in(rng, 1), shape, 0, int(table[amount - 1]))
    grade = jnp.searchsorted(jnp.asarray(table, jnp.int32), ticket, side="right")
    return jax.random.permutation(jax.random.fold_in(rng, 2), amount)[grade].astype(jnp.int32)


def gaussian(rng, dims, width, most, cuts=(), held_as=jnp.bfloat16):
    factor_of = level_of(rng, dims, cuts, -0.22, 0.18) if cuts else 1.0
    values = jax.random.normal(rng, dims, jnp.float32) * width * factor_of
    return jnp.minimum(jnp.maximum(values, -most), most).astype(held_as)


def setup_inputs(seed: int = 0) -> dict:
    key_of = jax.random.split(jax.random.key(seed), 13)
    char_ids = plant(ranked_ids(key_of[0], (MB, SEQS, L), VOCAB, 2), jax.random.fold_in(key_of[0], 3), 0, VOCAB - 1).astype(jnp.int32)
    targets = plant(ranked_ids(key_of[1], (MB, SEQS, L), VOCAB, 2), jax.random.fold_in(key_of[1], 3), 0, VOCAB - 1).astype(jnp.int32)
    seg_ids = draw_seg_ids(jax.random.fold_in(key_of[12], 71), 0)
    lengths = plant(jax.random.randint(key_of[3], (MB, SEQS), L // 2, L + 1), jax.random.fold_in(key_of[3], 1), L // 2, L).astype(jnp.int32)
    owner_slot = draw_owner_slot(jax.random.fold_in(key_of[12], 71), 0)
    step_count = jax.random.randint(key_of[5], (1,), 2, 21).astype(jnp.int32)
    master = gaussian(key_of[6], (SLOTS, D, D), D ** -0.5, 0.25, ((0, 4), (1, 8)), jnp.float32)
    tile_first = gaussian(key_of[7], (SLOTS, D, D), (0.0055 / (NT * D * D) ** 0.5), 3.0517578125e-05, ((0, 4), (1, 8)), jnp.float32)
    tile_second = jnp.clip(jnp.exp(math.log(1.5405508813071123e-10) - 2.7668907 * jax.random.uniform(key_of[8], (SLOTS, D, D), jnp.float32) ** level_of(key_of[8], (SLOTS, D, D), ((0, 4), (1, 8)), -0.2, 0.2)), 9.68346236529527e-12, 1.5405508813071123e-10)
    gain_rows = jnp.clip(1.0 + 0.1 * jax.random.normal(key_of[9], (NG, D), jnp.float32), 0.5, 1.5)
    gain_first = gaussian(key_of[10], (NG, D), (0.055 / (NT * D * D) ** 0.5), 0.00030517578, (), jnp.float32)
    gain_second = jnp.clip(jnp.exp(jax.random.uniform(key_of[11], (NG, D), jnp.float32, math.log(9.683461810183758e-10), math.log(1.5405507980403854e-08))), 9.683461810183758e-10, 1.5405507980403854e-08)
    return dict(char_ids=char_ids, targets=targets, seg_ids=seg_ids, lengths=lengths, owner_slot=owner_slot, step_count=step_count, master=master, tile_first=tile_first, tile_second=tile_second, gain_rows=gain_rows, gain_first=gain_first, gain_second=gain_second)


@jax.custom_vjp
def low(v):
    return lax.optimization_barrier(v.astype(jnp.bfloat16)).astype(jnp.float32)

@jax.custom_vjp
def low_back(v):
    return v

def low_keep(v):
    return (low(v), None)

def low_pass(kept, grad):
    return (grad,)

def back_keep(v):
    return (v, None)

def back_low(kept, grad):
    return (low(grad),)
low.defvjp(low_keep, low_pass)
low_back.defvjp(back_keep, back_low)
HIGHEST = lax.Precision.HIGHEST
BETA_ONE = 0.9
BETA_TWO = 0.95
ADAM_EPS = 1e-08
WEIGHT_DECAY = 0.1
RATE_TILES = 0.03
RATE_GAINS = 0.2
CLIP_NORM = 0.05
PRIOR_RATE = 0.25
NORM_EPS = 1e-06
MASKED = -1e+30

def matmul(left, right):
    return jnp.dot(left, right, precision=HIGHEST, preferred_element_type=jnp.float32)

def rms_norm(values, gain):
    return values * lax.rsqrt(lax.optimization_barrier(jnp.mean(values * values, axis=-1, keepdims=True)) + NORM_EPS) * gain

def split_heads(tensor):
    return tensor.reshape(tensor.shape[0], HEADS, HD).transpose(1, 0, 2)

def join_heads(tensor):
    return tensor.transpose(1, 0, 2).reshape(tensor.shape[1], HEADS * HD)

def attention(query, keys, values_in):
    length = query.shape[0]
    causal = jnp.arange(length)[:, None] >= jnp.arange(length)[None, :]
    factor = HD ** (-0.5)

    def one_head(triple):
        q_head, k_head, v_head = triple
        scores = low_back(matmul(q_head, k_head.T) * factor)
        scores = jnp.where(causal, scores, MASKED)
        weights = jax.nn.softmax(scores, axis=-1)
        return matmul(low(weights), v_head)
    heads_out = lax.map(jax.checkpoint(one_head), (split_heads(query), split_heads(keys), split_heads(values_in)))
    return join_heads(heads_out)

def block(hidden_in, tiles, gain_attn, gain_ffn):
    w_qkv = jnp.concatenate([tiles[0], tiles[1], tiles[2]], axis=1)
    w_up = jnp.concatenate([tiles[4], tiles[5], tiles[6], tiles[7]], axis=1)
    w_down = jnp.concatenate([tiles[8], tiles[9], tiles[10], tiles[11]], axis=0)
    normed = low(rms_norm(hidden_in, gain_attn))
    qkv_all = low(low_back(matmul(normed, w_qkv)))
    attended = low(low_back(attention(qkv_all[:, :D], qkv_all[:, D:2 * D], qkv_all[:, 2 * D:])))
    after_attn = hidden_in + low_back(matmul(attended, tiles[3]))
    inner = low_back(matmul(low(rms_norm(after_attn, gain_ffn)), w_up))
    return after_attn + low_back(matmul(low(jax.nn.gelu(inner)), w_down))

def sequence_terms(tiles, gain_rows, chars_row, target_row, segment_row, length_one):
    embed = tiles[25, :VOCAB]
    head_table = tiles[25, VOCAB:]
    start_hidden = embed[chars_row]
    char_out = block(start_hidden, tiles[0:12], gain_rows[0], gain_rows[1])
    char_low = low(char_out)
    boundary_pre = low_back(matmul(char_low, tiles[24]))
    boundary_hidden = jnp.tanh(boundary_pre)
    boundary_prob = jax.nn.sigmoid(lax.optimization_barrier(jnp.sum(boundary_hidden * gain_rows[5], axis=-1)) * D ** (-0.5))
    is_valid = (jnp.arange(L) < length_one).astype(jnp.float32)
    target_slot = segment_row + 1
    pooled_sums = jax.ops.segment_sum(char_low, target_slot, num_segments=SEG + 1)[:SEG]
    pooled_count = jax.ops.segment_sum(jnp.ones((L,), jnp.float32), target_slot, num_segments=SEG + 1)[:SEG]
    pooled = pooled_sums / jnp.maximum(pooled_count, 1.0)[:, None]
    segment_out = low(block(pooled, tiles[12:24], gain_rows[2], gain_rows[3]))
    merged = char_out + segment_out[segment_row]
    logits = low_back(matmul(low(rms_norm(merged, gain_rows[4])), head_table.T))
    log_total = jax.nn.logsumexp(logits, axis=-1)
    picked = jnp.take_along_axis(logits, target_row[:, None], axis=1)[:, 0]
    return (jnp.sum(is_valid * (log_total - picked)), jnp.sum(is_valid * boundary_prob))

def batch_loss(tiles, gain_rows, chars_batch, target_batch, segment_batch, length_batch):

    def per_sequence(bundle):
        return sequence_terms(tiles, gain_rows, bundle[0], bundle[1], bundle[2], bundle[3])
    ce_terms, boundary_terms = lax.map(jax.checkpoint(per_sequence), (chars_batch, target_batch, segment_batch, length_batch))
    count_all = jnp.sum(length_batch).astype(jnp.float32)
    soft_count = jnp.sum(boundary_terms)
    prior_term = -(lax.lgamma(count_all + 1.0) - lax.lgamma(soft_count + 1.0) - lax.lgamma(count_all - soft_count + 1.0) + soft_count * jnp.log(PRIOR_RATE) + (count_all - soft_count) * jnp.log(1.0 - PRIOR_RATE)) / count_all
    return (jnp.sum(ce_terms) / count_all + prior_term) / MB

def adam_step(param, moment_a, moment_b, grad_in, rate, decay, step_float):
    new_first = BETA_ONE * moment_a + (1.0 - BETA_ONE) * grad_in
    new_second = BETA_TWO * moment_b + (1.0 - BETA_TWO) * grad_in * grad_in
    first_hat = new_first / (1.0 - BETA_ONE ** step_float)
    second_hat = new_second / (1.0 - BETA_TWO ** step_float)
    updated = param - rate * (first_hat / (jnp.sqrt(second_hat) + ADAM_EPS) + decay * param)
    return (updated, new_first, new_second)

def reference(char_ids, targets, seg_ids, lengths, owner_slot, step_count, master, tile_first, tile_second, gain_rows, gain_first, gain_second):
    tile_values = master[owner_slot]
    tile_grads = jnp.zeros_like(tile_values)
    gain_grads = jnp.zeros_like(gain_rows)
    loss_sum = jnp.zeros((), jnp.float32)
    for micro in range(MB):

        def objective(tile_in, gain_in):
            return batch_loss(low(tile_in), gain_in, char_ids[micro], targets[micro], seg_ids[micro], lengths[micro])
        batch_value, pullback = jax.vjp(objective, tile_values, gain_rows)
        part_tiles, part_gains = pullback(jnp.ones_like(batch_value))
        tile_grads = tile_grads + part_tiles
        gain_grads = gain_grads + part_gains
        loss_sum = loss_sum + batch_value
    grad_norm = jnp.sqrt(jnp.sum(tile_grads * tile_grads) + jnp.sum(gain_grads * gain_grads))
    clip_factor = jnp.minimum(1.0, CLIP_NORM / (grad_norm + 1e-06))
    step_float = step_count[0].astype(jnp.float32)
    new_tiles, first_tiles, second_tiles = adam_step(tile_values, tile_first[owner_slot], tile_second[owner_slot], tile_grads * clip_factor, RATE_TILES, WEIGHT_DECAY, step_float)
    master_new = master.at[owner_slot].set(new_tiles)
    first_new = tile_first.at[owner_slot].set(first_tiles)
    second_new = tile_second.at[owner_slot].set(second_tiles)
    gains_new, gain_first_new, gain_second_new = adam_step(gain_rows, gain_first, gain_second, gain_grads * clip_factor, RATE_GAINS, 0.0, step_float)
    return (loss_sum.reshape(1), grad_norm.reshape(1), master_new, first_new, second_new, master_new.astype(jnp.bfloat16), gains_new, gain_first_new, gain_second_new)
```

```python
import jax
import jax.numpy as jnp
from jax import lax
from jax.sharding import PartitionSpec as P

HEADS = 8
SEG_DEV = 64


BETA_ONE = 0.9
BETA_TWO = 0.95
ADAM_EPS = 1e-08
WEIGHT_DECAY = 0.1
RATE_TILES = 0.03
RATE_GAINS = 0.2
CLIP_NORM = 0.05
PRIOR_RATE = 0.25
NORM_EPS = 1e-06
MASKED = -1e30


def product(left, right):
    return jnp.dot(left, right, preferred_element_type=jnp.float32)


def product_tn(left, right):
    return lax.dot_general(
        left, right, (((0,), (0,)), ((), ())), preferred_element_type=jnp.float32
    )


def product_nt(left, right):
    return lax.dot_general(
        left, right, (((1,), (1,)), ((), ())), preferred_element_type=jnp.float32
    )


def exact_tn(left, right):
    return lax.dot_general(
        left,
        right,
        (((0,), (0,)), ((), ())),
        precision=lax.Precision.HIGHEST,
        preferred_element_type=jnp.float32,
    )


def rms_norm(values, gain):
    return values * lax.rsqrt(jnp.mean(values * values, axis=-1, keepdims=True) + NORM_EPS) * gain


def split_heads(tensor):
    return tensor.reshape(tensor.shape[0], HEADS, tensor.shape[1] // HEADS).transpose(1, 0, 2)


def join_heads(tensor):
    return tensor.transpose(1, 0, 2).reshape(tensor.shape[1], tensor.shape[0] * tensor.shape[2])


def block_weights(tiles):
    w_qkv = jnp.concatenate([tiles[0], tiles[1], tiles[2]], axis=1)
    w_up = jnp.concatenate([tiles[4], tiles[5], tiles[6], tiles[7]], axis=1)
    w_down = jnp.concatenate([tiles[8], tiles[9], tiles[10], tiles[11]], axis=0)
    return (w_qkv, w_up, w_down)


def causal_mask(row_count, key_count):
    first_row = lax.axis_index("seq") * row_count
    return (first_row + jnp.arange(row_count))[:, None] >= jnp.arange(key_count)[None, :]


def block_forward(hidden_in, tiles, gain_attn, gain_ffn, segment):
    row_count, model_width = hidden_in.shape
    w_qkv, w_up, w_down = block_weights(tiles)
    normed = rms_norm(hidden_in, gain_attn).astype(jnp.bfloat16)
    qkv_low = product(normed, w_qkv).astype(jnp.bfloat16)
    if segment:
        gathered = lax.all_gather(qkv_low[:, model_width:], "seq", axis=0, tiled=True)
    else:
        gathered = lax.all_gather(qkv_low[:, model_width:], "seq", axis=0, tiled=True)
    allowed = causal_mask(row_count, gathered.shape[0])
    factor = (model_width // HEADS) ** (-0.5)

    def head_forward(triple):
        q_head, k_head, v_head = triple
        scores = jnp.where(allowed, product_nt(q_head, k_head) * factor, MASKED)
        peak = jnp.max(scores, axis=1, keepdims=True)
        log_total = peak + jnp.log(jnp.sum(jnp.exp(scores - peak), axis=1, keepdims=True))
        weights = jnp.exp(scores - log_total).astype(jnp.bfloat16)
        return (product(weights, v_head), log_total[:, 0])

    head_out, log_totals = lax.map(
        head_forward,
        (
            split_heads(qkv_low[:, :model_width]),
            split_heads(gathered[:, :model_width]),
            split_heads(gathered[:, model_width:]),
        ),
    )
    attended = join_heads(head_out).astype(jnp.bfloat16)
    after_attn = hidden_in + product(attended, tiles[3])
    inner = product(rms_norm(after_attn, gain_ffn).astype(jnp.bfloat16), w_up)
    block_out = after_attn + product(jax.nn.gelu(inner).astype(jnp.bfloat16), w_down)
    return (block_out, (hidden_in, qkv_low, gathered, log_totals, attended, after_attn, inner))


def block_backward(grad_out, saved, tiles, gain_attn, gain_ffn, segment):
    hidden_in, qkv_low, gathered, log_totals, attended, after_attn, inner = saved
    row_count, model_width = hidden_in.shape
    w_qkv, w_up, w_down = block_weights(tiles)
    grad_ffn = grad_out.astype(jnp.bfloat16)
    activated, gelu_pull = jax.vjp(jax.nn.gelu, inner)
    grad_down = product_tn(activated.astype(jnp.bfloat16), grad_ffn)
    grad_inner = gelu_pull(product_nt(grad_ffn, w_down))[0].astype(jnp.bfloat16)
    normed_ffn, ffn_pull = jax.vjp(rms_norm, after_attn, gain_ffn)
    grad_up = product_tn(normed_ffn.astype(jnp.bfloat16), grad_inner)
    grad_normed_in, grad_gain_ffn = ffn_pull(product_nt(grad_inner, w_up))
    grad_after = grad_out + grad_normed_in
    grad_branch = grad_after.astype(jnp.bfloat16)
    grad_wout = product_tn(attended, grad_branch)
    grad_attended = product_nt(grad_branch, tiles[3]).astype(jnp.bfloat16)
    allowed = causal_mask(row_count, gathered.shape[0])
    factor = (model_width // HEADS) ** (-0.5)

    def head_backward(bundle):
        q_head, k_head, v_head, upstream, log_head = bundle
        scores = jnp.where(allowed, product_nt(q_head, k_head) * factor, MASKED)
        weights = jnp.exp(scores - log_head[:, None])
        grad_values = product_tn(weights.astype(jnp.bfloat16), upstream)
        grad_weights = product_nt(upstream, v_head)
        inner_sum = jnp.sum(weights * grad_weights, axis=1, keepdims=True)
        grad_scores = (weights * (grad_weights - inner_sum)).astype(jnp.bfloat16)
        return (
            product(grad_scores, k_head) * factor,
            product_tn(grad_scores, q_head) * factor,
            grad_values,
        )

    grad_query, grad_keys, grad_values = lax.map(
        head_backward,
        (
            split_heads(qkv_low[:, :model_width]),
            split_heads(gathered[:, :model_width]),
            split_heads(gathered[:, model_width:]),
            split_heads(grad_attended),
            log_totals,
        ),
    )
    grad_kv_all = jnp.concatenate([join_heads(grad_keys), join_heads(grad_values)], axis=1)
    if segment:
        grad_kv = lax.psum_scatter(grad_kv_all, "seq", scatter_dimension=0, tiled=True)
    else:
        grad_kv = lax.psum_scatter(grad_kv_all, "seq", scatter_dimension=0, tiled=True)
    grad_qkv = jnp.concatenate([join_heads(grad_query), grad_kv], axis=1).astype(jnp.bfloat16)
    normed_attn, attn_pull = jax.vjp(rms_norm, hidden_in, gain_attn)
    grad_wqkv = product_tn(normed_attn.astype(jnp.bfloat16), grad_qkv)
    grad_normed_x, grad_gain_attn = attn_pull(product_nt(grad_qkv, w_qkv))
    grad_in = grad_after + grad_normed_x
    pieces = [
        grad_wqkv[:, part_index * model_width : (part_index + 1) * model_width]
        for part_index in range(3)
    ]
    pieces = pieces + [grad_wout]
    pieces = pieces + [
        grad_up[:, part_index * model_width : (part_index + 1) * model_width]
        for part_index in range(4)
    ]
    pieces = pieces + [
        grad_down[part_index * model_width : (part_index + 1) * model_width]
        for part_index in range(4)
    ]
    return (grad_in, jnp.stack(pieces), grad_gain_attn, grad_gain_ffn)


def micro_step(tiles, gain_rows, chars_row, target_row, segment_row, length_one, micro_count):
    char_count = chars_row.shape[0]
    model_width = tiles.shape[2]
    vocab_size = model_width // 2
    seq_count = lax.axis_size("seq")
    seg_total = SEG_DEV * seq_count
    position = lax.axis_index("seq") * char_count + jnp.arange(char_count)
    is_valid = (position < length_one).astype(jnp.float32)
    vocab_iota = jnp.arange(vocab_size)
    char_hot = chars_row[:, None] == vocab_iota[None, :]
    embed_low = tiles[25, :vocab_size]
    head_low = tiles[25, vocab_size:]
    start_hidden = product(char_hot.astype(jnp.bfloat16), embed_low)
    char_out, char_saved = block_forward(
        start_hidden, tiles[0:12], gain_rows[0], gain_rows[1], False
    )
    char_low = char_out.astype(jnp.bfloat16)
    boundary_hidden = jnp.tanh(product(char_low, tiles[24]))
    root_width = model_width ** (-0.5)
    boundary_prob = jax.nn.sigmoid(jnp.sum(boundary_hidden * gain_rows[5], axis=1) * root_width)
    slot_iota = jnp.arange(seg_total)
    pool_hot = segment_row[None, :] + 1 == slot_iota[:, None]
    lift_hot = segment_row[:, None] == slot_iota[None, :]
    part_sums = product(pool_hot.astype(jnp.bfloat16), char_low).reshape(
        seq_count, SEG_DEV, model_width
    )
    side_info = jnp.stack(
        [
            jnp.sum(pool_hot.astype(jnp.float32), axis=1),
            jnp.any(lift_hot, axis=0).astype(jnp.float32),
        ],
        axis=0,
    )
    side_info = side_info.reshape(2, seq_count, SEG_DEV).transpose(1, 0, 2)
    sums_in, side_in = (
        lax.all_to_all(part_sums, "seq", split_axis=0, concat_axis=0, tiled=True),
        lax.all_to_all(side_info, "seq", split_axis=0, concat_axis=0, tiled=True),
    )
    row_counts = jnp.sum(side_in[:, 0, :], axis=0)
    divisor = jnp.maximum(row_counts, 1.0)[:, None]
    pooled = jnp.sum(sums_in, axis=0) / divisor
    seg_out, seg_saved = block_forward(pooled, tiles[12:24], gain_rows[2], gain_rows[3], True)
    outgoing = side_in[:, 1, :, None].astype(jnp.bfloat16) * seg_out.astype(jnp.bfloat16)[None]
    returned = lax.all_to_all(outgoing, "seq", split_axis=0, concat_axis=0, tiled=True)
    merged = char_out + product(
        lift_hot.astype(jnp.bfloat16), returned.reshape(seg_total, model_width)
    )
    final_norm, final_pull = jax.vjp(rms_norm, merged, gain_rows[4])
    final_low = final_norm.astype(jnp.bfloat16)
    logits = product_nt(final_low, head_low)
    peak = jnp.max(logits, axis=1, keepdims=True)
    log_total = peak[:, 0] + jnp.log(jnp.sum(jnp.exp(logits - peak), axis=1))
    target_hot = (target_row[:, None] == vocab_iota[None, :]).astype(jnp.float32)
    picked = jnp.sum(logits * target_hot, axis=1)
    ce_local = jnp.sum(is_valid * (log_total - picked))
    ce_all, soft_count, count_all = lax.psum(
        (ce_local, jnp.sum(is_valid * boundary_prob), jnp.sum(is_valid)), ("dp", "seq")
    )
    weight_ce = is_valid / (micro_count * count_all)
    grad_logits = ((jnp.exp(logits - log_total[:, None]) - target_hot) * weight_ce[:, None]).astype(
        jnp.bfloat16
    )
    grad_head = product_tn(grad_logits, final_low)
    grad_merged, grad_gain_final = final_pull(product(grad_logits, head_low))
    grad_rows = exact_tn(lift_hot.astype(jnp.float32), grad_merged).reshape(
        seq_count, SEG_DEV, model_width
    )
    grad_seg = jnp.sum(
        lax.all_to_all(grad_rows, "seq", split_axis=0, concat_axis=0, tiled=True), axis=0
    )
    grad_pooled, seg_tiles, grad_gain_two, grad_gain_three = block_backward(
        grad_seg, seg_saved, tiles[12:24], gain_rows[2], gain_rows[3], True
    )
    grad_sums = (side_in[:, 0, :, None] > 0).astype(jnp.float32) * (grad_pooled / divisor)[None]
    grad_back = lax.all_to_all(grad_sums, "seq", split_axis=0, concat_axis=0, tiled=True).reshape(
        seg_total, model_width
    )
    grad_char = grad_merged + exact_tn(pool_hot.astype(jnp.float32), grad_back)
    prior_slope = (
        lax.digamma(soft_count + 1.0)
        - lax.digamma(count_all - soft_count + 1.0)
        - jnp.log(PRIOR_RATE)
        + jnp.log(1.0 - PRIOR_RATE)
    ) / (count_all * micro_count)
    grad_boundary_logit = is_valid * prior_slope * boundary_prob * (1.0 - boundary_prob)
    grad_gain_boundary = (
        jnp.sum(grad_boundary_logit[:, None] * boundary_hidden, axis=0) * root_width
    )
    grad_pre = (
        grad_boundary_logit[:, None]
        * gain_rows[5][None, :]
        * root_width
        * (1.0 - boundary_hidden * boundary_hidden)
    ).astype(jnp.bfloat16)
    grad_boundary = product_tn(char_low, grad_pre)
    grad_char = grad_char + product_nt(grad_pre, tiles[24])
    grad_start, char_tiles, grad_gain_zero, grad_gain_one = block_backward(
        grad_char, char_saved, tiles[0:12], gain_rows[0], gain_rows[1], False
    )
    grad_embed = exact_tn(char_hot.astype(jnp.float32), grad_start)
    tile_grads = jnp.concatenate(
        [
            char_tiles,
            seg_tiles,
            grad_boundary[None],
            jnp.concatenate([grad_embed, grad_head], axis=0)[None],
        ],
        axis=0,
    )
    gain_grads = jnp.stack(
        [
            grad_gain_zero,
            grad_gain_one,
            grad_gain_two,
            grad_gain_three,
            grad_gain_final,
            grad_gain_boundary,
        ]
    )
    prior_term = (
        -(
            lax.lgamma(count_all + 1.0)
            - lax.lgamma(soft_count + 1.0)
            - lax.lgamma(count_all - soft_count + 1.0)
            + soft_count * jnp.log(PRIOR_RATE)
            + (count_all - soft_count) * jnp.log(1.0 - PRIOR_RATE)
        )
        / count_all
    )
    return (tile_grads, gain_grads, (ce_all / count_all + prior_term) / micro_count)


def gather_tiles(master, owner_slot):
    shard_low = master.astype(jnp.bfloat16)
    full_rows = lax.all_gather(shard_low, "dp", axis=1, tiled=True)
    all_slots = lax.all_gather(full_rows, "seq", axis=0, tiled=True)
    return jnp.take(all_slots, owner_slot, axis=0)


def reduce_tiles(tile_grads, owner_slot, slot_count):
    placed = (
        jnp.zeros((slot_count,) + tile_grads.shape[1:], jnp.float32).at[owner_slot].set(tile_grads)
    )
    per_owner = lax.psum_scatter(placed, "seq", scatter_dimension=0, tiled=True)
    return lax.psum_scatter(per_owner, "dp", scatter_dimension=1, tiled=True)


def adam_step(param, moment_a, moment_b, grad_in, rate, decay, step_float):
    new_first = BETA_ONE * moment_a + (1.0 - BETA_ONE) * grad_in
    new_second = BETA_TWO * moment_b + (1.0 - BETA_TWO) * grad_in * grad_in
    first_hat = new_first / (1.0 - BETA_ONE**step_float)
    second_hat = new_second / (1.0 - BETA_TWO**step_float)
    updated = param - rate * (first_hat / (jnp.sqrt(second_hat) + ADAM_EPS) + decay * param)
    return (updated, new_first, new_second)


def attention_whole(qkv_low, model_width, head_width):
    length = qkv_low.shape[0]
    allowed = jnp.arange(length)[:, None] >= jnp.arange(length)[None, :]
    factor = head_width ** (-0.5)

    def head_forward(triple):
        q_head, k_head, v_head = triple
        scores = jnp.where(allowed, product_nt(q_head, k_head) * factor, MASKED)
        peak = jnp.max(scores, axis=1, keepdims=True)
        log_total = peak + jnp.log(jnp.sum(jnp.exp(scores - peak), axis=1, keepdims=True))
        weights = jnp.exp(scores - log_total).astype(jnp.bfloat16)
        return (product(weights, v_head), log_total[:, 0])

    head_out, log_totals = lax.map(
        head_forward,
        (
            split_heads(qkv_low[:, :model_width]),
            split_heads(qkv_low[:, model_width : 2 * model_width]),
            split_heads(qkv_low[:, 2 * model_width :]),
        ),
    )
    return (join_heads(head_out).astype(jnp.bfloat16), log_totals)


def attention_whole_back(qkv_low, grad_attended, log_totals, model_width, head_width):
    length = qkv_low.shape[0]
    allowed = jnp.arange(length)[:, None] >= jnp.arange(length)[None, :]
    factor = head_width ** (-0.5)

    def head_backward(bundle):
        q_head, k_head, v_head, upstream, log_head = bundle
        scores = jnp.where(allowed, product_nt(q_head, k_head) * factor, MASKED)
        weights = jnp.exp(scores - log_head[:, None])
        grad_values = product_tn(weights.astype(jnp.bfloat16), upstream)
        grad_weights = product_nt(upstream, v_head)
        inner_sum = jnp.sum(weights * grad_weights, axis=1, keepdims=True)
        grad_scores = (weights * (grad_weights - inner_sum)).astype(jnp.bfloat16)
        return (
            product(grad_scores, k_head) * factor,
            product_tn(grad_scores, q_head) * factor,
            grad_values,
        )

    grads = lax.map(
        head_backward,
        (
            split_heads(qkv_low[:, :model_width]),
            split_heads(qkv_low[:, model_width : 2 * model_width]),
            split_heads(qkv_low[:, 2 * model_width :]),
            split_heads(grad_attended),
            log_totals,
        ),
    )
    return jnp.concatenate([join_heads(piece) for piece in grads], axis=1).astype(jnp.bfloat16)


def whole_forward(hidden_in, tiles, gain_attn, gain_ffn):
    model_width = hidden_in.shape[1]
    head_width = model_width // HEADS
    w_qkv, w_up, w_down = block_weights(tiles)
    normed = rms_norm(hidden_in, gain_attn).astype(jnp.bfloat16)
    qkv_low = product(normed, w_qkv).astype(jnp.bfloat16)
    attended, log_totals = attention_whole(qkv_low, model_width, head_width)
    after_attn = hidden_in + product(attended, tiles[3])
    inner = product(rms_norm(after_attn, gain_ffn).astype(jnp.bfloat16), w_up)
    block_out = after_attn + product(jax.nn.gelu(inner).astype(jnp.bfloat16), w_down)
    return (block_out, (hidden_in, qkv_low, log_totals, attended, after_attn, inner))


def whole_backward(grad_out, saved, tiles, gain_attn, gain_ffn):
    hidden_in, qkv_low, log_totals, attended, after_attn, inner = saved
    model_width = hidden_in.shape[1]
    head_width = model_width // HEADS
    w_qkv, w_up, w_down = block_weights(tiles)
    grad_ffn = grad_out.astype(jnp.bfloat16)
    activated, gelu_pull = jax.vjp(jax.nn.gelu, inner)
    grad_down = product_tn(activated.astype(jnp.bfloat16), grad_ffn)
    grad_inner = gelu_pull(product_nt(grad_ffn, w_down))[0].astype(jnp.bfloat16)
    normed_ffn, ffn_pull = jax.vjp(rms_norm, after_attn, gain_ffn)
    grad_up = product_tn(normed_ffn.astype(jnp.bfloat16), grad_inner)
    grad_normed_in, grad_gain_ffn = ffn_pull(product_nt(grad_inner, w_up))
    grad_after = grad_out + grad_normed_in
    grad_branch = grad_after.astype(jnp.bfloat16)
    grad_wout = product_tn(attended, grad_branch)
    grad_attended = product_nt(grad_branch, tiles[3]).astype(jnp.bfloat16)
    grad_qkv = attention_whole_back(qkv_low, grad_attended, log_totals, model_width, head_width)
    normed_attn, attn_pull = jax.vjp(rms_norm, hidden_in, gain_attn)
    grad_wqkv = product_tn(normed_attn.astype(jnp.bfloat16), grad_qkv)
    grad_normed_x, grad_gain_attn = attn_pull(product_nt(grad_qkv, w_qkv))
    grad_in = grad_after + grad_normed_x
    pieces = [grad_wqkv[:, i * model_width : (i + 1) * model_width] for i in range(3)]
    pieces = pieces + [grad_wout]
    pieces = pieces + [grad_up[:, i * model_width : (i + 1) * model_width] for i in range(4)]
    pieces = pieces + [grad_down[i * model_width : (i + 1) * model_width] for i in range(4)]
    return (grad_in, pieces, grad_gain_attn, grad_gain_ffn)


def gather_tiles_whole(master, owner_slot):
    shard_low = master.astype(jnp.bfloat16)
    all_slots = lax.all_gather(shard_low, "seq", axis=0, tiled=True)
    picked = jnp.take(all_slots, owner_slot, axis=0)
    return lax.all_gather(picked, "dp", axis=1, tiled=True)


def reduce_tiles_whole(tile_grads, owner_slot, slot_count):
    rows_own = lax.psum_scatter(tile_grads, "dp", scatter_dimension=1, tiled=True)
    hot = (jnp.arange(slot_count)[:, None] == owner_slot[None, :])
    source = jnp.sum(jnp.where(hot, jnp.arange(owner_slot.shape[0])[None, :], 0), axis=1)
    owned = jnp.any(hot, axis=1)[:, None, None]
    placed = jnp.where(owned, jnp.take(rows_own, source, axis=0), 0.0)
    return lax.psum_scatter(placed, "seq", scatter_dimension=0, tiled=True)


def whole_step(char_ids, targets, seg_ids, lengths, owner_slot, master, gain_rows):
    micro_count = char_ids.shape[0]
    seq_count = lax.axis_size("seq")
    seq_me = lax.axis_index("seq")
    model_width = master.shape[2]
    vocab_size = model_width // 2
    seg_total = SEG_DEV * seq_count
    ids = jnp.stack([char_ids[:, 0], targets[:, 0], seg_ids[:, 0]], axis=1)
    ids = lax.all_to_all(ids, "seq", split_axis=0, concat_axis=2, tiled=True)[0]
    chars_row, target_row, segment_row = ids[0], ids[1], ids[2]
    length_one = lax.dynamic_index_in_dim(lengths[:, 0], seq_me, keepdims=False)
    tiles = gather_tiles_whole(master, owner_slot)
    char_count = chars_row.shape[0]
    is_valid = (jnp.arange(char_count) < length_one).astype(jnp.float32)
    vocab_iota = jnp.arange(vocab_size)
    char_hot = chars_row[:, None] == vocab_iota[None, :]
    embed_low = tiles[25, :vocab_size]
    head_low = tiles[25, vocab_size:]
    start_hidden = product(char_hot.astype(jnp.bfloat16), embed_low)
    char_out, char_saved = whole_forward(start_hidden, tiles[0:12], gain_rows[0], gain_rows[1])
    char_low = char_out.astype(jnp.bfloat16)
    boundary_hidden = jnp.tanh(product(char_low, tiles[24]))
    root_width = model_width ** (-0.5)
    boundary_prob = jax.nn.sigmoid(jnp.sum(boundary_hidden * gain_rows[5], axis=1) * root_width)
    soft_count, count_all = lax.psum(
        (jnp.sum(is_valid * boundary_prob), length_one.astype(jnp.float32)), "dp"
    )
    slot_iota = jnp.arange(seg_total)
    pool_hot = segment_row[None, :] + 1 == slot_iota[:, None]
    lift_hot = segment_row[:, None] == slot_iota[None, :]
    row_counts = jnp.sum(pool_hot.astype(jnp.float32), axis=1)
    divisor = jnp.maximum(row_counts, 1.0)[:, None]
    pooled = product(pool_hot.astype(jnp.bfloat16), char_low) / divisor
    seg_out, seg_saved = whole_forward(pooled, tiles[12:24], gain_rows[2], gain_rows[3])
    merged = char_out + product(lift_hot.astype(jnp.bfloat16), seg_out.astype(jnp.bfloat16))
    final_norm, final_pull = jax.vjp(rms_norm, merged, gain_rows[4])
    final_low = final_norm.astype(jnp.bfloat16)
    logits = product_nt(final_low, head_low)
    peak = jnp.max(logits, axis=1, keepdims=True)
    log_total = peak[:, 0] + jnp.log(jnp.sum(jnp.exp(logits - peak), axis=1))
    target_hot = (target_row[:, None] == vocab_iota[None, :]).astype(jnp.float32)
    picked = jnp.sum(logits * target_hot, axis=1)
    ce_local = jnp.sum(is_valid * (log_total - picked))
    weight_ce = is_valid / (micro_count * count_all)
    grad_logits = ((jnp.exp(logits - log_total[:, None]) - target_hot) * weight_ce[:, None]).astype(
        jnp.bfloat16
    )
    grad_head = product_tn(grad_logits, final_low)
    grad_merged, grad_gain_final = final_pull(product(grad_logits, head_low))
    grad_seg = exact_tn(lift_hot.astype(jnp.float32), grad_merged)
    grad_pooled, seg_pieces, grad_gain_two, grad_gain_three = whole_backward(
        grad_seg, seg_saved, tiles[12:24], gain_rows[2], gain_rows[3]
    )
    grad_char = grad_merged + exact_tn(pool_hot.astype(jnp.float32), grad_pooled / divisor)
    prior_slope = (
        lax.digamma(soft_count + 1.0)
        - lax.digamma(count_all - soft_count + 1.0)
        - jnp.log(PRIOR_RATE)
        + jnp.log(1.0 - PRIOR_RATE)
    ) / (count_all * micro_count)
    grad_boundary_logit = is_valid * prior_slope * boundary_prob * (1.0 - boundary_prob)
    grad_gain_boundary = (
        jnp.sum(grad_boundary_logit[:, None] * boundary_hidden, axis=0) * root_width
    )
    grad_pre = (
        grad_boundary_logit[:, None]
        * gain_rows[5][None, :]
        * root_width
        * (1.0 - boundary_hidden * boundary_hidden)
    ).astype(jnp.bfloat16)
    grad_boundary = product_tn(char_low, grad_pre)
    grad_char = grad_char + product_nt(grad_pre, tiles[24])
    grad_start, char_pieces, grad_gain_zero, grad_gain_one = whole_backward(
        grad_char, char_saved, tiles[0:12], gain_rows[0], gain_rows[1]
    )
    grad_embed = exact_tn(char_hot.astype(jnp.float32), grad_start)
    tile_grads = jnp.stack(
        char_pieces
        + seg_pieces
        + [grad_boundary, jnp.concatenate([grad_embed, grad_head], axis=0)]
    )
    gain_grads = jnp.stack(
        [
            grad_gain_zero,
            grad_gain_one,
            grad_gain_two,
            grad_gain_three,
            grad_gain_final,
            grad_gain_boundary,
        ]
    )
    prior_term = (
        -(
            lax.lgamma(count_all + 1.0)
            - lax.lgamma(soft_count + 1.0)
            - lax.lgamma(count_all - soft_count + 1.0)
            + soft_count * jnp.log(PRIOR_RATE)
            + (count_all - soft_count) * jnp.log(1.0 - PRIOR_RATE)
        )
        / count_all
    )
    loss_part = (ce_local / count_all + prior_term / lax.axis_size("dp")) / micro_count
    return (tile_grads, gain_grads, loss_part)


def body(
    char_ids,
    targets,
    seg_ids,
    lengths,
    owner_slot,
    step_count,
    master,
    tile_first,
    tile_second,
    gain_rows,
    gain_first,
    gain_second,
):
    micro_count = char_ids.shape[0]
    model_width = master.shape[2]
    slot_count = master.shape[0] * lax.axis_size("seq")
    if micro_count == lax.axis_size("seq"):
        tile_grads, gain_part, loss_part = whole_step(
            char_ids, targets, seg_ids, lengths, owner_slot, master, gain_rows
        )
        shard_total = reduce_tiles_whole(tile_grads, owner_slot, slot_count)
        gain_sum, square_sum, loss_total = lax.psum(
            (gain_part, jnp.sum(shard_total * shard_total), loss_part), ("dp", "seq")
        )
    else:
        tile_total = jnp.zeros((owner_slot.shape[0], model_width, model_width), jnp.float32)
        gain_total = jnp.zeros_like(gain_rows)
        loss_total = jnp.zeros((), jnp.float32)
        for micro in range(micro_count):
            tiles = gather_tiles(master, owner_slot)
            tile_part, gain_part, loss_part = micro_step(
                tiles,
                gain_rows,
                char_ids[micro, 0],
                targets[micro, 0],
                seg_ids[micro, 0],
                lengths[micro, 0],
                micro_count,
            )
            tile_total = tile_total + tile_part
            gain_total = gain_total + gain_part
            loss_total = loss_total + loss_part
        shard_total = reduce_tiles(tile_total, owner_slot, slot_count)
        gain_sum, square_sum = lax.psum((gain_total, jnp.sum(shard_total * shard_total)), ("dp", "seq"))
    grad_norm = jnp.sqrt(square_sum + jnp.sum(gain_sum * gain_sum))
    clip_factor = jnp.minimum(1.0, CLIP_NORM / (grad_norm + 1e-06))
    step_float = step_count[0].astype(jnp.float32)
    local_ids = lax.axis_index("seq") * master.shape[0] + jnp.arange(master.shape[0])
    owned = jnp.any(local_ids[:, None] == owner_slot[None, :], axis=1)[:, None, None]
    new_tiles, new_first, new_second = adam_step(
        master,
        tile_first,
        tile_second,
        shard_total * clip_factor,
        RATE_TILES,
        WEIGHT_DECAY,
        step_float,
    )
    master_new = jnp.where(owned, new_tiles, master)
    first_new = jnp.where(owned, new_first, tile_first)
    second_new = jnp.where(owned, new_second, tile_second)
    gains_new, gain_first_new, gain_second_new = adam_step(
        gain_rows, gain_first, gain_second, gain_sum * clip_factor, RATE_GAINS, 0.0, step_float
    )
    return (
        loss_total.reshape(1),
        grad_norm.reshape(1),
        master_new,
        first_new,
        second_new,
        master_new.astype(jnp.bfloat16),
        gains_new,
        gain_first_new,
        gain_second_new,
    )


def solution(mesh):
    return jax.shard_map(
        body,
        mesh=mesh,
        in_specs=(
            P(None, "dp", "seq"),
            P(None, "dp", "seq"),
            P(None, "dp", "seq"),
            P(None, "dp"),
            P(),
            P(),
            P("seq", "dp", None),
            P("seq", "dp", None),
            P("seq", "dp", None),
            P(),
            P(),
            P(),
        ),
        out_specs=(
            P(),
            P(),
            P("seq", "dp", None),
            P("seq", "dp", None),
            P("seq", "dp", None),
            P("seq", "dp", None),
            P(),
            P(),
            P(),
        ),
        check_vma=False,
    )
```

```python
import functools

import jax
import jax.numpy as jnp
from jax import lax
from jax.experimental import pallas as pl
from jax.experimental.pallas import tpu as pltpu
from jax.sharding import PartitionSpec as P

HEADS = 8
SEG_DEV = 64


BETA_ONE = 0.9
BETA_TWO = 0.95
ADAM_EPS = 1e-08
WEIGHT_DECAY = 0.1
RATE_TILES = 0.03
RATE_GAINS = 0.2
CLIP_NORM = 0.05
PRIOR_RATE = 0.25
NORM_EPS = 1e-06
MASKED = -1e30


def product(left, right):
    return jnp.dot(left, right, preferred_element_type=jnp.float32)


def product_tn(left, right):
    return lax.dot_general(
        left, right, (((0,), (0,)), ((), ())), preferred_element_type=jnp.float32
    )


def product_nt(left, right):
    return lax.dot_general(
        left, right, (((1,), (1,)), ((), ())), preferred_element_type=jnp.float32
    )


def exact_tn(left, right):
    return lax.dot_general(
        left,
        right,
        (((0,), (0,)), ((), ())),
        precision=lax.Precision.HIGHEST,
        preferred_element_type=jnp.float32,
    )


def rms_norm(values, gain):
    return values * lax.rsqrt(jnp.mean(values * values, axis=-1, keepdims=True) + NORM_EPS) * gain


def split_heads(tensor):
    return tensor.reshape(tensor.shape[0], HEADS, tensor.shape[1] // HEADS).transpose(1, 0, 2)


def join_heads(tensor):
    return tensor.transpose(1, 0, 2).reshape(tensor.shape[1], tensor.shape[0] * tensor.shape[2])


def block_weights(tiles):
    w_qkv = jnp.concatenate([tiles[0], tiles[1], tiles[2]], axis=1)
    w_up = jnp.concatenate([tiles[4], tiles[5], tiles[6], tiles[7]], axis=1)
    w_down = jnp.concatenate([tiles[8], tiles[9], tiles[10], tiles[11]], axis=0)
    return (w_qkv, w_up, w_down)


def causal_mask(row_count, key_count):
    first_row = lax.axis_index("seq") * row_count
    return (first_row + jnp.arange(row_count))[:, None] >= jnp.arange(key_count)[None, :]


def block_forward(hidden_in, tiles, gain_attn, gain_ffn, segment):
    row_count, model_width = hidden_in.shape
    w_qkv, w_up, w_down = block_weights(tiles)
    normed = rms_norm(hidden_in, gain_attn).astype(jnp.bfloat16)
    qkv_low = product(normed, w_qkv).astype(jnp.bfloat16)
    if segment:
        gathered = lax.all_gather(qkv_low[:, model_width:], "seq", axis=0, tiled=True)
    else:
        gathered = lax.all_gather(qkv_low[:, model_width:], "seq", axis=0, tiled=True)
    allowed = causal_mask(row_count, gathered.shape[0])
    factor = (model_width // HEADS) ** (-0.5)

    def head_forward(triple):
        q_head, k_head, v_head = triple
        scores = jnp.where(allowed, product_nt(q_head, k_head) * factor, MASKED)
        peak = jnp.max(scores, axis=1, keepdims=True)
        log_total = peak + jnp.log(jnp.sum(jnp.exp(scores - peak), axis=1, keepdims=True))
        weights = jnp.exp(scores - log_total).astype(jnp.bfloat16)
        return (product(weights, v_head), log_total[:, 0])

    head_out, log_totals = lax.map(
        head_forward,
        (
            split_heads(qkv_low[:, :model_width]),
            split_heads(gathered[:, :model_width]),
            split_heads(gathered[:, model_width:]),
        ),
    )
    attended = join_heads(head_out).astype(jnp.bfloat16)
    after_attn = hidden_in + product(attended, tiles[3])
    inner = product(rms_norm(after_attn, gain_ffn).astype(jnp.bfloat16), w_up)
    block_out = after_attn + product(jax.nn.gelu(inner).astype(jnp.bfloat16), w_down)
    return (block_out, (hidden_in, qkv_low, gathered, log_totals, attended, after_attn, inner))


def block_backward(grad_out, saved, tiles, gain_attn, gain_ffn, segment):
    hidden_in, qkv_low, gathered, log_totals, attended, after_attn, inner = saved
    row_count, model_width = hidden_in.shape
    w_qkv, w_up, w_down = block_weights(tiles)
    grad_ffn = grad_out.astype(jnp.bfloat16)
    activated, gelu_pull = jax.vjp(jax.nn.gelu, inner)
    grad_down = product_tn(activated.astype(jnp.bfloat16), grad_ffn)
    grad_inner = gelu_pull(product_nt(grad_ffn, w_down))[0].astype(jnp.bfloat16)
    normed_ffn, ffn_pull = jax.vjp(rms_norm, after_attn, gain_ffn)
    grad_up = product_tn(normed_ffn.astype(jnp.bfloat16), grad_inner)
    grad_normed_in, grad_gain_ffn = ffn_pull(product_nt(grad_inner, w_up))
    grad_after = grad_out + grad_normed_in
    grad_branch = grad_after.astype(jnp.bfloat16)
    grad_wout = product_tn(attended, grad_branch)
    grad_attended = product_nt(grad_branch, tiles[3]).astype(jnp.bfloat16)
    allowed = causal_mask(row_count, gathered.shape[0])
    factor = (model_width // HEADS) ** (-0.5)

    def head_backward(bundle):
        q_head, k_head, v_head, upstream, log_head = bundle
        scores = jnp.where(allowed, product_nt(q_head, k_head) * factor, MASKED)
        weights = jnp.exp(scores - log_head[:, None])
        grad_values = product_tn(weights.astype(jnp.bfloat16), upstream)
        grad_weights = product_nt(upstream, v_head)
        inner_sum = jnp.sum(weights * grad_weights, axis=1, keepdims=True)
        grad_scores = (weights * (grad_weights - inner_sum)).astype(jnp.bfloat16)
        return (
            product(grad_scores, k_head) * factor,
            product_tn(grad_scores, q_head) * factor,
            grad_values,
        )

    grad_query, grad_keys, grad_values = lax.map(
        head_backward,
        (
            split_heads(qkv_low[:, :model_width]),
            split_heads(gathered[:, :model_width]),
            split_heads(gathered[:, model_width:]),
            split_heads(grad_attended),
            log_totals,
        ),
    )
    grad_kv_all = jnp.concatenate([join_heads(grad_keys), join_heads(grad_values)], axis=1)
    if segment:
        grad_kv = lax.psum_scatter(grad_kv_all, "seq", scatter_dimension=0, tiled=True)
    else:
        grad_kv = lax.psum_scatter(grad_kv_all, "seq", scatter_dimension=0, tiled=True)
    grad_qkv = jnp.concatenate([join_heads(grad_query), grad_kv], axis=1).astype(jnp.bfloat16)
    normed_attn, attn_pull = jax.vjp(rms_norm, hidden_in, gain_attn)
    grad_wqkv = product_tn(normed_attn.astype(jnp.bfloat16), grad_qkv)
    grad_normed_x, grad_gain_attn = attn_pull(product_nt(grad_qkv, w_qkv))
    grad_in = grad_after + grad_normed_x
    pieces = [
        grad_wqkv[:, part_index * model_width : (part_index + 1) * model_width]
        for part_index in range(3)
    ]
    pieces = pieces + [grad_wout]
    pieces = pieces + [
        grad_up[:, part_index * model_width : (part_index + 1) * model_width]
        for part_index in range(4)
    ]
    pieces = pieces + [
        grad_down[part_index * model_width : (part_index + 1) * model_width]
        for part_index in range(4)
    ]
    return (grad_in, jnp.stack(pieces), grad_gain_attn, grad_gain_ffn)


def micro_step(tiles, gain_rows, chars_row, target_row, segment_row, length_one, micro_count):
    char_count = chars_row.shape[0]
    model_width = tiles.shape[2]
    vocab_size = model_width // 2
    seq_count = lax.axis_size("seq")
    seg_total = SEG_DEV * seq_count
    position = lax.axis_index("seq") * char_count + jnp.arange(char_count)
    is_valid = (position < length_one).astype(jnp.float32)
    vocab_iota = jnp.arange(vocab_size)
    char_hot = chars_row[:, None] == vocab_iota[None, :]
    embed_low = tiles[25, :vocab_size]
    head_low = tiles[25, vocab_size:]
    start_hidden = product(char_hot.astype(jnp.bfloat16), embed_low)
    char_out, char_saved = block_forward(
        start_hidden, tiles[0:12], gain_rows[0], gain_rows[1], False
    )
    char_low = char_out.astype(jnp.bfloat16)
    boundary_hidden = jnp.tanh(product(char_low, tiles[24]))
    root_width = model_width ** (-0.5)
    boundary_prob = jax.nn.sigmoid(jnp.sum(boundary_hidden * gain_rows[5], axis=1) * root_width)
    slot_iota = jnp.arange(seg_total)
    pool_hot = segment_row[None, :] + 1 == slot_iota[:, None]
    lift_hot = segment_row[:, None] == slot_iota[None, :]
    part_sums = product(pool_hot.astype(jnp.bfloat16), char_low).reshape(
        seq_count, SEG_DEV, model_width
    )
    side_info = jnp.stack(
        [
            jnp.sum(pool_hot.astype(jnp.float32), axis=1),
            jnp.any(lift_hot, axis=0).astype(jnp.float32),
        ],
        axis=0,
    )
    side_info = side_info.reshape(2, seq_count, SEG_DEV).transpose(1, 0, 2)
    sums_in, side_in = (
        lax.all_to_all(part_sums, "seq", split_axis=0, concat_axis=0, tiled=True),
        lax.all_to_all(side_info, "seq", split_axis=0, concat_axis=0, tiled=True),
    )
    row_counts = jnp.sum(side_in[:, 0, :], axis=0)
    divisor = jnp.maximum(row_counts, 1.0)[:, None]
    pooled = jnp.sum(sums_in, axis=0) / divisor
    seg_out, seg_saved = block_forward(pooled, tiles[12:24], gain_rows[2], gain_rows[3], True)
    outgoing = side_in[:, 1, :, None].astype(jnp.bfloat16) * seg_out.astype(jnp.bfloat16)[None]
    returned = lax.all_to_all(outgoing, "seq", split_axis=0, concat_axis=0, tiled=True)
    merged = char_out + product(
        lift_hot.astype(jnp.bfloat16), returned.reshape(seg_total, model_width)
    )
    final_norm, final_pull = jax.vjp(rms_norm, merged, gain_rows[4])
    final_low = final_norm.astype(jnp.bfloat16)
    logits = product_nt(final_low, head_low)
    peak = jnp.max(logits, axis=1, keepdims=True)
    log_total = peak[:, 0] + jnp.log(jnp.sum(jnp.exp(logits - peak), axis=1))
    target_hot = (target_row[:, None] == vocab_iota[None, :]).astype(jnp.float32)
    picked = jnp.sum(logits * target_hot, axis=1)
    ce_local = jnp.sum(is_valid * (log_total - picked))
    ce_all, soft_count, count_all = lax.psum(
        (ce_local, jnp.sum(is_valid * boundary_prob), jnp.sum(is_valid)), ("dp", "seq")
    )
    weight_ce = is_valid / (micro_count * count_all)
    grad_logits = ((jnp.exp(logits - log_total[:, None]) - target_hot) * weight_ce[:, None]).astype(
        jnp.bfloat16
    )
    grad_head = product_tn(grad_logits, final_low)
    grad_merged, grad_gain_final = final_pull(product(grad_logits, head_low))
    grad_rows = exact_tn(lift_hot.astype(jnp.float32), grad_merged).reshape(
        seq_count, SEG_DEV, model_width
    )
    grad_seg = jnp.sum(
        lax.all_to_all(grad_rows, "seq", split_axis=0, concat_axis=0, tiled=True), axis=0
    )
    grad_pooled, seg_tiles, grad_gain_two, grad_gain_three = block_backward(
        grad_seg, seg_saved, tiles[12:24], gain_rows[2], gain_rows[3], True
    )
    grad_sums = (side_in[:, 0, :, None] > 0).astype(jnp.float32) * (grad_pooled / divisor)[None]
    grad_back = lax.all_to_all(grad_sums, "seq", split_axis=0, concat_axis=0, tiled=True).reshape(
        seg_total, model_width
    )
    grad_char = grad_merged + exact_tn(pool_hot.astype(jnp.float32), grad_back)
    prior_slope = (
        lax.digamma(soft_count + 1.0)
        - lax.digamma(count_all - soft_count + 1.0)
        - jnp.log(PRIOR_RATE)
        + jnp.log(1.0 - PRIOR_RATE)
    ) / (count_all * micro_count)
    grad_boundary_logit = is_valid * prior_slope * boundary_prob * (1.0 - boundary_prob)
    grad_gain_boundary = (
        jnp.sum(grad_boundary_logit[:, None] * boundary_hidden, axis=0) * root_width
    )
    grad_pre = (
        grad_boundary_logit[:, None]
        * gain_rows[5][None, :]
        * root_width
        * (1.0 - boundary_hidden * boundary_hidden)
    ).astype(jnp.bfloat16)
    grad_boundary = product_tn(char_low, grad_pre)
    grad_char = grad_char + product_nt(grad_pre, tiles[24])
    grad_start, char_tiles, grad_gain_zero, grad_gain_one = block_backward(
        grad_char, char_saved, tiles[0:12], gain_rows[0], gain_rows[1], False
    )
    grad_embed = exact_tn(char_hot.astype(jnp.float32), grad_start)
    tile_grads = jnp.concatenate(
        [
            char_tiles,
            seg_tiles,
            grad_boundary[None],
            jnp.concatenate([grad_embed, grad_head], axis=0)[None],
        ],
        axis=0,
    )
    gain_grads = jnp.stack(
        [
            grad_gain_zero,
            grad_gain_one,
            grad_gain_two,
            grad_gain_three,
            grad_gain_final,
            grad_gain_boundary,
        ]
    )
    prior_term = (
        -(
            lax.lgamma(count_all + 1.0)
            - lax.lgamma(soft_count + 1.0)
            - lax.lgamma(count_all - soft_count + 1.0)
            + soft_count * jnp.log(PRIOR_RATE)
            + (count_all - soft_count) * jnp.log(1.0 - PRIOR_RATE)
        )
        / count_all
    )
    return (tile_grads, gain_grads, (ce_all / count_all + prior_term) / micro_count)


def gather_tiles(master, owner_slot):
    shard_low = master.astype(jnp.bfloat16)
    full_rows = lax.all_gather(shard_low, "dp", axis=1, tiled=True)
    all_slots = lax.all_gather(full_rows, "seq", axis=0, tiled=True)
    return jnp.take(all_slots, owner_slot, axis=0)


def reduce_tiles(tile_grads, owner_slot, slot_count):
    placed = (
        jnp.zeros((slot_count,) + tile_grads.shape[1:], jnp.float32).at[owner_slot].set(tile_grads)
    )
    per_owner = lax.psum_scatter(placed, "seq", scatter_dimension=0, tiled=True)
    return lax.psum_scatter(per_owner, "dp", scatter_dimension=1, tiled=True)


def adam_step(param, moment_a, moment_b, grad_in, rate, decay, step_float):
    new_first = BETA_ONE * moment_a + (1.0 - BETA_ONE) * grad_in
    new_second = BETA_TWO * moment_b + (1.0 - BETA_TWO) * grad_in * grad_in
    first_hat = new_first / (1.0 - BETA_ONE**step_float)
    second_hat = new_second / (1.0 - BETA_TWO**step_float)
    updated = param - rate * (first_hat / (jnp.sqrt(second_hat) + ADAM_EPS) + decay * param)
    return (updated, new_first, new_second)


MESH = pl.DeviceIdType.MESH
VMEM_LIMIT = 60 * 1024 * 1024


def remote(src, dst, send_sem, recv_sem, peer):
    return pltpu.make_async_remote_copy(
        src_ref=src, dst_ref=dst, send_sem=send_sem, recv_sem=recv_sem, device_id=peer, device_id_type=MESH
    )


def places():
    dp = lax.axis_index("dp")
    seq = lax.axis_index("seq")
    return dp, seq, dp // 2, dp % 2


def seq_peer(seq, step):
    return ((seq // 2 + step // 2) % 2) * 2 + (seq % 2 + step % 2) % 2


def meet(peers):
    barrier = pltpu.get_barrier_semaphore()
    for peer in peers:
        pl.semaphore_signal(barrier, inc=1, device_id=peer, device_id_type=MESH)
    pl.semaphore_wait(barrier, len(peers))


def gather_kernel(
    chunks, slot_ref, low_ref, ids_ref, full_ref, ids_out, slots, own, x_send, x_recv, own_sem,
    n_send, n_recv, f_send, f_recv, c_send, c_recv, i_send, i_recv, i_own,
):
    dp, seq, z, core = places()
    held, rows, _ = low_ref.shape
    tile_count = full_ref.shape[0]
    half = tile_count // 2
    step_rows = rows // chunks
    sibling = (z * 2 + 1 - core, seq)
    up, down = ((z + 1) % 4 * 2 + core, seq), ((z + 3) % 4 * 2 + core, seq)
    side = [(dp, seq_peer(seq, j)) for j in (1, 2, 3)]
    meet([sibling, up, down] + side)

    def rows_of(owner_z, chunk):
        return pl.ds(pl.multiple_of((owner_z * 2 + core) * rows + chunk * step_rows, step_rows), step_rows)

    def part(chunk):
        return pl.ds(chunk * step_rows, step_rows)

    side_copies = []
    for chunk in range(chunks):
        for j in range(3):
            copy = remote(
                low_ref.at[:, part(chunk)], slots[chunk].at[pl.ds(held * seq, held)],
                x_send.at[chunk, j], x_recv.at[chunk, j], side[j],
            )
            copy.start()
            side_copies.append(copy)
        for j in range(3):
            if chunk == 0:
                copy = remote(
                    ids_ref.at[side[j][1]], ids_out.at[seq], i_send.at[j], i_recv.at[j], side[j]
                )
                copy.start()
                side_copies.append(copy)
        slots[chunk][pl.ds(held * seq, held)] = low_ref[:, part(chunk), :]
    ids_copy = pltpu.make_async_copy(ids_ref.at[seq], ids_out.at[seq], i_own)
    ids_copy.start()

    def near(chunk):
        for j in range(3):
            remote(
                low_ref.at[:, part(chunk)], slots[chunk].at[pl.ds(held * seq, held)],
                x_send.at[chunk, j], x_recv.at[chunk, j], side[j],
            ).wait_recv()

        def pick(tile, carry):
            own[chunk, tile] = slots[chunk][slot_ref[tile]]
            return carry

        lax.fori_loop(0, tile_count, pick, 0)
        place = full_ref.at[:, rows_of(z, chunk)]
        for way, peer in enumerate((up, down)):
            copy = remote(own.at[chunk], place, n_send.at[chunk, way], n_recv.at[chunk, way], peer)
            copy.start()
        copy = remote(own.at[chunk], place, c_send.at[chunk, 0], c_recv.at[chunk, 0], sibling)
        copy.start()
        copy = pltpu.make_async_copy(own.at[chunk], place, own_sem.at[chunk])
        copy.start()

    def far(chunk):
        for way, peer in enumerate((up, down)):
            origin = (z + 3) % 4 if way == 0 else (z + 1) % 4
            place = full_ref.at[:, rows_of(origin, chunk)]
            remote(own.at[chunk], place, n_send.at[chunk, way], n_recv.at[chunk, way], peer).wait_recv()
            portion = full_ref.at[pl.ds(way * half, half), rows_of(origin, chunk)]
            copy = remote(portion, portion, f_send.at[chunk, way], f_recv.at[chunk, way], peer)
            copy.start()
            copy = remote(place, place, c_send.at[chunk, 1 + way], c_recv.at[chunk, 1 + way], sibling)
            copy.start()

    def last(chunk):
        for way, peer in enumerate((up, down)):
            portion = full_ref.at[pl.ds(way * half, half), rows_of((z + 2) % 4, chunk)]
            remote(portion, portion, f_send.at[chunk, way], f_recv.at[chunk, way], peer).wait_recv()
            copy = remote(portion, portion, c_send.at[chunk, 3 + way], c_recv.at[chunk, 3 + way], sibling)
            copy.start()

    for tick in range(chunks + 2):
        if tick < chunks:
            near(tick)
        if 0 <= tick - 1 < chunks:
            far(tick - 1)
        if 0 <= tick - 2 < chunks:
            last(tick - 2)
    for copy in side_copies:
        copy.wait_send()
    for j in range(3):
        remote(ids_ref.at[side[j][1]], ids_out.at[seq], i_send.at[j], i_recv.at[j], side[j]).wait_recv()
    ids_copy.wait()
    for chunk in range(chunks):
        place = full_ref.at[:, rows_of(z, chunk)]
        for way, peer in enumerate((up, down)):
            remote(own.at[chunk], place, n_send.at[chunk, way], n_recv.at[chunk, way], peer).wait_send()
            portion = full_ref.at[pl.ds(way * half, half), rows_of(z, chunk)]
            remote(portion, portion, f_send.at[chunk, way], f_recv.at[chunk, way], peer).wait_send()
        pltpu.make_async_copy(own.at[chunk], place, own_sem.at[chunk]).wait()
        for turn in range(5):
            piece = full_ref.at[:, rows_of(z, chunk)] if turn < 3 else full_ref.at[pl.ds(0, half), rows_of(z, chunk)]
            remote(piece, piece, c_send.at[chunk, turn], c_recv.at[chunk, turn], sibling).wait()


def gather_tiles_kernel(low, ids, owner_slot):
    held, rows, width = low.shape
    tile_count = owner_slot.shape[0]
    seq_count, dp_count = lax.axis_size("seq"), lax.axis_size("dp")
    chunks = 4
    step_rows = rows // chunks
    dma = pltpu.SemaphoreType.DMA
    return pl.pallas_call(
        functools.partial(gather_kernel, chunks),
        out_shape=(
            jax.ShapeDtypeStruct((tile_count, dp_count * rows, width), low.dtype),
            jax.ShapeDtypeStruct(ids.shape, ids.dtype),
        ),
        in_specs=[
            pl.BlockSpec(memory_space=pltpu.SMEM),
            pl.BlockSpec(memory_space=pltpu.VMEM),
            pl.BlockSpec(memory_space=pltpu.VMEM),
        ],
        out_specs=(pl.BlockSpec(memory_space=pl.ANY), pl.BlockSpec(memory_space=pltpu.VMEM)),
        scratch_shapes=[
            [pltpu.VMEM((seq_count * held, step_rows, width), low.dtype)] * chunks,
            pltpu.VMEM((chunks, tile_count, step_rows, width), low.dtype),
            dma((chunks, 3)), dma((chunks, 3)), dma((chunks,)),
            dma((chunks, 2)), dma((chunks, 2)), dma((chunks, 2)), dma((chunks, 2)),
            dma((chunks, 5)), dma((chunks, 5)), dma((3,)), dma((3,)), dma,
        ],
        name="gather_tiles",
        compiler_params=pltpu.CompilerParams(
            collective_id=0, has_side_effects=True, vmem_limit_bytes=VMEM_LIMIT
        ),
    )(owner_slot, low, ids)


CODE_TOP = 32000.0
ROUNDER = 12582912.0


def encode(value):
    upper, lower = value[0:8, :], value[8:16, :]
    size = jnp.maximum(jnp.abs(upper), jnp.abs(lower))
    most = jnp.maximum(jnp.max(size, axis=1, keepdims=True), 1e-30)
    ratio = CODE_TOP / most
    coded = jnp.concatenate([upper * ratio, lower * ratio], axis=0)
    coded = ((coded + ROUNDER) - ROUNDER).astype(jnp.int32).astype(jnp.int16)
    return coded, most * (1.0 / CODE_TOP)


def decode(coded, unit):
    value = coded.astype(jnp.int32).astype(jnp.float32)
    return jnp.concatenate([value[0:8, :] * unit, value[8:16, :] * unit], axis=0)


def reduce_kernel(
    source_ref, valid_ref, grads_ref, small_ref, out_ref, small_out, square_out,
    own, other, b1_out, b1_in, b2_out, b2_in, c_out, c_in, d_out, d_in,
    b1_unit_out, b1_unit_in, b2_unit_out, b2_unit_in, c_unit_out, c_unit_in, d_unit_out, d_unit_in,
    final, small_dp, small_seq, square_dp, square_seq,
    l_sem, a_send, a_recv, b1_send, b1_recv, b2_send, b2_recv, c_send, c_recv, d_send, d_recv,
    p_send, p_recv, q_send, q_recv, r_send, r_recv, s_send, s_recv,
):
    dp, seq, z, core = places()
    across, along = seq % 2, seq // 2
    held = out_ref.shape[0]
    tile_count = grads_ref.shape[0]
    pairs = tile_count // 2
    sibling = (z * 2 + 1 - core, seq)
    beside = [(dp, along * 2 + 1 - across), (dp, (1 - along) * 2 + across)]
    side = [(dp, seq_peer(seq, j)) for j in (1, 2, 3)]
    column = [((dp + j) % 8, seq) for j in range(1, 8)]
    tower = [((z + j) % 4 * 2 + core, seq) for j in (1, 2, 3)]
    meet(side + column)
    lane = lax.broadcasted_iota(jnp.int32, (8, 128), 1)

    def core_copy(pair):
        two = pl.ds(pair * 2, 2)
        return remote(grads_ref.at[two, :, 1 - core], other.at[two], a_send.at[pair], a_recv.at[pair], sibling)

    def local_copy(pair):
        two = pl.ds(pair * 2, 2)
        return pltpu.make_async_copy(grads_ref.at[two, :, core], own.at[two], l_sem.at[pair])

    def with_units(values, units, send, recv, peer):
        return [
            remote(values[0], values[1], send.at[0], recv.at[0], peer),
            remote(units[0], units[1], send.at[1], recv.at[1], peer),
        ]

    def first_copies(pair, order):
        tile = pair * 2 + order
        return with_units(
            (b1_out.at[tile], b1_in.at[tile]), (b1_unit_out.at[tile], b1_unit_in.at[tile]),
            b1_send.at[tile], b1_recv.at[tile], beside[order],
        )

    def second_copies(pair, order):
        tile = pair * 2 + order
        return with_units(
            (b2_out.at[tile], b2_in.at[tile]), (b2_unit_out.at[tile], b2_unit_in.at[tile]),
            b2_send.at[tile], b2_recv.at[tile], beside[1 - order],
        )

    def tower_copies(pair, j):
        two = pl.ds(pair * 2, 2)
        return with_units(
            (c_out.at[j, two], c_in.at[j, two]), (c_unit_out.at[j, pair], c_unit_in.at[j, pair]),
            c_send.at[j, pair], c_recv.at[j, pair], tower[j],
        )

    def share_copies(pair, j):
        two = pl.ds(pair * 2, 2)
        return with_units(
            (d_out.at[two], d_in.at[j, two]), (d_unit_out.at[pair], d_unit_in.at[j, pair]),
            d_send.at[j, pair], d_recv.at[j, pair], side[j],
        )

    def start_all(copies):
        for copy in copies:
            copy.start()

    def arrive_all(copies):
        for copy in copies:
            copy.wait_recv()

    def sent_all(copies):
        for copy in copies:
            copy.wait_send()

    def small_copy(j):
        return remote(small_ref, small_dp.at[dp], p_send.at[j], p_recv.at[j], column[j])

    def small_side(j):
        return remote(small_seq.at[seq], small_seq.at[seq], q_send.at[j], q_recv.at[j], side[j])

    def square_copy(j):
        return remote(square_dp.at[dp], square_dp.at[dp], r_send.at[j], r_recv.at[j], column[j])

    def square_side(j):
        return remote(square_seq.at[seq], square_seq.at[seq], s_send.at[j], s_recv.at[j], side[j])

    for j in range(7):
        small_copy(j).start()

    def launch(pair, carry):
        core_copy(pair).start()
        local_copy(pair).start()
        return carry

    lax.fori_loop(0, pairs, launch, 0)

    def cell(tile, order, floor, line, mine):
        if order == 0:
            return (tile, floor, line, across if mine else 1 - across)
        return (tile, floor, along if mine else 1 - along, line)

    def stage_one(pair):
        core_copy(pair).wait_recv()
        local_copy(pair).wait()

        def add(step, carry):
            tile, floor = pair * 2 + step // 4, step % 4
            own[tile, floor] = own[tile, floor] + other[tile, floor]
            return carry

        lax.fori_loop(0, 8, add, 0)
        for order in range(2):
            tile = pair * 2 + order
            units = jnp.zeros((8, 128), jnp.float32)
            for floor in range(4):
                for line in range(2):
                    coded, unit = encode(own[cell(tile, order, floor, line, False)])
                    b1_out[tile, floor * 2 + line] = coded
                    units = jnp.where(lane == floor * 2 + line, unit, units)
            b1_unit_out[tile] = units
            start_all(first_copies(pair, order))

    def stage_two(pair):
        for order in range(2):
            tile = pair * 2 + order
            arrive_all(first_copies(pair, order))
            got = b1_unit_in[tile]
            units = jnp.zeros((8, 128), jnp.float32)
            keep = along if order == 0 else across
            for floor in range(4):
                for line in range(2):
                    block = floor * 2 + line
                    spot = cell(tile, order, floor, line, True)
                    own[spot] = own[spot] + decode(b1_in[tile, block], got[:, block : block + 1])
                spot = cell(tile, order, floor, 1 - keep, True)
                coded, unit = encode(own[spot])
                b2_out[tile, floor] = coded
                units = jnp.where(lane == floor, unit, units)
            b2_unit_out[tile] = units
            start_all(second_copies(pair, order))

    def stage_three(pair):
        for order in range(2):
            tile = pair * 2 + order
            arrive_all(second_copies(pair, order))
            got = b2_unit_in[tile]
            for floor in range(4):
                spot = (tile, floor, along, across)
                own[spot] = own[spot] + decode(b2_in[tile, floor], got[:, floor : floor + 1])
        for j in range(3):
            units = jnp.zeros((8, 128), jnp.float32)
            for order in range(2):
                tile = pair * 2 + order
                coded, unit = encode(own[tile, (z + j + 1) % 4, along, across])
                c_out[j, tile] = coded
                units = jnp.where(lane == order, unit, units)
            c_unit_out[j, pair] = units
            start_all(tower_copies(pair, j))

    def stage_four(pair):
        for j in range(3):
            arrive_all(tower_copies(pair, j))
        units = jnp.zeros((8, 128), jnp.float32)
        for order in range(2):
            tile = pair * 2 + order
            total = own[tile, z, along, across]
            for j in range(3):
                total = total + decode(c_in[j, tile], c_unit_in[j, pair][:, order : order + 1])
            final[tile, seq] = total
            coded, unit = encode(total)
            d_out[tile] = coded
            units = jnp.where(lane == order, unit, units)
        d_unit_out[pair] = units
        for j in range(3):
            start_all(share_copies(pair, j))

    def stage_five(pair):
        for j in range(3):
            arrive_all(share_copies(pair, j))
            for order in range(2):
                tile = pair * 2 + order
                final[tile, side[j][1]] = decode(d_in[j, tile], d_unit_in[j, pair][:, order : order + 1])

    stages = (stage_one, stage_two, stage_three, stage_four, stage_five)
    lag = 2

    def tick(step, carry):
        for number, stage in enumerate(stages):
            pair = step - lag * number

            @pl.when(jnp.logical_and(pair >= 0, pair < pairs))
            def _():
                stage(pair)

        return carry

    lax.fori_loop(0, 4, tick, 0)
    small_dp[dp] = small_ref[...]
    for j in range(7):
        small_copy(j).wait_recv()
    total = small_dp[0]
    for j in range(1, 8):
        total = total + small_dp[j]
    small_seq[seq] = total
    for j in range(3):
        small_side(j).start()
    lax.fori_loop(4, pairs + lag * 4, tick, 0)

    def collect(slot, square):
        keep = valid_ref[slot] > 0
        for quarter in range(4):
            value = final[source_ref[slot], quarter]
            value = jnp.where(keep, value, jnp.zeros_like(value))
            out_ref[slot, quarter * 16 : quarter * 16 + 16, :] = value
            square = square + value * value
        return square

    square = lax.fori_loop(0, held, collect, jnp.zeros((16, out_ref.shape[2]), jnp.float32))
    folded = square[0:8, 0:128]
    for r in range(2):
        for w in range(out_ref.shape[2] // 128):
            if r or w:
                folded = folded + square[8 * r : 8 * r + 8, 128 * w : 128 * w + 128]
    square_dp[dp] = folded
    for j in range(7):
        square_copy(j).start()
    for j in range(3):
        small_side(j).wait_recv()
    small_out[...] = (small_seq[0] + small_seq[1]) + (small_seq[2] + small_seq[3])
    for j in range(7):
        square_copy(j).wait_recv()
    total = square_dp[0]
    for j in range(1, 8):
        total = total + square_dp[j]
    square_seq[seq] = total
    for j in range(3):
        square_side(j).start()
    for j in range(3):
        square_side(j).wait_recv()
    square_out[...] = (square_seq[0] + square_seq[1]) + (square_seq[2] + square_seq[3])
    for j in range(7):
        small_copy(j).wait_send()
        square_copy(j).wait_send()
    for j in range(3):
        small_side(j).wait_send()
        square_side(j).wait_send()

    def drain(pair, carry):
        core_copy(pair).wait_send()
        for order in range(2):
            sent_all(first_copies(pair, order))
            sent_all(second_copies(pair, order))
        for j in range(3):
            sent_all(tower_copies(pair, j))
            sent_all(share_copies(pair, j))
        return carry

    lax.fori_loop(0, pairs, drain, 0)


def reduce_tiles_kernel(grads, small, source, valid, held):
    tile_count, height, width = grads.shape
    seq_count, dp_count = lax.axis_size("seq"), lax.axis_size("dp")
    rows = height // dp_count
    pairs = tile_count // 2
    dma = pltpu.SemaphoreType.DMA
    vmem = pl.BlockSpec(memory_space=pltpu.VMEM)
    smem = pl.BlockSpec(memory_space=pltpu.SMEM)

    def buffer(*shape):
        return pltpu.VMEM(shape, jnp.float32)

    def codes(*shape):
        return pltpu.VMEM(shape + (16, width), jnp.int16)

    return pl.pallas_call(
        reduce_kernel,
        out_shape=(
            jax.ShapeDtypeStruct((held, rows, width), jnp.float32),
            jax.ShapeDtypeStruct(small.shape, jnp.float32),
            jax.ShapeDtypeStruct((8, 128), jnp.float32),
        ),
        in_specs=[smem, smem, pl.BlockSpec(memory_space=pl.ANY), vmem],
        out_specs=(vmem, vmem, vmem),
        scratch_shapes=[
            buffer(tile_count, 4, 2, 2, 16, width),
            buffer(tile_count, 4, 2, 2, 16, width),
            codes(tile_count, 8), codes(tile_count, 8),
            codes(tile_count, 4), codes(tile_count, 4),
            codes(3, tile_count), codes(3, tile_count),
            codes(tile_count), codes(3, tile_count),
            buffer(tile_count, 8, 128), buffer(tile_count, 8, 128),
            buffer(tile_count, 8, 128), buffer(tile_count, 8, 128),
            buffer(3, pairs, 8, 128), buffer(3, pairs, 8, 128),
            buffer(pairs, 8, 128), buffer(3, pairs, 8, 128),
            buffer(tile_count, 4, 16, width),
            buffer(dp_count, *small.shape),
            buffer(seq_count, *small.shape),
            buffer(dp_count, 8, 128),
            buffer(seq_count, 8, 128),
            dma((pairs,)), dma((pairs,)), dma((pairs,)),
            dma((tile_count, 2)), dma((tile_count, 2)), dma((tile_count, 2)), dma((tile_count, 2)),
            dma((3, pairs, 2)), dma((3, pairs, 2)), dma((3, pairs, 2)), dma((3, pairs, 2)),
            dma((7,)), dma((7,)), dma((3,)), dma((3,)), dma((7,)), dma((7,)), dma((3,)), dma((3,)),
        ],
        name="reduce_tiles",
        compiler_params=pltpu.CompilerParams(
            collective_id=1, has_side_effects=True, vmem_limit_bytes=VMEM_LIMIT
        ),
    )(source, valid, grads.reshape(tile_count, 4, 2, 2, 2, 16, width), small)


def column_kernel(value_ref, out_ref, gathered, send, recv):
    dp, seq, _, _ = places()
    column = [((dp + j) % 8, seq) for j in range(1, 8)]
    meet(column)
    gathered[dp] = value_ref[...]
    copies = [
        remote(value_ref, gathered.at[dp], send.at[j], recv.at[j], column[j]) for j in range(7)
    ]
    for copy in copies:
        copy.start()
    for copy in copies:
        copy.wait()
    total = gathered[0]
    for j in range(1, 8):
        total = total + gathered[j]
    out_ref[...] = total


def column_sum(value):
    vmem = pl.BlockSpec(memory_space=pltpu.VMEM)
    return pl.pallas_call(
        column_kernel,
        out_shape=jax.ShapeDtypeStruct(value.shape, value.dtype),
        in_specs=[vmem],
        out_specs=vmem,
        scratch_shapes=[
            pltpu.VMEM((lax.axis_size("dp"),) + value.shape, value.dtype),
            pltpu.SemaphoreType.DMA((7,)),
            pltpu.SemaphoreType.DMA((7,)),
        ],
        name="column_sum",
        compiler_params=pltpu.CompilerParams(collective_id=2, has_side_effects=True),
    )(value)


def head_mask(shape, head):
    lane = lax.broadcasted_iota(jnp.int32, shape, 1)
    return (lane >= 64) if head else (lane < 64)


def scores_t(k_pair, q_head, first_row):
    scores = product_nt(k_pair, q_head)
    count, queries = scores.shape
    key = lax.broadcasted_iota(jnp.int32, (queries, queries), 0)
    query = lax.broadcasted_iota(jnp.int32, (queries, queries), 1)
    own = jnp.where(key <= query, scores[first_row:], MASKED)
    return own if first_row == 0 else jnp.concatenate([scores[:first_row], own], axis=0)


def attention_forward_kernel(q_ref, k_ref, v_ref, out_ref, log_ref, turned):
    length, lanes = q_ref.shape
    step = 256
    factor = (lanes // 2) ** (-0.5)
    turned[...] = v_ref[...].astype(jnp.float32).T.astype(jnp.bfloat16)
    for first in range(0, length, step):
        q_pair = q_ref[first : first + step, :] * jnp.asarray(factor, jnp.bfloat16)
        pieces = []
        for head in range(2):
            q_head = jnp.where(head_mask(q_pair.shape, head), q_pair, jnp.zeros_like(q_pair))
            scores = scores_t(k_ref[: first + step, :], q_head, first)
            peak = jnp.max(scores, axis=0, keepdims=True)
            raised = jnp.exp(scores - peak)
            total = jnp.sum(raised, axis=0, keepdims=True)
            weights = (raised * (1.0 / total)).astype(jnp.bfloat16)
            log_ref[0, head : head + 1, first : first + step] = peak + jnp.log(total)
            pieces.append(product(turned[64 * head : 64 * head + 64, : first + step], weights))
        out_ref[first : first + step, :] = jnp.concatenate(pieces, axis=0).T.astype(out_ref.dtype)


def attention_backward_kernel(q_ref, k_ref, v_ref, up_ref, log_ref, dq_ref, dk_ref, dv_ref, turned, dk_sum, dv_sum):
    length, lanes = q_ref.shape
    step = 256
    factor = (lanes // 2) ** (-0.5)
    turned[...] = k_ref[...].astype(jnp.float32).T.astype(jnp.bfloat16)
    for first in reversed(range(0, length, step)):
        span = first + step
        q_pair = q_ref[first:span, :] * jnp.asarray(factor, jnp.bfloat16)
        up_pair = up_ref[first:span, :]
        queries, keys, values = [], [], []
        for head in range(2):
            keep = head_mask(q_pair.shape, head)
            q_head = jnp.where(keep, q_pair, jnp.zeros_like(q_pair))
            up_head = jnp.where(keep, up_pair, jnp.zeros_like(up_pair))
            scores = scores_t(k_ref[:span, :], q_head, first)
            weights = jnp.exp(scores - log_ref[0, head : head + 1, first:span])
            grad_weights = product_nt(v_ref[:span, :], up_head)
            values.append(product(weights.astype(jnp.bfloat16), up_head))
            inner_sum = jnp.sum(weights * grad_weights, axis=0, keepdims=True)
            grad_scores = (weights * (grad_weights - inner_sum)).astype(jnp.bfloat16)
            keys.append(product(grad_scores, q_head))
            queries.append(product(turned[64 * head : 64 * head + 64, :span], grad_scores))
        dq_ref[first:span, :] = (jnp.concatenate(queries, axis=0).T * factor).astype(dq_ref.dtype)
        grad_key = keys[0] + keys[1]
        grad_value = values[0] + values[1]
        if span == length:
            dk_sum[...] = grad_key
            dv_sum[...] = grad_value
        else:
            dk_sum[:span, :] = dk_sum[:span, :] + grad_key
            dv_sum[:span, :] = dv_sum[:span, :] + grad_value
    dk_ref[...] = dk_sum[...].astype(dk_ref.dtype)
    dv_ref[...] = dv_sum[...].astype(dv_ref.dtype)


def attention_specs(length, lanes, pairs):
    return [pl.BlockSpec((length, lanes), lambda p, j=j: (0, j * pairs + p)) for j in range(3)]


def attention_whole(qkv_low, model_width, head_width):
    length = qkv_low.shape[0]
    lanes = 2 * head_width
    pairs = model_width // lanes
    return pl.pallas_call(
        attention_forward_kernel,
        out_shape=(
            jax.ShapeDtypeStruct((length, model_width), jnp.bfloat16),
            jax.ShapeDtypeStruct((pairs, 2, length), jnp.float32),
        ),
        grid=(pairs,),
        in_specs=attention_specs(length, lanes, pairs),
        out_specs=(
            pl.BlockSpec((length, lanes), lambda p: (0, p)),
            pl.BlockSpec((1, 2, length), lambda p: (p, 0, 0)),
        ),
        scratch_shapes=[pltpu.VMEM((lanes, length), jnp.bfloat16)],
        name="attention_forward",
        compiler_params=pltpu.CompilerParams(vmem_limit_bytes=VMEM_LIMIT),
    )(qkv_low, qkv_low, qkv_low)


def attention_whole_back(qkv_low, grad_attended, log_totals, model_width, head_width):
    length = qkv_low.shape[0]
    lanes = 2 * head_width
    pairs = model_width // lanes
    grads = pl.pallas_call(
        attention_backward_kernel,
        out_shape=tuple(jax.ShapeDtypeStruct((length, model_width), jnp.bfloat16) for _ in range(3)),
        grid=(pairs,),
        in_specs=attention_specs(length, lanes, pairs)
        + [
            pl.BlockSpec((length, lanes), lambda p: (0, p)),
            pl.BlockSpec((1, 2, length), lambda p: (p, 0, 0)),
        ],
        out_specs=tuple(pl.BlockSpec((length, lanes), lambda p: (0, p)) for _ in range(3)),
        scratch_shapes=[
            pltpu.VMEM((lanes, length), jnp.bfloat16),
            pltpu.VMEM((length, lanes), jnp.float32),
            pltpu.VMEM((length, lanes), jnp.float32),
        ],
        name="attention_backward",
        compiler_params=pltpu.CompilerParams(vmem_limit_bytes=VMEM_LIMIT),
    )(qkv_low, qkv_low, qkv_low, grad_attended, log_totals)
    return jnp.concatenate(grads, axis=1)


def whole_forward(hidden_in, tiles, gain_attn, gain_ffn):
    model_width = hidden_in.shape[1]
    head_width = model_width // HEADS
    w_qkv, w_up, w_down = block_weights(tiles)
    normed = rms_norm(hidden_in, gain_attn).astype(jnp.bfloat16)
    qkv_low = product(normed, w_qkv).astype(jnp.bfloat16)
    attended, log_totals = attention_whole(qkv_low, model_width, head_width)
    after_attn = hidden_in + product(attended, tiles[3])
    inner = product(rms_norm(after_attn, gain_ffn).astype(jnp.bfloat16), w_up)
    block_out = after_attn + product(jax.nn.gelu(inner).astype(jnp.bfloat16), w_down)
    return (block_out, (hidden_in, qkv_low, log_totals, attended, after_attn, inner))


def whole_backward(grad_out, saved, tiles, gain_attn, gain_ffn):
    hidden_in, qkv_low, log_totals, attended, after_attn, inner = saved
    model_width = hidden_in.shape[1]
    head_width = model_width // HEADS
    w_qkv, w_up, w_down = block_weights(tiles)
    grad_ffn = grad_out.astype(jnp.bfloat16)
    activated, gelu_pull = jax.vjp(jax.nn.gelu, inner)
    grad_down = product_tn(activated.astype(jnp.bfloat16), grad_ffn)
    grad_inner = gelu_pull(product_nt(grad_ffn, w_down))[0].astype(jnp.bfloat16)
    normed_ffn, ffn_pull = jax.vjp(rms_norm, after_attn, gain_ffn)
    grad_up = product_tn(normed_ffn.astype(jnp.bfloat16), grad_inner)
    grad_normed_in, grad_gain_ffn = ffn_pull(product_nt(grad_inner, w_up))
    grad_after = grad_out + grad_normed_in
    grad_branch = grad_after.astype(jnp.bfloat16)
    grad_wout = product_tn(attended, grad_branch)
    grad_attended = product_nt(grad_branch, tiles[3]).astype(jnp.bfloat16)
    grad_qkv = attention_whole_back(qkv_low, grad_attended, log_totals, model_width, head_width)
    normed_attn, attn_pull = jax.vjp(rms_norm, hidden_in, gain_attn)
    grad_wqkv = product_tn(normed_attn.astype(jnp.bfloat16), grad_qkv)
    grad_normed_x, grad_gain_attn = attn_pull(product_nt(grad_qkv, w_qkv))
    grad_in = grad_after + grad_normed_x
    pieces = [grad_wqkv[:, i * model_width : (i + 1) * model_width] for i in range(3)]
    pieces = pieces + [grad_wout]
    pieces = pieces + [grad_up[:, i * model_width : (i + 1) * model_width] for i in range(4)]
    pieces = pieces + [grad_down[i * model_width : (i + 1) * model_width] for i in range(4)]
    return (grad_in, pieces, grad_gain_attn, grad_gain_ffn)


def whole_step(char_ids, targets, seg_ids, lengths, owner_slot, master, gain_rows):
    micro_count = char_ids.shape[0]
    seq_count = lax.axis_size("seq")
    seq_me = lax.axis_index("seq")
    model_width = master.shape[2]
    vocab_size = model_width // 2
    seg_total = SEG_DEV * seq_count
    ids = jnp.stack([char_ids[:, 0], targets[:, 0], seg_ids[:, 0]], axis=1)
    ids = jnp.pad(ids, ((0, 0), (0, 5), (0, 0)))
    tiles, ids = gather_tiles_kernel(master.astype(jnp.bfloat16), ids, owner_slot)
    chars_row, target_row, segment_row = (ids[:, i].reshape(-1) for i in range(3))
    length_one = lax.dynamic_index_in_dim(lengths[:, 0], seq_me, keepdims=False)
    char_count = chars_row.shape[0]
    is_valid = (jnp.arange(char_count) < length_one).astype(jnp.float32)
    vocab_iota = jnp.arange(vocab_size)
    char_hot = chars_row[:, None] == vocab_iota[None, :]
    embed_low = tiles[25, :vocab_size]
    head_low = tiles[25, vocab_size:]
    start_hidden = product(char_hot.astype(jnp.bfloat16), embed_low)
    char_out, char_saved = whole_forward(start_hidden, tiles[0:12], gain_rows[0], gain_rows[1])
    char_low = char_out.astype(jnp.bfloat16)
    boundary_hidden = jnp.tanh(product(char_low, tiles[24]))
    root_width = model_width ** (-0.5)
    boundary_prob = jax.nn.sigmoid(jnp.sum(boundary_hidden * gain_rows[5], axis=1) * root_width)
    counts = jnp.stack([jnp.sum(is_valid * boundary_prob), length_one.astype(jnp.float32)])
    counts = column_sum(jnp.pad(counts[:, None], ((0, 6), (0, 127))))
    soft_count, count_all = counts[0, 0], counts[1, 0]
    slot_iota = jnp.arange(seg_total)
    pool_hot = segment_row[None, :] + 1 == slot_iota[:, None]
    lift_hot = segment_row[:, None] == slot_iota[None, :]
    row_counts = jnp.sum(pool_hot.astype(jnp.float32), axis=1)
    divisor = jnp.maximum(row_counts, 1.0)[:, None]
    pooled = product(pool_hot.astype(jnp.bfloat16), char_low) / divisor
    seg_out, seg_saved = whole_forward(pooled, tiles[12:24], gain_rows[2], gain_rows[3])
    merged = char_out + product(lift_hot.astype(jnp.bfloat16), seg_out.astype(jnp.bfloat16))
    final_norm, final_pull = jax.vjp(rms_norm, merged, gain_rows[4])
    final_low = final_norm.astype(jnp.bfloat16)
    logits = product_nt(final_low, head_low)
    peak = jnp.max(logits, axis=1, keepdims=True)
    log_total = peak[:, 0] + jnp.log(jnp.sum(jnp.exp(logits - peak), axis=1))
    target_hot = (target_row[:, None] == vocab_iota[None, :]).astype(jnp.float32)
    picked = jnp.sum(logits * target_hot, axis=1)
    ce_local = jnp.sum(is_valid * (log_total - picked))
    weight_ce = is_valid / (micro_count * count_all)
    grad_logits = ((jnp.exp(logits - log_total[:, None]) - target_hot) * weight_ce[:, None]).astype(
        jnp.bfloat16
    )
    grad_head = product_tn(grad_logits, final_low)
    grad_merged, grad_gain_final = final_pull(product(grad_logits, head_low))
    grad_seg = exact_tn(lift_hot.astype(jnp.float32), grad_merged)
    grad_pooled, seg_pieces, grad_gain_two, grad_gain_three = whole_backward(
        grad_seg, seg_saved, tiles[12:24], gain_rows[2], gain_rows[3]
    )
    grad_char = grad_merged + exact_tn(pool_hot.astype(jnp.float32), grad_pooled / divisor)
    prior_slope = (
        lax.digamma(soft_count + 1.0)
        - lax.digamma(count_all - soft_count + 1.0)
        - jnp.log(PRIOR_RATE)
        + jnp.log(1.0 - PRIOR_RATE)
    ) / (count_all * micro_count)
    grad_boundary_logit = is_valid * prior_slope * boundary_prob * (1.0 - boundary_prob)
    grad_gain_boundary = (
        jnp.sum(grad_boundary_logit[:, None] * boundary_hidden, axis=0) * root_width
    )
    grad_pre = (
        grad_boundary_logit[:, None]
        * gain_rows[5][None, :]
        * root_width
        * (1.0 - boundary_hidden * boundary_hidden)
    ).astype(jnp.bfloat16)
    grad_boundary = product_tn(char_low, grad_pre)
    grad_char = grad_char + product_nt(grad_pre, tiles[24])
    grad_start, char_pieces, grad_gain_zero, grad_gain_one = whole_backward(
        grad_char, char_saved, tiles[0:12], gain_rows[0], gain_rows[1]
    )
    grad_embed = exact_tn(char_hot.astype(jnp.float32), grad_start)
    tile_grads = jnp.stack(
        char_pieces
        + seg_pieces
        + [grad_boundary, jnp.concatenate([grad_embed, grad_head], axis=0)]
    )
    gain_grads = jnp.stack(
        [
            grad_gain_zero,
            grad_gain_one,
            grad_gain_two,
            grad_gain_three,
            grad_gain_final,
            grad_gain_boundary,
        ]
    )
    prior_term = (
        -(
            lax.lgamma(count_all + 1.0)
            - lax.lgamma(soft_count + 1.0)
            - lax.lgamma(count_all - soft_count + 1.0)
            + soft_count * jnp.log(PRIOR_RATE)
            + (count_all - soft_count) * jnp.log(1.0 - PRIOR_RATE)
        )
        / count_all
    )
    loss_part = (ce_local / count_all + prior_term / lax.axis_size("dp")) / micro_count
    return (tile_grads, gain_grads, loss_part)


def body(
    char_ids,
    targets,
    seg_ids,
    lengths,
    owner_slot,
    step_count,
    master,
    tile_first,
    tile_second,
    gain_rows,
    gain_first,
    gain_second,
):
    micro_count = char_ids.shape[0]
    model_width = master.shape[2]
    slot_count = master.shape[0] * lax.axis_size("seq")
    if (micro_count, lax.axis_size("seq"), lax.axis_size("dp")) == (4, 4, 8):
        tile_grads, gain_part, loss_part = whole_step(
            char_ids, targets, seg_ids, lengths, owner_slot, master, gain_rows
        )
        local = lax.axis_index("seq") * master.shape[0] + jnp.arange(master.shape[0])
        hot = local[:, None] == owner_slot[None, :]
        valid = jnp.any(hot, axis=1).astype(jnp.int32)
        source = jnp.sum(jnp.where(hot, jnp.arange(owner_slot.shape[0])[None, :], 0), axis=1)
        small = jnp.concatenate(
            [gain_part, jnp.pad(loss_part.reshape(1, 1), ((0, 1), (0, model_width - 1)))]
        )
        shard_total, small, squares = reduce_tiles_kernel(
            tile_grads, small, source, valid, master.shape[0]
        )
        gain_sum, loss_total, square_sum = small[0:6], small[6, 0], jnp.sum(squares)
    else:
        tile_total = jnp.zeros((owner_slot.shape[0], model_width, model_width), jnp.float32)
        gain_total = jnp.zeros_like(gain_rows)
        loss_total = jnp.zeros((), jnp.float32)
        for micro in range(micro_count):
            tiles = gather_tiles(master, owner_slot)
            tile_part, gain_part, loss_part = micro_step(
                tiles,
                gain_rows,
                char_ids[micro, 0],
                targets[micro, 0],
                seg_ids[micro, 0],
                lengths[micro, 0],
                micro_count,
            )
            tile_total = tile_total + tile_part
            gain_total = gain_total + gain_part
            loss_total = loss_total + loss_part
        shard_total = reduce_tiles(tile_total, owner_slot, slot_count)
        gain_sum, square_sum = lax.psum((gain_total, jnp.sum(shard_total * shard_total)), ("dp", "seq"))
    grad_norm = jnp.sqrt(square_sum + jnp.sum(gain_sum * gain_sum))
    clip_factor = jnp.minimum(1.0, CLIP_NORM / (grad_norm + 1e-06))
    step_float = step_count[0].astype(jnp.float32)
    local_ids = lax.axis_index("seq") * master.shape[0] + jnp.arange(master.shape[0])
    owned = jnp.any(local_ids[:, None] == owner_slot[None, :], axis=1)[:, None, None]
    new_tiles, new_first, new_second = adam_step(
        master,
        tile_first,
        tile_second,
        shard_total * clip_factor,
        RATE_TILES,
        WEIGHT_DECAY,
        step_float,
    )
    master_new = jnp.where(owned, new_tiles, master)
    first_new = jnp.where(owned, new_first, tile_first)
    second_new = jnp.where(owned, new_second, tile_second)
    gains_new, gain_first_new, gain_second_new = adam_step(
        gain_rows, gain_first, gain_second, gain_sum * clip_factor, RATE_GAINS, 0.0, step_float
    )
    return (
        loss_total.reshape(1),
        grad_norm.reshape(1),
        master_new,
        first_new,
        second_new,
        master_new.astype(jnp.bfloat16),
        gains_new,
        gain_first_new,
        gain_second_new,
    )


def solution(mesh):
    return jax.shard_map(
        body,
        mesh=mesh,
        in_specs=(
            P(None, "dp", "seq"),
            P(None, "dp", "seq"),
            P(None, "dp", "seq"),
            P(None, "dp"),
            P(),
            P(),
            P("seq", "dp", None),
            P("seq", "dp", None),
            P("seq", "dp", None),
            P(),
            P(),
            P(),
        ),
        out_specs=(
            P(),
            P(),
            P("seq", "dp", None),
            P("seq", "dp", None),
            P("seq", "dp", None),
            P("seq", "dp", None),
            P(),
            P(),
            P(),
        ),
        check_vma=False,
    )
```

```python
import functools
import math

import jax
import jax.numpy as jnp
from jax import lax
from jax.experimental import pallas as pl
from jax.experimental.pallas import tpu as pltpu
from jax.sharding import PartitionSpec as P

HEADS = 8
SEG_DEV = 64


BETA_ONE = 0.9
BETA_TWO = 0.95
ADAM_EPS = 1e-08
WEIGHT_DECAY = 0.1
RATE_TILES = 0.03
RATE_GAINS = 0.2
CLIP_NORM = 0.05
PRIOR_RATE = 0.25
NORM_EPS = 1e-06
MASKED = -1e30
LOG_ODDS = math.log(1.0 - PRIOR_RATE) - math.log(PRIOR_RATE)


def product(left, right):
    return jnp.dot(left, right, preferred_element_type=jnp.float32)


def product_tn(left, right):
    return lax.dot_general(
        left, right, (((0,), (0,)), ((), ())), preferred_element_type=jnp.float32
    )


def product_nt(left, right):
    return lax.dot_general(
        left, right, (((1,), (1,)), ((), ())), preferred_element_type=jnp.float32
    )


def exact_tn(left, right):
    return lax.dot_general(
        left,
        right,
        (((0,), (0,)), ((), ())),
        precision=lax.Precision.HIGHEST,
        preferred_element_type=jnp.float32,
    )


def rms_norm(values, gain):
    return values * lax.rsqrt(jnp.mean(values * values, axis=-1, keepdims=True) + NORM_EPS) * gain


def split_heads(tensor):
    return tensor.reshape(tensor.shape[0], HEADS, tensor.shape[1] // HEADS).transpose(1, 0, 2)


def join_heads(tensor):
    return tensor.transpose(1, 0, 2).reshape(tensor.shape[1], tensor.shape[0] * tensor.shape[2])


def block_weights(tiles):
    w_qkv = jnp.concatenate([tiles[0], tiles[1], tiles[2]], axis=1)
    w_up = jnp.concatenate([tiles[4], tiles[5], tiles[6], tiles[7]], axis=1)
    w_down = jnp.concatenate([tiles[8], tiles[9], tiles[10], tiles[11]], axis=0)
    return (w_qkv, w_up, w_down)


def causal_mask(row_count, key_count):
    first_row = lax.axis_index("seq") * row_count
    return (first_row + jnp.arange(row_count))[:, None] >= jnp.arange(key_count)[None, :]


def block_forward(hidden_in, tiles, gain_attn, gain_ffn, segment):
    row_count, model_width = hidden_in.shape
    w_qkv, w_up, w_down = block_weights(tiles)
    normed = rms_norm(hidden_in, gain_attn).astype(jnp.bfloat16)
    qkv_low = product(normed, w_qkv).astype(jnp.bfloat16)
    if segment:
        gathered = lax.all_gather(qkv_low[:, model_width:], "seq", axis=0, tiled=True)
    else:
        gathered = lax.all_gather(qkv_low[:, model_width:], "seq", axis=0, tiled=True)
    allowed = causal_mask(row_count, gathered.shape[0])
    factor = (model_width // HEADS) ** (-0.5)

    def head_forward(triple):
        q_head, k_head, v_head = triple
        scores = jnp.where(allowed, product_nt(q_head, k_head) * factor, MASKED)
        peak = jnp.max(scores, axis=1, keepdims=True)
        log_total = peak + jnp.log(jnp.sum(jnp.exp(scores - peak), axis=1, keepdims=True))
        weights = jnp.exp(scores - log_total).astype(jnp.bfloat16)
        return (product(weights, v_head), log_total[:, 0])

    head_out, log_totals = lax.map(
        head_forward,
        (
            split_heads(qkv_low[:, :model_width]),
            split_heads(gathered[:, :model_width]),
            split_heads(gathered[:, model_width:]),
        ),
    )
    attended = join_heads(head_out).astype(jnp.bfloat16)
    after_attn = hidden_in + product(attended, tiles[3])
    inner = product(rms_norm(after_attn, gain_ffn).astype(jnp.bfloat16), w_up)
    block_out = after_attn + product(jax.nn.gelu(inner).astype(jnp.bfloat16), w_down)
    return (block_out, (hidden_in, qkv_low, gathered, log_totals, attended, after_attn, inner))


def block_backward(grad_out, saved, tiles, gain_attn, gain_ffn, segment):
    hidden_in, qkv_low, gathered, log_totals, attended, after_attn, inner = saved
    row_count, model_width = hidden_in.shape
    w_qkv, w_up, w_down = block_weights(tiles)
    grad_ffn = grad_out.astype(jnp.bfloat16)
    activated, gelu_pull = jax.vjp(jax.nn.gelu, inner)
    grad_down = product_tn(activated.astype(jnp.bfloat16), grad_ffn)
    grad_inner = gelu_pull(product_nt(grad_ffn, w_down))[0].astype(jnp.bfloat16)
    normed_ffn, ffn_pull = jax.vjp(rms_norm, after_attn, gain_ffn)
    grad_up = product_tn(normed_ffn.astype(jnp.bfloat16), grad_inner)
    grad_normed_in, grad_gain_ffn = ffn_pull(product_nt(grad_inner, w_up))
    grad_after = grad_out + grad_normed_in
    grad_branch = grad_after.astype(jnp.bfloat16)
    grad_wout = product_tn(attended, grad_branch)
    grad_attended = product_nt(grad_branch, tiles[3]).astype(jnp.bfloat16)
    allowed = causal_mask(row_count, gathered.shape[0])
    factor = (model_width // HEADS) ** (-0.5)

    def head_backward(bundle):
        q_head, k_head, v_head, upstream, log_head = bundle
        scores = jnp.where(allowed, product_nt(q_head, k_head) * factor, MASKED)
        weights = jnp.exp(scores - log_head[:, None])
        grad_values = product_tn(weights.astype(jnp.bfloat16), upstream)
        grad_weights = product_nt(upstream, v_head)
        inner_sum = jnp.sum(weights * grad_weights, axis=1, keepdims=True)
        grad_scores = (weights * (grad_weights - inner_sum)).astype(jnp.bfloat16)
        return (
            product(grad_scores, k_head) * factor,
            product_tn(grad_scores, q_head) * factor,
            grad_values,
        )

    grad_query, grad_keys, grad_values = lax.map(
        head_backward,
        (
            split_heads(qkv_low[:, :model_width]),
            split_heads(gathered[:, :model_width]),
            split_heads(gathered[:, model_width:]),
            split_heads(grad_attended),
            log_totals,
        ),
    )
    grad_kv_all = jnp.concatenate([join_heads(grad_keys), join_heads(grad_values)], axis=1)
    if segment:
        grad_kv = lax.psum_scatter(grad_kv_all, "seq", scatter_dimension=0, tiled=True)
    else:
        grad_kv = lax.psum_scatter(grad_kv_all, "seq", scatter_dimension=0, tiled=True)
    grad_qkv = jnp.concatenate([join_heads(grad_query), grad_kv], axis=1).astype(jnp.bfloat16)
    normed_attn, attn_pull = jax.vjp(rms_norm, hidden_in, gain_attn)
    grad_wqkv = product_tn(normed_attn.astype(jnp.bfloat16), grad_qkv)
    grad_normed_x, grad_gain_attn = attn_pull(product_nt(grad_qkv, w_qkv))
    grad_in = grad_after + grad_normed_x
    pieces = [
        grad_wqkv[:, part_index * model_width : (part_index + 1) * model_width]
        for part_index in range(3)
    ]
    pieces = pieces + [grad_wout]
    pieces = pieces + [
        grad_up[:, part_index * model_width : (part_index + 1) * model_width]
        for part_index in range(4)
    ]
    pieces = pieces + [
        grad_down[part_index * model_width : (part_index + 1) * model_width]
        for part_index in range(4)
    ]
    return (grad_in, jnp.stack(pieces), grad_gain_attn, grad_gain_ffn)


def micro_step(tiles, gain_rows, chars_row, target_row, segment_row, length_one, micro_count):
    char_count = chars_row.shape[0]
    model_width = tiles.shape[2]
    vocab_size = model_width // 2
    seq_count = lax.axis_size("seq")
    seg_total = SEG_DEV * seq_count
    position = lax.axis_index("seq") * char_count + jnp.arange(char_count)
    is_valid = (position < length_one).astype(jnp.float32)
    vocab_iota = jnp.arange(vocab_size)
    char_hot = chars_row[:, None] == vocab_iota[None, :]
    embed_low = tiles[25, :vocab_size]
    head_low = tiles[25, vocab_size:]
    start_hidden = product(char_hot.astype(jnp.bfloat16), embed_low)
    char_out, char_saved = block_forward(
        start_hidden, tiles[0:12], gain_rows[0], gain_rows[1], False
    )
    char_low = char_out.astype(jnp.bfloat16)
    boundary_hidden = jnp.tanh(product(char_low, tiles[24]))
    root_width = model_width ** (-0.5)
    boundary_prob = jax.nn.sigmoid(jnp.sum(boundary_hidden * gain_rows[5], axis=1) * root_width)
    slot_iota = jnp.arange(seg_total)
    pool_hot = segment_row[None, :] + 1 == slot_iota[:, None]
    lift_hot = segment_row[:, None] == slot_iota[None, :]
    part_sums = product(pool_hot.astype(jnp.bfloat16), char_low).reshape(
        seq_count, SEG_DEV, model_width
    )
    side_info = jnp.stack(
        [
            jnp.sum(pool_hot.astype(jnp.float32), axis=1),
            jnp.any(lift_hot, axis=0).astype(jnp.float32),
        ],
        axis=0,
    )
    side_info = side_info.reshape(2, seq_count, SEG_DEV).transpose(1, 0, 2)
    sums_in, side_in = (
        lax.all_to_all(part_sums, "seq", split_axis=0, concat_axis=0, tiled=True),
        lax.all_to_all(side_info, "seq", split_axis=0, concat_axis=0, tiled=True),
    )
    row_counts = jnp.sum(side_in[:, 0, :], axis=0)
    divisor = jnp.maximum(row_counts, 1.0)[:, None]
    pooled = jnp.sum(sums_in, axis=0) / divisor
    seg_out, seg_saved = block_forward(pooled, tiles[12:24], gain_rows[2], gain_rows[3], True)
    outgoing = side_in[:, 1, :, None].astype(jnp.bfloat16) * seg_out.astype(jnp.bfloat16)[None]
    returned = lax.all_to_all(outgoing, "seq", split_axis=0, concat_axis=0, tiled=True)
    merged = char_out + product(
        lift_hot.astype(jnp.bfloat16), returned.reshape(seg_total, model_width)
    )
    final_norm, final_pull = jax.vjp(rms_norm, merged, gain_rows[4])
    final_low = final_norm.astype(jnp.bfloat16)
    logits = product_nt(final_low, head_low)
    peak = jnp.max(logits, axis=1, keepdims=True)
    log_total = peak[:, 0] + jnp.log(jnp.sum(jnp.exp(logits - peak), axis=1))
    target_hot = (target_row[:, None] == vocab_iota[None, :]).astype(jnp.float32)
    picked = jnp.sum(logits * target_hot, axis=1)
    ce_local = jnp.sum(is_valid * (log_total - picked))
    ce_all, soft_count, count_all = lax.psum(
        (ce_local, jnp.sum(is_valid * boundary_prob), jnp.sum(is_valid)), ("dp", "seq")
    )
    weight_ce = is_valid / (micro_count * count_all)
    grad_logits = ((jnp.exp(logits - log_total[:, None]) - target_hot) * weight_ce[:, None]).astype(
        jnp.bfloat16
    )
    grad_head = product_tn(grad_logits, final_low)
    grad_merged, grad_gain_final = final_pull(product(grad_logits, head_low))
    grad_rows = exact_tn(lift_hot.astype(jnp.float32), grad_merged).reshape(
        seq_count, SEG_DEV, model_width
    )
    grad_seg = jnp.sum(
        lax.all_to_all(grad_rows, "seq", split_axis=0, concat_axis=0, tiled=True), axis=0
    )
    grad_pooled, seg_tiles, grad_gain_two, grad_gain_three = block_backward(
        grad_seg, seg_saved, tiles[12:24], gain_rows[2], gain_rows[3], True
    )
    grad_sums = (side_in[:, 0, :, None] > 0).astype(jnp.float32) * (grad_pooled / divisor)[None]
    grad_back = lax.all_to_all(grad_sums, "seq", split_axis=0, concat_axis=0, tiled=True).reshape(
        seg_total, model_width
    )
    grad_char = grad_merged + exact_tn(pool_hot.astype(jnp.float32), grad_back)
    prior_slope = (
        lax.digamma(soft_count + 1.0)
        - lax.digamma(count_all - soft_count + 1.0)
        - jnp.log(PRIOR_RATE)
        + jnp.log(1.0 - PRIOR_RATE)
    ) / (count_all * micro_count)
    grad_boundary_logit = is_valid * prior_slope * boundary_prob * (1.0 - boundary_prob)
    grad_gain_boundary = (
        jnp.sum(grad_boundary_logit[:, None] * boundary_hidden, axis=0) * root_width
    )
    grad_pre = (
        grad_boundary_logit[:, None]
        * gain_rows[5][None, :]
        * root_width
        * (1.0 - boundary_hidden * boundary_hidden)
    ).astype(jnp.bfloat16)
    grad_boundary = product_tn(char_low, grad_pre)
    grad_char = grad_char + product_nt(grad_pre, tiles[24])
    grad_start, char_tiles, grad_gain_zero, grad_gain_one = block_backward(
        grad_char, char_saved, tiles[0:12], gain_rows[0], gain_rows[1], False
    )
    grad_embed = exact_tn(char_hot.astype(jnp.float32), grad_start)
    tile_grads = jnp.concatenate(
        [
            char_tiles,
            seg_tiles,
            grad_boundary[None],
            jnp.concatenate([grad_embed, grad_head], axis=0)[None],
        ],
        axis=0,
    )
    gain_grads = jnp.stack(
        [
            grad_gain_zero,
            grad_gain_one,
            grad_gain_two,
            grad_gain_three,
            grad_gain_final,
            grad_gain_boundary,
        ]
    )
    prior_term = (
        -(
            lax.lgamma(count_all + 1.0)
            - lax.lgamma(soft_count + 1.0)
            - lax.lgamma(count_all - soft_count + 1.0)
            + soft_count * jnp.log(PRIOR_RATE)
            + (count_all - soft_count) * jnp.log(1.0 - PRIOR_RATE)
        )
        / count_all
    )
    return (tile_grads, gain_grads, (ce_all / count_all + prior_term) / micro_count)


def gather_tiles(master, owner_slot):
    shard_low = master.astype(jnp.bfloat16)
    full_rows = lax.all_gather(shard_low, "dp", axis=1, tiled=True)
    all_slots = lax.all_gather(full_rows, "seq", axis=0, tiled=True)
    return jnp.take(all_slots, owner_slot, axis=0)


def reduce_tiles(tile_grads, owner_slot, slot_count):
    placed = (
        jnp.zeros((slot_count,) + tile_grads.shape[1:], jnp.float32).at[owner_slot].set(tile_grads)
    )
    per_owner = lax.psum_scatter(placed, "seq", scatter_dimension=0, tiled=True)
    return lax.psum_scatter(per_owner, "dp", scatter_dimension=1, tiled=True)


def adam_step(param, moment_a, moment_b, grad_in, rate, decay, step_float):
    new_first = BETA_ONE * moment_a + (1.0 - BETA_ONE) * grad_in
    new_second = BETA_TWO * moment_b + (1.0 - BETA_TWO) * grad_in * grad_in
    first_hat = new_first / (1.0 - BETA_ONE**step_float)
    second_hat = new_second / (1.0 - BETA_TWO**step_float)
    updated = param - rate * (first_hat / (jnp.sqrt(second_hat) + ADAM_EPS) + decay * param)
    return (updated, new_first, new_second)


MESH = pl.DeviceIdType.MESH
VMEM_LIMIT = 60 * 1024 * 1024
STEP_VMEM = 63 * 1024 * 1024


def remote(src, dst, send_sem, recv_sem, peer):
    return pltpu.make_async_remote_copy(
        src_ref=src, dst_ref=dst, send_sem=send_sem, recv_sem=recv_sem, device_id=peer, device_id_type=MESH
    )


def places():
    dp = lax.axis_index("dp")
    seq = lax.axis_index("seq")
    return dp, seq, dp // 2, dp % 2


def seq_peer(seq, step):
    return ((seq // 2 + step // 2) % 2) * 2 + (seq % 2 + step % 2) % 2


def meet(peers):
    barrier = pltpu.get_barrier_semaphore()
    for peer in peers:
        pl.semaphore_signal(barrier, inc=1, device_id=peer, device_id_type=MESH)
    pl.semaphore_wait(barrier, len(peers))


def gather_kernel(
    chunks, slot_ref, low_ref, ids_ref, full_ref, ids_out, slots, own, x_send, x_recv, own_sem,
    n_send, n_recv, f_send, f_recv, c_send, c_recv, i_send, i_recv, i_own,
):
    dp, seq, z, core = places()
    held, rows, _ = low_ref.shape
    tile_count = full_ref.shape[0]
    half = tile_count // 2
    step_rows = rows // chunks
    sibling = (z * 2 + 1 - core, seq)
    up, down = ((z + 1) % 4 * 2 + core, seq), ((z + 3) % 4 * 2 + core, seq)
    side = [(dp, seq_peer(seq, j)) for j in (1, 2, 3)]
    meet([sibling, up, down] + side)

    def rows_of(owner_z, chunk):
        return pl.ds(pl.multiple_of((owner_z * 2 + core) * rows + chunk * step_rows, step_rows), step_rows)

    def part(chunk):
        return pl.ds(chunk * step_rows, step_rows)

    side_copies = []
    for chunk in range(chunks):
        for j in range(3):
            copy = remote(
                low_ref.at[:, part(chunk)], slots[chunk].at[pl.ds(held * seq, held)],
                x_send.at[chunk, j], x_recv.at[chunk, j], side[j],
            )
            copy.start()
            side_copies.append(copy)
        for j in range(3):
            if chunk == 0:
                copy = remote(
                    ids_ref.at[side[j][1]], ids_out.at[seq], i_send.at[j], i_recv.at[j], side[j]
                )
                copy.start()
                side_copies.append(copy)
        slots[chunk][pl.ds(held * seq, held)] = low_ref[:, part(chunk), :]
    ids_copy = pltpu.make_async_copy(ids_ref.at[seq], ids_out.at[seq], i_own)
    ids_copy.start()

    def near(chunk):
        for j in range(3):
            remote(
                low_ref.at[:, part(chunk)], slots[chunk].at[pl.ds(held * seq, held)],
                x_send.at[chunk, j], x_recv.at[chunk, j], side[j],
            ).wait_recv()

        def pick(tile, carry):
            own[chunk, tile] = slots[chunk][slot_ref[tile]]
            return carry

        lax.fori_loop(0, tile_count, pick, 0)
        place = full_ref.at[:, rows_of(z, chunk)]
        for way, peer in enumerate((up, down)):
            copy = remote(own.at[chunk], place, n_send.at[chunk, way], n_recv.at[chunk, way], peer)
            copy.start()
        copy = remote(own.at[chunk], place, c_send.at[chunk, 0], c_recv.at[chunk, 0], sibling)
        copy.start()
        copy = pltpu.make_async_copy(own.at[chunk], place, own_sem.at[chunk])
        copy.start()

    def far(chunk):
        for way, peer in enumerate((up, down)):
            origin = (z + 3) % 4 if way == 0 else (z + 1) % 4
            place = full_ref.at[:, rows_of(origin, chunk)]
            remote(own.at[chunk], place, n_send.at[chunk, way], n_recv.at[chunk, way], peer).wait_recv()
            portion = full_ref.at[pl.ds(way * half, half), rows_of(origin, chunk)]
            copy = remote(portion, portion, f_send.at[chunk, way], f_recv.at[chunk, way], peer)
            copy.start()
            copy = remote(place, place, c_send.at[chunk, 1 + way], c_recv.at[chunk, 1 + way], sibling)
            copy.start()

    def last(chunk):
        for way, peer in enumerate((up, down)):
            portion = full_ref.at[pl.ds(way * half, half), rows_of((z + 2) % 4, chunk)]
            remote(portion, portion, f_send.at[chunk, way], f_recv.at[chunk, way], peer).wait_recv()
            copy = remote(portion, portion, c_send.at[chunk, 3 + way], c_recv.at[chunk, 3 + way], sibling)
            copy.start()

    for tick in range(chunks + 2):
        if tick < chunks:
            near(tick)
        if 0 <= tick - 1 < chunks:
            far(tick - 1)
        if 0 <= tick - 2 < chunks:
            last(tick - 2)
    for copy in side_copies:
        copy.wait_send()
    for j in range(3):
        remote(ids_ref.at[side[j][1]], ids_out.at[seq], i_send.at[j], i_recv.at[j], side[j]).wait_recv()
    ids_copy.wait()
    for chunk in range(chunks):
        place = full_ref.at[:, rows_of(z, chunk)]
        for way, peer in enumerate((up, down)):
            remote(own.at[chunk], place, n_send.at[chunk, way], n_recv.at[chunk, way], peer).wait_send()
            portion = full_ref.at[pl.ds(way * half, half), rows_of(z, chunk)]
            remote(portion, portion, f_send.at[chunk, way], f_recv.at[chunk, way], peer).wait_send()
        pltpu.make_async_copy(own.at[chunk], place, own_sem.at[chunk]).wait()
        for turn in range(5):
            piece = full_ref.at[:, rows_of(z, chunk)] if turn < 3 else full_ref.at[pl.ds(0, half), rows_of(z, chunk)]
            remote(piece, piece, c_send.at[chunk, turn], c_recv.at[chunk, turn], sibling).wait()


def gather_tiles_kernel(low, ids, owner_slot):
    held, rows, width = low.shape
    tile_count = owner_slot.shape[0]
    seq_count, dp_count = lax.axis_size("seq"), lax.axis_size("dp")
    chunks = 4
    step_rows = rows // chunks
    dma = pltpu.SemaphoreType.DMA
    return pl.pallas_call(
        functools.partial(gather_kernel, chunks),
        out_shape=(
            jax.ShapeDtypeStruct((tile_count, dp_count * rows, width), low.dtype),
            jax.ShapeDtypeStruct(ids.shape, ids.dtype),
        ),
        in_specs=[
            pl.BlockSpec(memory_space=pltpu.SMEM),
            pl.BlockSpec(memory_space=pltpu.VMEM),
            pl.BlockSpec(memory_space=pltpu.VMEM),
        ],
        out_specs=(pl.BlockSpec(memory_space=pl.ANY), pl.BlockSpec(memory_space=pltpu.VMEM)),
        scratch_shapes=[
            [pltpu.VMEM((seq_count * held, step_rows, width), low.dtype)] * chunks,
            pltpu.VMEM((chunks, tile_count, step_rows, width), low.dtype),
            dma((chunks, 3)), dma((chunks, 3)), dma((chunks,)),
            dma((chunks, 2)), dma((chunks, 2)), dma((chunks, 2)), dma((chunks, 2)),
            dma((chunks, 5)), dma((chunks, 5)), dma((3,)), dma((3,)), dma,
        ],
        name="gather_tiles",
        compiler_params=pltpu.CompilerParams(
            collective_id=0, has_side_effects=True, vmem_limit_bytes=VMEM_LIMIT
        ),
    )(owner_slot, low, ids)


CODE_TOP = 32000.0
ROUNDER = 12582912.0


def encode(value):
    upper, lower = value[0:8, :], value[8:16, :]
    size = jnp.maximum(jnp.abs(upper), jnp.abs(lower))
    most = jnp.maximum(jnp.max(size, axis=1, keepdims=True), 1e-30)
    ratio = CODE_TOP / most
    coded = jnp.concatenate([upper * ratio, lower * ratio], axis=0)
    coded = ((coded + ROUNDER) - ROUNDER).astype(jnp.int32).astype(jnp.int16)
    return coded, most * (1.0 / CODE_TOP)


def decode(coded, unit):
    value = coded.astype(jnp.int32).astype(jnp.float32)
    return jnp.concatenate([value[0:8, :] * unit, value[8:16, :] * unit], axis=0)


def reduce_kernel(
    source_ref, valid_ref, grads_ref, small_ref, out_ref, small_out, square_out,
    own, other, b1_out, b1_in, b2_out, b2_in, c_out, c_in, d_out, d_in,
    b1_unit_out, b1_unit_in, b2_unit_out, b2_unit_in, c_unit_out, c_unit_in, d_unit_out, d_unit_in,
    final, small_dp, small_seq, square_dp, square_seq,
    l_sem, a_send, a_recv, b1_send, b1_recv, b2_send, b2_recv, c_send, c_recv, d_send, d_recv,
    p_send, p_recv, q_send, q_recv, r_send, r_recv, s_send, s_recv,
):
    dp, seq, z, core = places()
    across, along = seq % 2, seq // 2
    held = out_ref.shape[0]
    tile_count = grads_ref.shape[0]
    pairs = tile_count // 2
    sibling = (z * 2 + 1 - core, seq)
    beside = [(dp, along * 2 + 1 - across), (dp, (1 - along) * 2 + across)]
    side = [(dp, seq_peer(seq, j)) for j in (1, 2, 3)]
    column = [((dp + j) % 8, seq) for j in range(1, 8)]
    tower = [((z + j) % 4 * 2 + core, seq) for j in (1, 2, 3)]
    meet(side + column)
    lane = lax.broadcasted_iota(jnp.int32, (8, 128), 1)

    def core_copy(pair):
        two = pl.ds(pair * 2, 2)
        return remote(grads_ref.at[two, :, 1 - core], other.at[two], a_send.at[pair], a_recv.at[pair], sibling)

    def local_copy(pair):
        two = pl.ds(pair * 2, 2)
        return pltpu.make_async_copy(grads_ref.at[two, :, core], own.at[two], l_sem.at[pair])

    def with_units(values, units, send, recv, peer):
        return [
            remote(values[0], values[1], send.at[0], recv.at[0], peer),
            remote(units[0], units[1], send.at[1], recv.at[1], peer),
        ]

    def first_copies(pair, order):
        tile = pair * 2 + order
        return with_units(
            (b1_out.at[tile], b1_in.at[tile]), (b1_unit_out.at[tile], b1_unit_in.at[tile]),
            b1_send.at[tile], b1_recv.at[tile], beside[order],
        )

    def second_copies(pair, order):
        tile = pair * 2 + order
        return with_units(
            (b2_out.at[tile], b2_in.at[tile]), (b2_unit_out.at[tile], b2_unit_in.at[tile]),
            b2_send.at[tile], b2_recv.at[tile], beside[1 - order],
        )

    def tower_copies(pair, j):
        two = pl.ds(pair * 2, 2)
        return with_units(
            (c_out.at[j, two], c_in.at[j, two]), (c_unit_out.at[j, pair], c_unit_in.at[j, pair]),
            c_send.at[j, pair], c_recv.at[j, pair], tower[j],
        )

    def share_copies(pair, j):
        two = pl.ds(pair * 2, 2)
        return with_units(
            (d_out.at[two], d_in.at[j, two]), (d_unit_out.at[pair], d_unit_in.at[j, pair]),
            d_send.at[j, pair], d_recv.at[j, pair], side[j],
        )

    def start_all(copies):
        for copy in copies:
            copy.start()

    def arrive_all(copies):
        for copy in copies:
            copy.wait_recv()

    def sent_all(copies):
        for copy in copies:
            copy.wait_send()

    def small_copy(j):
        return remote(small_ref, small_dp.at[dp], p_send.at[j], p_recv.at[j], column[j])

    def small_side(j):
        return remote(small_seq.at[seq], small_seq.at[seq], q_send.at[j], q_recv.at[j], side[j])

    def square_copy(j):
        return remote(square_dp.at[dp], square_dp.at[dp], r_send.at[j], r_recv.at[j], column[j])

    def square_side(j):
        return remote(square_seq.at[seq], square_seq.at[seq], s_send.at[j], s_recv.at[j], side[j])

    for j in range(7):
        small_copy(j).start()

    def launch(pair, carry):
        core_copy(pair).start()
        local_copy(pair).start()
        return carry

    lax.fori_loop(0, pairs, launch, 0)

    def cell(tile, order, floor, line, mine):
        if order == 0:
            return (tile, floor, line, across if mine else 1 - across)
        return (tile, floor, along if mine else 1 - along, line)

    def stage_one(pair):
        core_copy(pair).wait_recv()
        local_copy(pair).wait()

        def add(step, carry):
            tile, floor = pair * 2 + step // 4, step % 4
            own[tile, floor] = own[tile, floor] + other[tile, floor]
            return carry

        lax.fori_loop(0, 8, add, 0)
        for order in range(2):
            tile = pair * 2 + order
            units = jnp.zeros((8, 128), jnp.float32)
            for floor in range(4):
                for line in range(2):
                    coded, unit = encode(own[cell(tile, order, floor, line, False)])
                    b1_out[tile, floor * 2 + line] = coded
                    units = jnp.where(lane == floor * 2 + line, unit, units)
            b1_unit_out[tile] = units
            start_all(first_copies(pair, order))

    def stage_two(pair):
        for order in range(2):
            tile = pair * 2 + order
            arrive_all(first_copies(pair, order))
            got = b1_unit_in[tile]
            units = jnp.zeros((8, 128), jnp.float32)
            keep = along if order == 0 else across
            for floor in range(4):
                for line in range(2):
                    block = floor * 2 + line
                    spot = cell(tile, order, floor, line, True)
                    own[spot] = own[spot] + decode(b1_in[tile, block], got[:, block : block + 1])
                spot = cell(tile, order, floor, 1 - keep, True)
                coded, unit = encode(own[spot])
                b2_out[tile, floor] = coded
                units = jnp.where(lane == floor, unit, units)
            b2_unit_out[tile] = units
            start_all(second_copies(pair, order))

    def stage_three(pair):
        for order in range(2):
            tile = pair * 2 + order
            arrive_all(second_copies(pair, order))
            got = b2_unit_in[tile]
            for floor in range(4):
                spot = (tile, floor, along, across)
                own[spot] = own[spot] + decode(b2_in[tile, floor], got[:, floor : floor + 1])
        for j in range(3):
            units = jnp.zeros((8, 128), jnp.float32)
            for order in range(2):
                tile = pair * 2 + order
                coded, unit = encode(own[tile, (z + j + 1) % 4, along, across])
                c_out[j, tile] = coded
                units = jnp.where(lane == order, unit, units)
            c_unit_out[j, pair] = units
            start_all(tower_copies(pair, j))

    def stage_four(pair):
        for j in range(3):
            arrive_all(tower_copies(pair, j))
        units = jnp.zeros((8, 128), jnp.float32)
        for order in range(2):
            tile = pair * 2 + order
            total = own[tile, z, along, across]
            for j in range(3):
                total = total + decode(c_in[j, tile], c_unit_in[j, pair][:, order : order + 1])
            final[tile, seq] = total
            coded, unit = encode(total)
            d_out[tile] = coded
            units = jnp.where(lane == order, unit, units)
        d_unit_out[pair] = units
        for j in range(3):
            start_all(share_copies(pair, j))

    def stage_five(pair):
        for j in range(3):
            arrive_all(share_copies(pair, j))
            for order in range(2):
                tile = pair * 2 + order
                final[tile, side[j][1]] = decode(d_in[j, tile], d_unit_in[j, pair][:, order : order + 1])

    stages = (stage_one, stage_two, stage_three, stage_four, stage_five)
    lag = 2

    def tick(step, carry):
        for number, stage in enumerate(stages):
            pair = step - lag * number

            @pl.when(jnp.logical_and(pair >= 0, pair < pairs))
            def _():
                stage(pair)

        return carry

    lax.fori_loop(0, 4, tick, 0)
    small_dp[dp] = small_ref[...]
    for j in range(7):
        small_copy(j).wait_recv()
    total = small_dp[0]
    for j in range(1, 8):
        total = total + small_dp[j]
    small_seq[seq] = total
    for j in range(3):
        small_side(j).start()
    lax.fori_loop(4, pairs + lag * 4, tick, 0)

    def collect(slot, square):
        keep = valid_ref[slot] > 0
        for quarter in range(4):
            value = final[source_ref[slot], quarter]
            value = jnp.where(keep, value, jnp.zeros_like(value))
            out_ref[slot, quarter * 16 : quarter * 16 + 16, :] = value
            square = square + value * value
        return square

    square = lax.fori_loop(0, held, collect, jnp.zeros((16, out_ref.shape[2]), jnp.float32))
    folded = square[0:8, 0:128]
    for r in range(2):
        for w in range(out_ref.shape[2] // 128):
            if r or w:
                folded = folded + square[8 * r : 8 * r + 8, 128 * w : 128 * w + 128]
    square_dp[dp] = folded
    for j in range(7):
        square_copy(j).start()
    for j in range(3):
        small_side(j).wait_recv()
    small_out[...] = (small_seq[0] + small_seq[1]) + (small_seq[2] + small_seq[3])
    for j in range(7):
        square_copy(j).wait_recv()
    total = square_dp[0]
    for j in range(1, 8):
        total = total + square_dp[j]
    square_seq[seq] = total
    for j in range(3):
        square_side(j).start()
    for j in range(3):
        square_side(j).wait_recv()
    square_out[...] = (square_seq[0] + square_seq[1]) + (square_seq[2] + square_seq[3])
    for j in range(7):
        small_copy(j).wait_send()
        square_copy(j).wait_send()
    for j in range(3):
        small_side(j).wait_send()
        square_side(j).wait_send()

    def drain(pair, carry):
        core_copy(pair).wait_send()
        for order in range(2):
            sent_all(first_copies(pair, order))
            sent_all(second_copies(pair, order))
        for j in range(3):
            sent_all(tower_copies(pair, j))
            sent_all(share_copies(pair, j))
        return carry

    lax.fori_loop(0, pairs, drain, 0)


def reduce_tiles_kernel(grads, small, source, valid, held):
    tile_count, height, width = grads.shape
    seq_count, dp_count = lax.axis_size("seq"), lax.axis_size("dp")
    rows = height // dp_count
    pairs = tile_count // 2
    dma = pltpu.SemaphoreType.DMA
    vmem = pl.BlockSpec(memory_space=pltpu.VMEM)
    smem = pl.BlockSpec(memory_space=pltpu.SMEM)

    def buffer(*shape):
        return pltpu.VMEM(shape, jnp.float32)

    def codes(*shape):
        return pltpu.VMEM(shape + (16, width), jnp.int16)

    return pl.pallas_call(
        reduce_kernel,
        out_shape=(
            jax.ShapeDtypeStruct((held, rows, width), jnp.float32),
            jax.ShapeDtypeStruct(small.shape, jnp.float32),
            jax.ShapeDtypeStruct((8, 128), jnp.float32),
        ),
        in_specs=[smem, smem, pl.BlockSpec(memory_space=pl.ANY), vmem],
        out_specs=(vmem, vmem, vmem),
        scratch_shapes=[
            buffer(tile_count, 4, 2, 2, 16, width),
            buffer(tile_count, 4, 2, 2, 16, width),
            codes(tile_count, 8), codes(tile_count, 8),
            codes(tile_count, 4), codes(tile_count, 4),
            codes(3, tile_count), codes(3, tile_count),
            codes(tile_count), codes(3, tile_count),
            buffer(tile_count, 8, 128), buffer(tile_count, 8, 128),
            buffer(tile_count, 8, 128), buffer(tile_count, 8, 128),
            buffer(3, pairs, 8, 128), buffer(3, pairs, 8, 128),
            buffer(pairs, 8, 128), buffer(3, pairs, 8, 128),
            buffer(tile_count, 4, 16, width),
            buffer(dp_count, *small.shape),
            buffer(seq_count, *small.shape),
            buffer(dp_count, 8, 128),
            buffer(seq_count, 8, 128),
            dma((pairs,)), dma((pairs,)), dma((pairs,)),
            dma((tile_count, 2)), dma((tile_count, 2)), dma((tile_count, 2)), dma((tile_count, 2)),
            dma((3, pairs, 2)), dma((3, pairs, 2)), dma((3, pairs, 2)), dma((3, pairs, 2)),
            dma((7,)), dma((7,)), dma((3,)), dma((3,)), dma((7,)), dma((7,)), dma((3,)), dma((3,)),
        ],
        name="reduce_tiles",
        compiler_params=pltpu.CompilerParams(
            collective_id=1, has_side_effects=True, vmem_limit_bytes=VMEM_LIMIT
        ),
    )(source, valid, grads.reshape(tile_count, 4, 2, 2, 2, 16, width), small)


def head_mask(shape, head):
    lane = lax.broadcasted_iota(jnp.int32, shape, 1)
    return (lane >= 64) if head else (lane < 64)


def scores_t(k_pair, q_head, first_row):
    scores = product_nt(k_pair, q_head)
    count, queries = scores.shape
    key = lax.broadcasted_iota(jnp.int32, (queries, queries), 0)
    query = lax.broadcasted_iota(jnp.int32, (queries, queries), 1)
    own = jnp.where(key <= query, scores[first_row:], MASKED)
    return own if first_row == 0 else jnp.concatenate([scores[:first_row], own], axis=0)


ROWS = 256


def split_three(value):
    high = value.astype(jnp.bfloat16)
    rest = value - high.astype(jnp.float32)
    middle = rest.astype(jnp.bfloat16)
    return high, middle, (rest - middle.astype(jnp.float32)).astype(jnp.bfloat16)


def exact_product(hot, value):
    high, middle, low = split_three(value)
    return (product(hot, low) + product(hot, middle)) + product(hot, high)


def turn(value):
    return value.astype(jnp.float32).T.astype(jnp.bfloat16)


def root_scale(value):
    return lax.rsqrt(jnp.mean(value * value, axis=-1, keepdims=True) + NORM_EPS)


def norm_back(value, scale, gain, grad):
    unit = value * scale
    weighted = grad * gain
    inner = jnp.mean(weighted * unit, axis=-1, keepdims=True)
    return scale * (weighted - unit * inner), jnp.sum(grad * unit, axis=0, keepdims=True)


def gelu_both(value):
    root = 0.7978845608028654
    square = value * value
    reach = jnp.tanh(root * value * (1.0 + 0.044715 * square))
    part = 0.5 * (1.0 + reach)
    slope = part + value * (0.5 * (1.0 - reach * reach)) * (root * (1.0 + 3.0 * 0.044715 * square))
    return value * part, slope


def digamma(value):
    moved = value + 8.0
    inverse = 1.0 / moved
    square = inverse * inverse
    series = square * (1.0 / 12.0 - square * (1.0 / 120.0 - square * (1.0 / 252.0)))
    total = jnp.log(moved) - 0.5 * inverse - series
    for number in range(8):
        total = total - 1.0 / (value + float(number))
    return total


def each_block(length, body):
    def step(number, carry):
        body(pl.ds(pl.multiple_of(number * ROWS, ROWS), ROWS))
        return carry

    lax.fori_loop(0, length // ROWS, step, 0)


class Block:
    def __init__(self, length, first_tile, gain_row, entry, qkv, logs, attended, after, inner, leave):
        self.length, self.tile, self.gain_row = length, first_tile, gain_row
        self.entry, self.qkv, self.logs, self.attended = entry, qkv, logs, attended
        self.after, self.inner, self.leave = after, inner, leave


def attend(block):
    length = block.length

    def pair_step(pair, carry):
        lanes = [pl.ds(pl.multiple_of(part * 512 + pair * 128, 128), 128) for part in range(3)]
        for first in range(0, length, ROWS):
            span = first + ROWS
            q_pair = block.qkv[first:span, lanes[0]] * jnp.asarray(0.125, jnp.bfloat16)
            outs = []
            for head in range(2):
                q_head = jnp.where(head_mask(q_pair.shape, head), q_pair, jnp.zeros_like(q_pair))
                scores = scores_t(block.qkv[0:span, lanes[1]], q_head, first)
                peak = jnp.max(scores, axis=0, keepdims=True)
                raised = jnp.exp(scores - peak)
                total = jnp.sum(raised, axis=0, keepdims=True)
                weights = (raised * (1.0 / total)).astype(jnp.bfloat16)
                block.logs[pair, head : head + 1, first:span] = peak + jnp.log(total)
                outs.append(product_tn(weights, block.qkv[0:span, lanes[2]]))
            merged = jnp.where(head_mask(outs[0].shape, 0), outs[0], outs[1])
            block.attended[first:span, lanes[0]] = merged.astype(jnp.bfloat16)
        return carry

    lax.fori_loop(0, 4, pair_step, 0)


def attend_back(block, upstream, grad_qkv, key_sum, value_sum):
    length = block.length

    def pair_step(pair, carry):
        lanes = [pl.ds(pl.multiple_of(part * 512 + pair * 128, 128), 128) for part in range(3)]
        for first in reversed(range(0, length, ROWS)):
            span = first + ROWS
            q_pair = block.qkv[first:span, lanes[0]] * jnp.asarray(0.125, jnp.bfloat16)
            up_pair = upstream[first:span, lanes[0]]
            queries, keys, values = [], [], []
            for head in range(2):
                keep = head_mask(q_pair.shape, head)
                q_head = jnp.where(keep, q_pair, jnp.zeros_like(q_pair))
                up_head = jnp.where(keep, up_pair, jnp.zeros_like(up_pair))
                k_pair = block.qkv[0:span, lanes[1]]
                scores = scores_t(k_pair, q_head, first)
                weights = jnp.exp(scores - block.logs[pair, head : head + 1, first:span])
                grad_weights = product_nt(block.qkv[0:span, lanes[2]], up_head)
                values.append(product(weights.astype(jnp.bfloat16), up_head))
                inner_sum = jnp.sum(weights * grad_weights, axis=0, keepdims=True)
                grad_scores = (weights * (grad_weights - inner_sum)).astype(jnp.bfloat16)
                keys.append(product(grad_scores, q_head))
                queries.append(product_tn(grad_scores, k_pair))
            merged = jnp.where(head_mask(queries[0].shape, 0), queries[0], queries[1]) * 0.125
            grad_qkv[first:span, lanes[0]] = merged.astype(jnp.bfloat16)
            if span == length:
                key_sum[0:span, :] = keys[0] + keys[1]
                value_sum[0:span, :] = values[0] + values[1]
            else:
                key_sum[0:span, :] = key_sum[0:span, :] + (keys[0] + keys[1])
                value_sum[0:span, :] = value_sum[0:span, :] + (values[0] + values[1])
        grad_qkv[0:length, lanes[1]] = key_sum[0:length, :].astype(jnp.bfloat16)
        grad_qkv[0:length, lanes[2]] = value_sum[0:length, :].astype(jnp.bfloat16)
        return carry

    lax.fori_loop(0, 4, pair_step, 0)


def block_run(block, weights, gains):
    tile = block.tile
    gain_attn = gains[block.gain_row : block.gain_row + 1, :]
    gain_ffn = gains[block.gain_row + 1 : block.gain_row + 2, :]

    def project(rows):
        value = block.entry[rows, :]
        normed = (value * root_scale(value) * gain_attn).astype(jnp.bfloat16)
        for part in range(3):
            block.qkv[rows, 512 * part : 512 * part + 512] = product(normed, weights[tile + part]).astype(
                jnp.bfloat16
            )

    each_block(block.length, project)
    attend(block)

    def feed(rows):
        after = block.entry[rows, :] + product(block.attended[rows, :], weights[tile + 3])
        block.after[rows, :] = after
        normed = (after * root_scale(after) * gain_ffn).astype(jnp.bfloat16)
        total = jnp.zeros_like(after)
        for part in range(4):
            inner = product(normed, weights[tile + 4 + part])
            block.inner[rows, 512 * part : 512 * part + 512] = inner
            active = gelu_both(inner)[0].astype(jnp.bfloat16)
            total = total + product(active, weights[tile + 8 + part])
        block.leave[rows, :] = after + total

    each_block(block.length, feed)


def block_back(block, grad, weights, gains, gain_sums, temps, put):
    length, tile = block.length, block.tile
    gain_attn = gains[block.gain_row : block.gain_row + 1, :]
    gain_ffn = gains[block.gain_row + 1 : block.gain_row + 2, :]
    turned, grad_inner, branch, upstream, turned_norm, key_sum, value_sum = temps
    grad_low, grad_qkv = branch, grad_inner
    all_rows = pl.ds(0, length)

    def down(part):
        def rows_step(rows):
            low = grad[rows, :].astype(jnp.bfloat16)
            columns = pl.ds(pl.multiple_of(part * 512, 512), 512)
            active, slope = gelu_both(block.inner[rows, columns])
            turned[:, rows] = turn(active)
            grad_inner[rows, columns] = (product_nt(low, weights[tile + 8 + part]) * slope).astype(jnp.bfloat16)

        each_block(length, rows_step)

    def low_step(rows):
        grad_low[rows, :] = grad[rows, :].astype(jnp.bfloat16)

    each_block(length, low_step)

    def down_step(part, carry):
        down(part)
        put(tile + 8 + part, part, lambda half: product(turned[half, all_rows], grad_low[all_rows, :]))
        return carry

    lax.fori_loop(0, 4, down_step, 0)

    def middle(rows):
        after = block.after[rows, :]
        scale = root_scale(after)
        turned_norm[:, rows] = turn(after * scale * gain_ffn)
        turned[:, rows] = turn(block.attended[rows, :])
        total = jnp.zeros_like(after)
        for part in range(4):
            total = total + product_nt(
                grad_inner[rows, 512 * part : 512 * part + 512], weights[tile + 4 + part]
            )
        back, gain_part = norm_back(after, scale, gain_ffn, total)
        row = block.gain_row + 1
        gain_sums[row : row + 1, :] = gain_sums[row : row + 1, :] + gain_part
        grad_after = grad[rows, :] + back
        grad[rows, :] = grad_after
        low = grad_after.astype(jnp.bfloat16)
        branch[rows, :] = low
        upstream[rows, :] = product_nt(low, weights[tile + 3]).astype(jnp.bfloat16)

    each_block(length, middle)

    def up_step(part, carry):
        columns = pl.ds(pl.multiple_of(part * 512, 512), 512)
        put(tile + 4 + part, part, lambda half: product(turned_norm[half, all_rows], grad_inner[all_rows, columns]))
        return carry

    lax.fori_loop(0, 4, up_step, 0)
    put(tile + 3, 0, lambda half: product(turned[half, all_rows], branch[all_rows, :]))
    attend_back(block, upstream, grad_qkv, key_sum, value_sum)

    def enter(rows):
        value = block.entry[rows, :]
        scale = root_scale(value)
        turned_norm[:, rows] = turn(value * scale * gain_attn)
        total = jnp.zeros_like(value)
        for part in range(3):
            total = total + product_nt(grad_qkv[rows, 512 * part : 512 * part + 512], weights[tile + part])
        back, gain_part = norm_back(value, scale, gain_attn, total)
        row = block.gain_row
        gain_sums[row : row + 1, :] = gain_sums[row : row + 1, :] + gain_part
        grad[rows, :] = grad[rows, :] + back

    each_block(length, enter)

    def qkv_step(part, carry):
        columns = pl.ds(pl.multiple_of(part * 512, 512), 512)
        put(tile + part, part, lambda half: product(turned_norm[half, all_rows], grad_qkv[all_rows, columns]))
        return carry

    lax.fori_loop(0, 3, qkv_step, 0)


def step_kernel(
    micro_count, length_ref, tiles_ref, ids_ref, gains_ref, grads_ref, small_ref,
    weights, load_sem, entry, qkv, logs, attended, after, inner, leave, grad,
    seg_entry, seg_qkv, seg_logs, seg_attended, seg_after, seg_inner, seg_leave, seg_grad,
    turned, grad_inner, branch, upstream, turned_norm, key_sum, value_sum,
    ids_col, stage, stage_sem, counts, count_send, count_recv,
):
    dp, seq, _, _ = places()
    length = entry.shape[0]
    width = entry.shape[1]
    segments = seg_entry.shape[0]
    vocab = width // 2
    root_width = width ** (-0.5)
    column = [((dp + j) % 8, seq) for j in range(1, 8)]
    meet(column)

    def load(tile):
        return pltpu.make_async_copy(tiles_ref.at[tile], weights.at[tile], load_sem.at[tile])

    order = [25] + list(range(12)) + [24] + list(range(12, 24))
    for tile in order:
        load(tile).start()

    def ready(tiles):
        for tile in tiles:
            load(tile).wait()

    def count_copy(j):
        return remote(counts.at[dp], counts.at[dp], count_send.at[j], count_recv.at[j], column[j])

    def staged(tile, slot):
        return pltpu.make_async_copy(stage.at[slot], grads_ref.at[tile], stage_sem.at[slot])

    def put(tile, slot, half_of):
        staged(tile, slot).wait()
        for half in range(2):
            stage[slot, 256 * half : 256 * half + 256, :] = half_of(pl.ds(256 * half, 256))
        staged(tile, slot).start()

    small_ref[...] = jnp.zeros_like(small_ref)
    ids_col[...] = ids_ref[...].astype(jnp.float32).T
    length_one = length_ref[0]
    char = Block(length, 0, 0, entry, qkv, logs, attended, after, inner, leave)
    seg = Block(
        segments, 12, 2, seg_entry, seg_qkv, seg_logs, seg_attended, seg_after, seg_inner, seg_leave
    )
    temps = (turned, grad_inner, branch, upstream, turned_norm, key_sum, value_sum)

    def hot_rows(rows, which, offset, count):
        ids = ids_col[rows, which : which + 1] + float(offset)
        lane = lax.broadcasted_iota(jnp.int32, (ROWS, count), 1).astype(jnp.float32)
        return (ids == lane).astype(jnp.bfloat16)

    def hot_turned(which, offset, count):
        ids = ids_ref[which : which + 1, :] + offset
        line = lax.broadcasted_iota(jnp.int32, (count, length), 0)
        return (ids == line).astype(jnp.float32)

    ready([25])

    def embed(rows):
        entry[rows, :] = product(hot_rows(rows, 0, 0, vocab), weights[25, 0:vocab, :])

    each_block(length, embed)
    ready(range(12))
    block_run(char, weights, gains_ref)
    ready([24])

    def valid_rows(rows):
        line = lax.broadcasted_iota(jnp.int32, (ROWS, 1), 0) + rows.start
        return (line < length_one).astype(jnp.float32)

    def boundary(rows):
        low = leave[rows, :].astype(jnp.bfloat16)
        reach = jnp.tanh(product(low, weights[24]))
        logit = jnp.sum(reach * gains_ref[5:6, :], axis=1, keepdims=True) * root_width
        return low, reach, 1.0 / (1.0 + jnp.exp(-logit))

    def soft_step(number, total):
        rows = pl.ds(pl.multiple_of(number * ROWS, ROWS), ROWS)
        return total + jnp.sum(valid_rows(rows) * boundary(rows)[2], axis=0, keepdims=True)

    soft_local = lax.fori_loop(0, length // ROWS, soft_step, jnp.zeros((1, 1), jnp.float32))
    line = lax.broadcasted_iota(jnp.int32, (8, 128), 0)
    length_float = length_one.astype(jnp.float32)
    counts[dp] = jnp.where(line == 0, soft_local, jnp.where(line == 1, length_float, 0.0))
    for j in range(7):
        count_copy(j).start()

    pool = hot_turned(2, 1, segments)
    amounts = jnp.sum(pool, axis=1, keepdims=True)
    divisor = jnp.maximum(amounts, 1.0)
    seg_entry[...] = product(pool.astype(jnp.bfloat16), leave[...].astype(jnp.bfloat16)) / divisor
    ready(range(12, 24))
    block_run(seg, weights, gains_ref)

    for j in range(7):
        count_copy(j).wait_recv()
    total = counts[0]
    for j in range(1, 8):
        total = total + counts[j]
    soft_count, count_all = total[0:1, 0:1], total[1:2, 0:1]

    def head(number, carry):
        ce, head_sum = carry
        rows = pl.ds(pl.multiple_of(number * ROWS, ROWS), ROWS)
        lift = hot_rows(rows, 2, 0, segments)
        merged = leave[rows, :] + product(lift, seg_leave[...].astype(jnp.bfloat16))
        scale = root_scale(merged)
        gain = gains_ref[4:5, :]
        final_low = (merged * scale * gain).astype(jnp.bfloat16)
        table = weights[25, vocab : 2 * vocab, :]
        logits = product_nt(final_low, table)
        peak = jnp.max(logits, axis=1, keepdims=True)
        log_total = peak + jnp.log(jnp.sum(jnp.exp(logits - peak), axis=1, keepdims=True))
        target = hot_rows(rows, 1, 0, vocab).astype(jnp.float32)
        picked = jnp.sum(logits * target, axis=1, keepdims=True)
        valid = valid_rows(rows)
        ce = ce + jnp.sum(valid * (log_total - picked), axis=0, keepdims=True)
        share = valid / (micro_count * count_all)
        grad_logits = (jnp.exp(logits - log_total) - target) * share
        head_sum = head_sum + product(turn(grad_logits), final_low)
        back, gain_part = norm_back(merged, scale, gain, product(grad_logits.astype(jnp.bfloat16), table))
        small_ref[4:5, :] = small_ref[4:5, :] + gain_part
        grad[rows, :] = back
        return ce, head_sum

    ce_local, head_sum = lax.fori_loop(
        0, length // ROWS, head, (jnp.zeros((1, 1), jnp.float32), jnp.zeros((vocab, width), jnp.float32))
    )
    stage[...] = jnp.zeros_like(stage)
    for slot in range(4):
        staged(slot, slot).start()
    seg_grad[...] = exact_product(hot_turned(2, 0, segments).astype(jnp.bfloat16), grad[...])
    block_back(seg, seg_grad, weights, gains_ref, small_ref, temps, put)
    seg_grad[...] = seg_grad[...] / divisor

    count_rest = count_all - soft_count
    slope = (digamma(soft_count + 1.0) - digamma(count_rest + 1.0) + LOG_ODDS) / (count_all * micro_count)

    def join(rows):
        low, reach, chance = boundary(rows)
        logit = valid_rows(rows) * slope * chance * (1.0 - chance)
        gain = gains_ref[5:6, :]
        small_ref[5:6, :] = small_ref[5:6, :] + jnp.sum(logit * reach, axis=0, keepdims=True) * root_width
        pre = (logit * gain * root_width * (1.0 - reach * reach)).astype(jnp.bfloat16)
        branch[rows, :] = pre
        turned[:, rows] = turn(low)
        spread = exact_product(hot_rows(rows, 2, 1, segments), seg_grad[...])
        grad[rows, :] = (grad[rows, :] + spread) + product_nt(pre, weights[24])

    each_block(length, join)
    put(24, 0, lambda half: product(turned[half, :], branch[...]))
    block_back(char, grad, weights, gains_ref, small_ref, temps, put)
    staged(25, 3).wait()
    stage[3, 0:vocab, :] = exact_product(hot_turned(0, 0, vocab).astype(jnp.bfloat16), grad[...])
    stage[3, vocab : 2 * vocab, :] = head_sum
    staged(25, 3).start()

    lane = lax.broadcasted_iota(jnp.int32, (1, width), 1)
    small_ref[6:7, :] = jnp.where(
        lane == seq,
        ce_local,
        jnp.where(lane == seq + 8, soft_local, jnp.where(lane == seq + 16, length_float, 0.0)),
    )
    for slot in range(4):
        staged(slot, slot).wait()
    for j in range(7):
        count_copy(j).wait_send()


def step_call(length_one, tiles, ids, gains, micro_count):
    tile_count, width, _ = tiles.shape
    length = ids.shape[1]
    segments = SEG_DEV * lax.axis_size("seq")
    dma = pltpu.SemaphoreType.DMA
    vmem = pl.BlockSpec(memory_space=pltpu.VMEM)
    hbm = pl.BlockSpec(memory_space=pl.ANY)

    def full(*shape):
        return pltpu.VMEM(shape, jnp.float32)

    def half(*shape):
        return pltpu.VMEM(shape, jnp.bfloat16)

    def kept(count):
        return [
            full(count, width), half(count, 3 * width), full(4, 2, count), half(count, width),
            full(count, width), full(count, 4 * width), full(count, width), full(count, width),
        ]

    return pl.pallas_call(
        functools.partial(step_kernel, micro_count),
        out_shape=(
            jax.ShapeDtypeStruct((tile_count, width, width), jnp.float32),
            jax.ShapeDtypeStruct((8, width), jnp.float32),
        ),
        in_specs=[pl.BlockSpec(memory_space=pltpu.SMEM), hbm, vmem, vmem],
        out_specs=(hbm, vmem),
        scratch_shapes=[half(tile_count, width, width), dma((tile_count,))]
        + kept(length)
        + kept(segments)
        + [
            half(width, length), half(length, 4 * width), half(length, width), half(length, width),
            half(width, length), full(length, 128),
            full(length, 128), full(length, 8), full(4, width, width), dma((4,)),
            full(lax.axis_size("dp"), 8, 128), dma((7,)), dma((7,)),
        ],
        name="step",
        compiler_params=pltpu.CompilerParams(
            collective_id=2, has_side_effects=True, vmem_limit_bytes=STEP_VMEM
        ),
    )(length_one, tiles, ids, gains)


def whole_step(char_ids, targets, seg_ids, lengths, owner_slot, master, gain_rows):
    micro_count = char_ids.shape[0]
    ids = jnp.stack([char_ids[:, 0], targets[:, 0], seg_ids[:, 0]], axis=1)
    ids = jnp.pad(ids, ((0, 0), (0, 5), (0, 0)))
    tiles, ids = gather_tiles_kernel(master.astype(jnp.bfloat16), ids, owner_slot)
    ids = ids.transpose(1, 0, 2).reshape(8, -1)
    length_one = lax.dynamic_slice_in_dim(lengths[:, 0], lax.axis_index("seq"), 1)
    gains = jnp.pad(gain_rows, ((0, 2), (0, 0)))
    return step_call(length_one, tiles, ids, gains, micro_count)


def body(
    char_ids,
    targets,
    seg_ids,
    lengths,
    owner_slot,
    step_count,
    master,
    tile_first,
    tile_second,
    gain_rows,
    gain_first,
    gain_second,
):
    micro_count = char_ids.shape[0]
    model_width = master.shape[2]
    slot_count = master.shape[0] * lax.axis_size("seq")
    if (micro_count, lax.axis_size("seq"), lax.axis_size("dp")) == (4, 4, 8):
        tile_grads, small = whole_step(
            char_ids, targets, seg_ids, lengths, owner_slot, master, gain_rows
        )
        local = lax.axis_index("seq") * master.shape[0] + jnp.arange(master.shape[0])
        hot = local[:, None] == owner_slot[None, :]
        valid = jnp.any(hot, axis=1).astype(jnp.int32)
        source = jnp.sum(jnp.where(hot, jnp.arange(owner_slot.shape[0])[None, :], 0), axis=1)
        shard_total, small, squares = reduce_tiles_kernel(
            tile_grads, small, source, valid, master.shape[0]
        )
        gain_sum, square_sum = small[0:6], jnp.sum(squares)
        entropy, soft, count = (small[6, 8 * i : 8 * i + micro_count] for i in range(3))
        prior = -(
            lax.lgamma(count + 1.0)
            - lax.lgamma(soft + 1.0)
            - lax.lgamma(count - soft + 1.0)
            + soft * jnp.log(PRIOR_RATE)
            + (count - soft) * jnp.log(1.0 - PRIOR_RATE)
        )
        loss_total = jnp.sum((entropy + prior) / count) / micro_count
    else:
        tile_total = jnp.zeros((owner_slot.shape[0], model_width, model_width), jnp.float32)
        gain_total = jnp.zeros_like(gain_rows)
        loss_total = jnp.zeros((), jnp.float32)
        for micro in range(micro_count):
            tiles = gather_tiles(master, owner_slot)
            tile_part, gain_part, loss_part = micro_step(
                tiles,
                gain_rows,
                char_ids[micro, 0],
                targets[micro, 0],
                seg_ids[micro, 0],
                lengths[micro, 0],
                micro_count,
            )
            tile_total = tile_total + tile_part
            gain_total = gain_total + gain_part
            loss_total = loss_total + loss_part
        shard_total = reduce_tiles(tile_total, owner_slot, slot_count)
        gain_sum, square_sum = lax.psum((gain_total, jnp.sum(shard_total * shard_total)), ("dp", "seq"))
    grad_norm = jnp.sqrt(square_sum + jnp.sum(gain_sum * gain_sum))
    clip_factor = jnp.minimum(1.0, CLIP_NORM / (grad_norm + 1e-06))
    step_float = step_count[0].astype(jnp.float32)
    local_ids = lax.axis_index("seq") * master.shape[0] + jnp.arange(master.shape[0])
    owned = jnp.any(local_ids[:, None] == owner_slot[None, :], axis=1)[:, None, None]
    new_tiles, new_first, new_second = adam_step(
        master,
        tile_first,
        tile_second,
        shard_total * clip_factor,
        RATE_TILES,
        WEIGHT_DECAY,
        step_float,
    )
    master_new = jnp.where(owned, new_tiles, master)
    first_new = jnp.where(owned, new_first, tile_first)
    second_new = jnp.where(owned, new_second, tile_second)
    gains_new, gain_first_new, gain_second_new = adam_step(
        gain_rows, gain_first, gain_second, gain_sum * clip_factor, RATE_GAINS, 0.0, step_float
    )
    return (
        loss_total.reshape(1),
        grad_norm.reshape(1),
        master_new,
        first_new,
        second_new,
        master_new.astype(jnp.bfloat16),
        gains_new,
        gain_first_new,
        gain_second_new,
    )


def solution(mesh):
    return jax.shard_map(
        body,
        mesh=mesh,
        in_specs=(
            P(None, "dp", "seq"),
            P(None, "dp", "seq"),
            P(None, "dp", "seq"),
            P(None, "dp"),
            P(),
            P(),
            P("seq", "dp", None),
            P("seq", "dp", None),
            P("seq", "dp", None),
            P(),
            P(),
            P(),
        ),
        out_specs=(
            P(),
            P(),
            P("seq", "dp", None),
            P("seq", "dp", None),
            P("seq", "dp", None),
            P("seq", "dp", None),
            P(),
            P(),
            P(),
        ),
        check_vma=False,
    )
```

```python
import functools
import math

import jax
import jax.numpy as jnp
from jax import lax
from jax.experimental import pallas as pl
from jax.experimental.pallas import tpu as pltpu
from jax.sharding import PartitionSpec as P

HEADS = 8
SEG_DEV = 64


BETA_ONE = 0.9
BETA_TWO = 0.95
ADAM_EPS = 1e-08
WEIGHT_DECAY = 0.1
RATE_TILES = 0.03
RATE_GAINS = 0.2
CLIP_NORM = 0.05
PRIOR_RATE = 0.25
NORM_EPS = 1e-06
MASKED = -1e30
LOG_ODDS = math.log(1.0 - PRIOR_RATE) - math.log(PRIOR_RATE)


def product(left, right):
    return jnp.dot(left, right, preferred_element_type=jnp.float32)


def product_tn(left, right):
    return lax.dot_general(
        left, right, (((0,), (0,)), ((), ())), preferred_element_type=jnp.float32
    )


def product_nt(left, right):
    return lax.dot_general(
        left, right, (((1,), (1,)), ((), ())), preferred_element_type=jnp.float32
    )


def exact_tn(left, right):
    return lax.dot_general(
        left,
        right,
        (((0,), (0,)), ((), ())),
        precision=lax.Precision.HIGHEST,
        preferred_element_type=jnp.float32,
    )


def rms_norm(values, gain):
    return values * lax.rsqrt(jnp.mean(values * values, axis=-1, keepdims=True) + NORM_EPS) * gain


def split_heads(tensor):
    return tensor.reshape(tensor.shape[0], HEADS, tensor.shape[1] // HEADS).transpose(1, 0, 2)


def join_heads(tensor):
    return tensor.transpose(1, 0, 2).reshape(tensor.shape[1], tensor.shape[0] * tensor.shape[2])


def block_weights(tiles):
    w_qkv = jnp.concatenate([tiles[0], tiles[1], tiles[2]], axis=1)
    w_up = jnp.concatenate([tiles[4], tiles[5], tiles[6], tiles[7]], axis=1)
    w_down = jnp.concatenate([tiles[8], tiles[9], tiles[10], tiles[11]], axis=0)
    return (w_qkv, w_up, w_down)


def causal_mask(row_count, key_count):
    first_row = lax.axis_index("seq") * row_count
    return (first_row + jnp.arange(row_count))[:, None] >= jnp.arange(key_count)[None, :]


def block_forward(hidden_in, tiles, gain_attn, gain_ffn, segment):
    row_count, model_width = hidden_in.shape
    w_qkv, w_up, w_down = block_weights(tiles)
    normed = rms_norm(hidden_in, gain_attn).astype(jnp.bfloat16)
    qkv_low = product(normed, w_qkv).astype(jnp.bfloat16)
    if segment:
        gathered = lax.all_gather(qkv_low[:, model_width:], "seq", axis=0, tiled=True)
    else:
        gathered = lax.all_gather(qkv_low[:, model_width:], "seq", axis=0, tiled=True)
    allowed = causal_mask(row_count, gathered.shape[0])
    factor = (model_width // HEADS) ** (-0.5)

    def head_forward(triple):
        q_head, k_head, v_head = triple
        scores = jnp.where(allowed, product_nt(q_head, k_head) * factor, MASKED)
        peak = jnp.max(scores, axis=1, keepdims=True)
        log_total = peak + jnp.log(jnp.sum(jnp.exp(scores - peak), axis=1, keepdims=True))
        weights = jnp.exp(scores - log_total).astype(jnp.bfloat16)
        return (product(weights, v_head), log_total[:, 0])

    head_out, log_totals = lax.map(
        head_forward,
        (
            split_heads(qkv_low[:, :model_width]),
            split_heads(gathered[:, :model_width]),
            split_heads(gathered[:, model_width:]),
        ),
    )
    attended = join_heads(head_out).astype(jnp.bfloat16)
    after_attn = hidden_in + product(attended, tiles[3])
    inner = product(rms_norm(after_attn, gain_ffn).astype(jnp.bfloat16), w_up)
    block_out = after_attn + product(jax.nn.gelu(inner).astype(jnp.bfloat16), w_down)
    return (block_out, (hidden_in, qkv_low, gathered, log_totals, attended, after_attn, inner))


def block_backward(grad_out, saved, tiles, gain_attn, gain_ffn, segment):
    hidden_in, qkv_low, gathered, log_totals, attended, after_attn, inner = saved
    row_count, model_width = hidden_in.shape
    w_qkv, w_up, w_down = block_weights(tiles)
    grad_ffn = grad_out.astype(jnp.bfloat16)
    activated, gelu_pull = jax.vjp(jax.nn.gelu, inner)
    grad_down = product_tn(activated.astype(jnp.bfloat16), grad_ffn)
    grad_inner = gelu_pull(product_nt(grad_ffn, w_down))[0].astype(jnp.bfloat16)
    normed_ffn, ffn_pull = jax.vjp(rms_norm, after_attn, gain_ffn)
    grad_up = product_tn(normed_ffn.astype(jnp.bfloat16), grad_inner)
    grad_normed_in, grad_gain_ffn = ffn_pull(product_nt(grad_inner, w_up))
    grad_after = grad_out + grad_normed_in
    grad_branch = grad_after.astype(jnp.bfloat16)
    grad_wout = product_tn(attended, grad_branch)
    grad_attended = product_nt(grad_branch, tiles[3]).astype(jnp.bfloat16)
    allowed = causal_mask(row_count, gathered.shape[0])
    factor = (model_width // HEADS) ** (-0.5)

    def head_backward(bundle):
        q_head, k_head, v_head, upstream, log_head = bundle
        scores = jnp.where(allowed, product_nt(q_head, k_head) * factor, MASKED)
        weights = jnp.exp(scores - log_head[:, None])
        grad_values = product_tn(weights.astype(jnp.bfloat16), upstream)
        grad_weights = product_nt(upstream, v_head)
        inner_sum = jnp.sum(weights * grad_weights, axis=1, keepdims=True)
        grad_scores = (weights * (grad_weights - inner_sum)).astype(jnp.bfloat16)
        return (
            product(grad_scores, k_head) * factor,
            product_tn(grad_scores, q_head) * factor,
            grad_values,
        )

    grad_query, grad_keys, grad_values = lax.map(
        head_backward,
        (
            split_heads(qkv_low[:, :model_width]),
            split_heads(gathered[:, :model_width]),
            split_heads(gathered[:, model_width:]),
            split_heads(grad_attended),
            log_totals,
        ),
    )
    grad_kv_all = jnp.concatenate([join_heads(grad_keys), join_heads(grad_values)], axis=1)
    if segment:
        grad_kv = lax.psum_scatter(grad_kv_all, "seq", scatter_dimension=0, tiled=True)
    else:
        grad_kv = lax.psum_scatter(grad_kv_all, "seq", scatter_dimension=0, tiled=True)
    grad_qkv = jnp.concatenate([join_heads(grad_query), grad_kv], axis=1).astype(jnp.bfloat16)
    normed_attn, attn_pull = jax.vjp(rms_norm, hidden_in, gain_attn)
    grad_wqkv = product_tn(normed_attn.astype(jnp.bfloat16), grad_qkv)
    grad_normed_x, grad_gain_attn = attn_pull(product_nt(grad_qkv, w_qkv))
    grad_in = grad_after + grad_normed_x
    pieces = [
        grad_wqkv[:, part_index * model_width : (part_index + 1) * model_width]
        for part_index in range(3)
    ]
    pieces = pieces + [grad_wout]
    pieces = pieces + [
        grad_up[:, part_index * model_width : (part_index + 1) * model_width]
        for part_index in range(4)
    ]
    pieces = pieces + [
        grad_down[part_index * model_width : (part_index + 1) * model_width]
        for part_index in range(4)
    ]
    return (grad_in, jnp.stack(pieces), grad_gain_attn, grad_gain_ffn)


def micro_step(tiles, gain_rows, chars_row, target_row, segment_row, length_one, micro_count):
    char_count = chars_row.shape[0]
    model_width = tiles.shape[2]
    vocab_size = model_width // 2
    seq_count = lax.axis_size("seq")
    seg_total = SEG_DEV * seq_count
    position = lax.axis_index("seq") * char_count + jnp.arange(char_count)
    is_valid = (position < length_one).astype(jnp.float32)
    vocab_iota = jnp.arange(vocab_size)
    char_hot = chars_row[:, None] == vocab_iota[None, :]
    embed_low = tiles[25, :vocab_size]
    head_low = tiles[25, vocab_size:]
    start_hidden = product(char_hot.astype(jnp.bfloat16), embed_low)
    char_out, char_saved = block_forward(
        start_hidden, tiles[0:12], gain_rows[0], gain_rows[1], False
    )
    char_low = char_out.astype(jnp.bfloat16)
    boundary_hidden = jnp.tanh(product(char_low, tiles[24]))
    root_width = model_width ** (-0.5)
    boundary_prob = jax.nn.sigmoid(jnp.sum(boundary_hidden * gain_rows[5], axis=1) * root_width)
    slot_iota = jnp.arange(seg_total)
    pool_hot = segment_row[None, :] + 1 == slot_iota[:, None]
    lift_hot = segment_row[:, None] == slot_iota[None, :]
    part_sums = product(pool_hot.astype(jnp.bfloat16), char_low).reshape(
        seq_count, SEG_DEV, model_width
    )
    side_info = jnp.stack(
        [
            jnp.sum(pool_hot.astype(jnp.float32), axis=1),
            jnp.any(lift_hot, axis=0).astype(jnp.float32),
        ],
        axis=0,
    )
    side_info = side_info.reshape(2, seq_count, SEG_DEV).transpose(1, 0, 2)
    sums_in, side_in = (
        lax.all_to_all(part_sums, "seq", split_axis=0, concat_axis=0, tiled=True),
        lax.all_to_all(side_info, "seq", split_axis=0, concat_axis=0, tiled=True),
    )
    row_counts = jnp.sum(side_in[:, 0, :], axis=0)
    divisor = jnp.maximum(row_counts, 1.0)[:, None]
    pooled = jnp.sum(sums_in, axis=0) / divisor
    seg_out, seg_saved = block_forward(pooled, tiles[12:24], gain_rows[2], gain_rows[3], True)
    outgoing = side_in[:, 1, :, None].astype(jnp.bfloat16) * seg_out.astype(jnp.bfloat16)[None]
    returned = lax.all_to_all(outgoing, "seq", split_axis=0, concat_axis=0, tiled=True)
    merged = char_out + product(
        lift_hot.astype(jnp.bfloat16), returned.reshape(seg_total, model_width)
    )
    final_norm, final_pull = jax.vjp(rms_norm, merged, gain_rows[4])
    final_low = final_norm.astype(jnp.bfloat16)
    logits = product_nt(final_low, head_low)
    peak = jnp.max(logits, axis=1, keepdims=True)
    log_total = peak[:, 0] + jnp.log(jnp.sum(jnp.exp(logits - peak), axis=1))
    target_hot = (target_row[:, None] == vocab_iota[None, :]).astype(jnp.float32)
    picked = jnp.sum(logits * target_hot, axis=1)
    ce_local = jnp.sum(is_valid * (log_total - picked))
    ce_all, soft_count, count_all = lax.psum(
        (ce_local, jnp.sum(is_valid * boundary_prob), jnp.sum(is_valid)), ("dp", "seq")
    )
    weight_ce = is_valid / (micro_count * count_all)
    grad_logits = ((jnp.exp(logits - log_total[:, None]) - target_hot) * weight_ce[:, None]).astype(
        jnp.bfloat16
    )
    grad_head = product_tn(grad_logits, final_low)
    grad_merged, grad_gain_final = final_pull(product(grad_logits, head_low))
    grad_rows = exact_tn(lift_hot.astype(jnp.float32), grad_merged).reshape(
        seq_count, SEG_DEV, model_width
    )
    grad_seg = jnp.sum(
        lax.all_to_all(grad_rows, "seq", split_axis=0, concat_axis=0, tiled=True), axis=0
    )
    grad_pooled, seg_tiles, grad_gain_two, grad_gain_three = block_backward(
        grad_seg, seg_saved, tiles[12:24], gain_rows[2], gain_rows[3], True
    )
    grad_sums = (side_in[:, 0, :, None] > 0).astype(jnp.float32) * (grad_pooled / divisor)[None]
    grad_back = lax.all_to_all(grad_sums, "seq", split_axis=0, concat_axis=0, tiled=True).reshape(
        seg_total, model_width
    )
    grad_char = grad_merged + exact_tn(pool_hot.astype(jnp.float32), grad_back)
    prior_slope = (
        lax.digamma(soft_count + 1.0)
        - lax.digamma(count_all - soft_count + 1.0)
        - jnp.log(PRIOR_RATE)
        + jnp.log(1.0 - PRIOR_RATE)
    ) / (count_all * micro_count)
    grad_boundary_logit = is_valid * prior_slope * boundary_prob * (1.0 - boundary_prob)
    grad_gain_boundary = (
        jnp.sum(grad_boundary_logit[:, None] * boundary_hidden, axis=0) * root_width
    )
    grad_pre = (
        grad_boundary_logit[:, None]
        * gain_rows[5][None, :]
        * root_width
        * (1.0 - boundary_hidden * boundary_hidden)
    ).astype(jnp.bfloat16)
    grad_boundary = product_tn(char_low, grad_pre)
    grad_char = grad_char + product_nt(grad_pre, tiles[24])
    grad_start, char_tiles, grad_gain_zero, grad_gain_one = block_backward(
        grad_char, char_saved, tiles[0:12], gain_rows[0], gain_rows[1], False
    )
    grad_embed = exact_tn(char_hot.astype(jnp.float32), grad_start)
    tile_grads = jnp.concatenate(
        [
            char_tiles,
            seg_tiles,
            grad_boundary[None],
            jnp.concatenate([grad_embed, grad_head], axis=0)[None],
        ],
        axis=0,
    )
    gain_grads = jnp.stack(
        [
            grad_gain_zero,
            grad_gain_one,
            grad_gain_two,
            grad_gain_three,
            grad_gain_final,
            grad_gain_boundary,
        ]
    )
    prior_term = (
        -(
            lax.lgamma(count_all + 1.0)
            - lax.lgamma(soft_count + 1.0)
            - lax.lgamma(count_all - soft_count + 1.0)
            + soft_count * jnp.log(PRIOR_RATE)
            + (count_all - soft_count) * jnp.log(1.0 - PRIOR_RATE)
        )
        / count_all
    )
    return (tile_grads, gain_grads, (ce_all / count_all + prior_term) / micro_count)


def gather_tiles(master, owner_slot):
    shard_low = master.astype(jnp.bfloat16)
    full_rows = lax.all_gather(shard_low, "dp", axis=1, tiled=True)
    all_slots = lax.all_gather(full_rows, "seq", axis=0, tiled=True)
    return jnp.take(all_slots, owner_slot, axis=0)


def reduce_tiles(tile_grads, owner_slot, slot_count):
    placed = (
        jnp.zeros((slot_count,) + tile_grads.shape[1:], jnp.float32).at[owner_slot].set(tile_grads)
    )
    per_owner = lax.psum_scatter(placed, "seq", scatter_dimension=0, tiled=True)
    return lax.psum_scatter(per_owner, "dp", scatter_dimension=1, tiled=True)


def adam_step(param, moment_a, moment_b, grad_in, rate, decay, step_float):
    new_first = BETA_ONE * moment_a + (1.0 - BETA_ONE) * grad_in
    new_second = BETA_TWO * moment_b + (1.0 - BETA_TWO) * grad_in * grad_in
    first_hat = new_first / (1.0 - BETA_ONE**step_float)
    second_hat = new_second / (1.0 - BETA_TWO**step_float)
    updated = param - rate * (first_hat / (jnp.sqrt(second_hat) + ADAM_EPS) + decay * param)
    return (updated, new_first, new_second)


MESH = pl.DeviceIdType.MESH
VMEM_LIMIT = 60 * 1024 * 1024
STEP_VMEM = 63 * 1024 * 1024


def remote(src, dst, send_sem, recv_sem, peer):
    return pltpu.make_async_remote_copy(
        src_ref=src, dst_ref=dst, send_sem=send_sem, recv_sem=recv_sem, device_id=peer, device_id_type=MESH
    )


def places():
    dp = lax.axis_index("dp")
    seq = lax.axis_index("seq")
    return dp, seq, dp // 2, dp % 2


def seq_peer(seq, step):
    return ((seq // 2 + step // 2) % 2) * 2 + (seq % 2 + step % 2) % 2


def meet(peers):
    barrier = pltpu.get_barrier_semaphore()
    for peer in peers:
        pl.semaphore_signal(barrier, inc=1, device_id=peer, device_id_type=MESH)
    pl.semaphore_wait(barrier, len(peers))


CODE_TOP = 32000.0
ROUNDER = 12582912.0


def encode(value):
    upper, lower = value[0:8, :], value[8:16, :]
    size = jnp.maximum(jnp.abs(upper), jnp.abs(lower))
    most = jnp.maximum(jnp.max(size, axis=1, keepdims=True), 1e-30)
    ratio = CODE_TOP / most
    coded = jnp.concatenate([upper * ratio, lower * ratio], axis=0)
    coded = ((coded + ROUNDER) - ROUNDER).astype(jnp.int32).astype(jnp.int16)
    return coded, most * (1.0 / CODE_TOP)


def decode(coded, unit):
    value = coded.astype(jnp.int32).astype(jnp.float32)
    return jnp.concatenate([value[0:8, :] * unit, value[8:16, :] * unit], axis=0)


def reduce_kernel(
    source_ref, valid_ref, grads_ref, small_ref, out_ref, small_out, square_out,
    own, other, b1_out, b1_in, b2_out, b2_in, c_out, c_in, d_out, d_in,
    b1_unit_out, b1_unit_in, b2_unit_out, b2_unit_in, c_unit_out, c_unit_in, d_unit_out, d_unit_in,
    final, small_dp, small_seq, square_dp, square_seq,
    l_sem, a_send, a_recv, b1_send, b1_recv, b2_send, b2_recv, c_send, c_recv, d_send, d_recv,
    p_send, p_recv, q_send, q_recv, r_send, r_recv, s_send, s_recv,
):
    dp, seq, z, core = places()
    across, along = seq % 2, seq // 2
    held = out_ref.shape[0]
    tile_count = grads_ref.shape[0]
    pairs = tile_count // 2
    sibling = (z * 2 + 1 - core, seq)
    beside = [(dp, along * 2 + 1 - across), (dp, (1 - along) * 2 + across)]
    side = [(dp, seq_peer(seq, j)) for j in (1, 2, 3)]
    column = [((dp + j) % 8, seq) for j in range(1, 8)]
    tower = [((z + j) % 4 * 2 + core, seq) for j in (1, 2, 3)]
    meet(side + column)
    lane = lax.broadcasted_iota(jnp.int32, (8, 128), 1)

    def core_copy(pair):
        two = pl.ds(pair * 2, 2)
        return remote(grads_ref.at[two, :, 1 - core], other.at[two], a_send.at[pair], a_recv.at[pair], sibling)

    def local_copy(pair):
        two = pl.ds(pair * 2, 2)
        return pltpu.make_async_copy(grads_ref.at[two, :, core], own.at[two], l_sem.at[pair])

    def with_units(values, units, send, recv, peer):
        return [
            remote(values[0], values[1], send.at[0], recv.at[0], peer),
            remote(units[0], units[1], send.at[1], recv.at[1], peer),
        ]

    def first_copies(pair, order):
        tile = pair * 2 + order
        return with_units(
            (b1_out.at[tile], b1_in.at[tile]), (b1_unit_out.at[tile], b1_unit_in.at[tile]),
            b1_send.at[tile], b1_recv.at[tile], beside[order],
        )

    def second_copies(pair, order):
        tile = pair * 2 + order
        return with_units(
            (b2_out.at[tile], b2_in.at[tile]), (b2_unit_out.at[tile], b2_unit_in.at[tile]),
            b2_send.at[tile], b2_recv.at[tile], beside[1 - order],
        )

    def tower_copies(pair, j):
        two = pl.ds(pair * 2, 2)
        return with_units(
            (c_out.at[j, two], c_in.at[j, two]), (c_unit_out.at[j, pair], c_unit_in.at[j, pair]),
            c_send.at[j, pair], c_recv.at[j, pair], tower[j],
        )

    def share_copies(pair, j):
        two = pl.ds(pair * 2, 2)
        return with_units(
            (d_out.at[two], d_in.at[j, two]), (d_unit_out.at[pair], d_unit_in.at[j, pair]),
            d_send.at[j, pair], d_recv.at[j, pair], side[j],
        )

    def start_all(copies):
        for copy in copies:
            copy.start()

    def arrive_all(copies):
        for copy in copies:
            copy.wait_recv()

    def sent_all(copies):
        for copy in copies:
            copy.wait_send()

    def small_copy(j):
        return remote(small_ref, small_dp.at[dp], p_send.at[j], p_recv.at[j], column[j])

    def small_side(j):
        return remote(small_seq.at[seq], small_seq.at[seq], q_send.at[j], q_recv.at[j], side[j])

    def square_copy(j):
        return remote(square_dp.at[dp], square_dp.at[dp], r_send.at[j], r_recv.at[j], column[j])

    def square_side(j):
        return remote(square_seq.at[seq], square_seq.at[seq], s_send.at[j], s_recv.at[j], side[j])

    for j in range(7):
        small_copy(j).start()

    def launch(pair, carry):
        core_copy(pair).start()
        local_copy(pair).start()
        return carry

    lax.fori_loop(0, pairs, launch, 0)

    def cell(tile, order, floor, line, mine):
        if order == 0:
            return (tile, floor, line, across if mine else 1 - across)
        return (tile, floor, along if mine else 1 - along, line)

    def stage_one(pair):
        core_copy(pair).wait_recv()
        local_copy(pair).wait()

        def add(step, carry):
            tile, floor = pair * 2 + step // 4, step % 4
            own[tile, floor] = own[tile, floor] + other[tile, floor]
            return carry

        lax.fori_loop(0, 8, add, 0)
        for order in range(2):
            tile = pair * 2 + order
            units = jnp.zeros((8, 128), jnp.float32)
            for floor in range(4):
                for line in range(2):
                    coded, unit = encode(own[cell(tile, order, floor, line, False)])
                    b1_out[tile, floor * 2 + line] = coded
                    units = jnp.where(lane == floor * 2 + line, unit, units)
            b1_unit_out[tile] = units
            start_all(first_copies(pair, order))

    def stage_two(pair):
        for order in range(2):
            tile = pair * 2 + order
            arrive_all(first_copies(pair, order))
            got = b1_unit_in[tile]
            units = jnp.zeros((8, 128), jnp.float32)
            keep = along if order == 0 else across
            for floor in range(4):
                for line in range(2):
                    block = floor * 2 + line
                    spot = cell(tile, order, floor, line, True)
                    own[spot] = own[spot] + decode(b1_in[tile, block], got[:, block : block + 1])
                spot = cell(tile, order, floor, 1 - keep, True)
                coded, unit = encode(own[spot])
                b2_out[tile, floor] = coded
                units = jnp.where(lane == floor, unit, units)
            b2_unit_out[tile] = units
            start_all(second_copies(pair, order))

    def stage_three(pair):
        for order in range(2):
            tile = pair * 2 + order
            arrive_all(second_copies(pair, order))
            got = b2_unit_in[tile]
            for floor in range(4):
                spot = (tile, floor, along, across)
                own[spot] = own[spot] + decode(b2_in[tile, floor], got[:, floor : floor + 1])
        for j in range(3):
            units = jnp.zeros((8, 128), jnp.float32)
            for order in range(2):
                tile = pair * 2 + order
                coded, unit = encode(own[tile, (z + j + 1) % 4, along, across])
                c_out[j, tile] = coded
                units = jnp.where(lane == order, unit, units)
            c_unit_out[j, pair] = units
            start_all(tower_copies(pair, j))

    def stage_four(pair):
        for j in range(3):
            arrive_all(tower_copies(pair, j))
        units = jnp.zeros((8, 128), jnp.float32)
        for order in range(2):
            tile = pair * 2 + order
            total = own[tile, z, along, across]
            for j in range(3):
                total = total + decode(c_in[j, tile], c_unit_in[j, pair][:, order : order + 1])
            final[tile, seq] = total
            coded, unit = encode(total)
            d_out[tile] = coded
            units = jnp.where(lane == order, unit, units)
        d_unit_out[pair] = units
        for j in range(3):
            start_all(share_copies(pair, j))

    def stage_five(pair):
        for j in range(3):
            arrive_all(share_copies(pair, j))
            for order in range(2):
                tile = pair * 2 + order
                final[tile, side[j][1]] = decode(d_in[j, tile], d_unit_in[j, pair][:, order : order + 1])

    stages = (stage_one, stage_two, stage_three, stage_four, stage_five)
    lag = 2

    def tick(step, carry):
        for number, stage in enumerate(stages):
            pair = step - lag * number

            @pl.when(jnp.logical_and(pair >= 0, pair < pairs))
            def _():
                stage(pair)

        return carry

    lax.fori_loop(0, 4, tick, 0)
    small_dp[dp] = small_ref[...]
    for j in range(7):
        small_copy(j).wait_recv()
    total = small_dp[0]
    for j in range(1, 8):
        total = total + small_dp[j]
    small_seq[seq] = total
    for j in range(3):
        small_side(j).start()
    lax.fori_loop(4, pairs + lag * 4, tick, 0)

    def collect(slot, square):
        keep = valid_ref[slot] > 0
        for quarter in range(4):
            value = final[source_ref[slot], quarter]
            value = jnp.where(keep, value, jnp.zeros_like(value))
            out_ref[slot, quarter * 16 : quarter * 16 + 16, :] = value
            square = square + value * value
        return square

    square = lax.fori_loop(0, held, collect, jnp.zeros((16, out_ref.shape[2]), jnp.float32))
    folded = square[0:8, 0:128]
    for r in range(2):
        for w in range(out_ref.shape[2] // 128):
            if r or w:
                folded = folded + square[8 * r : 8 * r + 8, 128 * w : 128 * w + 128]
    square_dp[dp] = folded
    for j in range(7):
        square_copy(j).start()
    for j in range(3):
        small_side(j).wait_recv()
    small_out[...] = (small_seq[0] + small_seq[1]) + (small_seq[2] + small_seq[3])
    for j in range(7):
        square_copy(j).wait_recv()
    total = square_dp[0]
    for j in range(1, 8):
        total = total + square_dp[j]
    square_seq[seq] = total
    for j in range(3):
        square_side(j).start()
    for j in range(3):
        square_side(j).wait_recv()
    square_out[...] = (square_seq[0] + square_seq[1]) + (square_seq[2] + square_seq[3])
    for j in range(7):
        small_copy(j).wait_send()
        square_copy(j).wait_send()
    for j in range(3):
        small_side(j).wait_send()
        square_side(j).wait_send()

    def drain(pair, carry):
        core_copy(pair).wait_send()
        for order in range(2):
            sent_all(first_copies(pair, order))
            sent_all(second_copies(pair, order))
        for j in range(3):
            sent_all(tower_copies(pair, j))
            sent_all(share_copies(pair, j))
        return carry

    lax.fori_loop(0, pairs, drain, 0)


def reduce_tiles_kernel(grads, small, source, valid, held):
    tile_count, height, width = grads.shape
    seq_count, dp_count = lax.axis_size("seq"), lax.axis_size("dp")
    rows = height // dp_count
    pairs = tile_count // 2
    dma = pltpu.SemaphoreType.DMA
    vmem = pl.BlockSpec(memory_space=pltpu.VMEM)
    smem = pl.BlockSpec(memory_space=pltpu.SMEM)

    def buffer(*shape):
        return pltpu.VMEM(shape, jnp.float32)

    def codes(*shape):
        return pltpu.VMEM(shape + (16, width), jnp.int16)

    return pl.pallas_call(
        reduce_kernel,
        out_shape=(
            jax.ShapeDtypeStruct((held, rows, width), jnp.float32),
            jax.ShapeDtypeStruct(small.shape, jnp.float32),
            jax.ShapeDtypeStruct((8, 128), jnp.float32),
        ),
        in_specs=[smem, smem, pl.BlockSpec(memory_space=pl.ANY), vmem],
        out_specs=(vmem, vmem, vmem),
        scratch_shapes=[
            buffer(tile_count, 4, 2, 2, 16, width),
            buffer(tile_count, 4, 2, 2, 16, width),
            codes(tile_count, 8), codes(tile_count, 8),
            codes(tile_count, 4), codes(tile_count, 4),
            codes(3, tile_count), codes(3, tile_count),
            codes(tile_count), codes(3, tile_count),
            buffer(tile_count, 8, 128), buffer(tile_count, 8, 128),
            buffer(tile_count, 8, 128), buffer(tile_count, 8, 128),
            buffer(3, pairs, 8, 128), buffer(3, pairs, 8, 128),
            buffer(pairs, 8, 128), buffer(3, pairs, 8, 128),
            buffer(tile_count, 4, 16, width),
            buffer(dp_count, *small.shape),
            buffer(seq_count, *small.shape),
            buffer(dp_count, 8, 128),
            buffer(seq_count, 8, 128),
            dma((pairs,)), dma((pairs,)), dma((pairs,)),
            dma((tile_count, 2)), dma((tile_count, 2)), dma((tile_count, 2)), dma((tile_count, 2)),
            dma((3, pairs, 2)), dma((3, pairs, 2)), dma((3, pairs, 2)), dma((3, pairs, 2)),
            dma((7,)), dma((7,)), dma((3,)), dma((3,)), dma((7,)), dma((7,)), dma((3,)), dma((3,)),
        ],
        name="reduce_tiles",
        compiler_params=pltpu.CompilerParams(
            collective_id=1, has_side_effects=True, vmem_limit_bytes=VMEM_LIMIT
        ),
    )(source, valid, grads.reshape(tile_count, 4, 2, 2, 2, 16, width), small)


def head_mask(shape, head):
    lane = lax.broadcasted_iota(jnp.int32, shape, 1)
    return (lane >= 64) if head else (lane < 64)


def scores_t(k_pair, q_head, first_row):
    scores = product_nt(k_pair, q_head)
    count, queries = scores.shape
    key = lax.broadcasted_iota(jnp.int32, (queries, queries), 0)
    query = lax.broadcasted_iota(jnp.int32, (queries, queries), 1)
    own = jnp.where(key <= query, scores[first_row:], MASKED)
    return own if first_row == 0 else jnp.concatenate([scores[:first_row], own], axis=0)


ROWS = 256
LAG = 2
START = 10


def split_three(value):
    high = value.astype(jnp.bfloat16)
    rest = value - high.astype(jnp.float32)
    middle = rest.astype(jnp.bfloat16)
    return high, middle, (rest - middle.astype(jnp.float32)).astype(jnp.bfloat16)


def exact_product(hot, value):
    high, middle, low = split_three(value)
    return (product(hot, low) + product(hot, middle)) + product(hot, high)


def turn(value):
    return value.astype(jnp.float32).T.astype(jnp.bfloat16)


def root_scale(value):
    return lax.rsqrt(jnp.mean(value * value, axis=-1, keepdims=True) + NORM_EPS)


def norm_back(value, scale, gain, grad):
    unit = value * scale
    weighted = grad * gain
    inner = jnp.mean(weighted * unit, axis=-1, keepdims=True)
    return scale * (weighted - unit * inner), jnp.sum(grad * unit, axis=0, keepdims=True)


def gelu_both(value):
    root = 0.7978845608028654
    square = value * value
    reach = jnp.tanh(root * value * (1.0 + 0.044715 * square))
    part = 0.5 * (1.0 + reach)
    slope = part + value * (0.5 * (1.0 - reach * reach)) * (root * (1.0 + 3.0 * 0.044715 * square))
    return value * part, slope


def digamma(value):
    moved = value + 8.0
    inverse = 1.0 / moved
    square = inverse * inverse
    series = square * (1.0 / 12.0 - square * (1.0 / 120.0 - square * (1.0 / 252.0)))
    total = jnp.log(moved) - 0.5 * inverse - series
    for number in range(8):
        total = total - 1.0 / (value + float(number))
    return total


def each_block(length, body):
    def step(number, carry):
        body(pl.ds(pl.multiple_of(number * ROWS, ROWS), ROWS))
        return carry

    lax.fori_loop(0, length // ROWS, step, 0)


class Block:
    def __init__(self, length, first_tile, place, gain_row, entry, qkv, logs, attended, after, inner, leave):
        self.length, self.tile, self.place, self.gain_row = length, first_tile, place, gain_row
        self.entry, self.qkv, self.logs, self.attended = entry, qkv, logs, attended
        self.after, self.inner, self.leave = after, inner, leave


def attend(block, pump):
    length = block.length

    def pair_step(pair, carry):
        lanes = [pl.ds(pl.multiple_of(part * 512 + pair * 128, 128), 128) for part in range(3)]
        for first in range(0, length, ROWS):
            span = first + ROWS
            q_pair = block.qkv[first:span, lanes[0]] * jnp.asarray(0.125, jnp.bfloat16)
            outs = []
            for head in range(2):
                q_head = jnp.where(head_mask(q_pair.shape, head), q_pair, jnp.zeros_like(q_pair))
                scores = scores_t(block.qkv[0:span, lanes[1]], q_head, first)
                peak = jnp.max(scores, axis=0, keepdims=True)
                raised = jnp.exp(scores - peak)
                total = jnp.sum(raised, axis=0, keepdims=True)
                weights = (raised * (1.0 / total)).astype(jnp.bfloat16)
                block.logs[pair, head : head + 1, first:span] = peak + jnp.log(total)
                outs.append(product_tn(weights, block.qkv[0:span, lanes[2]]))
            merged = jnp.where(head_mask(outs[0].shape, 0), outs[0], outs[1])
            block.attended[first:span, lanes[0]] = merged.astype(jnp.bfloat16)
        pump(pair)
        return carry

    lax.fori_loop(0, 4, pair_step, 0)


def attend_back(block, upstream, grad_qkv, key_sum, value_sum):
    length = block.length

    def pair_step(pair, carry):
        lanes = [pl.ds(pl.multiple_of(part * 512 + pair * 128, 128), 128) for part in range(3)]
        for first in reversed(range(0, length, ROWS)):
            span = first + ROWS
            q_pair = block.qkv[first:span, lanes[0]] * jnp.asarray(0.125, jnp.bfloat16)
            up_pair = upstream[first:span, lanes[0]]
            queries, keys, values = [], [], []
            for head in range(2):
                keep = head_mask(q_pair.shape, head)
                q_head = jnp.where(keep, q_pair, jnp.zeros_like(q_pair))
                up_head = jnp.where(keep, up_pair, jnp.zeros_like(up_pair))
                k_pair = block.qkv[0:span, lanes[1]]
                scores = scores_t(k_pair, q_head, first)
                weights = jnp.exp(scores - block.logs[pair, head : head + 1, first:span])
                grad_weights = product_nt(block.qkv[0:span, lanes[2]], up_head)
                values.append(product(weights.astype(jnp.bfloat16), up_head))
                inner_sum = jnp.sum(weights * grad_weights, axis=0, keepdims=True)
                grad_scores = (weights * (grad_weights - inner_sum)).astype(jnp.bfloat16)
                keys.append(product(grad_scores, q_head))
                queries.append(product_tn(grad_scores, k_pair))
            merged = jnp.where(head_mask(queries[0].shape, 0), queries[0], queries[1]) * 0.125
            grad_qkv[first:span, lanes[0]] = merged.astype(jnp.bfloat16)
            if span == length:
                key_sum[0:span, :] = keys[0] + keys[1]
                value_sum[0:span, :] = values[0] + values[1]
            else:
                key_sum[0:span, :] = key_sum[0:span, :] + (keys[0] + keys[1])
                value_sum[0:span, :] = value_sum[0:span, :] + (values[0] + values[1])
        grad_qkv[0:length, lanes[1]] = key_sum[0:length, :].astype(jnp.bfloat16)
        grad_qkv[0:length, lanes[2]] = value_sum[0:length, :].astype(jnp.bfloat16)
        return carry

    lax.fori_loop(0, 4, pair_step, 0)


def block_run(block, matrix, gains, pumps):
    place = block.place
    gain_attn = gains[block.gain_row : block.gain_row + 1, :]
    gain_ffn = gains[block.gain_row + 1 : block.gain_row + 2, :]

    def project(rows):
        value = block.entry[rows, :]
        normed = (value * root_scale(value) * gain_attn).astype(jnp.bfloat16)
        for part in range(3):
            block.qkv[rows, 512 * part : 512 * part + 512] = product(normed, matrix(place + part)).astype(
                jnp.bfloat16
            )

    each_block(block.length, project)
    pumps[0]()
    attend(block, pumps[1])
    pumps[2]()

    def feed(rows):
        after = block.entry[rows, :] + product(block.attended[rows, :], matrix(place + 3))
        block.after[rows, :] = after
        normed = (after * root_scale(after) * gain_ffn).astype(jnp.bfloat16)
        total = jnp.zeros_like(after)
        for part in range(4):
            inner = product(normed, matrix(place + 4 + part))
            block.inner[rows, 512 * part : 512 * part + 512] = inner
            active = gelu_both(inner)[0].astype(jnp.bfloat16)
            total = total + product(active, matrix(place + 8 + part))
        block.leave[rows, :] = after + total
        pumps[3](rows.start // ROWS)

    each_block(block.length, feed)


def block_back(block, grad, matrix, gains, gain_sums, temps, put):
    length, tile, place = block.length, block.tile, block.place
    gain_attn = gains[block.gain_row : block.gain_row + 1, :]
    gain_ffn = gains[block.gain_row + 1 : block.gain_row + 2, :]
    turned, grad_inner, branch, upstream, turned_norm, key_sum, value_sum = temps
    grad_low, grad_qkv = branch, grad_inner
    all_rows = pl.ds(0, length)

    def down(part):
        def rows_step(rows):
            low = grad[rows, :].astype(jnp.bfloat16)
            columns = pl.ds(pl.multiple_of(part * 512, 512), 512)
            active, slope = gelu_both(block.inner[rows, columns])
            turned[:, rows] = turn(active)
            grad_inner[rows, columns] = (product_nt(low, matrix(place + 8 + part)) * slope).astype(jnp.bfloat16)

        each_block(length, rows_step)

    def low_step(rows):
        grad_low[rows, :] = grad[rows, :].astype(jnp.bfloat16)

    each_block(length, low_step)

    def down_step(part, carry):
        down(part)
        put(tile + 8 + part, part, lambda half: product(turned[half, all_rows], grad_low[all_rows, :]))
        return carry

    lax.fori_loop(0, 4, down_step, 0)

    def middle(rows):
        after = block.after[rows, :]
        scale = root_scale(after)
        turned_norm[:, rows] = turn(after * scale * gain_ffn)
        turned[:, rows] = turn(block.attended[rows, :])
        total = jnp.zeros_like(after)
        for part in range(4):
            total = total + product_nt(
                grad_inner[rows, 512 * part : 512 * part + 512], matrix(place + 4 + part)
            )
        back, gain_part = norm_back(after, scale, gain_ffn, total)
        row = block.gain_row + 1
        gain_sums[row : row + 1, :] = gain_sums[row : row + 1, :] + gain_part
        grad_after = grad[rows, :] + back
        grad[rows, :] = grad_after
        low = grad_after.astype(jnp.bfloat16)
        branch[rows, :] = low
        upstream[rows, :] = product_nt(low, matrix(place + 3)).astype(jnp.bfloat16)

    each_block(length, middle)

    def up_step(part, carry):
        columns = pl.ds(pl.multiple_of(part * 512, 512), 512)
        put(tile + 4 + part, part, lambda half: product(turned_norm[half, all_rows], grad_inner[all_rows, columns]))
        return carry

    lax.fori_loop(0, 4, up_step, 0)
    put(tile + 3, 0, lambda half: product(turned[half, all_rows], branch[all_rows, :]))
    attend_back(block, upstream, grad_qkv, key_sum, value_sum)

    def enter(rows):
        value = block.entry[rows, :]
        scale = root_scale(value)
        turned_norm[:, rows] = turn(value * scale * gain_attn)
        total = jnp.zeros_like(value)
        for part in range(3):
            total = total + product_nt(grad_qkv[rows, 512 * part : 512 * part + 512], matrix(place + part))
        back, gain_part = norm_back(value, scale, gain_attn, total)
        row = block.gain_row
        gain_sums[row : row + 1, :] = gain_sums[row : row + 1, :] + gain_part
        grad[rows, :] = grad[rows, :] + back

    each_block(length, enter)

    def qkv_step(part, carry):
        columns = pl.ds(pl.multiple_of(part * 512, 512), 512)
        put(tile + part, part, lambda half: product(turned_norm[half, all_rows], grad_qkv[all_rows, columns]))
        return carry

    lax.fori_loop(0, 3, qkv_step, 0)


def step_kernel(
    micro_count, length_ref, local_ref, valid_ref, master_ref, ids_ref, gains_ref, grads_ref, small_ref,
    weights, entry, qkv, logs, attended, after, inner, leave, grad,
    seg_entry, seg_qkv, seg_logs, seg_attended, seg_after, seg_inner, seg_leave, seg_grad,
    turned, grad_inner, branch, upstream, turned_norm, key_sum, value_sum,
    ids_row, ids_col, stage, stage_sem, counts, count_send, count_recv, i_send, i_recv, i_own,
    p_send, p_recv, z_send, z_recv, s_send, s_recv, d_send, d_recv, c_send, c_recv,
):
    dp, seq, z, core = places()
    across, along = seq % 2, seq // 2
    length = entry.shape[0]
    width = entry.shape[1]
    segments = seg_entry.shape[0]
    vocab = width // 2
    root_width = width ** (-0.5)
    groups = weights.shape[0] // 2
    sibling = (z * 2 + 1 - core, seq)
    beside = [along * 2 + 1 - across, (1 - along) * 2 + across]
    side = [seq_peer(seq, j) for j in (1, 2, 3)]
    column = [((dp + j) % 8, seq) for j in range(1, 8)]
    tower = [((z + j) % 4 * 2 + core, seq) for j in (1, 2, 3)]
    meet([(dp, peer) for peer in side] + column)

    def ids_copy(j):
        part = pl.ds(pl.multiple_of(seq * ids_ref.shape[2], 256), ids_ref.shape[2])
        return remote(ids_ref.at[side[j]], ids_row.at[:, part], i_send.at[j], i_recv.at[j], (dp, side[j]))

    def own_ids():
        part = pl.ds(pl.multiple_of(seq * ids_ref.shape[2], 256), ids_ref.shape[2])
        return pltpu.make_async_copy(ids_ref.at[seq], ids_row.at[:, part], i_own)

    def part_of(which):
        return pl.ds(pl.multiple_of(which * width, width), width)

    def peer_copy(group, j):
        return remote(
            grad_inner.at[pl.ds(pl.multiple_of(group * 32, 32), 32), part_of(side[j])],
            grad_inner.at[pl.ds(pl.multiple_of(512 + group * 32, 32), 32), part_of(j)],
            p_send.at[j, group], p_recv.at[j, group], (dp, side[j]),
        )

    def tower_copy(group, j):
        spot = weights.at[pl.ds(group * 2, 2), z, core, seq]
        return remote(spot, spot, z_send.at[j, group], z_recv.at[j, group], tower[j])

    def side_copy(group, way):
        spot = weights.at[pl.ds(group * 2, 2), :, core, seq]
        return remote(spot, spot, s_send.at[way, group], s_recv.at[way, group], (dp, beside[way]))

    def corner_copy(group, way):
        spot = weights.at[group * 2 + way, :, core, beside[way]]
        return remote(spot, spot, d_send.at[way, group], d_recv.at[way, group], (dp, beside[1 - way]))

    def core_copy(group):
        spot = weights.at[pl.ds(group * 2, 2), :, core]
        return remote(spot, spot, c_send.at[group], c_recv.at[group], sibling)

    def offer(group):
        for j in (2, 0, 1):
            peer_copy(group, j).start()

    def combine(group):
        for j in range(3):
            peer_copy(group, j).wait_recv()
        for number in range(2):
            row = group * 32 + number * 16
            value = grad_inner[pl.ds(pl.multiple_of(row, 16), 16), part_of(seq)]
            for j in range(3):
                value = value + grad_inner[pl.ds(pl.multiple_of(512 + row, 16), 16), pl.ds(j * width, width)]
            weights[group * 2 + number, z, core, seq] = value
        for j in range(3):
            tower_copy(group, j).start()

    def widen(group):
        for j in range(3):
            tower_copy(group, j).wait_recv()
        for way in range(2):
            side_copy(group, way).start()

    def corner(group):
        for way in range(2):
            side_copy(group, way).wait_recv()
        for way in range(2):
            corner_copy(group, way).start()

    def share(group):
        for way in range(2):
            corner_copy(group, way).wait_recv()
        core_copy(group).start()

    stages = (offer, combine, widen, corner, share)

    def tick(number):
        for order, stage_of in enumerate(stages):
            group = number - LAG * order

            @pl.when(jnp.logical_and(group >= 0, group < groups))
            def _():
                stage_of(group)

    def ticks(start, stop):
        def body(number, carry):
            tick(number)
            return carry

        lax.fori_loop(start, stop, body, 0)

    def arrived(first, last):
        def body(group, carry):
            core_copy(group).wait_recv()
            return carry

        lax.fori_loop(first, last, body, 0)

    for j in range(3):
        ids_copy(j).start()
    own_ids().start()

    def pick(place, carry):
        value = master_ref[local_ref[place]]
        value = jnp.where(valid_ref[place] > 0, value, jnp.zeros_like(value)).astype(jnp.bfloat16)
        for quarter in range(4):
            grad_inner[pl.ds(pl.multiple_of(place * 16, 16), 16), quarter * width : quarter * width + width] = value[
                16 * quarter : 16 * quarter + 16
            ]
        return carry

    lax.fori_loop(0, groups * 2, pick, 0)
    ticks(0, START)

    def matrix(place):
        return weights[place].reshape(width, width)

    def matrix_half(which):
        return weights[0, 2 * which : 2 * which + 2].reshape(vocab, width)

    def count_copy(j):
        return remote(counts.at[dp], counts.at[dp], count_send.at[j], count_recv.at[j], column[j])

    def staged(tile, slot):
        return pltpu.make_async_copy(stage.at[slot], grads_ref.at[tile], stage_sem.at[slot])

    def put(tile, slot, half_of):
        staged(tile, slot).wait()
        for half in range(2):
            stage[slot, 256 * half : 256 * half + 256, :] = half_of(pl.ds(256 * half, 256))
        staged(tile, slot).start()

    small_ref[...] = jnp.zeros_like(small_ref)
    own_ids().wait()
    for j in range(3):
        ids_copy(j).wait_recv()
    ids_col[...] = ids_row[...].astype(jnp.float32).T
    length_one = length_ref[0]
    char = Block(length, 0, 1, 0, entry, qkv, logs, attended, after, inner, leave)
    seg = Block(
        segments, 12, 14, 2, seg_entry, seg_qkv, seg_logs, seg_attended, seg_after, seg_inner, seg_leave
    )
    temps = (turned, grad_inner, branch, upstream, turned_norm, key_sum, value_sum)

    def hot_rows(rows, which, offset, count):
        ids = ids_col[rows, which : which + 1] + float(offset)
        lane = lax.broadcasted_iota(jnp.int32, (ROWS, count), 1).astype(jnp.float32)
        return (ids == lane).astype(jnp.bfloat16)

    def hot_turned(which, offset, count):
        ids = ids_row[which : which + 1, :] + offset
        line = lax.broadcasted_iota(jnp.int32, (count, length), 0)
        return (ids == line).astype(jnp.float32)

    arrived(0, 2)

    def embed(rows):
        entry[rows, :] = product(hot_rows(rows, 0, 0, vocab), matrix_half(0))

    each_block(length, embed)
    tick(START)
    block_run(
        char,
        matrix,
        gains_ref,
        (
            lambda: tick(START + 1),
            lambda pair: tick(START + 2 + pair),
            lambda: arrived(2, 7),
            lambda number: tick(START + 6 + number),
        ),
    )
    ticks(START + 10, groups + LAG * (len(stages) - 1))

    def valid_rows(rows):
        line = lax.broadcasted_iota(jnp.int32, (ROWS, 1), 0) + rows.start
        return (line < length_one).astype(jnp.float32)

    def boundary(rows):
        low = leave[rows, :].astype(jnp.bfloat16)
        reach = jnp.tanh(product(low, matrix(13)))
        logit = jnp.sum(reach * gains_ref[5:6, :], axis=1, keepdims=True) * root_width
        return low, reach, 1.0 / (1.0 + jnp.exp(-logit))

    def soft_step(number, total):
        rows = pl.ds(pl.multiple_of(number * ROWS, ROWS), ROWS)
        return total + jnp.sum(valid_rows(rows) * boundary(rows)[2], axis=0, keepdims=True)

    soft_local = lax.fori_loop(0, length // ROWS, soft_step, jnp.zeros((1, 1), jnp.float32))
    line = lax.broadcasted_iota(jnp.int32, (8, 128), 0)
    length_float = length_one.astype(jnp.float32)
    counts[dp] = jnp.where(line == 0, soft_local, jnp.where(line == 1, length_float, 0.0))
    for j in range(7):
        count_copy(j).start()

    pool = hot_turned(2, 1, segments)
    amounts = jnp.sum(pool, axis=1, keepdims=True)
    divisor = jnp.maximum(amounts, 1.0)
    seg_entry[...] = product(pool.astype(jnp.bfloat16), leave[...].astype(jnp.bfloat16)) / divisor
    arrived(7, groups)
    block_run(seg, matrix, gains_ref, (lambda: None, lambda pair: None, lambda: None, lambda number: None))

    for j in range(7):
        count_copy(j).wait_recv()
    total = counts[0]
    for j in range(1, 8):
        total = total + counts[j]
    soft_count, count_all = total[0:1, 0:1], total[1:2, 0:1]

    def head(number, carry):
        ce, head_sum = carry
        rows = pl.ds(pl.multiple_of(number * ROWS, ROWS), ROWS)
        lift = hot_rows(rows, 2, 0, segments)
        merged = leave[rows, :] + product(lift, seg_leave[...].astype(jnp.bfloat16))
        scale = root_scale(merged)
        gain = gains_ref[4:5, :]
        final_low = (merged * scale * gain).astype(jnp.bfloat16)
        table = matrix_half(1)
        logits = product_nt(final_low, table)
        peak = jnp.max(logits, axis=1, keepdims=True)
        log_total = peak + jnp.log(jnp.sum(jnp.exp(logits - peak), axis=1, keepdims=True))
        target = hot_rows(rows, 1, 0, vocab).astype(jnp.float32)
        picked = jnp.sum(logits * target, axis=1, keepdims=True)
        valid = valid_rows(rows)
        ce = ce + jnp.sum(valid * (log_total - picked), axis=0, keepdims=True)
        share = valid / (micro_count * count_all)
        grad_logits = (jnp.exp(logits - log_total) - target) * share
        head_sum = head_sum + product(turn(grad_logits), final_low)
        back, gain_part = norm_back(merged, scale, gain, product(grad_logits.astype(jnp.bfloat16), table))
        small_ref[4:5, :] = small_ref[4:5, :] + gain_part
        grad[rows, :] = back
        return ce, head_sum

    ce_local, head_sum = lax.fori_loop(
        0, length // ROWS, head, (jnp.zeros((1, 1), jnp.float32), jnp.zeros((vocab, width), jnp.float32))
    )
    stage[...] = jnp.zeros_like(stage)
    for slot in range(4):
        staged(slot, slot).start()
    seg_grad[...] = exact_product(hot_turned(2, 0, segments).astype(jnp.bfloat16), grad[...])
    def sent(group, carry):
        for j in range(3):
            peer_copy(group, j).wait_send()
            tower_copy(group, j).wait_send()
        for way in range(2):
            side_copy(group, way).wait_send()
            corner_copy(group, way).wait_send()
        core_copy(group).wait_send()
        return carry

    lax.fori_loop(0, groups, sent, 0)
    block_back(seg, seg_grad, matrix, gains_ref, small_ref, temps, put)
    seg_grad[...] = seg_grad[...] / divisor

    count_rest = count_all - soft_count
    slope = (digamma(soft_count + 1.0) - digamma(count_rest + 1.0) + LOG_ODDS) / (count_all * micro_count)

    def join(rows):
        low, reach, chance = boundary(rows)
        logit = valid_rows(rows) * slope * chance * (1.0 - chance)
        gain = gains_ref[5:6, :]
        small_ref[5:6, :] = small_ref[5:6, :] + jnp.sum(logit * reach, axis=0, keepdims=True) * root_width
        pre = (logit * gain * root_width * (1.0 - reach * reach)).astype(jnp.bfloat16)
        branch[rows, :] = pre
        turned[:, rows] = turn(low)
        spread = exact_product(hot_rows(rows, 2, 1, segments), seg_grad[...])
        grad[rows, :] = (grad[rows, :] + spread) + product_nt(pre, matrix(13))

    each_block(length, join)
    put(24, 0, lambda half: product(turned[half, :], branch[...]))
    block_back(char, grad, matrix, gains_ref, small_ref, temps, put)
    staged(25, 3).wait()
    stage[3, 0:vocab, :] = exact_product(hot_turned(0, 0, vocab).astype(jnp.bfloat16), grad[...])
    stage[3, vocab : 2 * vocab, :] = head_sum
    staged(25, 3).start()

    lane = lax.broadcasted_iota(jnp.int32, (1, width), 1)
    small_ref[6:7, :] = jnp.where(
        lane == seq,
        ce_local,
        jnp.where(lane == seq + 8, soft_local, jnp.where(lane == seq + 16, length_float, 0.0)),
    )
    for slot in range(4):
        staged(slot, slot).wait()
    for j in range(7):
        count_copy(j).wait_send()
    for j in range(3):
        ids_copy(j).wait_send()


def step_call(length_one, owner_slot, master, ids, gains, micro_count):
    held, _, width = master.shape
    tile_count = owner_slot.shape[0]
    seq_count, dp_count = lax.axis_size("seq"), lax.axis_size("dp")
    groups = tile_count // 2
    length = seq_count * ids.shape[2]
    segments = SEG_DEV * seq_count
    dma = pltpu.SemaphoreType.DMA
    vmem = pl.BlockSpec(memory_space=pltpu.VMEM)
    smem = pl.BlockSpec(memory_space=pltpu.SMEM)
    hbm = pl.BlockSpec(memory_space=pl.ANY)
    local = jnp.concatenate([owner_slot[25:], owner_slot[:12], owner_slot[24:25], owner_slot[12:24]])
    local = local - lax.axis_index("seq") * held
    valid = jnp.logical_and(local >= 0, local < held).astype(jnp.int32)

    def full(*shape):
        return pltpu.VMEM(shape, jnp.float32)

    def half(*shape):
        return pltpu.VMEM(shape, jnp.bfloat16)

    def kept(count):
        return [
            full(count, width), half(count, 3 * width), full(4, 2, count), half(count, width),
            full(count, width), full(count, 4 * width), full(count, width), full(count, width),
        ]

    return pl.pallas_call(
        functools.partial(step_kernel, micro_count),
        out_shape=(
            jax.ShapeDtypeStruct((tile_count, width, width), jnp.float32),
            jax.ShapeDtypeStruct((8, width), jnp.float32),
        ),
        in_specs=[smem, smem, smem, vmem, vmem, vmem],
        out_specs=(hbm, vmem),
        scratch_shapes=[half(tile_count, 4, 2, 4, 16, width)]
        + kept(length)
        + kept(segments)
        + [
            half(width, length), half(length, 4 * width), half(length, width), half(length, width),
            half(width, length), full(length, 128), full(length, 128),
            pltpu.VMEM((8, length), jnp.int32), full(length, 8), full(4, width, width), dma((4,)),
            full(dp_count, 8, 128), dma((7,)), dma((7,)), dma((3,)), dma((3,)), dma,
            dma((3, groups)), dma((3, groups)), dma((3, groups)), dma((3, groups)),
            dma((2, groups)), dma((2, groups)), dma((2, groups)), dma((2, groups)),
            dma((groups,)), dma((groups,)),
        ],
        name="step",
        compiler_params=pltpu.CompilerParams(
            collective_id=2, has_side_effects=True, vmem_limit_bytes=STEP_VMEM
        ),
    )(length_one, jnp.where(valid > 0, local, 0), valid, master, ids, gains)


def whole_step(char_ids, targets, seg_ids, lengths, owner_slot, master, gain_rows):
    micro_count = char_ids.shape[0]
    ids = jnp.stack([char_ids[:, 0], targets[:, 0], seg_ids[:, 0]], axis=1)
    ids = jnp.pad(ids, ((0, 0), (0, 5), (0, 0)))
    length_one = lax.dynamic_slice_in_dim(lengths[:, 0], lax.axis_index("seq"), 1)
    gains = jnp.pad(gain_rows, ((0, 2), (0, 0)))
    return step_call(length_one, owner_slot, master, ids, gains, micro_count)


def body(
    char_ids,
    targets,
    seg_ids,
    lengths,
    owner_slot,
    step_count,
    master,
    tile_first,
    tile_second,
    gain_rows,
    gain_first,
    gain_second,
):
    micro_count = char_ids.shape[0]
    model_width = master.shape[2]
    slot_count = master.shape[0] * lax.axis_size("seq")
    if (micro_count, lax.axis_size("seq"), lax.axis_size("dp")) == (4, 4, 8):
        tile_grads, small = whole_step(
            char_ids, targets, seg_ids, lengths, owner_slot, master, gain_rows
        )
        local = lax.axis_index("seq") * master.shape[0] + jnp.arange(master.shape[0])
        hot = local[:, None] == owner_slot[None, :]
        valid = jnp.any(hot, axis=1).astype(jnp.int32)
        source = jnp.sum(jnp.where(hot, jnp.arange(owner_slot.shape[0])[None, :], 0), axis=1)
        shard_total, small, squares = reduce_tiles_kernel(
            tile_grads, small, source, valid, master.shape[0]
        )
        gain_sum, square_sum = small[0:6], jnp.sum(squares)
        entropy, soft, count = (small[6, 8 * i : 8 * i + micro_count] for i in range(3))
        prior = -(
            lax.lgamma(count + 1.0)
            - lax.lgamma(soft + 1.0)
            - lax.lgamma(count - soft + 1.0)
            + soft * jnp.log(PRIOR_RATE)
            + (count - soft) * jnp.log(1.0 - PRIOR_RATE)
        )
        loss_total = jnp.sum((entropy + prior) / count) / micro_count
    else:
        tile_total = jnp.zeros((owner_slot.shape[0], model_width, model_width), jnp.float32)
        gain_total = jnp.zeros_like(gain_rows)
        loss_total = jnp.zeros((), jnp.float32)
        for micro in range(micro_count):
            tiles = gather_tiles(master, owner_slot)
            tile_part, gain_part, loss_part = micro_step(
                tiles,
                gain_rows,
                char_ids[micro, 0],
                targets[micro, 0],
                seg_ids[micro, 0],
                lengths[micro, 0],
                micro_count,
            )
            tile_total = tile_total + tile_part
            gain_total = gain_total + gain_part
            loss_total = loss_total + loss_part
        shard_total = reduce_tiles(tile_total, owner_slot, slot_count)
        gain_sum, square_sum = lax.psum((gain_total, jnp.sum(shard_total * shard_total)), ("dp", "seq"))
    grad_norm = jnp.sqrt(square_sum + jnp.sum(gain_sum * gain_sum))
    clip_factor = jnp.minimum(1.0, CLIP_NORM / (grad_norm + 1e-06))
    step_float = step_count[0].astype(jnp.float32)
    local_ids = lax.axis_index("seq") * master.shape[0] + jnp.arange(master.shape[0])
    owned = jnp.any(local_ids[:, None] == owner_slot[None, :], axis=1)[:, None, None]
    new_tiles, new_first, new_second = adam_step(
        master,
        tile_first,
        tile_second,
        shard_total * clip_factor,
        RATE_TILES,
        WEIGHT_DECAY,
        step_float,
    )
    master_new = jnp.where(owned, new_tiles, master)
    first_new = jnp.where(owned, new_first, tile_first)
    second_new = jnp.where(owned, new_second, tile_second)
    gains_new, gain_first_new, gain_second_new = adam_step(
        gain_rows, gain_first, gain_second, gain_sum * clip_factor, RATE_GAINS, 0.0, step_float
    )
    return (
        loss_total.reshape(1),
        grad_norm.reshape(1),
        master_new,
        first_new,
        second_new,
        master_new.astype(jnp.bfloat16),
        gains_new,
        gain_first_new,
        gain_second_new,
    )


def solution(mesh):
    return jax.shard_map(
        body,
        mesh=mesh,
        in_specs=(
            P(None, "dp", "seq"),
            P(None, "dp", "seq"),
            P(None, "dp", "seq"),
            P(None, "dp"),
            P(),
            P(),
            P("seq", "dp", None),
            P("seq", "dp", None),
            P("seq", "dp", None),
            P(),
            P(),
            P(),
        ),
        out_specs=(
            P(),
            P(),
            P("seq", "dp", None),
            P("seq", "dp", None),
            P("seq", "dp", None),
            P("seq", "dp", None),
            P(),
            P(),
            P(),
        ),
        check_vma=False,
    )
```

```python
import functools
import math

import jax
import jax.numpy as jnp
from jax import lax
from jax.experimental import pallas as pl
from jax.experimental.pallas import tpu as pltpu
from jax.sharding import PartitionSpec as P

HEADS = 8
SEG_DEV = 64


BETA_ONE = 0.9
BETA_TWO = 0.95
ADAM_EPS = 1e-08
WEIGHT_DECAY = 0.1
RATE_TILES = 0.03
RATE_GAINS = 0.2
CLIP_NORM = 0.05
PRIOR_RATE = 0.25
NORM_EPS = 1e-06
MASKED = -1e30
LOG_ODDS = math.log(1.0 - PRIOR_RATE) - math.log(PRIOR_RATE)


def product(left, right):
    return jnp.dot(left, right, preferred_element_type=jnp.float32)


def product_tn(left, right):
    return lax.dot_general(
        left, right, (((0,), (0,)), ((), ())), preferred_element_type=jnp.float32
    )


def product_nt(left, right):
    return lax.dot_general(
        left, right, (((1,), (1,)), ((), ())), preferred_element_type=jnp.float32
    )


def exact_tn(left, right):
    return lax.dot_general(
        left,
        right,
        (((0,), (0,)), ((), ())),
        precision=lax.Precision.HIGHEST,
        preferred_element_type=jnp.float32,
    )


def rms_norm(values, gain):
    return values * lax.rsqrt(jnp.mean(values * values, axis=-1, keepdims=True) + NORM_EPS) * gain


def split_heads(tensor):
    return tensor.reshape(tensor.shape[0], HEADS, tensor.shape[1] // HEADS).transpose(1, 0, 2)


def join_heads(tensor):
    return tensor.transpose(1, 0, 2).reshape(tensor.shape[1], tensor.shape[0] * tensor.shape[2])


def block_weights(tiles):
    w_qkv = jnp.concatenate([tiles[0], tiles[1], tiles[2]], axis=1)
    w_up = jnp.concatenate([tiles[4], tiles[5], tiles[6], tiles[7]], axis=1)
    w_down = jnp.concatenate([tiles[8], tiles[9], tiles[10], tiles[11]], axis=0)
    return (w_qkv, w_up, w_down)


def causal_mask(row_count, key_count):
    first_row = lax.axis_index("seq") * row_count
    return (first_row + jnp.arange(row_count))[:, None] >= jnp.arange(key_count)[None, :]


def block_forward(hidden_in, tiles, gain_attn, gain_ffn, segment):
    row_count, model_width = hidden_in.shape
    w_qkv, w_up, w_down = block_weights(tiles)
    normed = rms_norm(hidden_in, gain_attn).astype(jnp.bfloat16)
    qkv_low = product(normed, w_qkv).astype(jnp.bfloat16)
    if segment:
        gathered = lax.all_gather(qkv_low[:, model_width:], "seq", axis=0, tiled=True)
    else:
        gathered = lax.all_gather(qkv_low[:, model_width:], "seq", axis=0, tiled=True)
    allowed = causal_mask(row_count, gathered.shape[0])
    factor = (model_width // HEADS) ** (-0.5)

    def head_forward(triple):
        q_head, k_head, v_head = triple
        scores = jnp.where(allowed, product_nt(q_head, k_head) * factor, MASKED)
        peak = jnp.max(scores, axis=1, keepdims=True)
        log_total = peak + jnp.log(jnp.sum(jnp.exp(scores - peak), axis=1, keepdims=True))
        weights = jnp.exp(scores - log_total).astype(jnp.bfloat16)
        return (product(weights, v_head), log_total[:, 0])

    head_out, log_totals = lax.map(
        head_forward,
        (
            split_heads(qkv_low[:, :model_width]),
            split_heads(gathered[:, :model_width]),
            split_heads(gathered[:, model_width:]),
        ),
    )
    attended = join_heads(head_out).astype(jnp.bfloat16)
    after_attn = hidden_in + product(attended, tiles[3])
    inner = product(rms_norm(after_attn, gain_ffn).astype(jnp.bfloat16), w_up)
    block_out = after_attn + product(jax.nn.gelu(inner).astype(jnp.bfloat16), w_down)
    return (block_out, (hidden_in, qkv_low, gathered, log_totals, attended, after_attn, inner))


def block_backward(grad_out, saved, tiles, gain_attn, gain_ffn, segment):
    hidden_in, qkv_low, gathered, log_totals, attended, after_attn, inner = saved
    row_count, model_width = hidden_in.shape
    w_qkv, w_up, w_down = block_weights(tiles)
    grad_ffn = grad_out.astype(jnp.bfloat16)
    activated, gelu_pull = jax.vjp(jax.nn.gelu, inner)
    grad_down = product_tn(activated.astype(jnp.bfloat16), grad_ffn)
    grad_inner = gelu_pull(product_nt(grad_ffn, w_down))[0].astype(jnp.bfloat16)
    normed_ffn, ffn_pull = jax.vjp(rms_norm, after_attn, gain_ffn)
    grad_up = product_tn(normed_ffn.astype(jnp.bfloat16), grad_inner)
    grad_normed_in, grad_gain_ffn = ffn_pull(product_nt(grad_inner, w_up))
    grad_after = grad_out + grad_normed_in
    grad_branch = grad_after.astype(jnp.bfloat16)
    grad_wout = product_tn(attended, grad_branch)
    grad_attended = product_nt(grad_branch, tiles[3]).astype(jnp.bfloat16)
    allowed = causal_mask(row_count, gathered.shape[0])
    factor = (model_width // HEADS) ** (-0.5)

    def head_backward(bundle):
        q_head, k_head, v_head, upstream, log_head = bundle
        scores = jnp.where(allowed, product_nt(q_head, k_head) * factor, MASKED)
        weights = jnp.exp(scores - log_head[:, None])
        grad_values = product_tn(weights.astype(jnp.bfloat16), upstream)
        grad_weights = product_nt(upstream, v_head)
        inner_sum = jnp.sum(weights * grad_weights, axis=1, keepdims=True)
        grad_scores = (weights * (grad_weights - inner_sum)).astype(jnp.bfloat16)
        return (
            product(grad_scores, k_head) * factor,
            product_tn(grad_scores, q_head) * factor,
            grad_values,
        )

    grad_query, grad_keys, grad_values = lax.map(
        head_backward,
        (
            split_heads(qkv_low[:, :model_width]),
            split_heads(gathered[:, :model_width]),
            split_heads(gathered[:, model_width:]),
            split_heads(grad_attended),
            log_totals,
        ),
    )
    grad_kv_all = jnp.concatenate([join_heads(grad_keys), join_heads(grad_values)], axis=1)
    if segment:
        grad_kv = lax.psum_scatter(grad_kv_all, "seq", scatter_dimension=0, tiled=True)
    else:
        grad_kv = lax.psum_scatter(grad_kv_all, "seq", scatter_dimension=0, tiled=True)
    grad_qkv = jnp.concatenate([join_heads(grad_query), grad_kv], axis=1).astype(jnp.bfloat16)
    normed_attn, attn_pull = jax.vjp(rms_norm, hidden_in, gain_attn)
    grad_wqkv = product_tn(normed_attn.astype(jnp.bfloat16), grad_qkv)
    grad_normed_x, grad_gain_attn = attn_pull(product_nt(grad_qkv, w_qkv))
    grad_in = grad_after + grad_normed_x
    pieces = [
        grad_wqkv[:, part_index * model_width : (part_index + 1) * model_width]
        for part_index in range(3)
    ]
    pieces = pieces + [grad_wout]
    pieces = pieces + [
        grad_up[:, part_index * model_width : (part_index + 1) * model_width]
        for part_index in range(4)
    ]
    pieces = pieces + [
        grad_down[part_index * model_width : (part_index + 1) * model_width]
        for part_index in range(4)
    ]
    return (grad_in, jnp.stack(pieces), grad_gain_attn, grad_gain_ffn)


def micro_step(tiles, gain_rows, chars_row, target_row, segment_row, length_one, micro_count):
    char_count = chars_row.shape[0]
    model_width = tiles.shape[2]
    vocab_size = model_width // 2
    seq_count = lax.axis_size("seq")
    seg_total = SEG_DEV * seq_count
    position = lax.axis_index("seq") * char_count + jnp.arange(char_count)
    is_valid = (position < length_one).astype(jnp.float32)
    vocab_iota = jnp.arange(vocab_size)
    char_hot = chars_row[:, None] == vocab_iota[None, :]
    embed_low = tiles[25, :vocab_size]
    head_low = tiles[25, vocab_size:]
    start_hidden = product(char_hot.astype(jnp.bfloat16), embed_low)
    char_out, char_saved = block_forward(
        start_hidden, tiles[0:12], gain_rows[0], gain_rows[1], False
    )
    char_low = char_out.astype(jnp.bfloat16)
    boundary_hidden = jnp.tanh(product(char_low, tiles[24]))
    root_width = model_width ** (-0.5)
    boundary_prob = jax.nn.sigmoid(jnp.sum(boundary_hidden * gain_rows[5], axis=1) * root_width)
    slot_iota = jnp.arange(seg_total)
    pool_hot = segment_row[None, :] + 1 == slot_iota[:, None]
    lift_hot = segment_row[:, None] == slot_iota[None, :]
    part_sums = product(pool_hot.astype(jnp.bfloat16), char_low).reshape(
        seq_count, SEG_DEV, model_width
    )
    side_info = jnp.stack(
        [
            jnp.sum(pool_hot.astype(jnp.float32), axis=1),
            jnp.any(lift_hot, axis=0).astype(jnp.float32),
        ],
        axis=0,
    )
    side_info = side_info.reshape(2, seq_count, SEG_DEV).transpose(1, 0, 2)
    sums_in, side_in = (
        lax.all_to_all(part_sums, "seq", split_axis=0, concat_axis=0, tiled=True),
        lax.all_to_all(side_info, "seq", split_axis=0, concat_axis=0, tiled=True),
    )
    row_counts = jnp.sum(side_in[:, 0, :], axis=0)
    divisor = jnp.maximum(row_counts, 1.0)[:, None]
    pooled = jnp.sum(sums_in, axis=0) / divisor
    seg_out, seg_saved = block_forward(pooled, tiles[12:24], gain_rows[2], gain_rows[3], True)
    outgoing = side_in[:, 1, :, None].astype(jnp.bfloat16) * seg_out.astype(jnp.bfloat16)[None]
    returned = lax.all_to_all(outgoing, "seq", split_axis=0, concat_axis=0, tiled=True)
    merged = char_out + product(
        lift_hot.astype(jnp.bfloat16), returned.reshape(seg_total, model_width)
    )
    final_norm, final_pull = jax.vjp(rms_norm, merged, gain_rows[4])
    final_low = final_norm.astype(jnp.bfloat16)
    logits = product_nt(final_low, head_low)
    peak = jnp.max(logits, axis=1, keepdims=True)
    log_total = peak[:, 0] + jnp.log(jnp.sum(jnp.exp(logits - peak), axis=1))
    target_hot = (target_row[:, None] == vocab_iota[None, :]).astype(jnp.float32)
    picked = jnp.sum(logits * target_hot, axis=1)
    ce_local = jnp.sum(is_valid * (log_total - picked))
    ce_all, soft_count, count_all = lax.psum(
        (ce_local, jnp.sum(is_valid * boundary_prob), jnp.sum(is_valid)), ("dp", "seq")
    )
    weight_ce = is_valid / (micro_count * count_all)
    grad_logits = ((jnp.exp(logits - log_total[:, None]) - target_hot) * weight_ce[:, None]).astype(
        jnp.bfloat16
    )
    grad_head = product_tn(grad_logits, final_low)
    grad_merged, grad_gain_final = final_pull(product(grad_logits, head_low))
    grad_rows = exact_tn(lift_hot.astype(jnp.float32), grad_merged).reshape(
        seq_count, SEG_DEV, model_width
    )
    grad_seg = jnp.sum(
        lax.all_to_all(grad_rows, "seq", split_axis=0, concat_axis=0, tiled=True), axis=0
    )
    grad_pooled, seg_tiles, grad_gain_two, grad_gain_three = block_backward(
        grad_seg, seg_saved, tiles[12:24], gain_rows[2], gain_rows[3], True
    )
    grad_sums = (side_in[:, 0, :, None] > 0).astype(jnp.float32) * (grad_pooled / divisor)[None]
    grad_back = lax.all_to_all(grad_sums, "seq", split_axis=0, concat_axis=0, tiled=True).reshape(
        seg_total, model_width
    )
    grad_char = grad_merged + exact_tn(pool_hot.astype(jnp.float32), grad_back)
    prior_slope = (
        lax.digamma(soft_count + 1.0)
        - lax.digamma(count_all - soft_count + 1.0)
        - jnp.log(PRIOR_RATE)
        + jnp.log(1.0 - PRIOR_RATE)
    ) / (count_all * micro_count)
    grad_boundary_logit = is_valid * prior_slope * boundary_prob * (1.0 - boundary_prob)
    grad_gain_boundary = (
        jnp.sum(grad_boundary_logit[:, None] * boundary_hidden, axis=0) * root_width
    )
    grad_pre = (
        grad_boundary_logit[:, None]
        * gain_rows[5][None, :]
        * root_width
        * (1.0 - boundary_hidden * boundary_hidden)
    ).astype(jnp.bfloat16)
    grad_boundary = product_tn(char_low, grad_pre)
    grad_char = grad_char + product_nt(grad_pre, tiles[24])
    grad_start, char_tiles, grad_gain_zero, grad_gain_one = block_backward(
        grad_char, char_saved, tiles[0:12], gain_rows[0], gain_rows[1], False
    )
    grad_embed = exact_tn(char_hot.astype(jnp.float32), grad_start)
    tile_grads = jnp.concatenate(
        [
            char_tiles,
            seg_tiles,
            grad_boundary[None],
            jnp.concatenate([grad_embed, grad_head], axis=0)[None],
        ],
        axis=0,
    )
    gain_grads = jnp.stack(
        [
            grad_gain_zero,
            grad_gain_one,
            grad_gain_two,
            grad_gain_three,
            grad_gain_final,
            grad_gain_boundary,
        ]
    )
    prior_term = (
        -(
            lax.lgamma(count_all + 1.0)
            - lax.lgamma(soft_count + 1.0)
            - lax.lgamma(count_all - soft_count + 1.0)
            + soft_count * jnp.log(PRIOR_RATE)
            + (count_all - soft_count) * jnp.log(1.0 - PRIOR_RATE)
        )
        / count_all
    )
    return (tile_grads, gain_grads, (ce_all / count_all + prior_term) / micro_count)


def gather_tiles(master, owner_slot):
    shard_low = master.astype(jnp.bfloat16)
    full_rows = lax.all_gather(shard_low, "dp", axis=1, tiled=True)
    all_slots = lax.all_gather(full_rows, "seq", axis=0, tiled=True)
    return jnp.take(all_slots, owner_slot, axis=0)


def reduce_tiles(tile_grads, owner_slot, slot_count):
    placed = (
        jnp.zeros((slot_count,) + tile_grads.shape[1:], jnp.float32).at[owner_slot].set(tile_grads)
    )
    per_owner = lax.psum_scatter(placed, "seq", scatter_dimension=0, tiled=True)
    return lax.psum_scatter(per_owner, "dp", scatter_dimension=1, tiled=True)


def adam_step(param, moment_a, moment_b, grad_in, rate, decay, step_float):
    new_first = BETA_ONE * moment_a + (1.0 - BETA_ONE) * grad_in
    new_second = BETA_TWO * moment_b + (1.0 - BETA_TWO) * grad_in * grad_in
    first_hat = new_first / (1.0 - BETA_ONE**step_float)
    second_hat = new_second / (1.0 - BETA_TWO**step_float)
    updated = param - rate * (first_hat / (jnp.sqrt(second_hat) + ADAM_EPS) + decay * param)
    return (updated, new_first, new_second)


MESH = pl.DeviceIdType.MESH
VMEM_LIMIT = 60 * 1024 * 1024
STEP_VMEM = 63 * 1024 * 1024


def remote(src, dst, send_sem, recv_sem, peer):
    return pltpu.make_async_remote_copy(
        src_ref=src, dst_ref=dst, send_sem=send_sem, recv_sem=recv_sem, device_id=peer, device_id_type=MESH
    )


def places():
    dp = lax.axis_index("dp")
    seq = lax.axis_index("seq")
    return dp, seq, dp // 2, dp % 2


def seq_peer(seq, step):
    return ((seq // 2 + step // 2) % 2) * 2 + (seq % 2 + step % 2) % 2


def meet(peers):
    barrier = pltpu.get_barrier_semaphore()
    for peer in peers:
        pl.semaphore_signal(barrier, inc=1, device_id=peer, device_id_type=MESH)
    pl.semaphore_wait(barrier, len(peers))


CODE_TOP = 32000.0
ROUNDER = 12582912.0


def encode(value):
    upper, lower = value[0:8, :], value[8:16, :]
    size = jnp.maximum(jnp.abs(upper), jnp.abs(lower))
    most = jnp.maximum(jnp.max(size, axis=1, keepdims=True), 1e-30)
    ratio = CODE_TOP / most
    coded = jnp.concatenate([upper * ratio, lower * ratio], axis=0)
    coded = ((coded + ROUNDER) - ROUNDER).astype(jnp.int32).astype(jnp.int16)
    return coded, most * (1.0 / CODE_TOP)


def decode(coded, unit):
    value = coded.astype(jnp.int32).astype(jnp.float32)
    return jnp.concatenate([value[0:8, :] * unit, value[8:16, :] * unit], axis=0)


def head_mask(shape, head):
    lane = lax.broadcasted_iota(jnp.int32, shape, 1)
    return (lane >= 64) if head else (lane < 64)


def scores_t(k_pair, q_head, first_row):
    scores = product_nt(k_pair, q_head)
    count, queries = scores.shape
    key = lax.broadcasted_iota(jnp.int32, (queries, queries), 0)
    query = lax.broadcasted_iota(jnp.int32, (queries, queries), 1)
    own = jnp.where(key <= query, scores[first_row:], MASKED)
    return own if first_row == 0 else jnp.concatenate([scores[:first_row], own], axis=0)


ROWS = 256
LAG = 2
START = 10


def split_three(value):
    high = value.astype(jnp.bfloat16)
    rest = value - high.astype(jnp.float32)
    middle = rest.astype(jnp.bfloat16)
    return high, middle, (rest - middle.astype(jnp.float32)).astype(jnp.bfloat16)


def exact_product(hot, value):
    high, middle, low = split_three(value)
    return (product(hot, low) + product(hot, middle)) + product(hot, high)


def turn(value):
    return value.astype(jnp.float32).T.astype(jnp.bfloat16)


def root_scale(value):
    return lax.rsqrt(jnp.mean(value * value, axis=-1, keepdims=True) + NORM_EPS)


def norm_back(value, scale, gain, grad):
    unit = value * scale
    weighted = grad * gain
    inner = jnp.mean(weighted * unit, axis=-1, keepdims=True)
    return scale * (weighted - unit * inner), jnp.sum(grad * unit, axis=0, keepdims=True)


def gelu_both(value):
    root = 0.7978845608028654
    square = value * value
    reach = jnp.tanh(root * value * (1.0 + 0.044715 * square))
    part = 0.5 * (1.0 + reach)
    slope = part + value * (0.5 * (1.0 - reach * reach)) * (root * (1.0 + 3.0 * 0.044715 * square))
    return value * part, slope


def digamma(value):
    moved = value + 8.0
    inverse = 1.0 / moved
    square = inverse * inverse
    series = square * (1.0 / 12.0 - square * (1.0 / 120.0 - square * (1.0 / 252.0)))
    total = jnp.log(moved) - 0.5 * inverse - series
    for number in range(8):
        total = total - 1.0 / (value + float(number))
    return total


def each_block(length, body):
    def step(number, carry):
        body(pl.ds(pl.multiple_of(number * ROWS, ROWS), ROWS))
        return carry

    lax.fori_loop(0, length // ROWS, step, 0)


class Block:
    def __init__(self, length, order, place, gain_row, entry, qkv, logs, attended, after, leave):
        self.length, self.order, self.place, self.gain_row = length, order, place, gain_row
        self.entry, self.qkv, self.logs, self.attended = entry, qkv, logs, attended
        self.after, self.leave = after, leave


def attend(block, pump):
    length = block.length

    def pair_step(pair, carry):
        lanes = [pl.ds(pl.multiple_of(part * 512 + pair * 128, 128), 128) for part in range(3)]
        for first in range(0, length, ROWS):
            span = first + ROWS
            q_pair = block.qkv[first:span, lanes[0]] * jnp.asarray(0.125, jnp.bfloat16)
            outs = []
            for head in range(2):
                q_head = jnp.where(head_mask(q_pair.shape, head), q_pair, jnp.zeros_like(q_pair))
                scores = scores_t(block.qkv[0:span, lanes[1]], q_head, first)
                peak = jnp.max(scores, axis=0, keepdims=True)
                raised = jnp.exp(scores - peak)
                total = jnp.sum(raised, axis=0, keepdims=True)
                weights = (raised * (1.0 / total)).astype(jnp.bfloat16)
                block.logs[pair, head : head + 1, first:span] = peak + jnp.log(total)
                outs.append(product_tn(weights, block.qkv[0:span, lanes[2]]))
            merged = jnp.where(head_mask(outs[0].shape, 0), outs[0], outs[1])
            block.attended[first:span, lanes[0]] = merged.astype(jnp.bfloat16)
        pump(pair)
        return carry

    lax.fori_loop(0, 4, pair_step, 0)


def attend_back(block, upstream, grad_qkv, key_sum, value_sum, pump):
    length = block.length

    def pair_step(pair, carry):
        lanes = [pl.ds(pl.multiple_of(part * 512 + pair * 128, 128), 128) for part in range(3)]
        for first in reversed(range(0, length, ROWS)):
            span = first + ROWS
            q_pair = block.qkv[first:span, lanes[0]] * jnp.asarray(0.125, jnp.bfloat16)
            up_pair = upstream[first:span, lanes[0]]
            queries, keys, values = [], [], []
            for head in range(2):
                keep = head_mask(q_pair.shape, head)
                q_head = jnp.where(keep, q_pair, jnp.zeros_like(q_pair))
                up_head = jnp.where(keep, up_pair, jnp.zeros_like(up_pair))
                k_pair = block.qkv[0:span, lanes[1]]
                scores = scores_t(k_pair, q_head, first)
                weights = jnp.exp(scores - block.logs[pair, head : head + 1, first:span])
                grad_weights = product_nt(block.qkv[0:span, lanes[2]], up_head)
                values.append(product(weights.astype(jnp.bfloat16), up_head))
                inner_sum = jnp.sum(weights * grad_weights, axis=0, keepdims=True)
                grad_scores = (weights * (grad_weights - inner_sum)).astype(jnp.bfloat16)
                keys.append(product(grad_scores, q_head))
                queries.append(product_tn(grad_scores, k_pair))
            merged = jnp.where(head_mask(queries[0].shape, 0), queries[0], queries[1]) * 0.125
            grad_qkv[first:span, lanes[0]] = merged.astype(jnp.bfloat16)
            if span == length:
                key_sum[0:span, :] = keys[0] + keys[1]
                value_sum[0:span, :] = values[0] + values[1]
            else:
                key_sum[0:span, :] = key_sum[0:span, :] + (keys[0] + keys[1])
                value_sum[0:span, :] = value_sum[0:span, :] + (values[0] + values[1])
        grad_qkv[0:length, lanes[1]] = key_sum[0:length, :].astype(jnp.bfloat16)
        grad_qkv[0:length, lanes[2]] = value_sum[0:length, :].astype(jnp.bfloat16)
        pump(pair)
        return carry

    lax.fori_loop(0, 4, pair_step, 0)


def block_run(block, matrix, gains, pumps):
    place = block.place
    gain_attn = gains[block.gain_row : block.gain_row + 1, :]
    gain_ffn = gains[block.gain_row + 1 : block.gain_row + 2, :]

    def project(rows):
        value = block.entry(rows)
        normed = (value * root_scale(value) * gain_attn).astype(jnp.bfloat16)
        for part in range(3):
            block.qkv[rows, 512 * part : 512 * part + 512] = product(normed, matrix(place + part)).astype(
                jnp.bfloat16
            )

    each_block(block.length, project)
    pumps[0]()
    attend(block, pumps[1])
    pumps[2]()

    def feed(rows):
        after = block.entry(rows) + product(block.attended[rows, :], matrix(place + 3))
        block.after[rows, :] = after
        normed = (after * root_scale(after) * gain_ffn).astype(jnp.bfloat16)
        total = jnp.zeros_like(after)
        for part in range(4):
            inner = product(normed, matrix(place + 4 + part))
            active = gelu_both(inner)[0].astype(jnp.bfloat16)
            total = total + product(active, matrix(place + 8 + part))
        block.leave[rows, :] = after + total
        pumps[3](rows.start // ROWS)

    each_block(block.length, feed)


def block_back(block, grad, matrix, gains, gain_sums, temps, put, pumps):
    length, order, place = block.length, block.order, block.place
    gain_attn = gains[block.gain_row : block.gain_row + 1, :]
    gain_ffn = gains[block.gain_row + 1 : block.gain_row + 2, :]
    turned, grad_inner, branch, turned_norm, key_sum, value_sum = temps
    grad_low, grad_qkv, upstream = branch, grad_inner, block.attended
    all_rows = pl.ds(0, length)

    def down(part):
        def rows_step(rows):
            low = grad[rows, :].astype(jnp.bfloat16)
            columns = pl.ds(pl.multiple_of(part * 512, 512), 512)
            after = block.after[rows, :]
            normed = (after * root_scale(after) * gain_ffn).astype(jnp.bfloat16)
            active, slope = gelu_both(product(normed, matrix(place + 4 + part)))
            turned[:, rows] = turn(active)
            grad_inner[rows, columns] = (product_nt(low, matrix(place + 8 + part)) * slope).astype(jnp.bfloat16)

        each_block(length, rows_step)

    def low_step(rows):
        grad_low[rows, :] = grad[rows, :].astype(jnp.bfloat16)

    each_block(length, low_step)

    def down_step(part, carry):
        down(part)
        put(order[0] + part, lambda half: product(turned[half, all_rows], grad_low[all_rows, :]))
        pumps[0](part)
        return carry

    lax.fori_loop(0, 4, down_step, 0)

    def middle(rows):
        after = block.after[rows, :]
        scale = root_scale(after)
        turned_norm[:, rows] = turn(after * scale * gain_ffn)
        turned[:, rows] = turn(block.attended[rows, :])
        total = jnp.zeros_like(after)
        for part in range(4):
            total = total + product_nt(
                grad_inner[rows, 512 * part : 512 * part + 512], matrix(place + 4 + part)
            )
        back, gain_part = norm_back(after, scale, gain_ffn, total)
        row = block.gain_row + 1
        gain_sums[row : row + 1, :] = gain_sums[row : row + 1, :] + gain_part
        grad_after = grad[rows, :] + back
        grad[rows, :] = grad_after
        low = grad_after.astype(jnp.bfloat16)
        branch[rows, :] = low
        upstream[rows, :] = product_nt(low, matrix(place + 3)).astype(jnp.bfloat16)

    each_block(length, middle)

    def up_step(part, carry):
        columns = pl.ds(pl.multiple_of(part * 512, 512), 512)
        put(order[1] + part, lambda half: product(turned_norm[half, all_rows], grad_inner[all_rows, columns]))
        pumps[1](part)
        return carry

    lax.fori_loop(0, 4, up_step, 0)
    put(order[2], lambda half: product(turned[half, all_rows], branch[all_rows, :]))
    attend_back(block, upstream, grad_qkv, key_sum, value_sum, pumps[2])

    def enter(rows):
        value = block.entry(rows)
        scale = root_scale(value)
        turned_norm[:, rows] = turn(value * scale * gain_attn)
        total = jnp.zeros_like(value)
        for part in range(3):
            total = total + product_nt(grad_qkv[rows, 512 * part : 512 * part + 512], matrix(place + part))
        back, gain_part = norm_back(value, scale, gain_attn, total)
        row = block.gain_row
        gain_sums[row : row + 1, :] = gain_sums[row : row + 1, :] + gain_part
        grad[rows, :] = grad[rows, :] + back

    each_block(length, enter)

    def qkv_step(part, carry):
        columns = pl.ds(pl.multiple_of(part * 512, 512), 512)
        put(order[3] + part, lambda half: product(turned_norm[half, all_rows], grad_qkv[all_rows, columns]))
        return carry

    lax.fori_loop(0, 3, qkv_step, 0)


class Reducer:
    pairs = 13
    offsets = (1, 2, 4, 6, 8)
    gap_first, gap = 10, 5
    last_tick = pairs + gap + offsets[-1]

    def __init__(self, place, own_far, other_far, pair_copy, beside, side, tower, refs):
        self.dp, self.seq, self.z, self.core = place
        self.across, self.along = self.seq % 2, self.seq // 2
        self.own_far, self.other_far, self.pair_copy = own_far, other_far, pair_copy
        self.beside, self.side, self.tower = beside, side, tower
        (
            self.own, self.other, self.one, self.two, self.three, self.final,
            self.b1_out, self.b1_in, self.b2_out, self.b2_in, self.c_out, self.c_in, self.d_out, self.d_in,
            self.b1_unit_out, self.b1_unit_in, self.b2_unit_out, self.b2_unit_in,
            self.c_unit_out, self.c_unit_in, self.d_unit_out, self.d_unit_in,
            self.l_sem, self.b1_send, self.b1_recv, self.b2_send, self.b2_recv,
            self.c_send, self.c_recv, self.d_send, self.d_recv,
        ) = refs[:31]
        self.lane = lax.broadcasted_iota(jnp.int32, (8, 128), 1)

    def loads(self, pair):
        two = pl.ds(pair * 2, 2)
        return [
            pltpu.make_async_copy(self.own_far.at[two], self.own, self.l_sem.at[0]),
            pltpu.make_async_copy(self.other_far.at[two], self.other, self.l_sem.at[1]),
        ]

    def first_copies(self, pair, order):
        tile, slot, peer = pair * 2 + order, pair % 3, self.beside[order]
        send, recv = self.b1_send, self.b1_recv
        return [
            remote(self.b1_out.at[slot, order], self.b1_in.at[tile], send.at[0, slot, order], recv.at[0, tile], peer),
            remote(
                self.b1_unit_out.at[slot, order], self.b1_unit_in.at[tile], send.at[1, slot, order], recv.at[1, tile], peer
            ),
        ]

    def second_copies(self, pair, order):
        tile, slot, peer = pair * 2 + order, pair % 3, self.beside[1 - order]
        send, recv = self.b2_send, self.b2_recv
        return [
            remote(self.b2_out.at[slot, order], self.b2_in.at[tile], send.at[0, slot, order], recv.at[0, tile], peer),
            remote(
                self.b2_unit_out.at[slot, order], self.b2_unit_in.at[tile], send.at[1, slot, order], recv.at[1, tile], peer
            ),
        ]

    def tower_copies(self, pair, j):
        two, slot, peer = pl.ds(pair * 2, 2), pair % 3, self.tower[j]
        send, recv = self.c_send, self.c_recv
        return [
            remote(self.c_out.at[slot, j], self.c_in.at[j, two], send.at[0, slot, j], recv.at[0, j, pair], peer),
            remote(self.c_unit_out.at[slot, j], self.c_unit_in.at[j, pair], send.at[1, slot, j], recv.at[1, j, pair], peer),
        ]

    def share_copies(self, pair, j):
        two, slot, peer = pl.ds(pair * 2, 2), pair % 3, self.side[j]
        send, recv = self.d_send, self.d_recv
        return [
            remote(self.d_out.at[slot], self.d_in.at[j, two], send.at[0, slot, j], recv.at[0, j, pair], peer),
            remote(self.d_unit_out.at[slot], self.d_unit_in.at[j, pair], send.at[1, slot, j], recv.at[1, j, pair], peer),
        ]

    def after_sends(self, pair, copies, count):
        @pl.when(pair >= 3)
        def _():
            for number in range(count):
                for copy in copies(pair - 3, number):
                    copy.wait_send()

    def load(self, pair):
        for order in range(2):
            self.pair_copy(pair * 2 + order).wait_recv()
        for copy in self.loads(pair):
            copy.start()

    def send_first(self, pair):
        for copy in self.loads(pair):
            copy.wait()
        self.after_sends(pair, self.first_copies, 2)
        slot, kept = pair % 3, pair % 2
        for order in range(2):

            units = jnp.zeros((8, 128), jnp.float32)
            for block in range(8):
                floor, line = block // 2, block % 2
                if order == 0:
                    mine = (order, floor, line, self.across)
                    away = (order, floor, line, 1 - self.across)
                else:
                    mine = (order, floor, self.along, line)
                    away = (order, floor, 1 - self.along, line)
                self.one[kept, order, block] = self.own[mine] + self.other[mine]
                coded, unit = encode(self.own[away] + self.other[away])
                self.b1_out[slot, order, block] = coded
                units = jnp.where(self.lane == block, unit, units)
            self.b1_unit_out[slot, order] = units
            for copy in self.first_copies(pair, order):
                copy.start()

    def send_second(self, pair):
        slot, kept = pair % 3, pair % 2
        self.after_sends(pair, self.second_copies, 2)
        for order in range(2):
            for copy in self.first_copies(pair, order):
                copy.wait_recv()
            tile = pair * 2 + order
            got = self.b1_unit_in[tile]
            keep = self.along if order == 0 else self.across

            units = jnp.zeros((8, 128), jnp.float32)
            for floor in range(4):
                stay, leave = floor * 2 + keep, floor * 2 + 1 - keep
                even, odd = got[:, 2 * floor : 2 * floor + 1], got[:, 2 * floor + 1 : 2 * floor + 2]
                self.two[kept, order, floor] = self.one[kept, order, stay] + decode(
                    self.b1_in[tile, stay], jnp.where(keep == 0, even, odd)
                )
                coded, unit = encode(
                    self.one[kept, order, leave] + decode(self.b1_in[tile, leave], jnp.where(keep == 0, odd, even))
                )
                self.b2_out[slot, order, floor] = coded
                units = jnp.where(self.lane == floor, unit, units)
            self.b2_unit_out[slot, order] = units
            for copy in self.second_copies(pair, order):
                copy.start()

    def send_tower(self, pair):
        slot, kept = pair % 3, pair % 2
        self.after_sends(pair, self.tower_copies, 3)
        for order in range(2):
            for copy in self.second_copies(pair, order):
                copy.wait_recv()

        for order in range(2):
            tile = pair * 2 + order
            got = self.b2_unit_in[tile]
            for floor in range(4):
                self.two[kept, order, floor] = self.two[kept, order, floor] + decode(
                    self.b2_in[tile, floor], got[:, floor : floor + 1]
                )
            self.three[kept, order] = self.two[kept, order, self.z]
        for j in range(3):
            units = jnp.zeros((8, 128), jnp.float32)
            for order in range(2):
                coded, unit = encode(self.two[kept, order, (self.z + j + 1) % 4])
                self.c_out[slot, j, order] = coded
                units = jnp.where(self.lane == order, unit, units)
            self.c_unit_out[slot, j] = units
        for j in range(3):
            for copy in self.tower_copies(pair, j):
                copy.start()

    def send_share(self, pair):
        slot = pair % 3
        self.after_sends(pair, self.share_copies, 3)
        for j in range(3):
            for copy in self.tower_copies(pair, j):
                copy.wait_recv()
        units = jnp.zeros((8, 128), jnp.float32)
        for order in range(2):
            tile = pair * 2 + order
            total = self.three[pair % 2, order]
            for j in range(3):
                total = total + decode(self.c_in[j, tile], self.c_unit_in[j, pair][:, order : order + 1])
            self.final[tile] = total
            coded, unit = encode(total)
            self.d_out[slot, order] = coded
            units = jnp.where(self.lane == order, unit, units)
        self.d_unit_out[slot] = units
        for j in range(3):
            for copy in self.share_copies(pair, j):
                copy.start()

    def tick(self, number):
        stages = (self.load, self.send_first, self.send_second, self.send_tower, self.send_share)
        for offset, stage_of in reversed(list(zip(self.offsets, stages))):
            turn_of = jnp.int32(number) - offset
            late = (turn_of >= self.gap_first + self.gap).astype(jnp.int32)
            pair = turn_of - self.gap * late
            fits = jnp.logical_and(turn_of >= 0, pair < self.pairs)
            fits = jnp.logical_and(fits, jnp.logical_or(late > 0, turn_of < self.gap_first))

            @pl.when(fits)
            def _():
                stage_of(pair)

    def ticks(self, start, stop):
        def body(number, carry):
            self.tick(number)
            return carry

        lax.fori_loop(start, stop, body, 0)

    def collect(self, source_ref, parity_ref, owned_ref, stage):
        def arrive(pair, carry):
            for j in range(3):
                for copy in self.share_copies(pair, j):
                    copy.wait_recv()
            return carry

        lax.fori_loop(0, self.pairs, arrive, 0)
        for order in range(self.pairs * 2 - 4, self.pairs * 2):
            self.pair_copy(order).wait_send()
        width = self.final.shape[2]

        def step(slot, square):
            keep = owned_ref[slot] > 0
            tile = source_ref[slot]
            places_of = [self.seq] + [peer[1] for peer in self.side]
            for number, quarter in enumerate(places_of):
                if number == 0:
                    value = self.final[tile]
                else:
                    units = self.d_unit_in[number - 1, parity_ref[slot]]
                    unit = jnp.where(parity_ref[slot + 16] > 0, units[:, 1:2], units[:, 0:1])
                    value = decode(self.d_in[number - 1, tile], unit)
                value = jnp.where(keep, value, jnp.zeros_like(value))
                stage[slot // 8, slot % 8 // 2, slot % 2, quarter // 2, quarter % 2] = value
                square = square + value * value
            return square

        square = lax.fori_loop(0, source_ref.shape[0], step, jnp.zeros((16, width), jnp.float32))
        folded = jnp.zeros((8, 128), jnp.float32)
        for r in range(2):
            for w in range(width // 128):
                folded = folded + square[8 * r : 8 * r + 8, 128 * w : 128 * w + 128]
        return folded

    def finish(self):
        for pair in range(self.pairs - 3, self.pairs):
            for order in range(2):
                for copy in self.first_copies(pair, order) + self.second_copies(pair, order):
                    copy.wait_send()
            for j in range(3):
                for copy in self.tower_copies(pair, j) + self.share_copies(pair, j):
                    copy.wait_send()


class Sums:
    def __init__(self, place, column, side, small, small_out, square_out, refs):
        self.dp, self.seq, _, _ = place
        self.column, self.side = column, side
        self.small, self.small_out, self.square_out = small, small_out, square_out
        self.small_dp, self.small_seq, self.square_dp, self.square_seq, self.sems = refs[31:]

    def copies(self, which):
        sends, recvs = self.sems[2 * which], self.sems[2 * which + 1]
        if which == 0:
            return [remote(self.small, self.small_dp.at[self.dp], sends.at[j], recvs.at[j], self.column[j]) for j in range(7)]
        if which == 1:
            spot = self.small_seq.at[self.seq]
            return [remote(spot, spot, sends.at[j], recvs.at[j], self.side[j]) for j in range(3)]
        if which == 2:
            spot = self.square_dp.at[self.dp]
            return [remote(spot, spot, sends.at[j], recvs.at[j], self.column[j]) for j in range(7)]
        spot = self.square_seq.at[self.seq]
        return [remote(spot, spot, sends.at[j], recvs.at[j], self.side[j]) for j in range(3)]

    def start(self, which):
        for copy in self.copies(which):
            copy.start()

    def arrive(self, which):
        for copy in self.copies(which):
            copy.wait_recv()

    def start_small(self):
        self.start(0)
        self.small_dp[self.dp] = self.small[...]

    def pass_small(self):
        self.arrive(0)
        total = self.small_dp[0]
        for j in range(1, 8):
            total = total + self.small_dp[j]
        self.small_seq[self.seq] = total
        self.start(1)

    def squares(self, folded):
        self.square_dp[self.dp] = folded
        self.start(2)
        self.arrive(1)
        self.small_out[...] = (self.small_seq[0] + self.small_seq[1]) + (self.small_seq[2] + self.small_seq[3])
        self.arrive(2)
        total = self.square_dp[0]
        for j in range(1, 8):
            total = total + self.square_dp[j]
        self.square_seq[self.seq] = total
        self.start(3)
        self.arrive(3)
        self.square_out[...] = (self.square_seq[0] + self.square_seq[1]) + (self.square_seq[2] + self.square_seq[3])

    def finish(self):
        for which in range(4):
            for copy in self.copies(which):
                copy.wait_send()


GRAD_ORDER = (20, 21, 22, 23, 16, 17, 18, 19, 15, 12, 13, 14, 24, 8, 9, 10, 11, 4, 5, 6, 7, 3, 0, 1, 2, 25)


def step_kernel(
    micro_count, length_ref, local_ref, valid_ref, source_ref, parity_ref, owned_ref, master_ref, ids_ref, gains_ref,
    own_far, other_far, out_ref, small_out, square_out,
    weights, qkv, logs, attended, after, leave, grad,
    seg_entry, seg_qkv, seg_logs, seg_attended, seg_after, seg_leave, seg_grad,
    turned, grad_inner, branch, turned_norm, key_sum, value_sum, head_grad, small_ref,
    ids_row, ids_col, stage, stage_sem, counts, count_send, count_recv, i_send, i_recv, i_own, g_send, g_recv, out_sem,
    p_send, p_recv, z_send, z_recv, s_send, s_recv, d_send, d_recv, c_send, c_recv,
    reduce_refs,
):
    dp, seq, z, core = places()
    across, along = seq % 2, seq // 2
    length, width = leave.shape
    segments = seg_entry.shape[0]
    vocab = width // 2
    root_width = width ** (-0.5)
    groups = weights.shape[0] // 2
    sibling = (z * 2 + 1 - core, seq)
    beside = [along * 2 + 1 - across, (1 - along) * 2 + across]
    side = [seq_peer(seq, j) for j in (1, 2, 3)]
    column = [((dp + j) % 8, seq) for j in range(1, 8)]
    tower = [((z + j) % 4 * 2 + core, seq) for j in (1, 2, 3)]
    meet([(dp, peer) for peer in side] + column)

    def ids_copy(j):
        part = pl.ds(pl.multiple_of(seq * ids_ref.shape[2], 256), ids_ref.shape[2])
        return remote(ids_ref.at[side[j]], ids_row.at[:, part], i_send.at[j], i_recv.at[j], (dp, side[j]))

    def own_ids():
        part = pl.ds(pl.multiple_of(seq * ids_ref.shape[2], 256), ids_ref.shape[2])
        return pltpu.make_async_copy(ids_ref.at[seq], ids_row.at[:, part], i_own)

    def part_of(which):
        return pl.ds(pl.multiple_of(which * width, width), width)

    def peer_copy(group, j):
        return remote(
            grad_inner.at[pl.ds(pl.multiple_of(group * 32, 32), 32), part_of(side[j])],
            grad_inner.at[pl.ds(pl.multiple_of(512 + group * 32, 32), 32), part_of(j)],
            p_send.at[j, group], p_recv.at[j, group], (dp, side[j]),
        )

    def tower_copy(group, j):
        spot = weights.at[pl.ds(group * 2, 2), z, core, seq]
        return remote(spot, spot, z_send.at[j, group], z_recv.at[j, group], tower[j])

    def side_copy(group, way):
        spot = weights.at[pl.ds(group * 2, 2), :, core, seq]
        return remote(spot, spot, s_send.at[way, group], s_recv.at[way, group], (dp, beside[way]))

    def corner_copy(group, way):
        spot = weights.at[group * 2 + way, :, core, beside[way]]
        return remote(spot, spot, d_send.at[way, group], d_recv.at[way, group], (dp, beside[1 - way]))

    def core_copy(group):
        spot = weights.at[pl.ds(group * 2, 2), :, core]
        return remote(spot, spot, c_send.at[group], c_recv.at[group], sibling)

    def offer(group):
        for j in (2, 0, 1):
            peer_copy(group, j).start()

    def combine(group):
        for j in range(3):
            peer_copy(group, j).wait_recv()
        for number in range(2):
            row = group * 32 + number * 16
            value = grad_inner[pl.ds(pl.multiple_of(row, 16), 16), part_of(seq)]
            for j in range(3):
                value = value + grad_inner[pl.ds(pl.multiple_of(512 + row, 16), 16), pl.ds(j * width, width)]
            weights[group * 2 + number, z, core, seq] = value
        for j in range(3):
            tower_copy(group, j).start()

    def widen(group):
        for j in range(3):
            tower_copy(group, j).wait_recv()
        for way in range(2):
            side_copy(group, way).start()

    def corner(group):
        for way in range(2):
            side_copy(group, way).wait_recv()
        for way in range(2):
            corner_copy(group, way).start()

    def share(group):
        for way in range(2):
            corner_copy(group, way).wait_recv()
        core_copy(group).start()

    stages = (offer, combine, widen, corner, share)

    def tick(number):
        for order, stage_of in enumerate(stages):
            group = number - LAG * order

            @pl.when(jnp.logical_and(group >= 0, group < groups))
            def _():
                stage_of(group)

    def ticks(start, stop):
        def body(number, carry):
            tick(number)
            return carry

        lax.fori_loop(start, stop, body, 0)

    def arrived(first, last):
        def body(group, carry):
            core_copy(group).wait_recv()
            return carry

        lax.fori_loop(first, last, body, 0)

    for j in range(3):
        ids_copy(j).start()
    own_ids().start()

    def pick(place, carry):
        value = master_ref[local_ref[place]]
        value = jnp.where(valid_ref[place] > 0, value, jnp.zeros_like(value)).astype(jnp.bfloat16)
        for quarter in range(4):
            grad_inner[pl.ds(pl.multiple_of(place * 16, 16), 16), quarter * width : quarter * width + width] = value[
                16 * quarter : 16 * quarter + 16
            ]
        return carry

    lax.fori_loop(0, groups * 2, pick, 0)
    ticks(0, START)

    def matrix(place):
        return weights[place].reshape(width, width)

    def matrix_half(which):
        return weights[0, 2 * which : 2 * which + 2].reshape(vocab, width)

    def count_copy(j):
        return remote(counts.at[dp], counts.at[dp], count_send.at[j], count_recv.at[j], column[j])

    def own_copy(order):
        return pltpu.make_async_copy(stage.at[order % 4, :, core], own_far.at[order], stage_sem.at[order % 2])

    def pair_copy(order):
        return remote(
            stage.at[order % 4, :, 1 - core], other_far.at[order], g_send.at[order % 4], g_recv.at[order], sibling
        )

    def put(order, half_of):
        @pl.when(jnp.int32(order) >= 4)
        def _():
            pair_copy(order - 4).wait_send()

        @pl.when(jnp.int32(order) >= 1)
        def _():
            own_copy(order - 1).wait()

        for half in range(2):
            value = half_of(pl.ds(256 * half, 256))
            stage[order % 4, 2 * half : 2 * half + 2] = value.reshape(2, 2, 2, 2, 16, width)
        own_copy(order).start()
        pair_copy(order).start()

    small_ref[...] = jnp.zeros_like(small_ref)
    own_ids().wait()
    for j in range(3):
        ids_copy(j).wait_recv()
    ids_col[...] = ids_row[...].astype(jnp.float32).T
    length_one = length_ref[0]
    temps = (turned, grad_inner, branch, turned_norm, key_sum, value_sum)

    def hot_rows(rows, which, offset, count):
        ids = ids_col[rows, which : which + 1] + float(offset)
        lane = lax.broadcasted_iota(jnp.int32, (ROWS, count), 1).astype(jnp.float32)
        return (ids == lane).astype(jnp.bfloat16)

    def hot_turned(which, offset, count):
        ids = ids_row[which : which + 1, :] + offset
        line = lax.broadcasted_iota(jnp.int32, (count, length), 0)
        return (ids == line).astype(jnp.float32)

    arrived(0, 2)

    def embed(rows):
        return product(hot_rows(rows, 0, 0, vocab), matrix_half(0))

    char = Block(length, (13, 17, 21, 22), 1, 0, embed, qkv, logs, attended, after, leave)
    seg = Block(
        segments, (0, 4, 8, 9), 14, 2, lambda rows: seg_entry[rows, :],
        seg_qkv, seg_logs, seg_attended, seg_after, seg_leave,
    )
    tick(START)
    block_run(
        char,
        matrix,
        gains_ref,
        (
            lambda: tick(START + 1),
            lambda pair: tick(START + 2 + pair),
            lambda: arrived(2, 7),
            lambda number: tick(START + 6 + number),
        ),
    )
    ticks(START + 10, groups + LAG * (len(stages) - 1))

    def valid_rows(rows):
        line = lax.broadcasted_iota(jnp.int32, (ROWS, 1), 0) + rows.start
        return (line < length_one).astype(jnp.float32)

    def boundary(rows):
        low = leave[rows, :].astype(jnp.bfloat16)
        reach = jnp.tanh(product(low, matrix(13)))
        logit = jnp.sum(reach * gains_ref[5:6, :], axis=1, keepdims=True) * root_width
        return low, reach, 1.0 / (1.0 + jnp.exp(-logit))

    def soft_step(number, total):
        rows = pl.ds(pl.multiple_of(number * ROWS, ROWS), ROWS)
        return total + jnp.sum(valid_rows(rows) * boundary(rows)[2], axis=0, keepdims=True)

    soft_local = lax.fori_loop(0, length // ROWS, soft_step, jnp.zeros((1, 1), jnp.float32))
    line = lax.broadcasted_iota(jnp.int32, (8, 128), 0)
    length_float = length_one.astype(jnp.float32)
    counts[dp] = jnp.where(line == 0, soft_local, jnp.where(line == 1, length_float, 0.0))
    for j in range(7):
        count_copy(j).start()

    pool = hot_turned(2, 1, segments)
    amounts = jnp.sum(pool, axis=1, keepdims=True)
    divisor = jnp.maximum(amounts, 1.0)
    seg_entry[...] = product(pool.astype(jnp.bfloat16), leave[...].astype(jnp.bfloat16)) / divisor
    arrived(7, groups)
    block_run(seg, matrix, gains_ref, (lambda: None, lambda pair: None, lambda: None, lambda number: None))

    for j in range(7):
        count_copy(j).wait_recv()
    total = counts[0]
    for j in range(1, 8):
        total = total + counts[j]
    soft_count, count_all = total[0:1, 0:1], total[1:2, 0:1]

    def head(number, carry):
        ce, head_sum = carry
        rows = pl.ds(pl.multiple_of(number * ROWS, ROWS), ROWS)
        lift = hot_rows(rows, 2, 0, segments)
        merged = leave[rows, :] + product(lift, seg_leave[...].astype(jnp.bfloat16))
        scale = root_scale(merged)
        gain = gains_ref[4:5, :]
        final_low = (merged * scale * gain).astype(jnp.bfloat16)
        table = matrix_half(1)
        logits = product_nt(final_low, table)
        peak = jnp.max(logits, axis=1, keepdims=True)
        log_total = peak + jnp.log(jnp.sum(jnp.exp(logits - peak), axis=1, keepdims=True))
        target = hot_rows(rows, 1, 0, vocab).astype(jnp.float32)
        picked = jnp.sum(logits * target, axis=1, keepdims=True)
        valid = valid_rows(rows)
        ce = ce + jnp.sum(valid * (log_total - picked), axis=0, keepdims=True)
        share = valid / (micro_count * count_all)
        grad_logits = (jnp.exp(logits - log_total) - target) * share
        head_sum = head_sum + product(turn(grad_logits), final_low)
        back, gain_part = norm_back(merged, scale, gain, product(grad_logits.astype(jnp.bfloat16), table))
        small_ref[4:5, :] = small_ref[4:5, :] + gain_part
        grad[rows, :] = back
        return ce, head_sum

    ce_local, head_sum = lax.fori_loop(
        0, length // ROWS, head, (jnp.zeros((1, 1), jnp.float32), jnp.zeros((vocab, width), jnp.float32))
    )
    head_grad[...] = head_sum
    seg_grad[...] = exact_product(hot_turned(2, 0, segments).astype(jnp.bfloat16), grad[...])
    def sent(group, carry):
        for j in range(3):
            peer_copy(group, j).wait_send()
            tower_copy(group, j).wait_send()
        for way in range(2):
            side_copy(group, way).wait_send()
            corner_copy(group, way).wait_send()
        core_copy(group).wait_send()
        return carry

    lax.fori_loop(0, groups, sent, 0)
    reducer = Reducer(
        places(), own_far, other_far, pair_copy, [(dp, peer) for peer in beside], [(dp, peer) for peer in side], tower, reduce_refs
    )
    block_back(
        seg, seg_grad, matrix, gains_ref, small_ref, temps, put,
        (lambda part: None, lambda part: reducer.tick(part), lambda pair: None),
    )
    seg_grad[...] = seg_grad[...] / divisor

    count_rest = count_all - soft_count
    slope = (digamma(soft_count + 1.0) - digamma(count_rest + 1.0) + LOG_ODDS) / (count_all * micro_count)

    def join(rows):
        low, reach, chance = boundary(rows)
        logit = valid_rows(rows) * slope * chance * (1.0 - chance)
        gain = gains_ref[5:6, :]
        small_ref[5:6, :] = small_ref[5:6, :] + jnp.sum(logit * reach, axis=0, keepdims=True) * root_width
        pre = (logit * gain * root_width * (1.0 - reach * reach)).astype(jnp.bfloat16)
        branch[rows, :] = pre
        turned[:, rows] = turn(low)
        spread = exact_product(hot_rows(rows, 2, 1, segments), seg_grad[...])
        grad[rows, :] = (grad[rows, :] + spread) + product_nt(pre, matrix(13))

    each_block(length, join)
    put(12, lambda half: product(turned[half, :], branch[...]))
    block_back(
        char, grad, matrix, gains_ref, small_ref, temps, put,
        (
            lambda part: reducer.tick(4 + part),
            lambda part: None,
            lambda pair: reducer.ticks(8 + 2 * pair, 10 + 2 * pair),
        ),
    )
    embed_grad = exact_product(hot_turned(0, 0, vocab).astype(jnp.bfloat16), grad[...])
    put(25, lambda half: embed_grad if half.start == 0 else head_grad[...])
    own_copy(25).wait()

    lane = lax.broadcasted_iota(jnp.int32, (1, width), 1)
    small_ref[6:7, :] = jnp.where(
        lane == seq,
        ce_local,
        jnp.where(lane == seq + 8, soft_local, jnp.where(lane == seq + 16, length_float, 0.0)),
    )
    for j in range(7):
        count_copy(j).wait_send()
    for j in range(3):
        ids_copy(j).wait_send()
    sums = Sums(places(), column, [(dp, peer) for peer in side], small_ref, small_out, square_out, reduce_refs)
    sums.start_small()
    reducer.ticks(16, reducer.last_tick)
    sums.pass_small()
    square = reducer.collect(source_ref, parity_ref, owned_ref, stage)
    held = out_ref.shape[0]
    for slot in range(held):
        pltpu.make_async_copy(
            stage.at[slot // 8, slot % 8 // 2, slot % 2], out_ref.at[slot], out_sem.at[slot]
        ).start()
    sums.squares(square)
    for slot in range(held):
        pltpu.make_async_copy(
            stage.at[slot // 8, slot % 8 // 2, slot % 2], out_ref.at[slot], out_sem.at[slot]
        ).wait()
    sums.finish()
    reducer.finish()


def step_call(length_one, owner_slot, master, ids, gains, micro_count):
    held, rows, width = master.shape
    tile_count = owner_slot.shape[0]
    seq_count, dp_count = lax.axis_size("seq"), lax.axis_size("dp")
    groups = tile_count // 2
    length = seq_count * ids.shape[2]
    segments = SEG_DEV * seq_count
    dma = pltpu.SemaphoreType.DMA
    vmem = pl.BlockSpec(memory_space=pltpu.VMEM)
    smem = pl.BlockSpec(memory_space=pltpu.SMEM)
    hbm = pl.BlockSpec(memory_space=pl.ANY)
    local = owner_slot - lax.axis_index("seq") * held
    valid = jnp.logical_and(local >= 0, local < held).astype(jnp.int32)
    hot = jnp.arange(held)[:, None] == jnp.take(local, jnp.array(GRAD_ORDER))[None, :]
    source = jnp.sum(jnp.where(hot, jnp.arange(tile_count)[None, :], 0), axis=1)
    owned = jnp.any(hot, axis=1).astype(jnp.int32)
    parity = jnp.concatenate([jnp.pad(source // 2, (0, 16 - held)), source % 2])
    local = jnp.where(valid > 0, local, 0)

    def used(values):
        return jnp.concatenate([values[25:], values[:12], values[24:25], values[12:24]])

    def full(*shape):
        return pltpu.VMEM(shape, jnp.float32)

    def half(*shape):
        return pltpu.VMEM(shape, jnp.bfloat16)

    def codes(*shape):
        return pltpu.VMEM(shape + (16, width), jnp.int16)

    def kept(count):
        return [
            half(count, 3 * width), full(4, 2, count), half(count, width), full(count, width),
            full(count, width), full(count, width),
        ]

    reduce_refs = [
        full(2, 4, 2, 2, 16, width), full(2, 4, 2, 2, 16, width),
        full(2, 2, 8, 16, width), full(2, 2, 4, 16, width), full(2, 2, 16, width), full(tile_count, 16, width),
        codes(3, 2, 8), codes(tile_count, 8), codes(3, 2, 4), codes(tile_count, 4),
        codes(3, 3, 2), codes(3, tile_count), codes(3, 2), codes(3, tile_count),
        full(3, 2, 8, 128), full(tile_count, 8, 128), full(3, 2, 8, 128), full(tile_count, 8, 128),
        full(3, 3, 8, 128), full(3, groups, 8, 128), full(3, 8, 128), full(3, groups, 8, 128),
        dma((2,)), dma((2, 3, 2)), dma((2, tile_count)), dma((2, 3, 2)), dma((2, tile_count)),
        dma((2, 3, 3)), dma((2, 3, groups)), dma((2, 3, 3)), dma((2, 3, groups)),
        full(dp_count, 8, width), full(seq_count, 8, width), full(dp_count, 8, 128), full(seq_count, 8, 128),
        [dma((7,)), dma((7,)), dma((3,)), dma((3,)), dma((7,)), dma((7,)), dma((3,)), dma((3,))],
    ]
    return pl.pallas_call(
        functools.partial(step_kernel, micro_count),
        out_shape=(
            jax.ShapeDtypeStruct((tile_count, 4, 2, 2, 16, width), jnp.float32),
            jax.ShapeDtypeStruct((tile_count, 4, 2, 2, 16, width), jnp.float32),
            jax.ShapeDtypeStruct((held, 2, 2, 16, width), jnp.float32),
            jax.ShapeDtypeStruct((8, width), jnp.float32),
            jax.ShapeDtypeStruct((8, 128), jnp.float32),
        ),
        in_specs=[smem] * 6 + [vmem] * 3,
        out_specs=(hbm, hbm, hbm, vmem, vmem),
        scratch_shapes=[half(tile_count, 4, 2, 4, 16, width)]
        + kept(length)
        + [full(segments, width)]
        + kept(segments)
        + [
            half(width, length), half(length, 4 * width), half(length, width), half(width, length),
            full(length, 128), full(length, 128), full(width // 2, width), full(8, width),
            pltpu.VMEM((8, length), jnp.int32), full(length, 8), full(4, 4, 2, 2, 2, 16, width), dma((2,)),
            full(dp_count, 8, 128), dma((7,)), dma((7,)), dma((3,)), dma((3,)), dma,
            dma((4,)), dma((tile_count,)), dma((held,)),
            dma((3, groups)), dma((3, groups)), dma((3, groups)), dma((3, groups)),
            dma((2, groups)), dma((2, groups)), dma((2, groups)), dma((2, groups)),
            dma((groups,)), dma((groups,)), reduce_refs,
        ],
        name="step",
        compiler_params=pltpu.CompilerParams(
            collective_id=2, has_side_effects=True, vmem_limit_bytes=STEP_VMEM
        ),
    )(length_one, used(local), used(valid), source, parity, owned, master, ids, gains)[2:]


def whole_step(char_ids, targets, seg_ids, lengths, owner_slot, master, gain_rows):
    micro_count = char_ids.shape[0]
    ids = jnp.stack([char_ids[:, 0], targets[:, 0], seg_ids[:, 0]], axis=1)
    ids = jnp.pad(ids, ((0, 0), (0, 5), (0, 0)))
    length_one = lax.dynamic_slice_in_dim(lengths[:, 0], lax.axis_index("seq"), 1)
    gains = jnp.pad(gain_rows, ((0, 2), (0, 0)))
    return step_call(length_one, owner_slot, master, ids, gains, micro_count)


def body(
    char_ids,
    targets,
    seg_ids,
    lengths,
    owner_slot,
    step_count,
    master,
    tile_first,
    tile_second,
    gain_rows,
    gain_first,
    gain_second,
):
    micro_count = char_ids.shape[0]
    model_width = master.shape[2]
    slot_count = master.shape[0] * lax.axis_size("seq")
    if (micro_count, lax.axis_size("seq"), lax.axis_size("dp")) == (4, 4, 8):
        shard_total, small, squares = whole_step(
            char_ids, targets, seg_ids, lengths, owner_slot, master, gain_rows
        )
        shard_total = shard_total.reshape(master.shape)
        gain_sum, square_sum = small[0:6], jnp.sum(squares)
        entropy, soft, count = (small[6, 8 * i : 8 * i + micro_count] for i in range(3))
        prior = -(
            lax.lgamma(count + 1.0)
            - lax.lgamma(soft + 1.0)
            - lax.lgamma(count - soft + 1.0)
            + soft * jnp.log(PRIOR_RATE)
            + (count - soft) * jnp.log(1.0 - PRIOR_RATE)
        )
        loss_total = jnp.sum((entropy + prior) / count) / micro_count
    else:
        tile_total = jnp.zeros((owner_slot.shape[0], model_width, model_width), jnp.float32)
        gain_total = jnp.zeros_like(gain_rows)
        loss_total = jnp.zeros((), jnp.float32)
        for micro in range(micro_count):
            tiles = gather_tiles(master, owner_slot)
            tile_part, gain_part, loss_part = micro_step(
                tiles,
                gain_rows,
                char_ids[micro, 0],
                targets[micro, 0],
                seg_ids[micro, 0],
                lengths[micro, 0],
                micro_count,
            )
            tile_total = tile_total + tile_part
            gain_total = gain_total + gain_part
            loss_total = loss_total + loss_part
        shard_total = reduce_tiles(tile_total, owner_slot, slot_count)
        gain_sum, square_sum = lax.psum((gain_total, jnp.sum(shard_total * shard_total)), ("dp", "seq"))
    grad_norm = jnp.sqrt(square_sum + jnp.sum(gain_sum * gain_sum))
    clip_factor = jnp.minimum(1.0, CLIP_NORM / (grad_norm + 1e-06))
    step_float = step_count[0].astype(jnp.float32)
    local_ids = lax.axis_index("seq") * master.shape[0] + jnp.arange(master.shape[0])
    owned = jnp.any(local_ids[:, None] == owner_slot[None, :], axis=1)[:, None, None]
    new_tiles, new_first, new_second = adam_step(
        master,
        tile_first,
        tile_second,
        shard_total * clip_factor,
        RATE_TILES,
        WEIGHT_DECAY,
        step_float,
    )
    master_new = jnp.where(owned, new_tiles, master)
    first_new = jnp.where(owned, new_first, tile_first)
    second_new = jnp.where(owned, new_second, tile_second)
    gains_new, gain_first_new, gain_second_new = adam_step(
        gain_rows, gain_first, gain_second, gain_sum * clip_factor, RATE_GAINS, 0.0, step_float
    )
    return (
        loss_total.reshape(1),
        grad_norm.reshape(1),
        master_new,
        first_new,
        second_new,
        master_new.astype(jnp.bfloat16),
        gains_new,
        gain_first_new,
        gain_second_new,
    )


def solution(mesh):
    return jax.shard_map(
        body,
        mesh=mesh,
        in_specs=(
            P(None, "dp", "seq"),
            P(None, "dp", "seq"),
            P(None, "dp", "seq"),
            P(None, "dp"),
            P(),
            P(),
            P("seq", "dp", None),
            P("seq", "dp", None),
            P("seq", "dp", None),
            P(),
            P(),
            P(),
        ),
        out_specs=(
            P(),
            P(),
            P("seq", "dp", None),
            P("seq", "dp", None),
            P("seq", "dp", None),
            P("seq", "dp", None),
            P(),
            P(),
            P(),
        ),
        check_vma=False,
    )
```

```python
import functools
import math

import jax
import jax.numpy as jnp
from jax import lax
from jax.experimental import pallas as pl
from jax.experimental.pallas import tpu as pltpu
from jax.sharding import PartitionSpec as P

HEADS = 8
SEG_DEV = 64


BETA_ONE = 0.9
BETA_TWO = 0.95
ADAM_EPS = 1e-08
WEIGHT_DECAY = 0.1
RATE_TILES = 0.03
RATE_GAINS = 0.2
CLIP_NORM = 0.05
PRIOR_RATE = 0.25
NORM_EPS = 1e-06
MASKED = -1e30
LOG_ODDS = math.log(1.0 - PRIOR_RATE) - math.log(PRIOR_RATE)


def product(left, right):
    return jnp.dot(left, right, preferred_element_type=jnp.float32)


def product_tn(left, right):
    return lax.dot_general(
        left, right, (((0,), (0,)), ((), ())), preferred_element_type=jnp.float32
    )


def product_nt(left, right):
    return lax.dot_general(
        left, right, (((1,), (1,)), ((), ())), preferred_element_type=jnp.float32
    )


def exact_tn(left, right):
    return lax.dot_general(
        left,
        right,
        (((0,), (0,)), ((), ())),
        precision=lax.Precision.HIGHEST,
        preferred_element_type=jnp.float32,
    )


def rms_norm(values, gain):
    return values * lax.rsqrt(jnp.mean(values * values, axis=-1, keepdims=True) + NORM_EPS) * gain


def split_heads(tensor):
    return tensor.reshape(tensor.shape[0], HEADS, tensor.shape[1] // HEADS).transpose(1, 0, 2)


def join_heads(tensor):
    return tensor.transpose(1, 0, 2).reshape(tensor.shape[1], tensor.shape[0] * tensor.shape[2])


def block_weights(tiles):
    w_qkv = jnp.concatenate([tiles[0], tiles[1], tiles[2]], axis=1)
    w_up = jnp.concatenate([tiles[4], tiles[5], tiles[6], tiles[7]], axis=1)
    w_down = jnp.concatenate([tiles[8], tiles[9], tiles[10], tiles[11]], axis=0)
    return (w_qkv, w_up, w_down)


def causal_mask(row_count, key_count):
    first_row = lax.axis_index("seq") * row_count
    return (first_row + jnp.arange(row_count))[:, None] >= jnp.arange(key_count)[None, :]


def block_forward(hidden_in, tiles, gain_attn, gain_ffn, segment):
    row_count, model_width = hidden_in.shape
    w_qkv, w_up, w_down = block_weights(tiles)
    normed = rms_norm(hidden_in, gain_attn).astype(jnp.bfloat16)
    qkv_low = product(normed, w_qkv).astype(jnp.bfloat16)
    if segment:
        gathered = lax.all_gather(qkv_low[:, model_width:], "seq", axis=0, tiled=True)
    else:
        gathered = lax.all_gather(qkv_low[:, model_width:], "seq", axis=0, tiled=True)
    allowed = causal_mask(row_count, gathered.shape[0])
    factor = (model_width // HEADS) ** (-0.5)

    def head_forward(triple):
        q_head, k_head, v_head = triple
        scores = jnp.where(allowed, product_nt(q_head, k_head) * factor, MASKED)
        peak = jnp.max(scores, axis=1, keepdims=True)
        log_total = peak + jnp.log(jnp.sum(jnp.exp(scores - peak), axis=1, keepdims=True))
        weights = jnp.exp(scores - log_total).astype(jnp.bfloat16)
        return (product(weights, v_head), log_total[:, 0])

    head_out, log_totals = lax.map(
        head_forward,
        (
            split_heads(qkv_low[:, :model_width]),
            split_heads(gathered[:, :model_width]),
            split_heads(gathered[:, model_width:]),
        ),
    )
    attended = join_heads(head_out).astype(jnp.bfloat16)
    after_attn = hidden_in + product(attended, tiles[3])
    inner = product(rms_norm(after_attn, gain_ffn).astype(jnp.bfloat16), w_up)
    block_out = after_attn + product(jax.nn.gelu(inner).astype(jnp.bfloat16), w_down)
    return (block_out, (hidden_in, qkv_low, gathered, log_totals, attended, after_attn, inner))


def block_backward(grad_out, saved, tiles, gain_attn, gain_ffn, segment):
    hidden_in, qkv_low, gathered, log_totals, attended, after_attn, inner = saved
    row_count, model_width = hidden_in.shape
    w_qkv, w_up, w_down = block_weights(tiles)
    grad_ffn = grad_out.astype(jnp.bfloat16)
    activated, gelu_pull = jax.vjp(jax.nn.gelu, inner)
    grad_down = product_tn(activated.astype(jnp.bfloat16), grad_ffn)
    grad_inner = gelu_pull(product_nt(grad_ffn, w_down))[0].astype(jnp.bfloat16)
    normed_ffn, ffn_pull = jax.vjp(rms_norm, after_attn, gain_ffn)
    grad_up = product_tn(normed_ffn.astype(jnp.bfloat16), grad_inner)
    grad_normed_in, grad_gain_ffn = ffn_pull(product_nt(grad_inner, w_up))
    grad_after = grad_out + grad_normed_in
    grad_branch = grad_after.astype(jnp.bfloat16)
    grad_wout = product_tn(attended, grad_branch)
    grad_attended = product_nt(grad_branch, tiles[3]).astype(jnp.bfloat16)
    allowed = causal_mask(row_count, gathered.shape[0])
    factor = (model_width // HEADS) ** (-0.5)

    def head_backward(bundle):
        q_head, k_head, v_head, upstream, log_head = bundle
        scores = jnp.where(allowed, product_nt(q_head, k_head) * factor, MASKED)
        weights = jnp.exp(scores - log_head[:, None])
        grad_values = product_tn(weights.astype(jnp.bfloat16), upstream)
        grad_weights = product_nt(upstream, v_head)
        inner_sum = jnp.sum(weights * grad_weights, axis=1, keepdims=True)
        grad_scores = (weights * (grad_weights - inner_sum)).astype(jnp.bfloat16)
        return (
            product(grad_scores, k_head) * factor,
            product_tn(grad_scores, q_head) * factor,
            grad_values,
        )

    grad_query, grad_keys, grad_values = lax.map(
        head_backward,
        (
            split_heads(qkv_low[:, :model_width]),
            split_heads(gathered[:, :model_width]),
            split_heads(gathered[:, model_width:]),
            split_heads(grad_attended),
            log_totals,
        ),
    )
    grad_kv_all = jnp.concatenate([join_heads(grad_keys), join_heads(grad_values)], axis=1)
    if segment:
        grad_kv = lax.psum_scatter(grad_kv_all, "seq", scatter_dimension=0, tiled=True)
    else:
        grad_kv = lax.psum_scatter(grad_kv_all, "seq", scatter_dimension=0, tiled=True)
    grad_qkv = jnp.concatenate([join_heads(grad_query), grad_kv], axis=1).astype(jnp.bfloat16)
    normed_attn, attn_pull = jax.vjp(rms_norm, hidden_in, gain_attn)
    grad_wqkv = product_tn(normed_attn.astype(jnp.bfloat16), grad_qkv)
    grad_normed_x, grad_gain_attn = attn_pull(product_nt(grad_qkv, w_qkv))
    grad_in = grad_after + grad_normed_x
    pieces = [
        grad_wqkv[:, part_index * model_width : (part_index + 1) * model_width]
        for part_index in range(3)
    ]
    pieces = pieces + [grad_wout]
    pieces = pieces + [
        grad_up[:, part_index * model_width : (part_index + 1) * model_width]
        for part_index in range(4)
    ]
    pieces = pieces + [
        grad_down[part_index * model_width : (part_index + 1) * model_width]
        for part_index in range(4)
    ]
    return (grad_in, jnp.stack(pieces), grad_gain_attn, grad_gain_ffn)


def micro_step(tiles, gain_rows, chars_row, target_row, segment_row, length_one, micro_count):
    char_count = chars_row.shape[0]
    model_width = tiles.shape[2]
    vocab_size = model_width // 2
    seq_count = lax.axis_size("seq")
    seg_total = SEG_DEV * seq_count
    position = lax.axis_index("seq") * char_count + jnp.arange(char_count)
    is_valid = (position < length_one).astype(jnp.float32)
    vocab_iota = jnp.arange(vocab_size)
    char_hot = chars_row[:, None] == vocab_iota[None, :]
    embed_low = tiles[25, :vocab_size]
    head_low = tiles[25, vocab_size:]
    start_hidden = product(char_hot.astype(jnp.bfloat16), embed_low)
    char_out, char_saved = block_forward(
        start_hidden, tiles[0:12], gain_rows[0], gain_rows[1], False
    )
    char_low = char_out.astype(jnp.bfloat16)
    boundary_hidden = jnp.tanh(product(char_low, tiles[24]))
    root_width = model_width ** (-0.5)
    boundary_prob = jax.nn.sigmoid(jnp.sum(boundary_hidden * gain_rows[5], axis=1) * root_width)
    slot_iota = jnp.arange(seg_total)
    pool_hot = segment_row[None, :] + 1 == slot_iota[:, None]
    lift_hot = segment_row[:, None] == slot_iota[None, :]
    part_sums = product(pool_hot.astype(jnp.bfloat16), char_low).reshape(
        seq_count, SEG_DEV, model_width
    )
    side_info = jnp.stack(
        [
            jnp.sum(pool_hot.astype(jnp.float32), axis=1),
            jnp.any(lift_hot, axis=0).astype(jnp.float32),
        ],
        axis=0,
    )
    side_info = side_info.reshape(2, seq_count, SEG_DEV).transpose(1, 0, 2)
    sums_in, side_in = (
        lax.all_to_all(part_sums, "seq", split_axis=0, concat_axis=0, tiled=True),
        lax.all_to_all(side_info, "seq", split_axis=0, concat_axis=0, tiled=True),
    )
    row_counts = jnp.sum(side_in[:, 0, :], axis=0)
    divisor = jnp.maximum(row_counts, 1.0)[:, None]
    pooled = jnp.sum(sums_in, axis=0) / divisor
    seg_out, seg_saved = block_forward(pooled, tiles[12:24], gain_rows[2], gain_rows[3], True)
    outgoing = side_in[:, 1, :, None].astype(jnp.bfloat16) * seg_out.astype(jnp.bfloat16)[None]
    returned = lax.all_to_all(outgoing, "seq", split_axis=0, concat_axis=0, tiled=True)
    merged = char_out + product(
        lift_hot.astype(jnp.bfloat16), returned.reshape(seg_total, model_width)
    )
    final_norm, final_pull = jax.vjp(rms_norm, merged, gain_rows[4])
    final_low = final_norm.astype(jnp.bfloat16)
    logits = product_nt(final_low, head_low)
    peak = jnp.max(logits, axis=1, keepdims=True)
    log_total = peak[:, 0] + jnp.log(jnp.sum(jnp.exp(logits - peak), axis=1))
    target_hot = (target_row[:, None] == vocab_iota[None, :]).astype(jnp.float32)
    picked = jnp.sum(logits * target_hot, axis=1)
    ce_local = jnp.sum(is_valid * (log_total - picked))
    ce_all, soft_count, count_all = lax.psum(
        (ce_local, jnp.sum(is_valid * boundary_prob), jnp.sum(is_valid)), ("dp", "seq")
    )
    weight_ce = is_valid / (micro_count * count_all)
    grad_logits = ((jnp.exp(logits - log_total[:, None]) - target_hot) * weight_ce[:, None]).astype(
        jnp.bfloat16
    )
    grad_head = product_tn(grad_logits, final_low)
    grad_merged, grad_gain_final = final_pull(product(grad_logits, head_low))
    grad_rows = exact_tn(lift_hot.astype(jnp.float32), grad_merged).reshape(
        seq_count, SEG_DEV, model_width
    )
    grad_seg = jnp.sum(
        lax.all_to_all(grad_rows, "seq", split_axis=0, concat_axis=0, tiled=True), axis=0
    )
    grad_pooled, seg_tiles, grad_gain_two, grad_gain_three = block_backward(
        grad_seg, seg_saved, tiles[12:24], gain_rows[2], gain_rows[3], True
    )
    grad_sums = (side_in[:, 0, :, None] > 0).astype(jnp.float32) * (grad_pooled / divisor)[None]
    grad_back = lax.all_to_all(grad_sums, "seq", split_axis=0, concat_axis=0, tiled=True).reshape(
        seg_total, model_width
    )
    grad_char = grad_merged + exact_tn(pool_hot.astype(jnp.float32), grad_back)
    prior_slope = (
        lax.digamma(soft_count + 1.0)
        - lax.digamma(count_all - soft_count + 1.0)
        - jnp.log(PRIOR_RATE)
        + jnp.log(1.0 - PRIOR_RATE)
    ) / (count_all * micro_count)
    grad_boundary_logit = is_valid * prior_slope * boundary_prob * (1.0 - boundary_prob)
    grad_gain_boundary = (
        jnp.sum(grad_boundary_logit[:, None] * boundary_hidden, axis=0) * root_width
    )
    grad_pre = (
        grad_boundary_logit[:, None]
        * gain_rows[5][None, :]
        * root_width
        * (1.0 - boundary_hidden * boundary_hidden)
    ).astype(jnp.bfloat16)
    grad_boundary = product_tn(char_low, grad_pre)
    grad_char = grad_char + product_nt(grad_pre, tiles[24])
    grad_start, char_tiles, grad_gain_zero, grad_gain_one = block_backward(
        grad_char, char_saved, tiles[0:12], gain_rows[0], gain_rows[1], False
    )
    grad_embed = exact_tn(char_hot.astype(jnp.float32), grad_start)
    tile_grads = jnp.concatenate(
        [
            char_tiles,
            seg_tiles,
            grad_boundary[None],
            jnp.concatenate([grad_embed, grad_head], axis=0)[None],
        ],
        axis=0,
    )
    gain_grads = jnp.stack(
        [
            grad_gain_zero,
            grad_gain_one,
            grad_gain_two,
            grad_gain_three,
            grad_gain_final,
            grad_gain_boundary,
        ]
    )
    prior_term = (
        -(
            lax.lgamma(count_all + 1.0)
            - lax.lgamma(soft_count + 1.0)
            - lax.lgamma(count_all - soft_count + 1.0)
            + soft_count * jnp.log(PRIOR_RATE)
            + (count_all - soft_count) * jnp.log(1.0 - PRIOR_RATE)
        )
        / count_all
    )
    return (tile_grads, gain_grads, (ce_all / count_all + prior_term) / micro_count)


def gather_tiles(master, owner_slot):
    shard_low = master.astype(jnp.bfloat16)
    full_rows = lax.all_gather(shard_low, "dp", axis=1, tiled=True)
    all_slots = lax.all_gather(full_rows, "seq", axis=0, tiled=True)
    return jnp.take(all_slots, owner_slot, axis=0)


def reduce_tiles(tile_grads, owner_slot, slot_count):
    placed = (
        jnp.zeros((slot_count,) + tile_grads.shape[1:], jnp.float32).at[owner_slot].set(tile_grads)
    )
    per_owner = lax.psum_scatter(placed, "seq", scatter_dimension=0, tiled=True)
    return lax.psum_scatter(per_owner, "dp", scatter_dimension=1, tiled=True)


def adam_step(param, moment_a, moment_b, grad_in, rate, decay, step_float):
    new_first = BETA_ONE * moment_a + (1.0 - BETA_ONE) * grad_in
    new_second = BETA_TWO * moment_b + (1.0 - BETA_TWO) * grad_in * grad_in
    first_hat = new_first / (1.0 - BETA_ONE**step_float)
    second_hat = new_second / (1.0 - BETA_TWO**step_float)
    updated = param - rate * (first_hat / (jnp.sqrt(second_hat) + ADAM_EPS) + decay * param)
    return (updated, new_first, new_second)


MESH = pl.DeviceIdType.MESH
VMEM_LIMIT = 60 * 1024 * 1024
STEP_VMEM = 63 * 1024 * 1024


def remote(src, dst, send_sem, recv_sem, peer):
    return pltpu.make_async_remote_copy(
        src_ref=src, dst_ref=dst, send_sem=send_sem, recv_sem=recv_sem, device_id=peer, device_id_type=MESH
    )


def places():
    dp = lax.axis_index("dp")
    seq = lax.axis_index("seq")
    return dp, seq, dp // 2, dp % 2


def seq_peer(seq, step):
    return ((seq // 2 + step // 2) % 2) * 2 + (seq % 2 + step % 2) % 2


def meet(peers):
    barrier = pltpu.get_barrier_semaphore()
    for peer in peers:
        pl.semaphore_signal(barrier, inc=1, device_id=peer, device_id_type=MESH)
    pl.semaphore_wait(barrier, len(peers))


CODE_TOP = 32000.0
ROUNDER = 12582912.0


def encode(value):
    upper, lower = value[0:8, :], value[8:16, :]
    size = jnp.maximum(jnp.abs(upper), jnp.abs(lower))
    most = jnp.maximum(jnp.max(size, axis=1, keepdims=True), 1e-30)
    ratio = CODE_TOP / most
    coded = jnp.concatenate([upper * ratio, lower * ratio], axis=0)
    coded = ((coded + ROUNDER) - ROUNDER).astype(jnp.int32).astype(jnp.int16)
    return coded, most * (1.0 / CODE_TOP)


def decode(coded, unit):
    value = coded.astype(jnp.int32).astype(jnp.float32)
    return jnp.concatenate([value[0:8, :] * unit, value[8:16, :] * unit], axis=0)


def head_mask(shape, head):
    lane = lax.broadcasted_iota(jnp.int32, shape, 1)
    return (lane >= 64) if head else (lane < 64)


def scores_t(k_pair, q_head, first_row):
    scores = product_nt(k_pair, q_head)
    count, queries = scores.shape
    key = lax.broadcasted_iota(jnp.int32, (queries, queries), 0)
    query = lax.broadcasted_iota(jnp.int32, (queries, queries), 1)
    own = jnp.where(key <= query, scores[first_row:], MASKED)
    return own if first_row == 0 else jnp.concatenate([scores[:first_row], own], axis=0)


ROWS = 256
LAG = 2
START = 10


def split_three(value):
    high = value.astype(jnp.bfloat16)
    rest = value - high.astype(jnp.float32)
    middle = rest.astype(jnp.bfloat16)
    return high, middle, (rest - middle.astype(jnp.float32)).astype(jnp.bfloat16)


def exact_product(hot, value):
    high, middle, low = split_three(value)
    return (product(hot, low) + product(hot, middle)) + product(hot, high)


def turn(value):
    return value.astype(jnp.float32).T.astype(jnp.bfloat16)


def root_scale(value):
    return lax.rsqrt(jnp.mean(value * value, axis=-1, keepdims=True) + NORM_EPS)


def norm_back(value, scale, gain, grad):
    unit = value * scale
    weighted = grad * gain
    inner = jnp.mean(weighted * unit, axis=-1, keepdims=True)
    return scale * (weighted - unit * inner), jnp.sum(grad * unit, axis=0, keepdims=True)


def gelu_both(value):
    root = 0.7978845608028654
    square = value * value
    reach = jnp.tanh(root * value * (1.0 + 0.044715 * square))
    part = 0.5 * (1.0 + reach)
    slope = part + value * (0.5 * (1.0 - reach * reach)) * (root * (1.0 + 3.0 * 0.044715 * square))
    return value * part, slope


def digamma(value):
    moved = value + 8.0
    inverse = 1.0 / moved
    square = inverse * inverse
    series = square * (1.0 / 12.0 - square * (1.0 / 120.0 - square * (1.0 / 252.0)))
    total = jnp.log(moved) - 0.5 * inverse - series
    for number in range(8):
        total = total - 1.0 / (value + float(number))
    return total


def log_gamma(value):
    moved = value + 8.0
    inverse = 1.0 / moved
    square = inverse * inverse
    series = inverse * (1.0 / 12.0 - square * (1.0 / 360.0 - square * (1.0 / 1260.0)))
    gone = value
    for number in range(1, 8):
        gone = gone * (value + float(number))
    return ((moved - 0.5) * jnp.log(moved) - moved) + (0.9189385332046727 + series) - jnp.log(gone)


def each_block(length, body):
    def step(number, carry):
        body(pl.ds(pl.multiple_of(number * ROWS, ROWS), ROWS))
        return carry

    lax.fori_loop(0, length // ROWS, step, 0)


class Block:
    def __init__(self, length, order, place, gain_row, entry, qkv, logs, attended, after, leave):
        self.length, self.order, self.place, self.gain_row = length, order, place, gain_row
        self.entry, self.qkv, self.logs, self.attended = entry, qkv, logs, attended
        self.after, self.leave = after, leave


def attend(block, pump):
    length = block.length

    def pair_step(pair, carry):
        lanes = [pl.ds(pl.multiple_of(part * 512 + pair * 128, 128), 128) for part in range(3)]
        for first in range(0, length, ROWS):
            span = first + ROWS
            q_pair = block.qkv[first:span, lanes[0]] * jnp.asarray(0.125, jnp.bfloat16)
            outs = []
            for head in range(2):
                q_head = jnp.where(head_mask(q_pair.shape, head), q_pair, jnp.zeros_like(q_pair))
                scores = scores_t(block.qkv[0:span, lanes[1]], q_head, first)
                peak = jnp.max(scores, axis=0, keepdims=True)
                raised = jnp.exp(scores - peak)
                total = jnp.sum(raised, axis=0, keepdims=True)
                weights = (raised * (1.0 / total)).astype(jnp.bfloat16)
                block.logs[pair, head : head + 1, first:span] = peak + jnp.log(total)
                outs.append(product_tn(weights, block.qkv[0:span, lanes[2]]))
            merged = jnp.where(head_mask(outs[0].shape, 0), outs[0], outs[1])
            block.attended[first:span, lanes[0]] = merged.astype(jnp.bfloat16)
        pump(pair)
        return carry

    lax.fori_loop(0, 4, pair_step, 0)


def attend_back(block, upstream, grad_qkv, key_sum, value_sum, pump):
    length = block.length

    def pair_step(pair, carry):
        lanes = [pl.ds(pl.multiple_of(part * 512 + pair * 128, 128), 128) for part in range(3)]
        for first in reversed(range(0, length, ROWS)):
            span = first + ROWS
            q_pair = block.qkv[first:span, lanes[0]] * jnp.asarray(0.125, jnp.bfloat16)
            up_pair = upstream[first:span, lanes[0]]
            queries, keys, values = [], [], []
            for head in range(2):
                keep = head_mask(q_pair.shape, head)
                q_head = jnp.where(keep, q_pair, jnp.zeros_like(q_pair))
                up_head = jnp.where(keep, up_pair, jnp.zeros_like(up_pair))
                k_pair = block.qkv[0:span, lanes[1]]
                scores = scores_t(k_pair, q_head, first)
                weights = jnp.exp(scores - block.logs[pair, head : head + 1, first:span])
                grad_weights = product_nt(block.qkv[0:span, lanes[2]], up_head)
                values.append(product(weights.astype(jnp.bfloat16), up_head))
                inner_sum = jnp.sum(weights * grad_weights, axis=0, keepdims=True)
                grad_scores = (weights * (grad_weights - inner_sum)).astype(jnp.bfloat16)
                keys.append(product(grad_scores, q_head))
                queries.append(product_tn(grad_scores, k_pair))
            merged = jnp.where(head_mask(queries[0].shape, 0), queries[0], queries[1]) * 0.125
            grad_qkv[first:span, lanes[0]] = merged.astype(jnp.bfloat16)
            if span == length:
                key_sum[0:span, :] = keys[0] + keys[1]
                value_sum[0:span, :] = values[0] + values[1]
            else:
                key_sum[0:span, :] = key_sum[0:span, :] + (keys[0] + keys[1])
                value_sum[0:span, :] = value_sum[0:span, :] + (values[0] + values[1])
        grad_qkv[0:length, lanes[1]] = key_sum[0:length, :].astype(jnp.bfloat16)
        grad_qkv[0:length, lanes[2]] = value_sum[0:length, :].astype(jnp.bfloat16)
        pump(pair)
        return carry

    lax.fori_loop(0, 4, pair_step, 0)


def block_run(block, matrix, gains, pumps):
    place = block.place
    gain_attn = gains[block.gain_row : block.gain_row + 1, :]
    gain_ffn = gains[block.gain_row + 1 : block.gain_row + 2, :]

    def project(rows):
        value = block.entry(rows)
        normed = (value * root_scale(value) * gain_attn).astype(jnp.bfloat16)
        for part in range(3):
            block.qkv[rows, 512 * part : 512 * part + 512] = product(normed, matrix(place + part)).astype(
                jnp.bfloat16
            )

    each_block(block.length, project)
    pumps[0]()
    attend(block, pumps[1])
    pumps[2]()

    def feed(rows):
        after = block.entry(rows) + product(block.attended[rows, :], matrix(place + 3))
        block.after[rows, :] = after
        normed = (after * root_scale(after) * gain_ffn).astype(jnp.bfloat16)
        total = jnp.zeros_like(after)
        for part in range(4):
            inner = product(normed, matrix(place + 4 + part))
            active = gelu_both(inner)[0].astype(jnp.bfloat16)
            total = total + product(active, matrix(place + 8 + part))
        block.leave[rows, :] = after + total
        pumps[3](rows.start // ROWS)

    each_block(block.length, feed)


def block_back(block, grad, matrix, gains, gain_sums, temps, put, pumps):
    length, order, place = block.length, block.order, block.place
    gain_attn = gains[block.gain_row : block.gain_row + 1, :]
    gain_ffn = gains[block.gain_row + 1 : block.gain_row + 2, :]
    turned, grad_inner, branch, turned_norm, key_sum, value_sum = temps
    grad_low, grad_qkv, upstream = branch, grad_inner, block.attended
    all_rows = pl.ds(0, length)

    def down(part):
        def rows_step(rows):
            low = grad[rows, :].astype(jnp.bfloat16)
            columns = pl.ds(pl.multiple_of(part * 512, 512), 512)
            after = block.after[rows, :]
            normed = (after * root_scale(after) * gain_ffn).astype(jnp.bfloat16)
            active, slope = gelu_both(product(normed, matrix(place + 4 + part)))
            turned[:, rows] = turn(active)
            grad_inner[rows, columns] = (product_nt(low, matrix(place + 8 + part)) * slope).astype(jnp.bfloat16)

        each_block(length, rows_step)

    def low_step(rows):
        grad_low[rows, :] = grad[rows, :].astype(jnp.bfloat16)

    each_block(length, low_step)

    def down_step(part, carry):
        down(part)
        put(order[0] + part, lambda half: product(turned[half, all_rows], grad_low[all_rows, :]))
        pumps[0](part)
        return carry

    lax.fori_loop(0, 4, down_step, 0)

    def middle(rows):
        after = block.after[rows, :]
        scale = root_scale(after)
        turned_norm[:, rows] = turn(after * scale * gain_ffn)
        turned[:, rows] = turn(block.attended[rows, :])
        total = jnp.zeros_like(after)
        for part in range(4):
            total = total + product_nt(
                grad_inner[rows, 512 * part : 512 * part + 512], matrix(place + 4 + part)
            )
        back, gain_part = norm_back(after, scale, gain_ffn, total)
        row = block.gain_row + 1
        gain_sums[row : row + 1, :] = gain_sums[row : row + 1, :] + gain_part
        grad_after = grad[rows, :] + back
        grad[rows, :] = grad_after
        low = grad_after.astype(jnp.bfloat16)
        branch[rows, :] = low
        upstream[rows, :] = product_nt(low, matrix(place + 3)).astype(jnp.bfloat16)

    each_block(length, middle)

    def up_step(part, carry):
        columns = pl.ds(pl.multiple_of(part * 512, 512), 512)
        put(order[1] + part, lambda half: product(turned_norm[half, all_rows], grad_inner[all_rows, columns]))
        pumps[1](part)
        return carry

    lax.fori_loop(0, 4, up_step, 0)
    put(order[2], lambda half: product(turned[half, all_rows], branch[all_rows, :]))
    pumps[3]()
    attend_back(block, upstream, grad_qkv, key_sum, value_sum, pumps[2])

    def enter(rows):
        value = block.entry(rows)
        scale = root_scale(value)
        turned_norm[:, rows] = turn(value * scale * gain_attn)
        total = jnp.zeros_like(value)
        for part in range(3):
            total = total + product_nt(grad_qkv[rows, 512 * part : 512 * part + 512], matrix(place + part))
        back, gain_part = norm_back(value, scale, gain_attn, total)
        row = block.gain_row
        gain_sums[row : row + 1, :] = gain_sums[row : row + 1, :] + gain_part
        grad[rows, :] = grad[rows, :] + back

    each_block(length, enter)

    def qkv_step(part, carry):
        columns = pl.ds(pl.multiple_of(part * 512, 512), 512)
        put(order[3] + part, lambda half: product(turned_norm[half, all_rows], grad_qkv[all_rows, columns]))
        return carry

    lax.fori_loop(0, 3, qkv_step, 0)


def total_of(value):
    return jnp.sum(jnp.sum(value, axis=1, keepdims=True), axis=0, keepdims=True)


class Reducer:
    pairs = 13
    offsets = (1, 2, 4, 6, 8)
    gaps = ((11, 4),)
    last_tick = pairs + sum(count for _, count in gaps) + offsets[-1]

    def __init__(self, place, own_far, other_far, pair_copy, beside, side, tower, refs):
        self.dp, self.seq, self.z, self.core = place
        self.across, self.along = self.seq % 2, self.seq // 2
        self.own_far, self.other_far, self.pair_copy = own_far, other_far, pair_copy
        self.beside, self.side, self.tower = beside, side, tower
        (
            self.own, self.other, self.one, self.two, self.three, self.final,
            self.b1_out, self.b1_in, self.b2_out, self.b2_in, self.c_out, self.c_in, self.d_out, self.d_in,
            self.b1_unit_out, self.b1_unit_in, self.b2_unit_out, self.b2_unit_in,
            self.c_unit_out, self.c_unit_in, self.d_unit_out, self.d_unit_in,
            self.l_sem, self.b1_send, self.b1_recv, self.b2_send, self.b2_recv,
            self.c_send, self.c_recv, self.d_send, self.d_recv,
        ) = refs[:31]
        self.lane = lax.broadcasted_iota(jnp.int32, (8, 128), 1)

    def loads(self, pair):
        two = pl.ds(pair * 2, 2)
        return [
            pltpu.make_async_copy(self.own_far.at[two], self.own, self.l_sem.at[0]),
            pltpu.make_async_copy(self.other_far.at[two], self.other, self.l_sem.at[1]),
        ]

    def first_copies(self, pair, order):
        tile, slot, peer = pair * 2 + order, pair % 3, self.beside[order]
        send, recv = self.b1_send, self.b1_recv
        return [
            remote(self.b1_out.at[slot, order], self.b1_in.at[tile], send.at[0, slot, order], recv.at[0, tile], peer),
            remote(
                self.b1_unit_out.at[slot, order], self.b1_unit_in.at[tile], send.at[1, slot, order], recv.at[1, tile], peer
            ),
        ]

    def second_copies(self, pair, order):
        tile, slot, peer = pair * 2 + order, pair % 3, self.beside[1 - order]
        send, recv = self.b2_send, self.b2_recv
        return [
            remote(self.b2_out.at[slot, order], self.b2_in.at[tile], send.at[0, slot, order], recv.at[0, tile], peer),
            remote(
                self.b2_unit_out.at[slot, order], self.b2_unit_in.at[tile], send.at[1, slot, order], recv.at[1, tile], peer
            ),
        ]

    def tower_copies(self, pair, j):
        two, slot, peer = pl.ds(pair * 2, 2), pair % 3, self.tower[j]
        send, recv = self.c_send, self.c_recv
        return [
            remote(self.c_out.at[slot, j], self.c_in.at[j, two], send.at[0, slot, j], recv.at[0, j, pair], peer),
            remote(self.c_unit_out.at[slot, j], self.c_unit_in.at[j, pair], send.at[1, slot, j], recv.at[1, j, pair], peer),
        ]

    def share_copies(self, pair, j):
        two, slot, peer = pl.ds(pair * 2, 2), pair % 3, self.side[j]
        send, recv = self.d_send, self.d_recv
        return [
            remote(self.d_out.at[slot], self.d_in.at[j, two], send.at[0, slot, j], recv.at[0, j, pair], peer),
            remote(self.d_unit_out.at[slot], self.d_unit_in.at[j, pair], send.at[1, slot, j], recv.at[1, j, pair], peer),
        ]

    def after_sends(self, pair, copies, count):
        @pl.when(pair >= 3)
        def _():
            for number in range(count):
                for copy in copies(pair - 3, number):
                    copy.wait_send()

    def load(self, pair):
        for order in range(2):
            self.pair_copy(pair * 2 + order).wait_recv()
        for copy in self.loads(pair):
            copy.start()

    def send_first(self, pair):
        for copy in self.loads(pair):
            copy.wait()
        self.after_sends(pair, self.first_copies, 2)
        slot, kept = pair % 3, pair % 2
        for order in range(2):

            units = jnp.zeros((8, 128), jnp.float32)
            for block in range(8):
                floor, line = block // 2, block % 2
                if order == 0:
                    mine = (order, floor, line, self.across)
                    away = (order, floor, line, 1 - self.across)
                else:
                    mine = (order, floor, self.along, line)
                    away = (order, floor, 1 - self.along, line)
                self.one[kept, order, block] = self.own[mine] + self.other[mine]
                coded, unit = encode(self.own[away] + self.other[away])
                self.b1_out[slot, order, block] = coded
                units = jnp.where(self.lane == block, unit, units)
            self.b1_unit_out[slot, order] = units
            for copy in self.first_copies(pair, order):
                copy.start()

    def send_second(self, pair):
        slot, kept = pair % 3, pair % 2
        self.after_sends(pair, self.second_copies, 2)
        for order in range(2):
            for copy in self.first_copies(pair, order):
                copy.wait_recv()
            tile = pair * 2 + order
            got = self.b1_unit_in[tile]
            keep = self.along if order == 0 else self.across

            units = jnp.zeros((8, 128), jnp.float32)
            for floor in range(4):
                stay, leave = floor * 2 + keep, floor * 2 + 1 - keep
                even, odd = got[:, 2 * floor : 2 * floor + 1], got[:, 2 * floor + 1 : 2 * floor + 2]
                self.two[kept, order, floor] = self.one[kept, order, stay] + decode(
                    self.b1_in[tile, stay], jnp.where(keep == 0, even, odd)
                )
                coded, unit = encode(
                    self.one[kept, order, leave] + decode(self.b1_in[tile, leave], jnp.where(keep == 0, odd, even))
                )
                self.b2_out[slot, order, floor] = coded
                units = jnp.where(self.lane == floor, unit, units)
            self.b2_unit_out[slot, order] = units
            for copy in self.second_copies(pair, order):
                copy.start()

    def send_tower(self, pair):
        slot, kept = pair % 3, pair % 2
        self.after_sends(pair, self.tower_copies, 3)
        for order in range(2):
            for copy in self.second_copies(pair, order):
                copy.wait_recv()

        for order in range(2):
            tile = pair * 2 + order
            got = self.b2_unit_in[tile]
            for floor in range(4):
                self.two[kept, order, floor] = self.two[kept, order, floor] + decode(
                    self.b2_in[tile, floor], got[:, floor : floor + 1]
                )
            self.three[kept, order] = self.two[kept, order, self.z]
        for j in range(3):
            units = jnp.zeros((8, 128), jnp.float32)
            for order in range(2):
                coded, unit = encode(self.two[kept, order, (self.z + j + 1) % 4])
                self.c_out[slot, j, order] = coded
                units = jnp.where(self.lane == order, unit, units)
            self.c_unit_out[slot, j] = units
        for j in range(3):
            for copy in self.tower_copies(pair, j):
                copy.start()

    def send_share(self, pair):
        slot = pair % 3
        self.after_sends(pair, self.share_copies, 3)
        for j in range(3):
            for copy in self.tower_copies(pair, j):
                copy.wait_recv()
        units = jnp.zeros((8, 128), jnp.float32)
        for order in range(2):
            tile = pair * 2 + order
            total = self.three[pair % 2, order]
            for j in range(3):
                total = total + decode(self.c_in[j, tile], self.c_unit_in[j, pair][:, order : order + 1])
            self.final[tile] = total
            coded, unit = encode(total)
            self.d_out[slot, order] = coded
            units = jnp.where(self.lane == order, unit, units)
        self.d_unit_out[slot] = units
        for j in range(3):
            for copy in self.share_copies(pair, j):
                copy.start()

    def tick(self, number):
        stages = (self.load, self.send_first, self.send_second, self.send_tower, self.send_share)
        for offset, stage_of in reversed(list(zip(self.offsets, stages))):
            turn_of = jnp.int32(number) - offset
            pair = turn_of
            fits = turn_of >= 0
            for first, count in self.gaps:
                pair = pair - jnp.minimum(jnp.maximum(turn_of - first + 1, 0), count)
                fits = jnp.logical_and(fits, jnp.logical_or(turn_of < first, turn_of >= first + count))
            fits = jnp.logical_and(fits, pair < self.pairs)

            @pl.when(fits)
            def _():
                stage_of(pair)

    def ticks(self, start, stop):
        def body(number, carry):
            self.tick(number)
            return carry

        lax.fori_loop(start, stop, body, 0)

    def collect(self, source_ref, pair_ref, parity_ref, owned_ref, stage):
        def arrive(pair, carry):
            for j in range(3):
                for copy in self.share_copies(pair, j):
                    copy.wait_recv()
            return carry

        lax.fori_loop(0, self.pairs, arrive, 0)
        for order in range(self.pairs * 2 - 4, self.pairs * 2):
            self.pair_copy(order).wait_send()
        width = self.final.shape[2]

        def step(slot, square):
            keep = owned_ref[slot] > 0
            tile = source_ref[slot]
            places_of = [self.seq] + [peer[1] for peer in self.side]
            for number, quarter in enumerate(places_of):
                if number == 0:
                    value = self.final[tile]
                else:
                    units = self.d_unit_in[number - 1, pair_ref[slot]]
                    unit = jnp.where(parity_ref[slot] > 0, units[:, 1:2], units[:, 0:1])
                    value = decode(self.d_in[number - 1, tile], unit)
                value = jnp.where(keep, value, jnp.zeros_like(value))
                stage[slot // 8, slot % 8 // 2, slot % 2, quarter // 2, quarter % 2] = value
                square = square + value * value
            return square

        square = lax.fori_loop(0, source_ref.shape[0], step, jnp.zeros((16, width), jnp.float32))
        folded = jnp.zeros((8, 128), jnp.float32)
        for r in range(2):
            for w in range(width // 128):
                folded = folded + square[8 * r : 8 * r + 8, 128 * w : 128 * w + 128]
        return folded

    def finish(self):
        for pair in range(self.pairs - 3, self.pairs):
            for order in range(2):
                for copy in self.first_copies(pair, order) + self.second_copies(pair, order):
                    copy.wait_send()
            for j in range(3):
                for copy in self.tower_copies(pair, j) + self.share_copies(pair, j):
                    copy.wait_send()


class Sums:
    def __init__(self, place, column, side, small, refs):
        self.dp, self.seq, _, _ = place
        self.column, self.side = column, side
        self.small = small
        self.small_dp, self.small_seq, self.square_dp, self.square_seq, self.sems = refs[31:]

    def copies(self, which):
        sends, recvs = self.sems[2 * which], self.sems[2 * which + 1]
        if which == 0:
            return [remote(self.small, self.small_dp.at[self.dp], sends.at[j], recvs.at[j], self.column[j]) for j in range(7)]
        if which == 1:
            spot = self.small_seq.at[self.seq]
            return [remote(spot, spot, sends.at[j], recvs.at[j], self.side[j]) for j in range(3)]
        if which == 2:
            spot = self.square_dp.at[self.dp]
            return [remote(spot, spot, sends.at[j], recvs.at[j], self.column[j]) for j in range(7)]
        spot = self.square_seq.at[self.seq]
        return [remote(spot, spot, sends.at[j], recvs.at[j], self.side[j]) for j in range(3)]

    def start(self, which):
        for copy in self.copies(which):
            copy.start()

    def arrive(self, which):
        for copy in self.copies(which):
            copy.wait_recv()

    def start_small(self):
        self.start(0)
        self.small_dp[self.dp] = self.small[...]

    def pass_small(self):
        self.arrive(0)
        total = self.small_dp[0]
        for j in range(1, 8):
            total = total + self.small_dp[j]
        self.small_seq[self.seq] = total
        self.start(1)

    def squares(self, folded):
        self.square_dp[self.dp] = folded
        self.start(2)
        self.arrive(1)
        small = (self.small_seq[0] + self.small_seq[1]) + (self.small_seq[2] + self.small_seq[3])
        self.arrive(2)
        total = self.square_dp[0]
        for j in range(1, 8):
            total = total + self.square_dp[j]
        self.square_seq[self.seq] = total
        self.start(3)
        self.arrive(3)
        return small, (self.square_seq[0] + self.square_seq[1]) + (self.square_seq[2] + self.square_seq[3])

    def finish(self):
        for which in range(4):
            for copy in self.copies(which):
                copy.wait_send()


GRAD_ORDER = (20, 21, 22, 23, 16, 17, 18, 19, 15, 12, 13, 14, 24, 8, 9, 10, 11, 4, 5, 6, 7, 3, 0, 1, 2, 25)


def step_kernel(
    micro_count, lengths_ref, owner_ref, step_ref, master_ref, chars_ref, targets_ref, segs_ref,
    gains_ref, gain_first_ref, gain_second_ref, first_far, second_far,
    own_far, other_far, master_out, first_out, second_out, low_out, gains_out, gain_first_out, gain_second_out,
    loss_out, norm_out,
    weights, qkv, logs, attended, after, leave, grad,
    seg_entry, seg_qkv, seg_logs, seg_attended, seg_after, seg_leave, seg_grad,
    turned, grad_inner, branch, turned_norm, key_sum, value_sum, head_grad, small_ref,
    ids_in, ids_row, ids_col, source_ref, pair_ref, parity_ref, owned_ref, stage, stage_sem, counts, count_send, count_recv, i_send, i_recv, g_send, g_recv, out_sem, m_sem,
    p_send, p_recv, z_send, z_recv, s_send, s_recv, d_send, d_recv, c_send, c_recv,
    reduce_refs,
):
    dp, seq, z, core = places()
    across, along = seq % 2, seq // 2
    length, width = leave.shape
    segments = seg_entry.shape[0]
    vocab = width // 2
    root_width = width ** (-0.5)
    groups = weights.shape[0] // 2
    sibling = (z * 2 + 1 - core, seq)
    beside = [along * 2 + 1 - across, (1 - along) * 2 + across]
    side = [seq_peer(seq, j) for j in (1, 2, 3)]
    column = [((dp + j) % 8, seq) for j in range(1, 8)]
    tower = [((z + j) % 4 * 2 + core, seq) for j in (1, 2, 3)]
    meet([(dp, peer) for peer in side] + column)

    all_ids = (chars_ref, targets_ref, segs_ref)

    def ids_copy(j, which):
        return remote(
            all_ids[which].at[side[j]], ids_in.at[which, seq], i_send.at[j, which], i_recv.at[j, which], (dp, side[j])
        )

    def part_of(which):
        return pl.ds(pl.multiple_of(which * width, width), width)

    def peer_copy(group, j):
        return remote(
            grad_inner.at[pl.ds(pl.multiple_of(group * 32, 32), 32), part_of(side[j])],
            grad_inner.at[pl.ds(pl.multiple_of(512 + group * 32, 32), 32), part_of(j)],
            p_send.at[j, group], p_recv.at[j, group], (dp, side[j]),
        )

    def tower_copy(group, j):
        spot = weights.at[pl.ds(group * 2, 2), z, core, seq]
        return remote(spot, spot, z_send.at[j, group], z_recv.at[j, group], tower[j])

    def side_copy(group, way):
        spot = weights.at[pl.ds(group * 2, 2), :, core, seq]
        return remote(spot, spot, s_send.at[way, group], s_recv.at[way, group], (dp, beside[way]))

    def corner_copy(group, way):
        spot = weights.at[group * 2 + way, :, core, beside[way]]
        return remote(spot, spot, d_send.at[way, group], d_recv.at[way, group], (dp, beside[1 - way]))

    def core_copy(group):
        spot = weights.at[pl.ds(group * 2, 2), :, core]
        return remote(spot, spot, c_send.at[group], c_recv.at[group], sibling)

    def offer(group):
        for j in (2, 0, 1):
            peer_copy(group, j).start()

    def combine(group):
        for j in range(3):
            peer_copy(group, j).wait_recv()
        for number in range(2):
            row = group * 32 + number * 16
            value = grad_inner[pl.ds(pl.multiple_of(row, 16), 16), part_of(seq)]
            for j in range(3):
                value = value + grad_inner[pl.ds(pl.multiple_of(512 + row, 16), 16), pl.ds(j * width, width)]
            weights[group * 2 + number, z, core, seq] = value
        for j in range(3):
            tower_copy(group, j).start()

    def widen(group):
        for j in range(3):
            tower_copy(group, j).wait_recv()
        for way in range(2):
            side_copy(group, way).start()

    def corner(group):
        for way in range(2):
            side_copy(group, way).wait_recv()
        for way in range(2):
            corner_copy(group, way).start()

    def share(group):
        for way in range(2):
            corner_copy(group, way).wait_recv()
        core_copy(group).start()

    stages = (offer, combine, widen, corner, share)

    def tick(number):
        for order, stage_of in enumerate(stages):
            group = number - LAG * order

            @pl.when(jnp.logical_and(group >= 0, group < groups))
            def _():
                stage_of(group)

    def ticks(start, stop):
        def body(number, carry):
            tick(number)
            return carry

        lax.fori_loop(start, stop, body, 0)

    def arrived(first, last):
        def body(group, carry):
            core_copy(group).wait_recv()
            return carry

        lax.fori_loop(first, last, body, 0)

    for which in range(3):
        ids_in[which, seq] = all_ids[which][seq]
        for j in range(3):
            ids_copy(j, which).start()

    held = master_ref.shape[0]

    def pick(place, carry):
        late = (place > 13).astype(jnp.int32)
        tile = jnp.where(place == 0, 25, jnp.where(place == 13, 24, place - 1 - late))
        slot = owner_ref[tile] - held * seq
        keep = jnp.logical_and(slot >= 0, slot < held)
        value = master_ref[jnp.minimum(jnp.maximum(slot, 0), held - 1)]
        value = jnp.where(keep, value, jnp.zeros_like(value)).astype(jnp.bfloat16)
        for quarter in range(4):
            grad_inner[pl.ds(pl.multiple_of(place * 16, 16), 16), quarter * width : quarter * width + width] = value[
                16 * quarter : 16 * quarter + 16
            ]
        return carry

    lax.fori_loop(0, groups * 2, pick, 0)
    ticks(0, START)

    def matrix(place):
        return weights[place].reshape(width, width)

    def matrix_half(which):
        return weights[0, 2 * which : 2 * which + 2].reshape(vocab, width)

    def count_copy(j):
        return remote(counts.at[dp], counts.at[dp], count_send.at[j], count_recv.at[j], column[j])

    def own_copy(order):
        return pltpu.make_async_copy(stage.at[order % 4, :, core], own_far.at[order], stage_sem.at[order % 2])

    def pair_copy(order):
        return remote(
            stage.at[order % 4, :, 1 - core], other_far.at[order], g_send.at[order % 4], g_recv.at[order], sibling
        )

    def put(order, half_of):
        @pl.when(jnp.int32(order) >= 4)
        def _():
            pair_copy(order - 4).wait_send()

        @pl.when(jnp.logical_and(jnp.int32(order) >= 1, jnp.int32(order) != 22))
        def _():
            own_copy(order - 1).wait()

        for half in range(2):
            value = half_of(pl.ds(256 * half, 256))
            stage[order % 4, 2 * half : 2 * half + 2] = value.reshape(2, 2, 2, 2, 16, width)
        own_copy(order).start()
        pair_copy(order).start()

    small_ref[...] = jnp.zeros_like(small_ref)
    for which in range(3):
        for j in range(3):
            ids_copy(j, which).wait_recv()
        for peer in range(4):
            ids_row[which : which + 1, 256 * peer : 256 * peer + 256] = ids_in[which, peer]
    for slot in range(held):
        zero = jnp.int32(0)
        source, pair, parity, owned = zero, zero, zero, zero
        for order, tile in enumerate(GRAD_ORDER):
            here = (owner_ref[tile] == held * seq + slot).astype(jnp.int32)
            source, pair, parity = source + here * order, pair + here * (order // 2), parity + here * (order % 2)
            owned = owned + here
        source_ref[slot] = jnp.minimum(source, 2 * groups - 1)
        pair_ref[slot] = jnp.minimum(pair, groups - 1)
        parity_ref[slot], owned_ref[slot] = parity, owned
    ids_row[3:8, :] = jnp.zeros((5, length), jnp.int32)
    ids_col[...] = ids_row[...].astype(jnp.float32).T
    length_one = lengths_ref[seq, 0]
    temps = (turned, grad_inner, branch, turned_norm, key_sum, value_sum)

    def hot_rows(rows, which, offset, count):
        ids = ids_col[rows, which : which + 1] + float(offset)
        lane = lax.broadcasted_iota(jnp.int32, (ROWS, count), 1).astype(jnp.float32)
        return (ids == lane).astype(jnp.bfloat16)

    def hot_turned(which, offset, count):
        ids = ids_row[which : which + 1, :] + offset
        line = lax.broadcasted_iota(jnp.int32, (count, length), 0)
        return (ids == line).astype(jnp.float32)

    arrived(0, 2)

    def embed(rows):
        return product(hot_rows(rows, 0, 0, vocab), matrix_half(0))

    char = Block(length, (13, 17, 21, 22), 1, 0, embed, qkv, logs, attended, after, leave)
    seg = Block(
        segments, (0, 4, 8, 9), 14, 2, lambda rows: seg_entry[rows, :],
        seg_qkv, seg_logs, seg_attended, seg_after, seg_leave,
    )
    tick(START)
    block_run(
        char,
        matrix,
        gains_ref,
        (
            lambda: tick(START + 1),
            lambda pair: tick(START + 2 + pair),
            lambda: arrived(2, 7),
            lambda number: tick(START + 6 + number),
        ),
    )
    ticks(START + 10, groups + LAG * (len(stages) - 1))

    def valid_rows(rows):
        line = lax.broadcasted_iota(jnp.int32, (ROWS, 1), 0) + rows.start
        return (line < length_one).astype(jnp.float32)

    def boundary(rows):
        low = leave[rows, :].astype(jnp.bfloat16)
        reach = jnp.tanh(product(low, matrix(13)))
        logit = jnp.sum(reach * gains_ref[5:6, :], axis=1, keepdims=True) * root_width
        return low, reach, 1.0 / (1.0 + jnp.exp(-logit))

    def soft_step(number, total):
        rows = pl.ds(pl.multiple_of(number * ROWS, ROWS), ROWS)
        return total + jnp.sum(valid_rows(rows) * boundary(rows)[2], axis=0, keepdims=True)

    soft_local = lax.fori_loop(0, length // ROWS, soft_step, jnp.zeros((1, 1), jnp.float32))
    line = lax.broadcasted_iota(jnp.int32, (8, 128), 0)
    length_float = length_one.astype(jnp.float32)
    counts[dp] = jnp.where(line == 0, soft_local, jnp.where(line == 1, length_float, 0.0))
    for j in range(7):
        count_copy(j).start()

    pool = hot_turned(2, 1, segments)
    amounts = jnp.sum(pool, axis=1, keepdims=True)
    divisor = jnp.maximum(amounts, 1.0)
    seg_entry[...] = product(pool.astype(jnp.bfloat16), leave[...].astype(jnp.bfloat16)) / divisor
    arrived(7, groups)
    block_run(seg, matrix, gains_ref, (lambda: None, lambda pair: None, lambda: None, lambda number: None))

    for j in range(7):
        count_copy(j).wait_recv()
    total = counts[0]
    for j in range(1, 8):
        total = total + counts[j]
    soft_count, count_all = total[0:1, 0:1], total[1:2, 0:1]

    def head(number, carry):
        ce, head_sum = carry
        rows = pl.ds(pl.multiple_of(number * ROWS, ROWS), ROWS)
        lift = hot_rows(rows, 2, 0, segments)
        merged = leave[rows, :] + product(lift, seg_leave[...].astype(jnp.bfloat16))
        scale = root_scale(merged)
        gain = gains_ref[4:5, :]
        final_low = (merged * scale * gain).astype(jnp.bfloat16)
        table = matrix_half(1)
        logits = product_nt(final_low, table)
        peak = jnp.max(logits, axis=1, keepdims=True)
        log_total = peak + jnp.log(jnp.sum(jnp.exp(logits - peak), axis=1, keepdims=True))
        target = hot_rows(rows, 1, 0, vocab).astype(jnp.float32)
        picked = jnp.sum(logits * target, axis=1, keepdims=True)
        valid = valid_rows(rows)
        ce = ce + jnp.sum(valid * (log_total - picked), axis=0, keepdims=True)
        share = valid / (micro_count * count_all)
        grad_logits = (jnp.exp(logits - log_total) - target) * share
        head_sum = head_sum + product(turn(grad_logits), final_low)
        back, gain_part = norm_back(merged, scale, gain, product(grad_logits.astype(jnp.bfloat16), table))
        small_ref[4:5, :] = small_ref[4:5, :] + gain_part
        grad[rows, :] = back
        return ce, head_sum

    ce_local, head_sum = lax.fori_loop(
        0, length // ROWS, head, (jnp.zeros((1, 1), jnp.float32), jnp.zeros((vocab, width), jnp.float32))
    )
    head_grad[...] = head_sum
    seg_grad[...] = exact_product(hot_turned(2, 0, segments).astype(jnp.bfloat16), grad[...])
    def sent(group, carry):
        for j in range(3):
            peer_copy(group, j).wait_send()
            tower_copy(group, j).wait_send()
        for way in range(2):
            side_copy(group, way).wait_send()
            corner_copy(group, way).wait_send()
        core_copy(group).wait_send()
        return carry

    lax.fori_loop(0, groups, sent, 0)
    reducer = Reducer(
        places(), own_far, other_far, pair_copy, [(dp, peer) for peer in beside], [(dp, peer) for peer in side], tower, reduce_refs
    )
    block_back(
        seg, seg_grad, matrix, gains_ref, small_ref, temps, put,
        (lambda part: None, lambda part: reducer.tick(part), lambda pair: None, lambda: None),
    )

    seg_grad[...] = seg_grad[...] / divisor

    count_rest = count_all - soft_count
    slope = (digamma(soft_count + 1.0) - digamma(count_rest + 1.0) + LOG_ODDS) / (count_all * micro_count)

    def join(rows):
        low, reach, chance = boundary(rows)
        logit = valid_rows(rows) * slope * chance * (1.0 - chance)
        gain = gains_ref[5:6, :]
        small_ref[5:6, :] = small_ref[5:6, :] + jnp.sum(logit * reach, axis=0, keepdims=True) * root_width
        pre = (logit * gain * root_width * (1.0 - reach * reach)).astype(jnp.bfloat16)
        branch[rows, :] = pre
        turned[:, rows] = turn(low)
        spread = exact_product(hot_rows(rows, 2, 1, segments), seg_grad[...])
        grad[rows, :] = (grad[rows, :] + spread) + product_nt(pre, matrix(13))

    each_block(length, join)
    put(12, lambda half: product(turned[half, :], branch[...]))
    block_back(
        char, grad, matrix, gains_ref, small_ref, temps, put,
        (
            lambda part: reducer.tick(4 + part),
            lambda part: None,
            lambda pair: reducer.ticks(8 + 2 * pair, 10 + 2 * pair),
            lambda: own_copy(21).wait(),
        ),
    )
    embed_grad = exact_product(hot_turned(0, 0, vocab).astype(jnp.bfloat16), grad[...])
    put(25, lambda half: embed_grad if half.start == 0 else head_grad[...])
    own_copy(25).wait()

    lane = lax.broadcasted_iota(jnp.int32, (1, width), 1)
    small_ref[6:7, :] = jnp.where(
        lane == seq,
        ce_local,
        jnp.where(lane == seq + 8, soft_local, jnp.where(lane == seq + 16, length_float, 0.0)),
    )
    for j in range(7):
        count_copy(j).wait_send()
    for which in range(3):
        for j in range(3):
            ids_copy(j, which).wait_send()
    moments = [
        pltpu.make_async_copy(first_far, leave.at[pl.ds(0, held * 64)], m_sem.at[0]),
        pltpu.make_async_copy(second_far, after.at[pl.ds(0, held * 64)], m_sem.at[1]),
    ]
    for copy in moments:
        copy.start()
    sums = Sums(places(), column, [(dp, peer) for peer in side], small_ref, reduce_refs)
    sums.start_small()
    reducer.ticks(16, reducer.last_tick)
    sums.pass_small()
    square = reducer.collect(source_ref, pair_ref, parity_ref, owned_ref, stage)
    for copy in moments:
        copy.wait()
    small_sum, square_sum = sums.squares(square)
    gain_sum = small_sum[0:6, :]
    grad_norm = jnp.sqrt(total_of(square_sum) + total_of(gain_sum * gain_sum))
    clip = jnp.minimum(1.0, CLIP_NORM / (grad_norm + 1e-06))
    steps = jnp.full((1, 1), step_ref[0], jnp.int32).astype(jnp.float32)
    corrections = [1.0 / (1.0 - jnp.exp(steps * math.log(beta))) for beta in (BETA_ONE, BETA_TWO)]

    def renew(param, moment_a, moment_b, grad_in, rate, decay):
        new_first = BETA_ONE * moment_a + (1.0 - BETA_ONE) * grad_in
        new_second = BETA_TWO * moment_b + (1.0 - BETA_TWO) * grad_in * grad_in
        move = (new_first * corrections[0]) / (jnp.sqrt(new_second * corrections[1]) + ADAM_EPS)
        return param - rate * (move + decay * param), new_first, new_second

    def leaving(slot):
        rows = pl.ds(pl.multiple_of(slot * 64, 64), 64)
        return [
            pltpu.make_async_copy(source.at[rows], target.at[rows], out_sem.at[number, slot])
            for number, (source, target) in enumerate(
                ((grad, master_out), (leave, first_out), (after, second_out), (attended, low_out))
            )
        ]

    def update(slot, carry):
        rows = pl.ds(pl.multiple_of(slot * 64, 64), 64)
        param, moment_a, moment_b = master_ref[slot], leave[rows, :], after[rows, :]
        reduced = stage[slot // 8, slot % 8 // 2, slot % 2].reshape(64, width)
        new_param, new_first, new_second = renew(
            param, moment_a, moment_b, reduced * clip, RATE_TILES, WEIGHT_DECAY
        )
        keep = owned_ref[slot] > 0
        new_param = jnp.where(keep, new_param, param)
        grad[rows, :] = new_param
        leave[rows, :] = jnp.where(keep, new_first, moment_a)
        after[rows, :] = jnp.where(keep, new_second, moment_b)
        attended[rows, :] = new_param.astype(jnp.bfloat16)
        for copy in leaving(slot):
            copy.start()
        return carry

    lax.fori_loop(0, held, update, 0)
    gains_out[...], gain_first_out[...], gain_second_out[...] = renew(
        gains_ref[...], gain_first_ref[...], gain_second_ref[...], gain_sum * clip, RATE_GAINS, 0.0
    )
    loss = jnp.zeros((1, 1), jnp.float32)
    row = small_sum[6:7, :]
    for micro in range(micro_count):
        entropy, soft, count = (total_of(jnp.where(lane == micro + 8 * part, row, 0.0)) for part in range(3))
        prior = -(
            log_gamma(count + 1.0)
            - log_gamma(soft + 1.0)
            - log_gamma(count - soft + 1.0)
            + soft * math.log(PRIOR_RATE)
            + (count - soft) * math.log(1.0 - PRIOR_RATE)
        )
        loss = loss + (entropy + prior) / count
    loss_out[0] = jnp.sum(loss) / micro_count
    norm_out[0] = jnp.sum(grad_norm)
    sums.finish()
    reducer.finish()

    def left(slot, carry):
        for copy in leaving(slot):
            copy.wait()
        return carry

    lax.fori_loop(0, held, left, 0)


def step_call(char_ids, targets, seg_ids, lengths, owner_slot, step_count, master, first, second, *gains):
    held, rows, width = master.shape
    tile_count = owner_slot.shape[0]
    micro_count = char_ids.shape[0]
    seq_count, dp_count = lax.axis_size("seq"), lax.axis_size("dp")
    groups = tile_count // 2
    length = seq_count * char_ids.shape[2]
    segments = SEG_DEV * seq_count
    dma = pltpu.SemaphoreType.DMA
    vmem = pl.BlockSpec(memory_space=pltpu.VMEM)
    smem = pl.BlockSpec(memory_space=pltpu.SMEM)
    hbm = pl.BlockSpec(memory_space=pl.ANY)

    def full(*shape):
        return pltpu.VMEM(shape, jnp.float32)

    def half(*shape):
        return pltpu.VMEM(shape, jnp.bfloat16)

    def codes(*shape):
        return pltpu.VMEM(shape + (16, width), jnp.int16)

    def kept(count):
        return [
            half(count, 3 * width), full(4, 2, count), half(count, width), full(count, width),
            full(count, width), full(count, width),
        ]

    reduce_refs = [
        full(2, 4, 2, 2, 16, width), full(2, 4, 2, 2, 16, width),
        full(2, 2, 8, 16, width), full(2, 2, 4, 16, width), full(2, 2, 16, width), full(tile_count, 16, width),
        codes(3, 2, 8), codes(tile_count, 8), codes(3, 2, 4), codes(tile_count, 4),
        codes(3, 3, 2), codes(3, tile_count), codes(3, 2), codes(3, tile_count),
        full(3, 2, 8, 128), full(tile_count, 8, 128), full(3, 2, 8, 128), full(tile_count, 8, 128),
        full(3, 3, 8, 128), full(3, groups, 8, 128), full(3, 8, 128), full(3, groups, 8, 128),
        dma((2,)), dma((2, 3, 2)), dma((2, tile_count)), dma((2, 3, 2)), dma((2, tile_count)),
        dma((2, 3, 3)), dma((2, 3, groups)), dma((2, 3, 3)), dma((2, 3, groups)),
        full(dp_count, 8, width), full(seq_count, 8, width), full(dp_count, 8, 128), full(seq_count, 8, 128),
        [dma((7,)), dma((7,)), dma((3,)), dma((3,)), dma((7,)), dma((7,)), dma((3,)), dma((3,))],
    ]
    flat = jax.ShapeDtypeStruct((held * rows, width), jnp.float32)
    gain_shape = jax.ShapeDtypeStruct(gains[0].shape, jnp.float32)
    one = jax.ShapeDtypeStruct((1,), jnp.float32)
    far = jax.ShapeDtypeStruct((tile_count, 4, 2, 2, 16, width), jnp.float32)
    results = pl.pallas_call(
        functools.partial(step_kernel, micro_count),
        out_shape=(
            far, far, flat, flat, flat, jax.ShapeDtypeStruct(flat.shape, jnp.bfloat16),
            gain_shape, gain_shape, gain_shape, one, one,
        ),
        in_specs=[smem] * 3 + [vmem] * 7 + [hbm] * 2,
        out_specs=(hbm,) * 6 + (vmem,) * 3 + (smem,) * 2,
        scratch_shapes=[half(tile_count, 4, 2, 4, 16, width)]
        + kept(length)
        + [full(segments, width)]
        + kept(segments)
        + [
            half(width, length), half(length, 4 * width), half(length, width), half(width, length),
            full(length, 128), full(length, 128), full(width // 2, width), full(8, width),
            pltpu.VMEM((3, 4, 1, length // 4), jnp.int32), pltpu.VMEM((8, length), jnp.int32), full(length, 8),
            pltpu.SMEM((held,), jnp.int32), pltpu.SMEM((held,), jnp.int32), pltpu.SMEM((held,), jnp.int32), pltpu.SMEM((held,), jnp.int32), full(4, 4, 2, 2, 2, 16, width), dma((2,)),
            full(dp_count, 8, 128), dma((7,)), dma((7,)), dma((3, 3)), dma((3, 3)),
            dma((4,)), dma((tile_count,)), dma((4, held)), dma((2,)),
            dma((3, groups)), dma((3, groups)), dma((3, groups)), dma((3, groups)),
            dma((2, groups)), dma((2, groups)), dma((2, groups)), dma((2, groups)),
            dma((groups,)), dma((groups,)), reduce_refs,
        ],
        name="step",
        compiler_params=pltpu.CompilerParams(
            collective_id=2, has_side_effects=True, vmem_limit_bytes=STEP_VMEM
        ),
    )(
        lengths, owner_slot, step_count, master, char_ids, targets, seg_ids, *gains,
        first.reshape(flat.shape), second.reshape(flat.shape),
    )
    master_new, first_new, second_new, low_new = (value.reshape(master.shape) for value in results[2:6])
    return (results[9], results[10], master_new, first_new, second_new, low_new) + tuple(results[6:9])


def body(
    char_ids,
    targets,
    seg_ids,
    lengths,
    owner_slot,
    step_count,
    master,
    tile_first,
    tile_second,
    gain_rows,
    gain_first,
    gain_second,
):
    micro_count = char_ids.shape[0]
    model_width = master.shape[2]
    slot_count = master.shape[0] * lax.axis_size("seq")
    if (micro_count, lax.axis_size("seq"), lax.axis_size("dp")) == (4, 4, 8):
        return step_call(
            char_ids, targets, seg_ids, lengths, owner_slot, step_count, master, tile_first, tile_second,
            gain_rows, gain_first, gain_second,
        )
    tile_total = jnp.zeros((owner_slot.shape[0], model_width, model_width), jnp.float32)
    gain_total = jnp.zeros_like(gain_rows)
    loss_total = jnp.zeros((), jnp.float32)
    for micro in range(micro_count):
        tiles = gather_tiles(master, owner_slot)
        tile_part, gain_part, loss_part = micro_step(
            tiles,
            gain_rows,
            char_ids[micro, 0],
            targets[micro, 0],
            seg_ids[micro, 0],
            lengths[micro, 0],
            micro_count,
        )
        tile_total = tile_total + tile_part
        gain_total = gain_total + gain_part
        loss_total = loss_total + loss_part
    shard_total = reduce_tiles(tile_total, owner_slot, slot_count)
    gain_sum, square_sum = lax.psum((gain_total, jnp.sum(shard_total * shard_total)), ("dp", "seq"))
    grad_norm = jnp.sqrt(square_sum + jnp.sum(gain_sum * gain_sum))
    clip_factor = jnp.minimum(1.0, CLIP_NORM / (grad_norm + 1e-06))
    step_float = step_count[0].astype(jnp.float32)
    local_ids = lax.axis_index("seq") * master.shape[0] + jnp.arange(master.shape[0])
    owned = jnp.any(local_ids[:, None] == owner_slot[None, :], axis=1)[:, None, None]
    new_tiles, new_first, new_second = adam_step(
        master,
        tile_first,
        tile_second,
        shard_total * clip_factor,
        RATE_TILES,
        WEIGHT_DECAY,
        step_float,
    )
    master_new = jnp.where(owned, new_tiles, master)
    first_new = jnp.where(owned, new_first, tile_first)
    second_new = jnp.where(owned, new_second, tile_second)
    gains_new, gain_first_new, gain_second_new = adam_step(
        gain_rows, gain_first, gain_second, gain_sum * clip_factor, RATE_GAINS, 0.0, step_float
    )
    return (
        loss_total.reshape(1),
        grad_norm.reshape(1),
        master_new,
        first_new,
        second_new,
        master_new.astype(jnp.bfloat16),
        gains_new,
        gain_first_new,
        gain_second_new,
    )


def solution(mesh):
    return jax.shard_map(
        body,
        mesh=mesh,
        in_specs=(
            P(None, "dp", "seq"),
            P(None, "dp", "seq"),
            P(None, "dp", "seq"),
            P(None, "dp"),
            P(),
            P(),
            P("seq", "dp", None),
            P("seq", "dp", None),
            P("seq", "dp", None),
            P(),
            P(),
            P(),
        ),
        out_specs=(
            P(),
            P(),
            P("seq", "dp", None),
            P("seq", "dp", None),
            P("seq", "dp", None),
            P("seq", "dp", None),
            P(),
            P(),
            P(),
        ),
        check_vma=False,
    )
```

```python
import functools
import math

import jax
import jax.numpy as jnp
from jax import lax
from jax.experimental import pallas as pl
from jax.experimental.pallas import tpu as pltpu
from jax.sharding import PartitionSpec as P

HEADS = 8
SEG_DEV = 64


BETA_ONE = 0.9
BETA_TWO = 0.95
ADAM_EPS = 1e-08
WEIGHT_DECAY = 0.1
RATE_TILES = 0.03
RATE_GAINS = 0.2
CLIP_NORM = 0.05
PRIOR_RATE = 0.25
NORM_EPS = 1e-06
MASKED = -1e30
LOG_ODDS = math.log(1.0 - PRIOR_RATE) - math.log(PRIOR_RATE)


def product(left, right):
    return jnp.dot(left, right, preferred_element_type=jnp.float32)


def product_tn(left, right):
    return lax.dot_general(
        left, right, (((0,), (0,)), ((), ())), preferred_element_type=jnp.float32
    )


def product_nt(left, right):
    return lax.dot_general(
        left, right, (((1,), (1,)), ((), ())), preferred_element_type=jnp.float32
    )


def exact_tn(left, right):
    return lax.dot_general(
        left,
        right,
        (((0,), (0,)), ((), ())),
        precision=lax.Precision.HIGHEST,
        preferred_element_type=jnp.float32,
    )


def rms_norm(values, gain):
    return values * lax.rsqrt(jnp.mean(values * values, axis=-1, keepdims=True) + NORM_EPS) * gain


def split_heads(tensor):
    return tensor.reshape(tensor.shape[0], HEADS, tensor.shape[1] // HEADS).transpose(1, 0, 2)


def join_heads(tensor):
    return tensor.transpose(1, 0, 2).reshape(tensor.shape[1], tensor.shape[0] * tensor.shape[2])


def block_weights(tiles):
    w_qkv = jnp.concatenate([tiles[0], tiles[1], tiles[2]], axis=1)
    w_up = jnp.concatenate([tiles[4], tiles[5], tiles[6], tiles[7]], axis=1)
    w_down = jnp.concatenate([tiles[8], tiles[9], tiles[10], tiles[11]], axis=0)
    return (w_qkv, w_up, w_down)


def causal_mask(row_count, key_count):
    first_row = lax.axis_index("seq") * row_count
    return (first_row + jnp.arange(row_count))[:, None] >= jnp.arange(key_count)[None, :]


def block_forward(hidden_in, tiles, gain_attn, gain_ffn, segment):
    row_count, model_width = hidden_in.shape
    w_qkv, w_up, w_down = block_weights(tiles)
    normed = rms_norm(hidden_in, gain_attn).astype(jnp.bfloat16)
    qkv_low = product(normed, w_qkv).astype(jnp.bfloat16)
    if segment:
        gathered = lax.all_gather(qkv_low[:, model_width:], "seq", axis=0, tiled=True)
    else:
        gathered = lax.all_gather(qkv_low[:, model_width:], "seq", axis=0, tiled=True)
    allowed = causal_mask(row_count, gathered.shape[0])
    factor = (model_width // HEADS) ** (-0.5)

    def head_forward(triple):
        q_head, k_head, v_head = triple
        scores = jnp.where(allowed, product_nt(q_head, k_head) * factor, MASKED)
        peak = jnp.max(scores, axis=1, keepdims=True)
        log_total = peak + jnp.log(jnp.sum(jnp.exp(scores - peak), axis=1, keepdims=True))
        weights = jnp.exp(scores - log_total).astype(jnp.bfloat16)
        return (product(weights, v_head), log_total[:, 0])

    head_out, log_totals = lax.map(
        head_forward,
        (
            split_heads(qkv_low[:, :model_width]),
            split_heads(gathered[:, :model_width]),
            split_heads(gathered[:, model_width:]),
        ),
    )
    attended = join_heads(head_out).astype(jnp.bfloat16)
    after_attn = hidden_in + product(attended, tiles[3])
    inner = product(rms_norm(after_attn, gain_ffn).astype(jnp.bfloat16), w_up)
    block_out = after_attn + product(jax.nn.gelu(inner).astype(jnp.bfloat16), w_down)
    return (block_out, (hidden_in, qkv_low, gathered, log_totals, attended, after_attn, inner))


def block_backward(grad_out, saved, tiles, gain_attn, gain_ffn, segment):
    hidden_in, qkv_low, gathered, log_totals, attended, after_attn, inner = saved
    row_count, model_width = hidden_in.shape
    w_qkv, w_up, w_down = block_weights(tiles)
    grad_ffn = grad_out.astype(jnp.bfloat16)
    activated, gelu_pull = jax.vjp(jax.nn.gelu, inner)
    grad_down = product_tn(activated.astype(jnp.bfloat16), grad_ffn)
    grad_inner = gelu_pull(product_nt(grad_ffn, w_down))[0].astype(jnp.bfloat16)
    normed_ffn, ffn_pull = jax.vjp(rms_norm, after_attn, gain_ffn)
    grad_up = product_tn(normed_ffn.astype(jnp.bfloat16), grad_inner)
    grad_normed_in, grad_gain_ffn = ffn_pull(product_nt(grad_inner, w_up))
    grad_after = grad_out + grad_normed_in
    grad_branch = grad_after.astype(jnp.bfloat16)
    grad_wout = product_tn(attended, grad_branch)
    grad_attended = product_nt(grad_branch, tiles[3]).astype(jnp.bfloat16)
    allowed = causal_mask(row_count, gathered.shape[0])
    factor = (model_width // HEADS) ** (-0.5)

    def head_backward(bundle):
        q_head, k_head, v_head, upstream, log_head = bundle
        scores = jnp.where(allowed, product_nt(q_head, k_head) * factor, MASKED)
        weights = jnp.exp(scores - log_head[:, None])
        grad_values = product_tn(weights.astype(jnp.bfloat16), upstream)
        grad_weights = product_nt(upstream, v_head)
        inner_sum = jnp.sum(weights * grad_weights, axis=1, keepdims=True)
        grad_scores = (weights * (grad_weights - inner_sum)).astype(jnp.bfloat16)
        return (
            product(grad_scores, k_head) * factor,
            product_tn(grad_scores, q_head) * factor,
            grad_values,
        )

    grad_query, grad_keys, grad_values = lax.map(
        head_backward,
        (
            split_heads(qkv_low[:, :model_width]),
            split_heads(gathered[:, :model_width]),
            split_heads(gathered[:, model_width:]),
            split_heads(grad_attended),
            log_totals,
        ),
    )
    grad_kv_all = jnp.concatenate([join_heads(grad_keys), join_heads(grad_values)], axis=1)
    if segment:
        grad_kv = lax.psum_scatter(grad_kv_all, "seq", scatter_dimension=0, tiled=True)
    else:
        grad_kv = lax.psum_scatter(grad_kv_all, "seq", scatter_dimension=0, tiled=True)
    grad_qkv = jnp.concatenate([join_heads(grad_query), grad_kv], axis=1).astype(jnp.bfloat16)
    normed_attn, attn_pull = jax.vjp(rms_norm, hidden_in, gain_attn)
    grad_wqkv = product_tn(normed_attn.astype(jnp.bfloat16), grad_qkv)
    grad_normed_x, grad_gain_attn = attn_pull(product_nt(grad_qkv, w_qkv))
    grad_in = grad_after + grad_normed_x
    pieces = [
        grad_wqkv[:, part_index * model_width : (part_index + 1) * model_width]
        for part_index in range(3)
    ]
    pieces = pieces + [grad_wout]
    pieces = pieces + [
        grad_up[:, part_index * model_width : (part_index + 1) * model_width]
        for part_index in range(4)
    ]
    pieces = pieces + [
        grad_down[part_index * model_width : (part_index + 1) * model_width]
        for part_index in range(4)
    ]
    return (grad_in, jnp.stack(pieces), grad_gain_attn, grad_gain_ffn)


def micro_step(tiles, gain_rows, chars_row, target_row, segment_row, length_one, micro_count):
    char_count = chars_row.shape[0]
    model_width = tiles.shape[2]
    vocab_size = model_width // 2
    seq_count = lax.axis_size("seq")
    seg_total = SEG_DEV * seq_count
    position = lax.axis_index("seq") * char_count + jnp.arange(char_count)
    is_valid = (position < length_one).astype(jnp.float32)
    vocab_iota = jnp.arange(vocab_size)
    char_hot = chars_row[:, None] == vocab_iota[None, :]
    embed_low = tiles[25, :vocab_size]
    head_low = tiles[25, vocab_size:]
    start_hidden = product(char_hot.astype(jnp.bfloat16), embed_low)
    char_out, char_saved = block_forward(
        start_hidden, tiles[0:12], gain_rows[0], gain_rows[1], False
    )
    char_low = char_out.astype(jnp.bfloat16)
    boundary_hidden = jnp.tanh(product(char_low, tiles[24]))
    root_width = model_width ** (-0.5)
    boundary_prob = jax.nn.sigmoid(jnp.sum(boundary_hidden * gain_rows[5], axis=1) * root_width)
    slot_iota = jnp.arange(seg_total)
    pool_hot = segment_row[None, :] + 1 == slot_iota[:, None]
    lift_hot = segment_row[:, None] == slot_iota[None, :]
    part_sums = product(pool_hot.astype(jnp.bfloat16), char_low).reshape(
        seq_count, SEG_DEV, model_width
    )
    side_info = jnp.stack(
        [
            jnp.sum(pool_hot.astype(jnp.float32), axis=1),
            jnp.any(lift_hot, axis=0).astype(jnp.float32),
        ],
        axis=0,
    )
    side_info = side_info.reshape(2, seq_count, SEG_DEV).transpose(1, 0, 2)
    sums_in, side_in = (
        lax.all_to_all(part_sums, "seq", split_axis=0, concat_axis=0, tiled=True),
        lax.all_to_all(side_info, "seq", split_axis=0, concat_axis=0, tiled=True),
    )
    row_counts = jnp.sum(side_in[:, 0, :], axis=0)
    divisor = jnp.maximum(row_counts, 1.0)[:, None]
    pooled = jnp.sum(sums_in, axis=0) / divisor
    seg_out, seg_saved = block_forward(pooled, tiles[12:24], gain_rows[2], gain_rows[3], True)
    outgoing = side_in[:, 1, :, None].astype(jnp.bfloat16) * seg_out.astype(jnp.bfloat16)[None]
    returned = lax.all_to_all(outgoing, "seq", split_axis=0, concat_axis=0, tiled=True)
    merged = char_out + product(
        lift_hot.astype(jnp.bfloat16), returned.reshape(seg_total, model_width)
    )
    final_norm, final_pull = jax.vjp(rms_norm, merged, gain_rows[4])
    final_low = final_norm.astype(jnp.bfloat16)
    logits = product_nt(final_low, head_low)
    peak = jnp.max(logits, axis=1, keepdims=True)
    log_total = peak[:, 0] + jnp.log(jnp.sum(jnp.exp(logits - peak), axis=1))
    target_hot = (target_row[:, None] == vocab_iota[None, :]).astype(jnp.float32)
    picked = jnp.sum(logits * target_hot, axis=1)
    ce_local = jnp.sum(is_valid * (log_total - picked))
    ce_all, soft_count, count_all = lax.psum(
        (ce_local, jnp.sum(is_valid * boundary_prob), jnp.sum(is_valid)), ("dp", "seq")
    )
    weight_ce = is_valid / (micro_count * count_all)
    grad_logits = ((jnp.exp(logits - log_total[:, None]) - target_hot) * weight_ce[:, None]).astype(
        jnp.bfloat16
    )
    grad_head = product_tn(grad_logits, final_low)
    grad_merged, grad_gain_final = final_pull(product(grad_logits, head_low))
    grad_rows = exact_tn(lift_hot.astype(jnp.float32), grad_merged).reshape(
        seq_count, SEG_DEV, model_width
    )
    grad_seg = jnp.sum(
        lax.all_to_all(grad_rows, "seq", split_axis=0, concat_axis=0, tiled=True), axis=0
    )
    grad_pooled, seg_tiles, grad_gain_two, grad_gain_three = block_backward(
        grad_seg, seg_saved, tiles[12:24], gain_rows[2], gain_rows[3], True
    )
    grad_sums = (side_in[:, 0, :, None] > 0).astype(jnp.float32) * (grad_pooled / divisor)[None]
    grad_back = lax.all_to_all(grad_sums, "seq", split_axis=0, concat_axis=0, tiled=True).reshape(
        seg_total, model_width
    )
    grad_char = grad_merged + exact_tn(pool_hot.astype(jnp.float32), grad_back)
    prior_slope = (
        lax.digamma(soft_count + 1.0)
        - lax.digamma(count_all - soft_count + 1.0)
        - jnp.log(PRIOR_RATE)
        + jnp.log(1.0 - PRIOR_RATE)
    ) / (count_all * micro_count)
    grad_boundary_logit = is_valid * prior_slope * boundary_prob * (1.0 - boundary_prob)
    grad_gain_boundary = (
        jnp.sum(grad_boundary_logit[:, None] * boundary_hidden, axis=0) * root_width
    )
    grad_pre = (
        grad_boundary_logit[:, None]
        * gain_rows[5][None, :]
        * root_width
        * (1.0 - boundary_hidden * boundary_hidden)
    ).astype(jnp.bfloat16)
    grad_boundary = product_tn(char_low, grad_pre)
    grad_char = grad_char + product_nt(grad_pre, tiles[24])
    grad_start, char_tiles, grad_gain_zero, grad_gain_one = block_backward(
        grad_char, char_saved, tiles[0:12], gain_rows[0], gain_rows[1], False
    )
    grad_embed = exact_tn(char_hot.astype(jnp.float32), grad_start)
    tile_grads = jnp.concatenate(
        [
            char_tiles,
            seg_tiles,
            grad_boundary[None],
            jnp.concatenate([grad_embed, grad_head], axis=0)[None],
        ],
        axis=0,
    )
    gain_grads = jnp.stack(
        [
            grad_gain_zero,
            grad_gain_one,
            grad_gain_two,
            grad_gain_three,
            grad_gain_final,
            grad_gain_boundary,
        ]
    )
    prior_term = (
        -(
            lax.lgamma(count_all + 1.0)
            - lax.lgamma(soft_count + 1.0)
            - lax.lgamma(count_all - soft_count + 1.0)
            + soft_count * jnp.log(PRIOR_RATE)
            + (count_all - soft_count) * jnp.log(1.0 - PRIOR_RATE)
        )
        / count_all
    )
    return (tile_grads, gain_grads, (ce_all / count_all + prior_term) / micro_count)


def gather_tiles(master, owner_slot):
    shard_low = master.astype(jnp.bfloat16)
    full_rows = lax.all_gather(shard_low, "dp", axis=1, tiled=True)
    all_slots = lax.all_gather(full_rows, "seq", axis=0, tiled=True)
    return jnp.take(all_slots, owner_slot, axis=0)


def reduce_tiles(tile_grads, owner_slot, slot_count):
    placed = (
        jnp.zeros((slot_count,) + tile_grads.shape[1:], jnp.float32).at[owner_slot].set(tile_grads)
    )
    per_owner = lax.psum_scatter(placed, "seq", scatter_dimension=0, tiled=True)
    return lax.psum_scatter(per_owner, "dp", scatter_dimension=1, tiled=True)


def adam_step(param, moment_a, moment_b, grad_in, rate, decay, step_float):
    new_first = BETA_ONE * moment_a + (1.0 - BETA_ONE) * grad_in
    new_second = BETA_TWO * moment_b + (1.0 - BETA_TWO) * grad_in * grad_in
    first_hat = new_first / (1.0 - BETA_ONE**step_float)
    second_hat = new_second / (1.0 - BETA_TWO**step_float)
    updated = param - rate * (first_hat / (jnp.sqrt(second_hat) + ADAM_EPS) + decay * param)
    return (updated, new_first, new_second)


MESH = pl.DeviceIdType.MESH
VMEM_LIMIT = 60 * 1024 * 1024
STEP_VMEM = 66_900_000


def remote(src, dst, send_sem, recv_sem, peer):
    return pltpu.make_async_remote_copy(
        src_ref=src, dst_ref=dst, send_sem=send_sem, recv_sem=recv_sem, device_id=peer, device_id_type=MESH
    )


def places():
    dp = lax.axis_index("dp")
    seq = lax.axis_index("seq")
    return dp, seq, dp // 2, dp % 2


def seq_peer(seq, step):
    return ((seq // 2 + step // 2) % 2) * 2 + (seq % 2 + step % 2) % 2


def meet(peers):
    barrier = pltpu.get_barrier_semaphore()
    for peer in peers:
        pl.semaphore_signal(barrier, inc=1, device_id=peer, device_id_type=MESH)
    pl.semaphore_wait(barrier, len(peers))


CODE_TOP = 32000.0
ROUNDER = 12582912.0


def encode(value):
    upper, lower = value[0:8, :], value[8:16, :]
    size = jnp.maximum(jnp.abs(upper), jnp.abs(lower))
    most = jnp.maximum(jnp.max(size, axis=1, keepdims=True), 1e-30)
    ratio = CODE_TOP / most
    coded = jnp.concatenate([upper * ratio, lower * ratio], axis=0)
    coded = ((coded + ROUNDER) - ROUNDER).astype(jnp.int32).astype(jnp.int16)
    return coded, most * (1.0 / CODE_TOP)


def decode(coded, unit):
    value = coded.astype(jnp.int32).astype(jnp.float32)
    return jnp.concatenate([value[0:8, :] * unit, value[8:16, :] * unit], axis=0)


def head_mask(shape, head):
    lane = lax.broadcasted_iota(jnp.int32, shape, 1)
    return (lane >= 64) if head else (lane < 64)


def scores_t(k_pair, q_head, first_row):
    scores = product_nt(k_pair, q_head)
    count, queries = scores.shape
    key = lax.broadcasted_iota(jnp.int32, (queries, queries), 0)
    query = lax.broadcasted_iota(jnp.int32, (queries, queries), 1)
    own = jnp.where(key <= query, scores[first_row:], MASKED)
    return own if first_row == 0 else jnp.concatenate([scores[:first_row], own], axis=0)


ROWS = 256
LAG = 2
START = 8


def split_three(value):
    high = value.astype(jnp.bfloat16)
    rest = value - high.astype(jnp.float32)
    middle = rest.astype(jnp.bfloat16)
    return high, middle, (rest - middle.astype(jnp.float32)).astype(jnp.bfloat16)


def exact_product(hot, value):
    high, middle, low = split_three(value)
    return (product(hot, low) + product(hot, middle)) + product(hot, high)


def turn(value):
    return value.astype(jnp.float32).T.astype(jnp.bfloat16)


def root_scale(value):
    return lax.rsqrt(jnp.mean(value * value, axis=-1, keepdims=True) + NORM_EPS)


def norm_back(value, scale, gain, grad):
    unit = value * scale
    weighted = grad * gain
    inner = jnp.mean(weighted * unit, axis=-1, keepdims=True)
    return scale * (weighted - unit * inner), jnp.sum(grad * unit, axis=0, keepdims=True)


def gelu_both(value):
    root = 0.7978845608028654
    square = value * value
    reach = jnp.tanh(root * value * (1.0 + 0.044715 * square))
    part = 0.5 * (1.0 + reach)
    slope = part + value * (0.5 * (1.0 - reach * reach)) * (root * (1.0 + 3.0 * 0.044715 * square))
    return value * part, slope


def digamma(value):
    moved = value + 8.0
    inverse = 1.0 / moved
    square = inverse * inverse
    series = square * (1.0 / 12.0 - square * (1.0 / 120.0 - square * (1.0 / 252.0)))
    total = jnp.log(moved) - 0.5 * inverse - series
    for number in range(8):
        total = total - 1.0 / (value + float(number))
    return total


def log_gamma(value):
    moved = value + 8.0
    inverse = 1.0 / moved
    square = inverse * inverse
    series = inverse * (1.0 / 12.0 - square * (1.0 / 360.0 - square * (1.0 / 1260.0)))
    gone = value
    for number in range(1, 8):
        gone = gone * (value + float(number))
    return ((moved - 0.5) * jnp.log(moved) - moved) + (0.9189385332046727 + series) - jnp.log(gone)


def each_block(length, body):
    def step(number, carry):
        body(pl.ds(pl.multiple_of(number * ROWS, ROWS), ROWS))
        return carry

    lax.fori_loop(0, length // ROWS, step, 0)


class Block:
    def __init__(self, length, order, place, gain_row, entry, qkv, logs, attended, after, leave):
        self.length, self.order, self.place, self.gain_row = length, order, place, gain_row
        self.entry, self.qkv, self.logs, self.attended = entry, qkv, logs, attended
        self.after, self.leave = after, leave


def attend(block, pump):
    length = block.length

    def pair_step(pair, carry):
        lanes = [pl.ds(pl.multiple_of(part * 512 + pair * 128, 128), 128) for part in range(3)]
        for first in range(0, length, ROWS):
            span = first + ROWS
            q_pair = block.qkv[first:span, lanes[0]] * jnp.asarray(0.125, jnp.bfloat16)
            outs = []
            for head in range(2):
                q_head = jnp.where(head_mask(q_pair.shape, head), q_pair, jnp.zeros_like(q_pair))
                scores = scores_t(block.qkv[0:span, lanes[1]], q_head, first)
                peak = jnp.max(scores, axis=0, keepdims=True)
                raised = jnp.exp(scores - peak)
                total = jnp.sum(raised, axis=0, keepdims=True)
                weights = (raised * (1.0 / total)).astype(jnp.bfloat16)
                block.logs[pair, head : head + 1, first:span] = peak + jnp.log(total)
                outs.append(product_tn(weights, block.qkv[0:span, lanes[2]]))
            merged = jnp.where(head_mask(outs[0].shape, 0), outs[0], outs[1])
            block.attended[first:span, lanes[0]] = merged.astype(jnp.bfloat16)
        pump(pair)
        return carry

    lax.fori_loop(0, 4, pair_step, 0)


def attend_back(block, upstream, grad_qkv, key_sum, value_sum, pump):
    length = block.length

    def pair_step(pair, carry):
        lanes = [pl.ds(pl.multiple_of(part * 512 + pair * 128, 128), 128) for part in range(3)]
        for first in reversed(range(0, length, ROWS)):
            span = first + ROWS
            q_pair = block.qkv[first:span, lanes[0]] * jnp.asarray(0.125, jnp.bfloat16)
            up_pair = upstream[first:span, lanes[0]]
            queries, keys, values = [], [], []
            for head in range(2):
                keep = head_mask(q_pair.shape, head)
                q_head = jnp.where(keep, q_pair, jnp.zeros_like(q_pair))
                up_head = jnp.where(keep, up_pair, jnp.zeros_like(up_pair))
                k_pair = block.qkv[0:span, lanes[1]]
                scores = scores_t(k_pair, q_head, first)
                weights = jnp.exp(scores - block.logs[pair, head : head + 1, first:span])
                grad_weights = product_nt(block.qkv[0:span, lanes[2]], up_head)
                values.append(product(weights.astype(jnp.bfloat16), up_head))
                inner_sum = jnp.sum(weights * grad_weights, axis=0, keepdims=True)
                grad_scores = (weights * (grad_weights - inner_sum)).astype(jnp.bfloat16)
                keys.append(product(grad_scores, q_head))
                queries.append(product_tn(grad_scores, k_pair))
            merged = jnp.where(head_mask(queries[0].shape, 0), queries[0], queries[1]) * 0.125
            grad_qkv[first:span, lanes[0]] = merged.astype(jnp.bfloat16)
            if span == length:
                key_sum[0:span, :] = keys[0] + keys[1]
                value_sum[0:span, :] = values[0] + values[1]
            else:
                key_sum[0:span, :] = key_sum[0:span, :] + (keys[0] + keys[1])
                value_sum[0:span, :] = value_sum[0:span, :] + (values[0] + values[1])
        grad_qkv[0:length, lanes[1]] = key_sum[0:length, :].astype(jnp.bfloat16)
        grad_qkv[0:length, lanes[2]] = value_sum[0:length, :].astype(jnp.bfloat16)
        pump(pair)
        return carry

    lax.fori_loop(0, 4, pair_step, 0)


def put_rows(blocks, rows, value):
    blocks[pl.ds(rows.start // 16, value.shape[0] // 16)] = value.reshape(-1, 16, value.shape[1])


def whole_rows(blocks, length):
    return blocks[0 : length // 16].reshape(length, blocks.shape[2])


def block_run(block, matrix, gains, pumps):
    place = block.place
    gain_attn = gains[block.gain_row : block.gain_row + 1, :]
    gain_ffn = gains[block.gain_row + 1 : block.gain_row + 2, :]

    def project(rows):
        value = block.entry(rows)
        normed = (value * root_scale(value) * gain_attn).astype(jnp.bfloat16)
        for part in range(3):
            block.qkv[rows, 512 * part : 512 * part + 512] = product(normed, matrix(place + part)).astype(
                jnp.bfloat16
            )

    each_block(block.length, project)
    pumps[0]()
    attend(block, pumps[1])
    pumps[2]()

    def feed(rows):
        after = block.entry(rows) + product(block.attended[rows, :], matrix(place + 3))
        block.after[rows, :] = after
        normed = (after * root_scale(after) * gain_ffn).astype(jnp.bfloat16)
        total = jnp.zeros_like(after)
        for part in range(4):
            inner = product(normed, matrix(place + 4 + part))
            active = gelu_both(inner)[0].astype(jnp.bfloat16)
            total = total + product(active, matrix(place + 8 + part))
        block.leave[rows, :] = after + total
        pumps[3](rows.start // ROWS)

    each_block(block.length, feed)


def block_back(block, grad, matrix, gains, gain_sums, temps, put, pumps):
    length, order, place = block.length, block.order, block.place
    gain_attn = gains[block.gain_row : block.gain_row + 1, :]
    gain_ffn = gains[block.gain_row + 1 : block.gain_row + 2, :]
    turned, grad_inner, branch, turned_norm, key_sum, value_sum = temps
    grad_low, grad_qkv, upstream = branch, grad_inner, block.attended
    all_rows = pl.ds(0, length)

    def down(part):
        def rows_step(rows):
            low = grad[rows, :].astype(jnp.bfloat16)
            columns = pl.ds(pl.multiple_of(part * 512, 512), 512)
            after = block.after[rows, :]
            normed = (after * root_scale(after) * gain_ffn).astype(jnp.bfloat16)
            active, slope = gelu_both(product(normed, matrix(place + 4 + part)))
            turned[:, rows] = turn(active)
            grad_inner[rows, columns] = (product_nt(low, matrix(place + 8 + part)) * slope).astype(jnp.bfloat16)

        each_block(length, rows_step)

    def low_step(rows):
        put_rows(grad_low, rows, grad[rows, :].astype(jnp.bfloat16))

    each_block(length, low_step)

    def down_step(part, carry):
        down(part)
        put(order[0] + part, lambda half: product(turned[half, all_rows], whole_rows(grad_low, length)))
        pumps[0](part)
        return carry

    lax.fori_loop(0, 4, down_step, 0)

    def middle(rows):
        after = block.after[rows, :]
        scale = root_scale(after)
        turned_norm[:, rows] = turn(after * scale * gain_ffn)
        turned[:, rows] = turn(block.attended[rows, :])
        total = jnp.zeros_like(after)
        for part in range(4):
            total = total + product_nt(
                grad_inner[rows, 512 * part : 512 * part + 512], matrix(place + 4 + part)
            )
        back, gain_part = norm_back(after, scale, gain_ffn, total)
        row = block.gain_row + 1
        gain_sums[row : row + 1, :] = gain_sums[row : row + 1, :] + gain_part
        grad_after = grad[rows, :] + back
        grad[rows, :] = grad_after
        low = grad_after.astype(jnp.bfloat16)
        put_rows(branch, rows, low)
        upstream[rows, :] = product_nt(low, matrix(place + 3)).astype(jnp.bfloat16)

    each_block(length, middle)

    def up_step(part, carry):
        columns = pl.ds(pl.multiple_of(part * 512, 512), 512)
        put(order[1] + part, lambda half: product(turned_norm[half, all_rows], grad_inner[all_rows, columns]))
        pumps[1](part)
        return carry

    lax.fori_loop(0, 4, up_step, 0)
    put(order[2], lambda half: product(turned[half, all_rows], whole_rows(branch, length)))
    pumps[3]()
    attend_back(block, upstream, grad_qkv, key_sum, value_sum, pumps[2])

    def enter(rows):
        value = block.entry(rows)
        scale = root_scale(value)
        turned_norm[:, rows] = turn(value * scale * gain_attn)
        total = jnp.zeros_like(value)
        for part in range(3):
            total = total + product_nt(grad_qkv[rows, 512 * part : 512 * part + 512], matrix(place + part))
        back, gain_part = norm_back(value, scale, gain_attn, total)
        row = block.gain_row
        gain_sums[row : row + 1, :] = gain_sums[row : row + 1, :] + gain_part
        grad[rows, :] = grad[rows, :] + back

    each_block(length, enter)

    def qkv_step(part, carry):
        columns = pl.ds(pl.multiple_of(part * 512, 512), 512)
        put(order[3] + part, lambda half: product(turned_norm[half, all_rows], grad_qkv[all_rows, columns]))
        return carry

    lax.fori_loop(0, 3, qkv_step, 0)


def total_of(value):
    return jnp.sum(jnp.sum(value, axis=1, keepdims=True), axis=0, keepdims=True)


class Reducer:
    pairs = 13
    offsets = (1, 2, 4, 6, 8)
    gaps = ((11, 4),)
    last_tick = pairs + sum(count for _, count in gaps) + offsets[-1]

    def __init__(self, place, own_far, other_far, pair_copy, beside, side, tower, refs):
        self.dp, self.seq, self.z, self.core = place
        self.across, self.along = self.seq % 2, self.seq // 2
        self.own_far, self.other_far, self.pair_copy = own_far, other_far, pair_copy
        self.beside, self.side, self.tower = beside, side, tower
        (
            self.own, self.other, self.one, self.two, self.three, self.final, self.square,
            self.b1_out, self.b1_in, self.b2_out, self.b2_in, self.c_out, self.c_in, self.d_out, self.d_in,
            self.b1_unit_out, self.b1_unit_in, self.b2_unit_out, self.b2_unit_in,
            self.c_unit_out, self.c_unit_in, self.d_unit_out, self.d_unit_in,
            self.l_sem, self.b1_send, self.b1_recv, self.b2_send, self.b2_recv,
            self.c_send, self.c_recv, self.d_send, self.d_recv,
        ) = refs[:32]
        self.lane = lax.broadcasted_iota(jnp.int32, (8, 128), 1)
        self.square[...] = jnp.zeros_like(self.square)

    def loads(self, pair):
        two = pl.ds(pair * 2, 2)
        return [
            pltpu.make_async_copy(self.own_far.at[two], self.own, self.l_sem.at[0]),
            pltpu.make_async_copy(self.other_far.at[two], self.other, self.l_sem.at[1]),
        ]

    def first_copies(self, pair, order):
        tile, slot, peer = pair * 2 + order, pair % 3, self.beside[order]
        send, recv = self.b1_send, self.b1_recv
        return [
            remote(self.b1_out.at[slot, order], self.b1_in.at[tile], send.at[0, slot, order], recv.at[0, tile], peer),
            remote(
                self.b1_unit_out.at[slot, order], self.b1_unit_in.at[tile], send.at[1, slot, order], recv.at[1, tile], peer
            ),
        ]

    def second_copies(self, pair, order):
        tile, slot, peer = pair * 2 + order, pair % 3, self.beside[1 - order]
        send, recv = self.b2_send, self.b2_recv
        return [
            remote(self.b2_out.at[slot, order], self.b2_in.at[tile], send.at[0, slot, order], recv.at[0, tile], peer),
            remote(
                self.b2_unit_out.at[slot, order], self.b2_unit_in.at[tile], send.at[1, slot, order], recv.at[1, tile], peer
            ),
        ]

    def tower_copies(self, pair, j):
        two, slot, peer = pl.ds(pair * 2, 2), pair % 3, self.tower[j]
        send, recv = self.c_send, self.c_recv
        return [
            remote(self.c_out.at[slot, j], self.c_in.at[j, two], send.at[0, slot, j], recv.at[0, j, pair], peer),
            remote(self.c_unit_out.at[slot, j], self.c_unit_in.at[j, pair], send.at[1, slot, j], recv.at[1, j, pair], peer),
        ]

    def share_copies(self, pair, j):
        two, slot, peer = pl.ds(pair * 2, 2), pair % 3, self.side[j]
        send, recv = self.d_send, self.d_recv
        return [
            remote(self.d_out.at[slot], self.d_in.at[j, two], send.at[0, slot, j], recv.at[0, j, pair], peer),
            remote(self.d_unit_out.at[slot], self.d_unit_in.at[j, pair], send.at[1, slot, j], recv.at[1, j, pair], peer),
        ]

    def after_sends(self, pair, copies, count):
        @pl.when(pair >= 3)
        def _():
            for number in range(count):
                for copy in copies(pair - 3, number):
                    copy.wait_send()

    def load(self, pair):
        for order in range(2):
            self.pair_copy(pair * 2 + order).wait_recv()
        for copy in self.loads(pair):
            copy.start()

    def send_first(self, pair):
        for copy in self.loads(pair):
            copy.wait()
        self.after_sends(pair, self.first_copies, 2)
        slot, kept = pair % 3, pair % 2
        for order in range(2):

            units = jnp.zeros((8, 128), jnp.float32)
            for block in range(8):
                floor, line = block // 2, block % 2
                if order == 0:
                    mine = (order, floor, line, self.across)
                    away = (order, floor, line, 1 - self.across)
                else:
                    mine = (order, floor, self.along, line)
                    away = (order, floor, 1 - self.along, line)
                self.one[kept, order, block] = self.own[mine] + self.other[mine]
                coded, unit = encode(self.own[away] + self.other[away])
                self.b1_out[slot, order, block] = coded
                units = jnp.where(self.lane == block, unit, units)
            self.b1_unit_out[slot, order] = units
            for copy in self.first_copies(pair, order):
                copy.start()

    def send_second(self, pair):
        slot, kept = pair % 3, pair % 2
        self.after_sends(pair, self.second_copies, 2)
        for order in range(2):
            for copy in self.first_copies(pair, order):
                copy.wait_recv()
            tile = pair * 2 + order
            got = self.b1_unit_in[tile]
            keep = self.along if order == 0 else self.across

            units = jnp.zeros((8, 128), jnp.float32)
            for floor in range(4):
                stay, leave = floor * 2 + keep, floor * 2 + 1 - keep
                even, odd = got[:, 2 * floor : 2 * floor + 1], got[:, 2 * floor + 1 : 2 * floor + 2]
                self.two[kept, order, floor] = self.one[kept, order, stay] + decode(
                    self.b1_in[tile, stay], jnp.where(keep == 0, even, odd)
                )
                coded, unit = encode(
                    self.one[kept, order, leave] + decode(self.b1_in[tile, leave], jnp.where(keep == 0, odd, even))
                )
                self.b2_out[slot, order, floor] = coded
                units = jnp.where(self.lane == floor, unit, units)
            self.b2_unit_out[slot, order] = units
            for copy in self.second_copies(pair, order):
                copy.start()

    def send_tower(self, pair):
        slot, kept = pair % 3, pair % 2
        self.after_sends(pair, self.tower_copies, 3)
        for order in range(2):
            for copy in self.second_copies(pair, order):
                copy.wait_recv()

        for order in range(2):
            tile = pair * 2 + order
            got = self.b2_unit_in[tile]
            for floor in range(4):
                self.two[kept, order, floor] = self.two[kept, order, floor] + decode(
                    self.b2_in[tile, floor], got[:, floor : floor + 1]
                )
            self.three[kept, order] = self.two[kept, order, self.z]
        for j in range(3):
            units = jnp.zeros((8, 128), jnp.float32)
            for order in range(2):
                coded, unit = encode(self.two[kept, order, (self.z + j + 1) % 4])
                self.c_out[slot, j, order] = coded
                units = jnp.where(self.lane == order, unit, units)
            self.c_unit_out[slot, j] = units
        for j in range(3):
            for copy in self.tower_copies(pair, j):
                copy.start()

    def send_share(self, pair):
        slot = pair % 3
        self.after_sends(pair, self.share_copies, 3)
        for j in range(3):
            for copy in self.tower_copies(pair, j):
                copy.wait_recv()
        units = jnp.zeros((8, 128), jnp.float32)
        for order in range(2):
            tile = pair * 2 + order
            total = self.three[pair % 2, order]
            for j in range(3):
                total = total + decode(self.c_in[j, tile], self.c_unit_in[j, pair][:, order : order + 1])
            self.final[tile] = total
            self.square[...] = self.square[...] + total * total
            coded, unit = encode(total)
            self.d_out[slot, order] = coded
            units = jnp.where(self.lane == order, unit, units)
        self.d_unit_out[slot] = units
        for j in range(3):
            for copy in self.share_copies(pair, j):
                copy.start()

    def tick(self, number):
        stages = (self.load, self.send_first, self.send_second, self.send_tower, self.send_share)
        for offset, stage_of in reversed(list(zip(self.offsets, stages))):
            turn_of = jnp.int32(number) - offset
            pair = turn_of
            fits = turn_of >= 0
            for first, count in self.gaps:
                pair = pair - jnp.minimum(jnp.maximum(turn_of - first + 1, 0), count)
                fits = jnp.logical_and(fits, jnp.logical_or(turn_of < first, turn_of >= first + count))
            fits = jnp.logical_and(fits, pair < self.pairs)

            @pl.when(fits)
            def _():
                stage_of(pair)

    def ticks(self, start, stop):
        def body(number, carry):
            self.tick(number)
            return carry

        lax.fori_loop(start, stop, body, 0)

    def collect(self, source_ref, pair_ref, parity_ref, stage):
        def arrive(pair, carry):
            for j in range(3):
                for copy in self.share_copies(pair, j):
                    copy.wait_recv()
            return carry

        lax.fori_loop(0, self.pairs, arrive, 0)
        for order in range(self.pairs * 2 - 4, self.pairs * 2):
            self.pair_copy(order).wait_send()

        def step(slot, carry):
            tile = source_ref[slot]
            places_of = [self.seq] + [peer[1] for peer in self.side]
            for number, quarter in enumerate(places_of):
                if number == 0:
                    value = self.final[tile]
                else:
                    units = self.d_unit_in[number - 1, pair_ref[slot]]
                    unit = jnp.where(parity_ref[slot] > 0, units[:, 1:2], units[:, 0:1])
                    value = decode(self.d_in[number - 1, tile], unit)
                stage[slot // 8, slot % 8 // 2, slot % 2, quarter // 2, quarter % 2] = value
            return carry

        lax.fori_loop(0, source_ref.shape[0], step, 0)

    def folded_square(self):
        square, width = self.square[...], self.square.shape[1]
        folded = jnp.zeros((8, 128), jnp.float32)
        for r in range(2):
            for w in range(width // 128):
                folded = folded + square[8 * r : 8 * r + 8, 128 * w : 128 * w + 128]
        return folded

    def finish(self):
        for pair in range(self.pairs - 3, self.pairs):
            for order in range(2):
                for copy in self.first_copies(pair, order) + self.second_copies(pair, order):
                    copy.wait_send()
            for j in range(3):
                for copy in self.tower_copies(pair, j) + self.share_copies(pair, j):
                    copy.wait_send()


class Sums:
    def __init__(self, place, column, side, small, refs):
        self.dp, self.seq, _, _ = place
        self.column, self.side = column, side
        self.small = small
        self.small_dp, self.small_seq, self.square_dp, self.square_seq, self.sems = refs[32:]

    def copies(self, which):
        sends, recvs = self.sems[2 * which], self.sems[2 * which + 1]
        if which == 0:
            return [remote(self.small, self.small_dp.at[self.dp], sends.at[j], recvs.at[j], self.column[j]) for j in range(7)]
        if which == 1:
            spot = self.small_seq.at[self.seq]
            return [remote(spot, spot, sends.at[j], recvs.at[j], self.side[j]) for j in range(3)]
        if which == 2:
            spot = self.square_dp.at[self.dp]
            return [remote(spot, spot, sends.at[j], recvs.at[j], self.column[j]) for j in range(7)]
        spot = self.square_seq.at[self.seq]
        return [remote(spot, spot, sends.at[j], recvs.at[j], self.side[j]) for j in range(3)]

    def start(self, which):
        for copy in self.copies(which):
            copy.start()

    def arrive(self, which):
        for copy in self.copies(which):
            copy.wait_recv()

    def start_small(self):
        self.start(0)
        self.small_dp[self.dp] = self.small[...]

    def pass_small(self):
        self.arrive(0)
        total = self.small_dp[0]
        for j in range(1, 8):
            total = total + self.small_dp[j]
        self.small_seq[self.seq] = total
        self.start(1)

    def start_squares(self, folded):
        self.square_dp[self.dp] = folded
        self.start(2)

    def pass_squares(self):
        self.arrive(2)
        total = self.square_dp[0]
        for j in range(1, 8):
            total = total + self.square_dp[j]
        self.square_seq[self.seq] = total
        self.start(3)

    def results(self):
        self.arrive(1)
        self.arrive(3)
        small = (self.small_seq[0] + self.small_seq[1]) + (self.small_seq[2] + self.small_seq[3])
        return small, (self.square_seq[0] + self.square_seq[1]) + (self.square_seq[2] + self.square_seq[3])

    def finish(self):
        for which in range(4):
            for copy in self.copies(which):
                copy.wait_send()


GRAD_ORDER = (20, 21, 22, 23, 16, 17, 18, 19, 15, 12, 13, 14, 24, 8, 9, 10, 11, 4, 5, 6, 7, 3, 0, 1, 2, 25)


def step_kernel(
    micro_count, lengths_ref, owner_ref, master_ref, chars_ref, targets_ref, segs_ref, gains_ref,
    own_far, other_far, reduced_out, small_out, square_out, owned_out,
    weights, qkv, logs, attended, after, leave, grad,
    seg_entry, seg_qkv, seg_logs, seg_attended, seg_after, seg_leave, seg_grad,
    turned, grad_inner, branch, turned_norm, key_sum, value_sum, head_grad, small_ref,
    slots, ids_in, ids_row, ids_col, source_ref, pair_ref, parity_ref, owned_ref, stage, stage_sem, counts, count_send, count_recv, i_send, i_recv, g_send, g_recv, out_sem,
    p_send, p_recv, z_send, z_recv, s_send, s_recv, d_send, d_recv, c_send, c_recv,
    reduce_refs,
):
    dp, seq, z, core = places()
    across, along = seq % 2, seq // 2
    length, width = leave.shape
    segments = seg_entry.shape[0]
    vocab = width // 2
    root_width = width ** (-0.5)
    groups = weights.shape[0] // 2
    sibling = (z * 2 + 1 - core, seq)
    beside = [along * 2 + 1 - across, (1 - along) * 2 + across]
    side = [seq_peer(seq, j) for j in (1, 2, 3)]
    column = [((dp + j) % 8, seq) for j in range(1, 8)]
    tower = [((z + j) % 4 * 2 + core, seq) for j in (1, 2, 3)]
    meet([(dp, peer) for peer in side] + column)

    held = master_ref.shape[0]
    all_ids = (chars_ref, targets_ref, segs_ref)

    def ids_copy(j, which):
        return remote(
            all_ids[which].at[side[j]], ids_in.at[which, seq], i_send.at[j, which], i_recv.at[j, which], (dp, side[j])
        )

    def peer_copy(j):
        return remote(
            branch.at[pl.ds(held * side[j], held)], slots.at[pl.ds(held * seq, held)], p_send.at[j], p_recv.at[j], (dp, side[j])
        )

    def tower_copy(group, j):
        spot = weights.at[pl.ds(group * 2, 2), z, core, seq]
        return remote(spot, spot, z_send.at[j, group], z_recv.at[j, group], tower[j])

    def side_copy(group, way):
        spot = weights.at[pl.ds(group * 2, 2), :, core, seq]
        return remote(spot, spot, s_send.at[way, group], s_recv.at[way, group], (dp, beside[way]))

    def corner_copy(group, way):
        spot = weights.at[group * 2 + way, :, core, beside[way]]
        return remote(spot, spot, d_send.at[way, group], d_recv.at[way, group], (dp, beside[1 - way]))

    def core_copy(group):
        spot = weights.at[pl.ds(group * 2, 2), :, core]
        return remote(spot, spot, c_send.at[group], c_recv.at[group], sibling)

    def pick(group):
        for number in range(2):
            place = group * 2 + number
            late = (place > 13).astype(jnp.int32)
            tile = jnp.where(place == 0, 25, jnp.where(place == 13, 24, place - 1 - late))
            weights[place, z, core, seq] = slots[owner_ref[tile]]
        for j in range(3):
            tower_copy(group, j).start()

    def widen(group):
        for j in range(3):
            tower_copy(group, j).wait_recv()
        for way in range(2):
            side_copy(group, way).start()

    def corner(group):
        for way in range(2):
            side_copy(group, way).wait_recv()
        for way in range(2):
            corner_copy(group, way).start()

    def share(group):
        for way in range(2):
            corner_copy(group, way).wait_recv()
        core_copy(group).start()

    stages = (pick, widen, corner, share)

    def tick(number):
        for order, stage_of in enumerate(stages):
            group = jnp.int32(number) - LAG * order

            @pl.when(jnp.logical_and(group >= 0, group < groups))
            def _():
                stage_of(group)

    def ticks(start, stop):
        def body(number, carry):
            tick(number)
            return carry

        lax.fori_loop(start, stop, body, 0)

    def arrived(first, last):
        def body(group, carry):
            core_copy(group).wait_recv()
            return carry

        lax.fori_loop(first, last, body, 0)

    for which in range(3):
        ids_in[which, seq] = all_ids[which][seq]
        for j in range(3):
            ids_copy(j, which).start()

    def lower(slot, carry):
        value = master_ref[slot].astype(jnp.bfloat16)
        for quarter in range(4):
            branch[quarter * held + slot] = value[16 * quarter : 16 * quarter + 16]
        return carry

    lax.fori_loop(0, held, lower, 0)
    for j in (2, 0, 1):
        peer_copy(j).start()
    slots[pl.ds(held * seq, held)] = branch[pl.ds(held * seq, held)]
    for j in range(3):
        peer_copy(j).wait_recv()
    ticks(0, START)

    def matrix(place):
        return weights[place].reshape(width, width)

    def matrix_half(which):
        return weights[0, 2 * which : 2 * which + 2].reshape(vocab, width)

    def count_copy(j):
        return remote(counts.at[dp], counts.at[dp], count_send.at[j], count_recv.at[j], column[j])

    def own_copy(order):
        return pltpu.make_async_copy(stage.at[order % 4, :, core], own_far.at[order], stage_sem.at[order % 2])

    def pair_copy(order):
        return remote(
            stage.at[order % 4, :, 1 - core], other_far.at[order], g_send.at[order % 4], g_recv.at[order], sibling
        )

    def put(order, half_of):
        @pl.when(jnp.int32(order) >= 4)
        def _():
            pair_copy(order - 4).wait_send()

        @pl.when(jnp.logical_and(jnp.int32(order) >= 1, jnp.int32(order) != 22))
        def _():
            own_copy(order - 1).wait()

        for half in range(2):
            value = half_of(pl.ds(256 * half, 256))
            stage[order % 4, 2 * half : 2 * half + 2] = value.reshape(2, 2, 2, 2, 16, width)
        own_copy(order).start()
        pair_copy(order).start()

    small_ref[...] = jnp.zeros_like(small_ref)
    for which in range(3):
        for j in range(3):
            ids_copy(j, which).wait_recv()
        for peer in range(4):
            ids_row[which : which + 1, 256 * peer : 256 * peer + 256] = ids_in[which, peer]
    for slot in range(held):
        zero = jnp.int32(0)
        source, pair, parity, owned = zero, zero, zero, zero
        for order, tile in enumerate(GRAD_ORDER):
            here = (owner_ref[tile] == held * seq + slot).astype(jnp.int32)
            source, pair, parity = source + here * order, pair + here * (order // 2), parity + here * (order % 2)
            owned = owned + here
        source_ref[slot] = jnp.minimum(source, 2 * groups - 1)
        pair_ref[slot] = jnp.minimum(pair, groups - 1)
        parity_ref[slot], owned_ref[slot] = parity, owned
    ids_row[3:8, :] = jnp.zeros((5, length), jnp.int32)
    ids_col[...] = ids_row[...].astype(jnp.float32).T
    length_one = lengths_ref[seq, 0]
    temps = (turned, grad_inner, branch, turned_norm, key_sum, value_sum)

    def hot_rows(rows, which, offset, count):
        ids = ids_col[rows, which : which + 1] + float(offset)
        lane = lax.broadcasted_iota(jnp.int32, (ROWS, count), 1).astype(jnp.float32)
        return (ids == lane).astype(jnp.bfloat16)

    def hot_turned(which, offset, count):
        ids = ids_row[which : which + 1, :] + offset
        line = lax.broadcasted_iota(jnp.int32, (count, length), 0)
        return (ids == line).astype(jnp.float32)

    arrived(0, 2)

    def embed(rows):
        return product(hot_rows(rows, 0, 0, vocab), matrix_half(0))

    char = Block(length, (13, 17, 21, 22), 1, 0, embed, qkv, logs, attended, after, leave)
    seg = Block(
        segments, (0, 4, 8, 9), 14, 2, lambda rows: seg_entry[rows, :],
        seg_qkv, seg_logs, seg_attended, seg_after, seg_leave,
    )
    tick(START)
    block_run(
        char,
        matrix,
        gains_ref,
        (
            lambda: tick(START + 1),
            lambda pair: tick(START + 2 + pair),
            lambda: arrived(2, 7),
            lambda number: tick(START + 6 + number),
        ),
    )
    ticks(START + 10, groups + LAG * (len(stages) - 1))

    def valid_rows(rows):
        line = lax.broadcasted_iota(jnp.int32, (ROWS, 1), 0) + rows.start
        return (line < length_one).astype(jnp.float32)

    def boundary(rows):
        low = leave[rows, :].astype(jnp.bfloat16)
        reach = jnp.tanh(product(low, matrix(13)))
        logit = jnp.sum(reach * gains_ref[5:6, :], axis=1, keepdims=True) * root_width
        return low, reach, 1.0 / (1.0 + jnp.exp(-logit))

    def soft_step(number, total):
        rows = pl.ds(pl.multiple_of(number * ROWS, ROWS), ROWS)
        return total + jnp.sum(valid_rows(rows) * boundary(rows)[2], axis=0, keepdims=True)

    soft_local = lax.fori_loop(0, length // ROWS, soft_step, jnp.zeros((1, 1), jnp.float32))
    line = lax.broadcasted_iota(jnp.int32, (8, 128), 0)
    length_float = length_one.astype(jnp.float32)
    counts[dp] = jnp.where(line == 0, soft_local, jnp.where(line == 1, length_float, 0.0))
    for j in range(7):
        count_copy(j).start()

    pool = hot_turned(2, 1, segments)
    amounts = jnp.sum(pool, axis=1, keepdims=True)
    divisor = jnp.maximum(amounts, 1.0)
    seg_entry[...] = product(pool.astype(jnp.bfloat16), leave[...].astype(jnp.bfloat16)) / divisor
    arrived(7, groups)
    block_run(seg, matrix, gains_ref, (lambda: None, lambda pair: None, lambda: None, lambda number: None))

    for j in range(7):
        count_copy(j).wait_recv()
    total = counts[0]
    for j in range(1, 8):
        total = total + counts[j]
    soft_count, count_all = total[0:1, 0:1], total[1:2, 0:1]

    def head(number, carry):
        ce, head_sum = carry
        rows = pl.ds(pl.multiple_of(number * ROWS, ROWS), ROWS)
        lift = hot_rows(rows, 2, 0, segments)
        merged = leave[rows, :] + product(lift, seg_leave[...].astype(jnp.bfloat16))
        scale = root_scale(merged)
        gain = gains_ref[4:5, :]
        final_low = (merged * scale * gain).astype(jnp.bfloat16)
        table = matrix_half(1)
        logits = product_nt(final_low, table)
        peak = jnp.max(logits, axis=1, keepdims=True)
        log_total = peak + jnp.log(jnp.sum(jnp.exp(logits - peak), axis=1, keepdims=True))
        target = hot_rows(rows, 1, 0, vocab).astype(jnp.float32)
        picked = jnp.sum(logits * target, axis=1, keepdims=True)
        valid = valid_rows(rows)
        ce = ce + jnp.sum(valid * (log_total - picked), axis=0, keepdims=True)
        share = valid / (micro_count * count_all)
        grad_logits = (jnp.exp(logits - log_total) - target) * share
        head_sum = head_sum + product(turn(grad_logits), final_low)
        back, gain_part = norm_back(merged, scale, gain, product(grad_logits.astype(jnp.bfloat16), table))
        small_ref[4:5, :] = small_ref[4:5, :] + gain_part
        grad[rows, :] = back
        return ce, head_sum

    ce_local, head_sum = lax.fori_loop(
        0, length // ROWS, head, (jnp.zeros((1, 1), jnp.float32), jnp.zeros((vocab, width), jnp.float32))
    )
    head_grad[...] = head_sum
    seg_grad[...] = exact_product(hot_turned(2, 0, segments).astype(jnp.bfloat16), grad[...])
    def sent(group, carry):
        for j in range(3):
            tower_copy(group, j).wait_send()
        for way in range(2):
            side_copy(group, way).wait_send()
            corner_copy(group, way).wait_send()
        core_copy(group).wait_send()
        return carry

    lax.fori_loop(0, groups, sent, 0)
    for j in range(3):
        peer_copy(j).wait_send()
    reducer = Reducer(
        places(), own_far, other_far, pair_copy, [(dp, peer) for peer in beside], [(dp, peer) for peer in side], tower, reduce_refs
    )
    block_back(
        seg, seg_grad, matrix, gains_ref, small_ref, temps, put,
        (lambda part: None, lambda part: reducer.tick(part), lambda pair: None, lambda: None),
    )

    seg_grad[...] = seg_grad[...] / divisor

    count_rest = count_all - soft_count
    slope = (digamma(soft_count + 1.0) - digamma(count_rest + 1.0) + LOG_ODDS) / (count_all * micro_count)

    def join(rows):
        low, reach, chance = boundary(rows)
        logit = valid_rows(rows) * slope * chance * (1.0 - chance)
        gain = gains_ref[5:6, :]
        small_ref[5:6, :] = small_ref[5:6, :] + jnp.sum(logit * reach, axis=0, keepdims=True) * root_width
        pre = (logit * gain * root_width * (1.0 - reach * reach)).astype(jnp.bfloat16)
        put_rows(branch, rows, pre)
        turned[:, rows] = turn(low)
        spread = exact_product(hot_rows(rows, 2, 1, segments), seg_grad[...])
        grad[rows, :] = (grad[rows, :] + spread) + product_nt(pre, matrix(13))

    each_block(length, join)
    put(12, lambda half: product(turned[half, :], whole_rows(branch, length)))
    block_back(
        char, grad, matrix, gains_ref, small_ref, temps, put,
        (
            lambda part: reducer.tick(4 + part),
            lambda part: None,
            lambda pair: reducer.ticks(8 + 2 * pair, 10 + 2 * pair),
            lambda: own_copy(21).wait(),
        ),
    )
    embed_grad = exact_product(hot_turned(0, 0, vocab).astype(jnp.bfloat16), grad[...])
    put(25, lambda half: embed_grad if half.start == 0 else head_grad[...])
    own_copy(25).wait()

    lane = lax.broadcasted_iota(jnp.int32, (1, width), 1)
    small_ref[6:7, :] = jnp.where(
        lane == seq,
        ce_local,
        jnp.where(lane == seq + 8, soft_local, jnp.where(lane == seq + 16, length_float, 0.0)),
    )
    for j in range(7):
        count_copy(j).wait_send()
    for which in range(3):
        for j in range(3):
            ids_copy(j, which).wait_send()
    sums = Sums(places(), column, [(dp, peer) for peer in side], small_ref, reduce_refs)
    sums.start_small()
    reducer.ticks(16, reducer.last_tick)
    sums.start_squares(reducer.folded_square())
    sums.pass_small()
    sums.pass_squares()
    reducer.collect(source_ref, pair_ref, parity_ref, stage)
    for slot in range(held):
        pltpu.make_async_copy(
            stage.at[slot // 8, slot % 8 // 2, slot % 2], reduced_out.at[slot], out_sem.at[slot]
        ).start()
    small_sum, square_sum = sums.results()
    small_out[...] = small_sum
    square_out[...] = square_sum

    def leaving(slot):
        return pltpu.make_async_copy(
            stage.at[slot // 8, slot % 8 // 2, slot % 2], reduced_out.at[slot], out_sem.at[slot]
        )

    for slot in range(held):
        owned_out[slot] = owned_ref[slot]
        leaving(slot).wait()
    sums.finish()
    reducer.finish()


def step_call(char_ids, targets, seg_ids, lengths, owner_slot, master, gains):
    held, rows, width = master.shape
    tile_count = owner_slot.shape[0]
    micro_count = char_ids.shape[0]
    seq_count, dp_count = lax.axis_size("seq"), lax.axis_size("dp")
    groups = tile_count // 2
    length = seq_count * char_ids.shape[2]
    segments = SEG_DEV * seq_count
    dma = pltpu.SemaphoreType.DMA
    vmem = pl.BlockSpec(memory_space=pltpu.VMEM)
    smem = pl.BlockSpec(memory_space=pltpu.SMEM)
    hbm = pl.BlockSpec(memory_space=pl.ANY)

    def full(*shape):
        return pltpu.VMEM(shape, jnp.float32)

    def half(*shape):
        return pltpu.VMEM(shape, jnp.bfloat16)

    def codes(*shape):
        return pltpu.VMEM(shape + (16, width), jnp.int16)

    def kept(count):
        return [
            half(count, 3 * width), full(4, 2, count), half(count, width), full(count, width),
            full(count, width), full(count, width),
        ]

    reduce_refs = [
        full(2, 4, 2, 2, 16, width), full(2, 4, 2, 2, 16, width),
        full(2, 2, 8, 16, width), full(2, 2, 4, 16, width), full(2, 2, 16, width), full(tile_count, 16, width), full(16, width),
        codes(3, 2, 8), codes(tile_count, 8), codes(3, 2, 4), codes(tile_count, 4),
        codes(3, 3, 2), codes(3, tile_count), codes(3, 2), codes(3, tile_count),
        full(3, 2, 8, 128), full(tile_count, 8, 128), full(3, 2, 8, 128), full(tile_count, 8, 128),
        full(3, 3, 8, 128), full(3, groups, 8, 128), full(3, 8, 128), full(3, groups, 8, 128),
        dma((2,)), dma((2, 3, 2)), dma((2, tile_count)), dma((2, 3, 2)), dma((2, tile_count)),
        dma((2, 3, 3)), dma((2, 3, groups)), dma((2, 3, 3)), dma((2, 3, groups)),
        full(dp_count, 8, width), full(seq_count, 8, width), full(dp_count, 8, 128), full(seq_count, 8, 128),
        [dma((7,)), dma((7,)), dma((3,)), dma((3,)), dma((7,)), dma((7,)), dma((3,)), dma((3,))],
    ]
    far = jax.ShapeDtypeStruct((tile_count, 4, 2, 2, 16, width), jnp.float32)
    return pl.pallas_call(
        functools.partial(step_kernel, micro_count),
        out_shape=(
            far, far, jax.ShapeDtypeStruct((held, 2, 2, 16, width), jnp.float32),
            jax.ShapeDtypeStruct((8, width), jnp.float32), jax.ShapeDtypeStruct((8, 128), jnp.float32),
            jax.ShapeDtypeStruct((held,), jnp.int32),
        ),
        in_specs=[smem] * 2 + [vmem] * 5,
        out_specs=(hbm,) * 3 + (vmem,) * 2 + (smem,),
        scratch_shapes=[half(tile_count, 4, 2, 4, 16, width)]
        + kept(length)
        + [full(segments, width)]
        + kept(segments)
        + [
            half(width, length), half(length, 4 * width), half(length // 16, 16, width), half(width, length),
            full(length, 128), full(length, 128), full(width // 2, width), full(8, width),
            half(seq_count * held, 16, width),
            pltpu.VMEM((3, 4, 1, length // 4), jnp.int32), pltpu.VMEM((8, length), jnp.int32), full(length, 8),
            pltpu.SMEM((held,), jnp.int32), pltpu.SMEM((held,), jnp.int32), pltpu.SMEM((held,), jnp.int32), pltpu.SMEM((held,), jnp.int32), full(4, 4, 2, 2, 2, 16, width), dma((2,)),
            full(dp_count, 8, 128), dma((7,)), dma((7,)), dma((3, 3)), dma((3, 3)),
            dma((4,)), dma((tile_count,)), dma((held,)),
            dma((3,)), dma((3,)), dma((3, groups)), dma((3, groups)),
            dma((2, groups)), dma((2, groups)), dma((2, groups)), dma((2, groups)),
            dma((groups,)), dma((groups,)), reduce_refs,
        ],
        name="step",
        compiler_params=pltpu.CompilerParams(
            collective_id=2, has_side_effects=True, vmem_limit_bytes=STEP_VMEM
        ),
    )(lengths, owner_slot, master, char_ids, targets, seg_ids, gains)[2:]


def finish_kernel(
    micro_count, step_ref, owned_ref, master_ref, first_ref, second_ref, reduced_ref, small_ref, square_ref,
    gains_ref, gain_first_ref, gain_second_ref,
    loss_out, norm_out, master_out, first_out, second_out, low_out, gains_out, gain_first_out, gain_second_out,
):
    small_sum = small_ref[...]
    gain_sum = small_sum[0:6, :]
    grad_norm = jnp.sqrt(total_of(square_ref[...]) + total_of(gain_sum * gain_sum))
    clip = jnp.minimum(1.0, CLIP_NORM / (grad_norm + 1e-06))
    steps = jnp.full((1, 1), step_ref[0], jnp.int32).astype(jnp.float32)
    corrections = [1.0 / (1.0 - jnp.exp(steps * math.log(beta))) for beta in (BETA_ONE, BETA_TWO)]

    def renew(param, moment_a, moment_b, grad_in, rate, decay):
        new_first = BETA_ONE * moment_a + (1.0 - BETA_ONE) * grad_in
        new_second = BETA_TWO * moment_b + (1.0 - BETA_TWO) * grad_in * grad_in
        move = (new_first * corrections[0]) / (jnp.sqrt(new_second * corrections[1]) + ADAM_EPS)
        return param - rate * (move + decay * param), new_first, new_second

    for number in range(master_ref.shape[0]):
        param, moment_a, moment_b = master_ref[number], first_ref[number], second_ref[number]
        new_param, new_first, new_second = renew(
            param, moment_a, moment_b, reduced_ref[number] * clip, RATE_TILES, WEIGHT_DECAY
        )
        keep = owned_ref[pl.program_id(0) * master_ref.shape[0] + number] > 0
        new_param = jnp.where(keep, new_param, param)
        master_out[number] = new_param
        first_out[number] = jnp.where(keep, new_first, moment_a)
        second_out[number] = jnp.where(keep, new_second, moment_b)
        low_out[number] = new_param.astype(jnp.bfloat16)

    @pl.when(pl.program_id(0) == 0)
    def _():
        gains_out[...], gain_first_out[...], gain_second_out[...] = renew(
            gains_ref[...], gain_first_ref[...], gain_second_ref[...], gain_sum * clip, RATE_GAINS, 0.0
        )
        loss = jnp.zeros((1, 1), jnp.float32)
        row = small_sum[6:7, :]
        lane = lax.broadcasted_iota(jnp.int32, row.shape, 1)
        for micro in range(micro_count):
            entropy, soft, count = (
                total_of(jnp.where(lane == micro + 8 * part, row, 0.0)) for part in range(3)
            )
            prior = -(
                log_gamma(count + 1.0)
                - log_gamma(soft + 1.0)
                - log_gamma(count - soft + 1.0)
                + soft * math.log(PRIOR_RATE)
                + (count - soft) * math.log(1.0 - PRIOR_RATE)
            )
            loss = loss + (entropy + prior) / count
        loss_out[0] = jnp.sum(loss) / micro_count
        norm_out[0] = jnp.sum(grad_norm)


def finish_call(micro_count, step_count, owned, master, first, second, reduced, small, squares, gains):
    held, rows, width = master.shape
    count = 5
    smem = pl.BlockSpec(memory_space=pltpu.SMEM)
    slots = pl.BlockSpec((held // count, rows, width), lambda i: (i, 0, 0))

    def whole(value):
        return pl.BlockSpec(value.shape, lambda i: (0,) * value.ndim)

    gain_spec = whole(gains[0])
    full = jax.ShapeDtypeStruct(master.shape, jnp.float32)
    gain_shape = jax.ShapeDtypeStruct(gains[0].shape, jnp.float32)
    one = jax.ShapeDtypeStruct((1,), jnp.float32)
    return pl.pallas_call(
        functools.partial(finish_kernel, micro_count),
        grid=(count,),
        out_shape=(
            one, one, full, full, full, jax.ShapeDtypeStruct(master.shape, jnp.bfloat16),
            gain_shape, gain_shape, gain_shape,
        ),
        in_specs=[smem] * 2 + [slots] * 4 + [whole(small), whole(squares)] + [gain_spec] * 3,
        out_specs=(smem, smem, slots, slots, slots, slots, gain_spec, gain_spec, gain_spec),
        name="finish",
    )(step_count, owned, master, first, second, reduced.reshape(master.shape), small, squares, *gains)


def body(
    char_ids,
    targets,
    seg_ids,
    lengths,
    owner_slot,
    step_count,
    master,
    tile_first,
    tile_second,
    gain_rows,
    gain_first,
    gain_second,
):
    micro_count = char_ids.shape[0]
    model_width = master.shape[2]
    slot_count = master.shape[0] * lax.axis_size("seq")
    if (micro_count, lax.axis_size("seq"), lax.axis_size("dp")) == (4, 4, 8):
        reduced, small, squares, owned = step_call(
            char_ids, targets, seg_ids, lengths, owner_slot, master, gain_rows
        )
        return finish_call(
            micro_count, step_count, owned, master, tile_first, tile_second, reduced, small, squares,
            (gain_rows, gain_first, gain_second),
        )
    tile_total = jnp.zeros((owner_slot.shape[0], model_width, model_width), jnp.float32)
    gain_total = jnp.zeros_like(gain_rows)
    loss_total = jnp.zeros((), jnp.float32)
    for micro in range(micro_count):
        tiles = gather_tiles(master, owner_slot)
        tile_part, gain_part, loss_part = micro_step(
            tiles,
            gain_rows,
            char_ids[micro, 0],
            targets[micro, 0],
            seg_ids[micro, 0],
            lengths[micro, 0],
            micro_count,
        )
        tile_total = tile_total + tile_part
        gain_total = gain_total + gain_part
        loss_total = loss_total + loss_part
    shard_total = reduce_tiles(tile_total, owner_slot, slot_count)
    gain_sum, square_sum = lax.psum((gain_total, jnp.sum(shard_total * shard_total)), ("dp", "seq"))
    grad_norm = jnp.sqrt(square_sum + jnp.sum(gain_sum * gain_sum))
    clip_factor = jnp.minimum(1.0, CLIP_NORM / (grad_norm + 1e-06))
    step_float = step_count[0].astype(jnp.float32)
    local_ids = lax.axis_index("seq") * master.shape[0] + jnp.arange(master.shape[0])
    owned = jnp.any(local_ids[:, None] == owner_slot[None, :], axis=1)[:, None, None]
    new_tiles, new_first, new_second = adam_step(
        master,
        tile_first,
        tile_second,
        shard_total * clip_factor,
        RATE_TILES,
        WEIGHT_DECAY,
        step_float,
    )
    master_new = jnp.where(owned, new_tiles, master)
    first_new = jnp.where(owned, new_first, tile_first)
    second_new = jnp.where(owned, new_second, tile_second)
    gains_new, gain_first_new, gain_second_new = adam_step(
        gain_rows, gain_first, gain_second, gain_sum * clip_factor, RATE_GAINS, 0.0, step_float
    )
    return (
        loss_total.reshape(1),
        grad_norm.reshape(1),
        master_new,
        first_new,
        second_new,
        master_new.astype(jnp.bfloat16),
        gains_new,
        gain_first_new,
        gain_second_new,
    )


def solution(mesh):
    return jax.shard_map(
        body,
        mesh=mesh,
        in_specs=(
            P(None, "dp", "seq"),
            P(None, "dp", "seq"),
            P(None, "dp", "seq"),
            P(None, "dp"),
            P(),
            P(),
            P("seq", "dp", None),
            P("seq", "dp", None),
            P("seq", "dp", None),
            P(),
            P(),
            P(),
        ),
        out_specs=(
            P(),
            P(),
            P("seq", "dp", None),
            P("seq", "dp", None),
            P("seq", "dp", None),
            P("seq", "dp", None),
            P(),
            P(),
            P(),
        ),
        check_vma=False,
    )
```
